32 devices in a mesh: blk: 4 (over x, core), docs: 8 (over z, y).
Axes of the slice: x: 2, y: 2, z: 4, core: 2. Of those that a mesh axis runs over, the one named last changes fastest.
Arguments:
- tokens: bfloat16 [8, 512, 1024], P('docs', 'blk'), may hold values from -6 to 6
- lengths: int32 [8], P('docs'), may hold values from 51 to 512, as said below
- positions: int32 [8, 512], P('docs', 'blk'), may hold values from 0 to 1022, as said below
- token_boxes: int32 [4, 8, 512], P(None, 'docs', 'blk'), may hold values from 0 to 1000, as said below
- ln1_gain: float32 [1024], replicated, may hold values from 0.5 to 1.5
- ln1_bias: float32 [1024], replicated, may hold values from -1.75 to 1.75
- w_query: bfloat16 [1024, 1024], replicated, may hold values from -0.1875 to 0.1875
- w_key: bfloat16 [1024, 1024], replicated, may hold values from -0.1875 to 0.1875
- w_value: bfloat16 [1024, 1024], replicated, may hold values from -0.1875 to 0.1875
- w_out: bfloat16 [1024, 1024], replicated, may hold values from -0.75 to 0.75
- rel_table: bfloat16 [128, 1024], replicated, may hold values from -6 to 6
- xbias_table: bfloat16 [64, 16], replicated, may hold values from -3 to 3
- ybias_table: bfloat16 [64, 16], replicated, may hold values from -3 to 3
- ln2_gain: float32 [1024], replicated, may hold values from 0.5 to 1.5
- ln2_bias: float32 [1024], replicated, may hold values from -1.75 to 1.75
- w_in: bfloat16 [1024, 4096], replicated, may hold values from -0.1875 to 0.1875
- b_in: float32 [4096], replicated, may hold values from -3 to 3
- w_down: bfloat16 [4096, 1024], replicated, may hold values from -0.09375 to 0.09375
- cotangent: bfloat16 [8, 512, 1024], P('docs', 'blk'), may hold values from -6 to 6
Outputs:
- block_out: bfloat16 [8, 512, 1024], P('docs', 'blk')
- grad_tokens: float32 [8, 512, 1024], P('docs', 'blk')
- grad_ln1_gain: float32 [1024], P('docs')
- grad_ln1_bias: float32 [1024], P('docs')
- grad_w_query: float32 [1024, 1024], P('docs')
- grad_w_key: float32 [1024, 1024], P('docs')
- grad_w_value: float32 [1024, 1024], P('docs')
- grad_w_out: float32 [1024, 1024], P('docs')
- grad_rel_table: float32 [128, 1024], P('docs')
- grad_xbias_table: float32 [64, 16], P('docs')
- grad_ybias_table: float32 [64, 16], P('docs')
- grad_ln2_gain: float32 [1024], P('docs')
- grad_ln2_bias: float32 [1024], P('docs')
- grad_w_in: float32 [1024, 4096], P('docs')
- grad_b_in: float32 [4096], P('docs')
- grad_w_down: float32 [4096, 1024], P('docs')
The draws below stay inside these ranges and needn't reach their ends.
Inputs may be any that keep to these rules, and one draw needn't show every extreme that they name: `lengths`: each document's count of text slots; its later slots are padding, never attended to as keys. `positions`: a document's first slot has position 0 and each next slot 0, 1 or 2 more. `token_boxes`: each box has x0 < x1 and y0 < y1.
All inputs are finite; a program needn't handle non-finite values.
Results may differ from the reference program's by a relative error of at most 0.035.
Values may be sent and summed in bfloat16 or wider, within the bound.
No kernel may reach another device: no remote copies, remote signals or barrier semaphores. Data moves between devices by JAX's collectives and lax.ppermute only.
A program may use at most 192 MiB of HBM per device.

```python
import math
import jax
import jax.numpy as jnp
from jax import lax

D = 1024
H = 16
HD = 64
FF = 4096
SLOTS = 512
NREL = 128
NBOX = 64
DOC_DEV = 1
DOCS = 8


def draw_lengths(key, part):
    low_len = max(1, SLOTS // 10)
    first_key, second_key = jax.random.split(key)
    drawn = jax.random.randint(first_key, (DOCS,), low_len, SLOTS + 1)
    chosen = jax.random.randint(second_key, (), 0, DOCS)
    slot_ids = jnp.arange(DOCS)
    drawn = jnp.where(slot_ids == chosen, SLOTS, drawn)
    drawn = jnp.where(slot_ids == (chosen + 1) % DOCS, low_len, drawn)
    return drawn.astype(jnp.int32)


def draw_positions(key, part):
    first_key, second_key = jax.random.split(key)
    step_sizes = jax.random.randint(first_key, (DOCS, SLOTS), 0, 3)
    chosen = jax.random.randint(second_key, (), 0, DOCS)
    doc_ids = jnp.arange(DOCS)[:, None]
    step_sizes = jnp.where(doc_ids == chosen, 2, step_sizes)
    is_first = jnp.arange(SLOTS)[None, :] == 0
    return jnp.cumsum(jnp.where(is_first, 0, step_sizes), axis=1).astype(jnp.int32)


def draw_token_boxes(key, part):
    split_keys = jax.random.split(key, 4)
    x_left = jax.random.randint(split_keys[0], (DOCS, SLOTS), 0, 1000)
    y_top = jax.random.randint(split_keys[1], (DOCS, SLOTS), 0, 1000)
    x_right = jnp.minimum(x_left + jax.random.randint(split_keys[2], (DOCS, SLOTS), 8, 121), 1000)
    y_bottom = jnp.minimum(y_top + jax.random.randint(split_keys[3], (DOCS, SLOTS), 8, 121), 1000)
    return jnp.stack([x_left, y_top, x_right, y_bottom]).astype(jnp.int32)


def level_of(stream_key, extent, cuts, low, top_value):
    gain = 1.0
    for axis_at, blocks in cuts:
        steps = jax.random.uniform(jax.random.fold_in(jax.random.fold_in(stream_key, 6), axis_at), (blocks,), jnp.float32, low / len(cuts), top_value / len(cuts))
        gain = gain * jnp.repeat(jnp.exp(steps), extent[axis_at] // blocks).reshape((-1,) + (1,) * (len(extent) - 1 - axis_at))
    return gain


def scatter_about(own_key, extent, spread, most, pieces=(), kind=jnp.bfloat16):
    gain = level_of(own_key, extent, pieces, -0.22, 0.18) if pieces else 1.0
    entries = jax.random.normal(own_key, extent, jnp.float32) * spread * gain
    return jnp.minimum(jnp.maximum(entries, -most), most).astype(kind)


def setup_inputs(seed: int = 0) -> dict:
    arg_keys = jax.random.split(jax.random.key(seed), 20)
    return {
        "tokens": scatter_about(arg_keys[0], (DOCS, SLOTS, D), 1.0, 6.0, ((0, 8), (1, 4))),
        "lengths": draw_lengths(jax.random.fold_in(arg_keys[19], 71), 0),
        "positions": draw_positions(jax.random.fold_in(arg_keys[19], 71), 0),
        "token_boxes": draw_token_boxes(jax.random.fold_in(arg_keys[19], 71), 0),
        "ln1_gain": jnp.clip(1.0 + 0.1 * jax.random.normal(arg_keys[4], (D,), jnp.float32), 0.5, 1.5),
        "ln1_bias": scatter_about(arg_keys[5], (D,), 0.3, 1.75, (), jnp.float32),
        "w_query": scatter_about(arg_keys[6], (D, D), D ** -0.5, 0.1875),
        "w_key": scatter_about(arg_keys[7], (D, D), D ** -0.5, 0.1875),
        "w_value": scatter_about(arg_keys[8], (D, D), D ** -0.5, 0.1875),
        "w_out": scatter_about(arg_keys[9], (D, D), (D // 16) ** -0.5, 0.75),
        "rel_table": scatter_about(arg_keys[10], (NREL, D), 1.0, 6.0),
        "xbias_table": scatter_about(arg_keys[11], (NBOX, H), 0.5, 3.0),
        "ybias_table": scatter_about(arg_keys[12], (NBOX, H), 0.5, 3.0),
        "ln2_gain": jnp.clip(1.0 + 0.1 * jax.random.normal(arg_keys[13], (D,), jnp.float32), 0.5, 1.5),
        "ln2_bias": scatter_about(arg_keys[14], (D,), 0.3, 1.75, (), jnp.float32),
        "w_in": scatter_about(arg_keys[15], (D, FF), D ** -0.5, 0.1875),
        "b_in": scatter_about(arg_keys[16], (FF,), 0.5, 3.0, (), jnp.float32),
        "w_down": scatter_about(arg_keys[17], (FF, D), FF ** -0.5, 0.09375),
        "cotangent": scatter_about(arg_keys[18], (DOCS, SLOTS, D), 1.0, 6.0, ((0, 8), (1, 4))),
    }


norm_eps = 1e-05
mask_value = -1e+30
box_step = 32
highest_precision = lax.Precision.HIGHEST

@jax.custom_vjp
def low(v):
    return lax.optimization_barrier(v.astype(jnp.bfloat16)).astype(jnp.float32)

@jax.custom_vjp
def low_back(v):
    return v

def low_keep(v):
    return (low(v), None)

def low_pass(kept, grad):
    return (grad,)

def back_keep(v):
    return (v, None)

def back_low(kept, grad):
    return (low(grad),)
low.defvjp(low_keep, low_pass)
low_back.defvjp(back_keep, back_low)

def matmul(first_mat, second_mat):
    return jnp.dot(first_mat, second_mat, precision=highest_precision)

def layer_norm(inputs, gain_vec, bias_vec):
    row_mean = lax.optimization_barrier(jnp.mean(inputs, axis=-1, keepdims=True))
    centered = inputs - row_mean
    variance = lax.optimization_barrier(jnp.mean(centered * centered, axis=-1, keepdims=True))
    return centered * lax.rsqrt(variance + norm_eps) * gain_vec + bias_vec

def forward_docs(parameters, group_tokens, group_positions, centers_x, centers_y, group_lengths):
    ln1_gain, ln1_bias, w_query, w_key, w_value, w_out, rel_table, xbias_table, ybias_table, ln2_gain, ln2_bias, w_in, b_in, w_down = parameters
    relative_key_rows = low(matmul(rel_table, w_key)).reshape(NREL, H, HD)
    rel_queries = low(matmul(rel_table, w_query)).reshape(NREL, H, HD)
    score_scale_factor = 1.0 / math.sqrt(3 * HD)
    half_bucket = NREL // 2
    half_boxes = NBOX // 2

    def one_doc(x_doc, doc_positions, document_center_x, doc_cy, length):
        query_matrix = low_back(low(matmul(x_doc, w_query))).reshape(SLOTS, H, HD)
        key_rows = low_back(low(matmul(x_doc, w_key))).reshape(SLOTS, H, HD)
        value_rows = low_back(low(matmul(x_doc, w_value))).reshape(SLOTS, H, HD)
        content = jnp.einsum('ihe,jhe->hij', query_matrix, key_rows, precision=highest_precision)
        relative_score_rows = low(jnp.einsum('czk,pzk->zcp', query_matrix, relative_key_rows, precision=highest_precision))
        key_rel = low(jnp.einsum('jhe,bhe->hjb', key_rows, rel_queries, precision=highest_precision))
        ahead_bucket = jnp.clip(doc_positions[:, None] - doc_positions[None, :], -half_bucket, half_bucket - 1) + half_bucket
        spread_index = jnp.broadcast_to(ahead_bucket[None], (H, SLOTS, SLOTS))
        gathered = jnp.take_along_axis(relative_score_rows, spread_index, axis=2)
        mirrored = jnp.swapaxes(jnp.take_along_axis(key_rel, spread_index, axis=2), 1, 2)
        across = jnp.clip(jnp.floor_divide(document_center_x[:, None] - document_center_x[None, :], box_step), -half_boxes, half_boxes - 1) + half_boxes
        vertical = jnp.clip(jnp.floor_divide(doc_cy[:, None] - doc_cy[None, :], box_step), -half_boxes, half_boxes - 1) + half_boxes
        box_bias = jnp.transpose(xbias_table[across] + ybias_table[vertical], (2, 0, 1))
        raw_scores = score_scale_factor * (content + gathered + mirrored) + box_bias
        is_valid = jnp.arange(SLOTS, dtype=jnp.int32) < length
        scores = low_back(jnp.where(is_valid[None, None, :], raw_scores, mask_value))
        probs = jax.nn.softmax(scores, axis=-1)
        attended = low_back(low(jnp.einsum('hij,jhe->ihe', low(probs), value_rows, precision=highest_precision))).reshape(SLOTS, D)
        attn_out = low_back(matmul(attended, w_out))
        hidden = layer_norm(x_doc + attn_out, ln1_gain, ln1_bias)
        up_proj = low_back(matmul(low(hidden), w_in) + b_in)
        activated = low(jax.nn.gelu(up_proj, approximate=True))
        ffn_out = low_back(matmul(activated, w_down))
        return layer_norm(hidden + ffn_out, ln2_gain, ln2_bias)
    return jax.vmap(one_doc)(group_tokens, group_positions, centers_x, centers_y, group_lengths)

def reference(tokens, lengths, positions, token_boxes, ln1_gain, ln1_bias, w_query, w_key, w_value, w_out, rel_table, xbias_table, ybias_table, ln2_gain, ln2_bias, w_in, b_in, w_down, cotangent):
    parameters = tuple((member.astype(jnp.float32) for member in (ln1_gain, ln1_bias, w_query, w_key, w_value, w_out, rel_table, xbias_table, ybias_table, ln2_gain, ln2_bias, w_in, b_in, w_down)))
    centers_x = jnp.floor_divide(token_boxes[0] + token_boxes[2], 2)
    centers_y = jnp.floor_divide(token_boxes[1] + token_boxes[3], 2)
    groups = DOCS // DOC_DEV

    def regroup(array):
        return array.reshape((groups, DOC_DEV) + array.shape[1:])
    inputs_all = (regroup(tokens), regroup(positions), regroup(centers_x), regroup(centers_y), regroup(lengths), regroup(cotangent))
    zero_grads = tuple((jnp.zeros(member.shape, jnp.float32) for member in parameters))

    def group_step(totals, one_group):
        group_tokens, group_positions, group_cx, group_cy, group_lengths, group_cotan = one_group

        def forward_here(params_in, tokens_in):
            return forward_docs(params_in, tokens_in, group_positions, group_cx, group_cy, group_lengths)
        outputs, pull_back = jax.vjp(forward_here, parameters, group_tokens.astype(jnp.float32))
        grad_params, grad_inputs = pull_back(group_cotan.astype(jnp.float32))
        totals = tuple((total + extra for total, extra in zip(totals, grad_params)))
        return (totals, (outputs.astype(jnp.bfloat16), grad_inputs))
    totals, (outputs, grads_in) = lax.scan(group_step, zero_grads, inputs_all)
    return (outputs.reshape(DOCS, SLOTS, D), grads_in.reshape(DOCS, SLOTS, D), totals[0], totals[1], totals[2], totals[3], totals[4], totals[5], totals[6], totals[7], totals[8], totals[9], totals[10], totals[11], totals[12], totals[13])
```

```python
import math

import jax
import jax.numpy as jnp
from jax import lax
from jax.experimental import pallas as pl
from jax.experimental.pallas import tpu as pltpu
from jax.sharding import PartitionSpec as P

norm_eps = 1e-05
mask_value = -1e30
f32 = jnp.float32
bf16 = jnp.bfloat16
lanes = 128


def dot(a, b, contract=((1,), (0,))):
    return lax.dot_general(a, b, (contract, ((), ())), preferred_element_type=f32)


def pick(table, index):
    return jnp.take_along_axis(table, index, axis=1, mode="promise_in_bounds")


def ahead_of(first, second):
    return jnp.clip(first - second, -64, 63) + 64


def attn_fwd_kernel(
    place, x_ref, wq_ref, wk_ref, wv_ref, rel_ref, tab_ref, row_ref, col_ref,
    att_ref, probs_ref, qkv_ref, relkq_ref, key_rel,
):
    scale = 1.0 / math.sqrt(192.0)
    step = pl.program_id(0)
    rows = x_ref.shape[0]
    width = wq_ref.shape[1]
    heads = tab_ref.shape[1]
    size = width // heads
    tiles = rows // lanes

    @pl.when(step == 0)
    def _():
        for at, w_ref in enumerate((wq_ref, wk_ref, wv_ref)):
            for t in range(tiles):
                qkv_ref[t * lanes : (t + 1) * lanes, at * width : (at + 1) * width] = dot(
                    x_ref[t * lanes : (t + 1) * lanes, :], w_ref[...]
                ).astype(bf16)
        relkq_ref[:, :width] = dot(rel_ref[...], wk_ref[...]).astype(bf16)
        relkq_ref[:, width:] = dot(rel_ref[...], wq_ref[...]).astype(bf16)
        for h in range(heads):
            key_rel[h] = (
                dot(
                    qkv_ref[:, width + h * size : width + (h + 1) * size],
                    relkq_ref[:, width + h * size : width + (h + 1) * size],
                    ((1,), (1,)),
                )
                .astype(bf16)
                .astype(f32)
            )

    here = pl.ds(pl.multiple_of(step * lanes, lanes), lanes)
    pos_i = col_ref[here, 0:1]
    cx_i = col_ref[here, 1:2]
    cy_i = col_ref[here, 2:3]
    own_row = row_ref[0:1, here]
    ahead, mirror, across, vertical = [], [], [], []
    for t in range(tiles):
        span = slice(t * lanes, (t + 1) * lanes)
        ahead.append(ahead_of(pos_i, row_ref[0:1, span]))
        mirror.append(ahead_of(col_ref[span, 0:1], own_row))
        across.append(jnp.clip(jnp.right_shift(cx_i - row_ref[1:2, span], 5), -32, 31) + 32)
        vertical.append(jnp.clip(jnp.right_shift(cy_i - row_ref[2:3, span], 5), -32, 31) + 96)
    valid = row_ref[3:4, :] > 0
    for h in range(heads):
        cols = slice(h * size, (h + 1) * size)
        query = qkv_ref[here, cols]
        rel_scores = (
            dot(query, relkq_ref[:, cols], ((1,), (1,))).astype(bf16).astype(f32)
        )
        table = jnp.broadcast_to(tab_ref[0, h : h + 1, :], (lanes, lanes))
        pieces = []
        for t in range(tiles):
            span = slice(t * lanes, (t + 1) * lanes)
            content = dot(
                query, qkv_ref[span, width + h * size : width + (h + 1) * size], ((1,), (1,))
            )
            mirrored = pick(key_rel[h, span, :], mirror[t]).T
            bias = pick(table, across[t]) + pick(table, vertical[t])
            pieces.append(
                scale * (content + pick(rel_scores, ahead[t]) + mirrored) + bias
            )
        scores = jnp.where(valid, jnp.concatenate(pieces, axis=1), mask_value)
        top = jnp.max(scores, axis=1, keepdims=True)
        raised = jnp.exp(scores - top)
        probs = (raised * (1.0 / jnp.sum(raised, axis=1, keepdims=True))).astype(bf16)
        probs_ref[h] = probs
        att_ref[:, cols] = dot(
            probs, qkv_ref[:, 2 * width + h * size : 2 * width + (h + 1) * size]
        ).astype(bf16)


def attn_fwd(place, x_all, w_query, w_key, w_value, rel_table, tables, ints_row, ints_col):
    rows, model = x_all.shape
    parts, heads, _ = tables.shape
    width = w_query.shape[1] // parts
    tiles = rows // lanes
    buckets = rel_table.shape[0]
    whole = lambda *shape: pl.BlockSpec(shape, lambda i, at: (0,) * len(shape))
    column = pl.BlockSpec((model, width), lambda i, at: (0, at[0]))
    return pl.pallas_call(
        attn_fwd_kernel,
        out_shape=(
            jax.ShapeDtypeStruct((rows, width), bf16),
            jax.ShapeDtypeStruct((heads, rows, rows), bf16),
            jax.ShapeDtypeStruct((rows, 3 * width), bf16),
            jax.ShapeDtypeStruct((buckets, 2 * width), bf16),
        ),
        grid_spec=pltpu.PrefetchScalarGridSpec(
            num_scalar_prefetch=1,
            grid=(tiles,),
            in_specs=[
                whole(rows, model),
                column,
                column,
                column,
                whole(buckets, model),
                pl.BlockSpec((1, heads, lanes), lambda i, at: (at[0], 0, 0)),
                whole(8, rows),
                whole(rows, 8),
            ],
            out_specs=[
                pl.BlockSpec((lanes, width), lambda i, at: (i, 0)),
                pl.BlockSpec((heads, lanes, rows), lambda i, at: (0, i, 0)),
                whole(rows, 3 * width),
                whole(buckets, 2 * width),
            ],
            scratch_shapes=[pltpu.VMEM((heads, rows, lanes), f32)],
        ),
        compiler_params=pltpu.CompilerParams(vmem_limit_bytes=40 << 20),
        cost_estimate=pl.CostEstimate(
            flops=6 * 10**9, transcendentals=10**6, bytes_accessed=8 << 20
        ),
        name="attn_fwd",
    )(place, x_all, w_query, w_key, w_value, rel_table, tables, ints_row, ints_col)


def attn_bwd_kernel(
    ga_ref, qkv_ref, probs_ref, relkq_ref, row_ref, col_ref,
    dqkv_ref, drel_ref, boxes_ref, ds_ref,
):
    scale = 1.0 / math.sqrt(192.0)
    rows = ga_ref.shape[0]
    heads = probs_ref.shape[0]
    width = ga_ref.shape[1]
    size = width // heads
    tiles = rows // lanes
    span_width = 3 * lanes
    drel_ref[...] = jnp.zeros_like(drel_ref)
    boxes_ref[...] = jnp.zeros_like(boxes_ref)
    window = lax.broadcasted_iota(jnp.int32, (rows, span_width), 1)
    bucket = lax.broadcasted_iota(jnp.int32, (lanes, lanes), 1)
    label = lax.broadcasted_iota(jnp.int32, (rows, lanes), 1)
    all_pos = col_ref[:, 0:1]
    all_x, all_y = col_ref[:, 1:2], col_ref[:, 2:3]
    sector_x, sector_y = jnp.right_shift(all_x, 5), jnp.right_shift(all_y, 5)
    hot_x = (label == sector_x).astype(bf16)
    hot_y = (label == sector_y + 64).astype(bf16)
    hot_both = ((label == sector_x) | (label == sector_y + 64)).astype(bf16)

    def histogram(sums, total, at, base_row):
        first = at - base_row + (2 * lanes // 2 - 1) - bucket
        low = jnp.bitwise_and(first, lanes - 1)
        group = jnp.right_shift(first, 7)
        found = jnp.where(
            group == 0,
            pick(sums[:, :lanes], low),
            jnp.where(
                group == 1,
                pick(sums[:, lanes : 2 * lanes], low),
                pick(sums[:, 2 * lanes :], low),
            ),
        )
        found = jnp.where(bucket == 0, total, found)
        later = jnp.where(bucket == lanes - 1, 0.0, pltpu.roll(found, lanes - 1, 1))
        return found - later

    def by_rows(ib, carry):
        here = pl.ds(pl.multiple_of(ib * lanes, lanes), lanes)
        pos_i = col_ref[here, 0:1]
        cx_i, cy_i = col_ref[here, 1:2], col_ref[here, 2:3]
        base = jnp.min(pos_i, axis=0, keepdims=True)
        below = (all_pos <= base - 63 + window).astype(bf16)
        short_x = jnp.bitwise_and(cx_i, 31) < jnp.bitwise_and(row_ref[1:2, :], 31)
        short_y = jnp.bitwise_and(cy_i, 31) < jnp.bitwise_and(row_ref[2:3, :], 31)
        step_x = jnp.right_shift(cx_i, 5) + 32 - bucket
        step_y = jnp.right_shift(cy_i, 5) + 32 - (bucket - 64)
        in_x = (bucket < 64) & (step_x >= 0) & (step_x < 32)
        in_y = (bucket >= 64) & (step_y >= 0) & (step_y < 32)
        seek = jnp.where(in_x, step_x, jnp.where(in_y, step_y + 64, 0))
        inside = in_x | in_y
        for h in range(heads):
            cols = slice(h * size, (h + 1) * size)
            kcols = slice(width + h * size, width + (h + 1) * size)
            vcols = slice(2 * width + h * size, 2 * width + (h + 1) * size)
            probs = probs_ref[h, here, :].astype(f32)
            gained = dot(ga_ref[here, cols], qkv_ref[:, vcols], ((1,), (1,)))
            row_dots = jnp.sum(probs * gained, axis=1, keepdims=True)
            grad32 = probs * (gained - row_dots)
            grad = grad32.astype(bf16)
            ds_ref[h, here, :] = grad
            exact = grad.astype(f32)
            total = jnp.sum(exact, axis=1, keepdims=True)
            rel = histogram(dot(grad, below), total, pos_i, base)
            rel = (scale * rel).astype(bf16)
            query = qkv_ref[here, cols]
            dqkv_ref[here, cols] = (
                scale * dot(grad, qkv_ref[:, kcols]) + dot(rel, relkq_ref[:, cols])
            ).astype(bf16)
            drel_ref[:, cols] += dot(rel, query, ((0,), (0,)))
            grad_x = jnp.where(short_x, exact, 0.0).astype(bf16)
            grad_y = jnp.where(short_y, exact, 0.0).astype(bf16)
            plain = dot(grad, hot_both)
            less = dot(grad_x, hot_x) + dot(grad_y, hot_y)
            plain = jnp.where(inside, pick(plain, seek), 0.0)
            less = jnp.where(inside, pick(less, seek), 0.0)
            boxes_ref[2 * h : 2 * h + 1, :] += jnp.sum(plain, axis=0, keepdims=True)
            boxes_ref[2 * h + 1 : 2 * h + 2, :] += jnp.sum(less, axis=0, keepdims=True)
        return carry

    lax.fori_loop(0, tiles, by_rows, 0)

    def by_columns(jb, carry):
        here = pl.ds(pl.multiple_of(jb * lanes, lanes), lanes)
        pos_j = col_ref[here, 0:1]
        base = jnp.min(pos_j, axis=0, keepdims=True)
        below = (all_pos <= base - 63 + window).astype(bf16)
        for h in range(heads):
            cols = slice(h * size, (h + 1) * size)
            kcols = slice(width + h * size, width + (h + 1) * size)
            vcols = slice(2 * width + h * size, 2 * width + (h + 1) * size)
            grad = ds_ref[h, :, here]
            total = dot(grad, jnp.ones((rows, lanes), bf16), ((0,), (0,)))
            sums = dot(grad, below, ((0,), (0,)))
            mirror = (scale * histogram(sums, total, pos_j, base)).astype(bf16)
            dqkv_ref[here, kcols] = (
                scale * dot(grad, qkv_ref[:, cols], ((0,), (0,)))
                + dot(mirror, relkq_ref[:, kcols])
            ).astype(bf16)
            drel_ref[:, kcols] += dot(mirror, qkv_ref[here, kcols], ((0,), (0,)))
            dqkv_ref[here, vcols] = dot(
                probs_ref[h, :, here], ga_ref[:, cols], ((0,), (0,))
            ).astype(bf16)
        return carry

    lax.fori_loop(0, tiles, by_columns, 0)


def attn_bwd(grad_att, qkv, probs, relkq, ints_row, ints_col):
    rows, width = grad_att.shape
    heads = probs.shape[0]
    buckets = relkq.shape[0]
    inside = pl.BlockSpec(memory_space=pltpu.VMEM)
    return pl.pallas_call(
        attn_bwd_kernel,
        out_shape=(
            jax.ShapeDtypeStruct((rows, 3 * width), bf16),
            jax.ShapeDtypeStruct((buckets, 2 * width), f32),
            jax.ShapeDtypeStruct((2 * heads, lanes), f32),
        ),
        in_specs=[inside] * 6,
        out_specs=[inside] * 3,
        scratch_shapes=[pltpu.VMEM((heads, rows, rows), bf16)],
        compiler_params=pltpu.CompilerParams(vmem_limit_bytes=40 << 20),
        cost_estimate=pl.CostEstimate(
            flops=12 * 10**9, transcendentals=0, bytes_accessed=6 << 20
        ),
        name="attn_bwd",
    )(grad_att, qkv, probs, relkq, ints_row, ints_col)


def layer_norm(inputs, gain_vec, bias_vec):
    row_mean = jnp.mean(inputs, axis=-1, keepdims=True)
    centered = inputs - row_mean
    inverse = lax.rsqrt(jnp.mean(centered * centered, axis=-1, keepdims=True) + norm_eps)
    normed = centered * inverse
    return (normed * gain_vec + bias_vec, normed, inverse)


def norm_backward(grad_in, normed, inverse, gain_vec):
    grad_gain = jnp.sum(grad_in * normed, axis=0)
    grad_shift = jnp.sum(grad_in, axis=0)
    scaled = grad_in * gain_vec
    grad_input = inverse * (
        scaled
        - jnp.mean(scaled, axis=-1, keepdims=True)
        - normed * jnp.mean(scaled * normed, axis=-1, keepdims=True)
    )
    return (grad_input, grad_gain, grad_shift)


def bits_of(count):
    assert count & (count - 1) == 0
    return [1 << at for at in range(count.bit_length() - 1)]


def swap(array, axis, by):
    count = lax.axis_size(axis)
    return lax.ppermute(array, axis, [(i, i ^ by) for i in range(count)])


def offsets(count):
    order = [0]
    for bit in reversed(bits_of(count)):
        order = order + [at ^ bit for at in order]
    return order


def spread(shared, pieces):
    count = lax.axis_size("blk")
    got = {0: shared} if shared is not None else {}
    held = {(0, at): piece for at, piece in pieces.items()} if pieces else {}
    for bit in reversed(bits_of(count)):
        out_keys = [key for key in sorted(held) if key[1] & bit]
        out_shared = sorted(got)
        parts = [got[at] for at in out_shared] + [held[key] for key in out_keys]
        if bit == 1:
            came = [swap(part, "blk", bit) for part in parts]
        else:
            came = swap(jnp.concatenate(parts, axis=1), "blk", bit)
            edges = [0]
            for part in parts:
                edges.append(edges[-1] + part.shape[1])
            came = [came[:, a:b] for a, b in zip(edges[:-1], edges[1:])]
        for at, part in zip(out_shared, came):
            got[at ^ bit] = part
        for key, part in zip(out_keys, came[len(out_shared) :]):
            del held[key]
            held[(key[0] ^ bit, key[1] ^ bit)] = part
    return got, {key[0]: part for key, part in held.items()}


def by_place(stacked, place):
    count = len(stacked)
    for bit in bits_of(count):
        turned = (place & bit) != 0
        stacked = [jnp.where(turned, stacked[at ^ bit], stacked[at]) for at in range(count)]
    return stacked


def chunk_order(count):
    order = [0]
    for bit in reversed(bits_of(count)):
        order = order + [at | bit for at in order]
    return order


def for_docs(chunks, doc_place):
    moved = by_place(chunks, doc_place)
    return [moved[at] for at in chunk_order(len(chunks))]


def halve(keep, send, bits):
    count = lax.axis_size("docs")
    first = True
    current = keep
    for bit in bits:
        if not first:
            half = current.shape[0] // 2
            current, send = current[:half], current[half:]
        first = False
        came = swap(send, "docs", bit)
        current = (current.astype(f32) + came.astype(f32)).astype(bf16)
    return current


def shards(
    tokens, lengths, positions, token_boxes, ln1_gain, ln1_bias, w_query, w_key, w_value, w_out,
    rel_table, xbias_table, ybias_table, ln2_gain, ln2_bias, w_in, b_in, w_down, cotangent,
):
    doc_count, row_count, model = tokens.shape
    assert doc_count == 1 and row_count == lanes
    parts = lax.axis_size("blk")
    docs = lax.axis_size("docs")
    place = lax.axis_index("blk")
    doc_place = lax.axis_index("docs")
    heads = xbias_table.shape[1]
    own_heads = heads // parts
    width = model // parts
    buckets = rel_table.shape[0]
    boxes = xbias_table.shape[0]
    hidden_units = w_in.shape[1]
    order = offsets(parts)
    x_own = tokens[0]

    centers_x = jnp.right_shift(token_boxes[0] + token_boxes[2], 1)
    centers_y = jnp.right_shift(token_boxes[1] + token_boxes[3], 1)
    own_ints = jnp.concatenate([positions, centers_x, centers_y], axis=0)
    coded = jnp.concatenate(
        [jnp.right_shift(own_ints, 5), jnp.bitwise_and(own_ints, 31)], axis=0
    ).astype(bf16)
    coded = jnp.pad(coded.reshape(1, -1), ((0, 7), (0, model - coded.size)))
    got, _ = spread(jnp.concatenate([x_own, coded], axis=0), None)
    x_all = jnp.concatenate([got[at][:row_count] for at in order], axis=0)
    decoded = jnp.concatenate(
        [got[at][row_count : row_count + 1, : 6 * row_count].reshape(6, row_count) for at in order], axis=1
    ).astype(jnp.int32)
    ints = decoded[:3] * 32 + decoded[3:]
    slot_ids = jnp.concatenate(
        [
            (place ^ at) * row_count + lax.broadcasted_iota(jnp.int32, (1, row_count), 1)
            for at in order
        ],
        axis=1,
    )
    ints = jnp.concatenate(
        [ints, (slot_ids < lengths[0]).astype(jnp.int32), jnp.zeros((4, ints.shape[1]), jnp.int32)],
        axis=0,
    )
    ints_col = ints.T
    tables = jnp.concatenate([xbias_table.T, ybias_table.T], axis=1).astype(f32)
    tables = tables.reshape(parts, own_heads, 2 * boxes)

    attended_own, probs, qkv, relkq = attn_fwd(
        place.reshape(1), x_all, w_query, w_key, w_value, rel_table, tables, ints, ints_col
    )

    def row_block(array, at):
        t = order.index(at)
        return array[t * row_count : (t + 1) * row_count]

    _, came = spread(None, {at: row_block(attended_own, at) for at in order})
    attended = jnp.concatenate(by_place([came[at] for at in range(parts)], place), axis=1)
    attn_out = jnp.dot(attended, w_out, preferred_element_type=f32)
    hidden, normed1, inverse1 = layer_norm(x_own.astype(f32) + attn_out, ln1_gain, ln1_bias)
    hidden_low = hidden.astype(bf16)
    up_proj = jnp.dot(hidden_low, w_in, preferred_element_type=f32) + b_in
    activated, gelu_back = jax.vjp(lambda inputs: jax.nn.gelu(inputs, approximate=True), up_proj)
    activated_low = activated.astype(bf16)
    ffn_out = jnp.dot(activated_low, w_down, preferred_element_type=f32)
    normed_out, normed2, inverse2 = layer_norm(hidden + ffn_out, ln2_gain, ln2_bias)
    block_out = normed_out.astype(bf16)[None]
    grad_output = cotangent[0].astype(f32)
    grad_mix, grad_ln2_gain, grad_ln2_bias = norm_backward(grad_output, normed2, inverse2, ln2_gain)
    grad_ffn = grad_mix.astype(bf16)
    grad_act = jnp.dot(grad_ffn, w_down.T, preferred_element_type=f32)
    grad_up = gelu_back(grad_act)[0].astype(bf16)
    grad_b_in = jnp.sum(grad_up, axis=0, dtype=f32)
    grad_hidden = grad_mix + jnp.dot(grad_up, w_in.T, preferred_element_type=f32)
    grad_resid, grad_ln1_gain, grad_ln1_bias = norm_backward(
        grad_hidden, normed1, inverse1, ln1_gain
    )
    grad_attn = grad_resid.astype(bf16)
    grad_att = jnp.dot(grad_attn, w_out.T, preferred_element_type=f32).astype(bf16)

    def column_block(array, at, count):
        size = array.shape[1] // count
        return lax.dynamic_slice_in_dim(array, at * size, size, axis=1)

    _, came = spread(None, {at: column_block(grad_att, place ^ at, parts) for at in order})
    grad_att_own = jnp.concatenate([came[at] for at in order], axis=0)
    dqkv, drel, box_sums = attn_bwd(grad_att_own, qkv, probs, relkq, ints, ints_col)

    def docs_columns(array):
        size = array.shape[1] // docs
        chunks = [array[:, at * size : (at + 1) * size] for at in range(docs)]
        return jnp.concatenate(for_docs(chunks, doc_place), axis=1)

    strips = activated_low.reshape(row_count, docs, parts, -1)
    strips = [
        docs_columns(
            lax.dynamic_index_in_dim(strips, place ^ at, axis=2, keepdims=False).reshape(row_count, -1)
        )
        for at in range(parts)
    ]
    got, came = spread(docs_columns(hidden_low), dict(enumerate(strips)))
    hidden_all = jnp.concatenate([got[at] for at in order], axis=0)
    activated_all = jnp.concatenate([came[at] for at in order], axis=0)
    got, came = spread(grad_ffn, {at: column_block(grad_up, place ^ at, parts) for at in order})
    grad_ffn_all = jnp.concatenate([got[at] for at in order], axis=0)
    grad_up_all = jnp.concatenate([came[at] for at in order], axis=0)
    got, came = spread(
        docs_columns(attended), {at: column_block(grad_attn, place ^ at, parts) for at in order}
    )
    attended_all = jnp.concatenate([got[at] for at in order], axis=0)
    grad_attn_all = jnp.concatenate([came[at] for at in order], axis=0)

    def halves(left, right):
        middle = left.shape[1] // 2
        send = dot(left[:, middle:], right, ((0,), (0,))).astype(bf16)
        keep = dot(left[:, :middle], right, ((0,), (0,))).astype(bf16)
        return keep, send

    bits = bits_of(docs)
    down_part = halve(*halves(activated_all, grad_ffn_all), bits)
    in_part = halve(*halves(hidden_all, grad_up_all), bits)
    out_part = halve(*halves(attended_all, grad_attn_all), bits)

    drel_low = drel.astype(bf16)
    left = docs_columns(jnp.concatenate([x_all, rel_table], axis=0))
    right = jnp.concatenate(
        [
            dqkv,
            jnp.concatenate(
                [drel_low[:, width:], drel_low[:, :width], jnp.zeros((buckets, width), bf16)], axis=1
            ),
        ],
        axis=0,
    )
    grad_rel_table = dot(
        drel_low[:, :width], column_block(w_key, place, parts), ((1,), (1,))
    ) + dot(drel_low[:, width:], column_block(w_query, place, parts), ((1,), (1,)))
    plain, less = box_sums[0::2], box_sums[1::2]

    def box_grad(at):
        plain_here, less_here = plain[:, at : at + boxes], less[:, at : at + boxes]
        later = jnp.pad(less_here[:, 1:], ((0, 0), (0, 1)))
        grad = (plain_here - less_here + later).T
        return lax.dynamic_update_slice(jnp.zeros((boxes, heads), f32), grad, (0, place * own_heads))

    small = jnp.concatenate(
        [
            grad_rel_table.reshape(docs, -1),
            grad_ln1_gain.reshape(docs, -1),
            grad_ln1_bias.reshape(docs, -1),
            grad_ln2_gain.reshape(docs, -1),
            grad_ln2_bias.reshape(docs, -1),
            grad_b_in.reshape(docs, -1),
            box_grad(0).reshape(docs, -1),
            box_grad(boxes).reshape(docs, -1),
        ],
        axis=1,
    ).astype(bf16)
    small_width = small.shape[1]
    across = 3 * width
    small = jnp.pad(small, ((0, 0), (0, -small_width % (8 * across))))
    small = for_docs([small[at] for at in range(docs)], doc_place)
    small = jnp.stack(small).reshape(docs, -1, across)
    keep, send = halves(left, right)
    middle = docs // 2
    chunk_rows = model // docs

    def with_small(main, extra):
        main = main.reshape(middle, chunk_rows, across)
        return jnp.concatenate([main, extra], axis=1).reshape(-1, across)

    qkv_part = halve(with_small(keep, small[:middle]), with_small(send, small[middle:]), bits)

    _, came = spread(None, {at: row_block(dqkv, at) for at in order})
    came = by_place([came[at] for at in range(parts)], place)
    grad_tokens = grad_resid
    for at, weight in enumerate((w_query, w_key, w_value)):
        grad = jnp.concatenate([rows[:, at * width : (at + 1) * width] for rows in came], axis=1)
        grad_tokens = grad_tokens + dot(grad, weight, ((1,), (1,)))

    def whole(part):
        got, _ = spread(part, None)
        return by_place([got[at] for at in range(parts)], place)

    grad_w_down = jnp.concatenate(whole(down_part), axis=0).astype(f32)
    grad_w_in = jnp.concatenate(whole(in_part), axis=1).astype(f32)
    grad_w_out = jnp.concatenate(whole(out_part), axis=1).astype(f32)
    pieces = whole(qkv_part)
    grads = [
        jnp.concatenate(
            [piece[:chunk_rows, at * width : (at + 1) * width] for piece in pieces], axis=1
        ).astype(f32)
        for at in range(3)
    ]
    total = sum(piece[chunk_rows:].astype(f32) for piece in pieces).reshape(-1)
    sizes = [
        (buckets // docs, model),
        (model // docs,),
        (model // docs,),
        (model // docs,),
        (model // docs,),
        (hidden_units // docs,),
        (boxes // docs, heads),
        (boxes // docs, heads),
    ]
    small_out = []
    start = 0
    for size in sizes:
        small_out.append(total[start : start + math.prod(size)].reshape(size))
        start += math.prod(size)
    rel_out, ln1g, ln1b, ln2g, ln2b, b_in_out, xb, yb = small_out
    return (
        block_out, grad_tokens[None], ln1g, ln1b, grads[0], grads[1], grads[2], grad_w_out,
        rel_out, xb, yb, ln2g, ln2b, grad_w_in, b_in_out, grad_w_down,
    )


def solution(mesh):
    rows = P("docs", "blk", None)
    placed = (
        rows, P("docs"), P("docs", "blk"), P(None, "docs", "blk"),
        *([P()] * 14), rows,
    )
    over_docs, over_docs2 = P("docs"), P("docs", None)
    return jax.shard_map(
        shards,
        mesh=mesh,
        in_specs=placed,
        out_specs=(
            rows, rows, over_docs, over_docs, over_docs2, over_docs2, over_docs2, over_docs2,
            over_docs2, over_docs2, over_docs2, over_docs, over_docs, over_docs2, over_docs, over_docs2,
        ),
        check_vma=False,
    )
```

```python
import math

import jax
import jax.numpy as jnp
from jax import lax
from jax.experimental import pallas as pl
from jax.experimental.pallas import tpu as pltpu
from jax.sharding import PartitionSpec as P

norm_eps = 1e-05
mask_value = -1e30
f32 = jnp.float32
bf16 = jnp.bfloat16
lanes = 128


def dot(a, b, contract=((1,), (0,))):
    return lax.dot_general(a, b, (contract, ((), ())), preferred_element_type=f32)


def pick(table, index):
    return jnp.take_along_axis(table, index, axis=1, mode="promise_in_bounds")


def ahead_of(first, second):
    return jnp.clip(first - second, -64, 63) + 64


def attn_fwd_kernel(
    place, x_ref, wq_ref, wk_ref, wv_ref, rel_ref, tab_ref, row_ref, col_ref,
    att_ref, probs_ref, qkv_ref, relkq_ref, key_rel,
):
    scale = 1.0 / math.sqrt(192.0)
    step = pl.program_id(0)
    rows = x_ref.shape[0]
    width = wq_ref.shape[1]
    heads = tab_ref.shape[1]
    size = width // heads
    tiles = rows // lanes

    @pl.when(step == 0)
    def _():
        for at, w_ref in enumerate((wq_ref, wk_ref, wv_ref)):
            for t in range(tiles):
                qkv_ref[t * lanes : (t + 1) * lanes, at * width : (at + 1) * width] = dot(
                    x_ref[t * lanes : (t + 1) * lanes, :], w_ref[...]
                ).astype(bf16)
        relkq_ref[:, :width] = dot(rel_ref[...], wk_ref[...]).astype(bf16)
        relkq_ref[:, width:] = dot(rel_ref[...], wq_ref[...]).astype(bf16)
        for h in range(heads):
            key_rel[h] = (
                dot(
                    qkv_ref[:, width + h * size : width + (h + 1) * size],
                    relkq_ref[:, width + h * size : width + (h + 1) * size],
                    ((1,), (1,)),
                )
                .astype(bf16)
                .astype(f32)
            )

    here = pl.ds(pl.multiple_of(step * lanes, lanes), lanes)
    pos_i = col_ref[here, 0:1]
    cx_i = col_ref[here, 1:2]
    cy_i = col_ref[here, 2:3]
    own_row = row_ref[0:1, here]
    ahead, mirror, across, vertical = [], [], [], []
    for t in range(tiles):
        span = slice(t * lanes, (t + 1) * lanes)
        ahead.append(ahead_of(pos_i, row_ref[0:1, span]))
        mirror.append(ahead_of(col_ref[span, 0:1], own_row))
        across.append(jnp.clip(jnp.right_shift(cx_i - row_ref[1:2, span], 5), -32, 31) + 32)
        vertical.append(jnp.clip(jnp.right_shift(cy_i - row_ref[2:3, span], 5), -32, 31) + 96)
    valid = row_ref[3:4, :] > 0
    for h in range(heads):
        cols = slice(h * size, (h + 1) * size)
        query = qkv_ref[here, cols]
        rel_scores = (
            dot(query, relkq_ref[:, cols], ((1,), (1,))).astype(bf16).astype(f32)
        )
        table = jnp.broadcast_to(tab_ref[0, h : h + 1, :], (lanes, lanes))
        pieces = []
        for t in range(tiles):
            span = slice(t * lanes, (t + 1) * lanes)
            content = dot(
                query, qkv_ref[span, width + h * size : width + (h + 1) * size], ((1,), (1,))
            )
            mirrored = pick(key_rel[h, span, :], mirror[t]).T
            bias = pick(table, across[t]) + pick(table, vertical[t])
            pieces.append(
                scale * (content + pick(rel_scores, ahead[t]) + mirrored) + bias
            )
        scores = jnp.where(valid, jnp.concatenate(pieces, axis=1), mask_value)
        top = jnp.max(scores, axis=1, keepdims=True)
        raised = jnp.exp(scores - top)
        probs = (raised * (1.0 / jnp.sum(raised, axis=1, keepdims=True))).astype(bf16)
        probs_ref[h] = probs
        att_ref[:, cols] = dot(
            probs, qkv_ref[:, 2 * width + h * size : 2 * width + (h + 1) * size]
        ).astype(bf16)


def attn_fwd(place, x_all, w_query, w_key, w_value, rel_table, tables, ints_row, ints_col):
    rows, model = x_all.shape
    parts, heads, _ = tables.shape
    width = w_query.shape[1] // parts
    tiles = rows // lanes
    buckets = rel_table.shape[0]
    whole = lambda *shape: pl.BlockSpec(shape, lambda i, at: (0,) * len(shape))
    column = pl.BlockSpec((model, width), lambda i, at: (0, at[0]))
    return pl.pallas_call(
        attn_fwd_kernel,
        out_shape=(
            jax.ShapeDtypeStruct((rows, width), bf16),
            jax.ShapeDtypeStruct((heads, rows, rows), bf16),
            jax.ShapeDtypeStruct((rows, 3 * width), bf16),
            jax.ShapeDtypeStruct((buckets, 2 * width), bf16),
        ),
        grid_spec=pltpu.PrefetchScalarGridSpec(
            num_scalar_prefetch=1,
            grid=(tiles,),
            in_specs=[
                whole(rows, model),
                column,
                column,
                column,
                whole(buckets, model),
                pl.BlockSpec((1, heads, lanes), lambda i, at: (at[0], 0, 0)),
                whole(8, rows),
                whole(rows, 8),
            ],
            out_specs=[
                pl.BlockSpec((lanes, width), lambda i, at: (i, 0)),
                pl.BlockSpec((heads, lanes, rows), lambda i, at: (0, i, 0)),
                whole(rows, 3 * width),
                whole(buckets, 2 * width),
            ],
            scratch_shapes=[pltpu.VMEM((heads, rows, lanes), f32)],
        ),
        compiler_params=pltpu.CompilerParams(vmem_limit_bytes=40 << 20),
        cost_estimate=pl.CostEstimate(
            flops=6 * 10**9, transcendentals=10**6, bytes_accessed=8 << 20
        ),
        name="attn_fwd",
    )(place, x_all, w_query, w_key, w_value, rel_table, tables, ints_row, ints_col)


def attn_bwd_kernel(
    ga_ref, qkv_ref, probs_ref, relkq_ref, row_ref, col_ref,
    dqkv_ref, drel_ref, boxes_ref, ds_ref,
):
    scale = 1.0 / math.sqrt(192.0)
    rows = ga_ref.shape[0]
    heads = probs_ref.shape[0]
    width = ga_ref.shape[1]
    size = width // heads
    tiles = rows // lanes
    span_width = 3 * lanes
    drel_ref[...] = jnp.zeros_like(drel_ref)
    boxes_ref[...] = jnp.zeros_like(boxes_ref)
    window = lax.broadcasted_iota(jnp.int32, (rows, span_width), 1)
    bucket = lax.broadcasted_iota(jnp.int32, (lanes, lanes), 1)
    label = lax.broadcasted_iota(jnp.int32, (rows, lanes), 1)
    all_pos = col_ref[:, 0:1]
    all_x, all_y = col_ref[:, 1:2], col_ref[:, 2:3]
    sector_x, sector_y = jnp.right_shift(all_x, 5), jnp.right_shift(all_y, 5)
    hot_x = (label == sector_x).astype(bf16)
    hot_y = (label == sector_y + 64).astype(bf16)
    hot_both = ((label == sector_x) | (label == sector_y + 64)).astype(bf16)

    def histogram(sums, total, at, base_row):
        first = at - base_row + (2 * lanes // 2 - 1) - bucket
        low = jnp.bitwise_and(first, lanes - 1)
        group = jnp.right_shift(first, 7)
        found = jnp.where(
            group == 0,
            pick(sums[:, :lanes], low),
            jnp.where(
                group == 1,
                pick(sums[:, lanes : 2 * lanes], low),
                pick(sums[:, 2 * lanes :], low),
            ),
        )
        found = jnp.where(bucket == 0, total, found)
        later = jnp.where(bucket == lanes - 1, 0.0, pltpu.roll(found, lanes - 1, 1))
        return found - later

    def by_rows(ib, carry):
        here = pl.ds(pl.multiple_of(ib * lanes, lanes), lanes)
        pos_i = col_ref[here, 0:1]
        cx_i, cy_i = col_ref[here, 1:2], col_ref[here, 2:3]
        base = jnp.min(pos_i, axis=0, keepdims=True)
        below = (all_pos <= base - 63 + window).astype(bf16)
        short_x = jnp.bitwise_and(cx_i, 31) < jnp.bitwise_and(row_ref[1:2, :], 31)
        short_y = jnp.bitwise_and(cy_i, 31) < jnp.bitwise_and(row_ref[2:3, :], 31)
        step_x = jnp.right_shift(cx_i, 5) + 32 - bucket
        step_y = jnp.right_shift(cy_i, 5) + 32 - (bucket - 64)
        in_x = (bucket < 64) & (step_x >= 0) & (step_x < 32)
        in_y = (bucket >= 64) & (step_y >= 0) & (step_y < 32)
        seek = jnp.where(in_x, step_x, jnp.where(in_y, step_y + 64, 0))
        inside = in_x | in_y
        for h in range(heads):
            cols = slice(h * size, (h + 1) * size)
            kcols = slice(width + h * size, width + (h + 1) * size)
            vcols = slice(2 * width + h * size, 2 * width + (h + 1) * size)
            probs = probs_ref[h, here, :].astype(f32)
            gained = dot(ga_ref[here, cols], qkv_ref[:, vcols], ((1,), (1,)))
            row_dots = jnp.sum(probs * gained, axis=1, keepdims=True)
            grad32 = probs * (gained - row_dots)
            grad = grad32.astype(bf16)
            ds_ref[h, here, :] = grad
            exact = grad.astype(f32)
            total = jnp.sum(exact, axis=1, keepdims=True)
            rel = histogram(dot(grad, below), total, pos_i, base)
            rel = (scale * rel).astype(bf16)
            query = qkv_ref[here, cols]
            dqkv_ref[here, cols] = (
                scale * dot(grad, qkv_ref[:, kcols]) + dot(rel, relkq_ref[:, cols])
            ).astype(bf16)
            drel_ref[:, cols] += dot(rel, query, ((0,), (0,)))
            grad_x = jnp.where(short_x, exact, 0.0).astype(bf16)
            grad_y = jnp.where(short_y, exact, 0.0).astype(bf16)
            plain = dot(grad, hot_both)
            less = dot(grad_x, hot_x) + dot(grad_y, hot_y)
            plain = jnp.where(inside, pick(plain, seek), 0.0)
            less = jnp.where(inside, pick(less, seek), 0.0)
            boxes_ref[2 * h : 2 * h + 1, :] += jnp.sum(plain, axis=0, keepdims=True)
            boxes_ref[2 * h + 1 : 2 * h + 2, :] += jnp.sum(less, axis=0, keepdims=True)
        return carry

    lax.fori_loop(0, tiles, by_rows, 0)

    def by_columns(jb, carry):
        here = pl.ds(pl.multiple_of(jb * lanes, lanes), lanes)
        pos_j = col_ref[here, 0:1]
        base = jnp.min(pos_j, axis=0, keepdims=True)
        below = (all_pos <= base - 63 + window).astype(bf16)
        for h in range(heads):
            cols = slice(h * size, (h + 1) * size)
            kcols = slice(width + h * size, width + (h + 1) * size)
            vcols = slice(2 * width + h * size, 2 * width + (h + 1) * size)
            grad = ds_ref[h, :, here]
            total = dot(grad, jnp.ones((rows, lanes), bf16), ((0,), (0,)))
            sums = dot(grad, below, ((0,), (0,)))
            mirror = (scale * histogram(sums, total, pos_j, base)).astype(bf16)
            dqkv_ref[here, kcols] = (
                scale * dot(grad, qkv_ref[:, cols], ((0,), (0,)))
                + dot(mirror, relkq_ref[:, kcols])
            ).astype(bf16)
            drel_ref[:, kcols] += dot(mirror, qkv_ref[here, kcols], ((0,), (0,)))
            dqkv_ref[here, vcols] = dot(
                probs_ref[h, :, here], ga_ref[:, cols], ((0,), (0,))
            ).astype(bf16)
        return carry

    lax.fori_loop(0, tiles, by_columns, 0)


def attn_bwd(grad_att, qkv, probs, relkq, ints_row, ints_col):
    rows, width = grad_att.shape
    heads = probs.shape[0]
    buckets = relkq.shape[0]
    inside = pl.BlockSpec(memory_space=pltpu.VMEM)
    return pl.pallas_call(
        attn_bwd_kernel,
        out_shape=(
            jax.ShapeDtypeStruct((rows, 3 * width), bf16),
            jax.ShapeDtypeStruct((buckets, 2 * width), f32),
            jax.ShapeDtypeStruct((2 * heads, lanes), f32),
        ),
        in_specs=[inside] * 6,
        out_specs=[inside] * 3,
        scratch_shapes=[pltpu.VMEM((heads, rows, rows), bf16)],
        compiler_params=pltpu.CompilerParams(vmem_limit_bytes=40 << 20),
        cost_estimate=pl.CostEstimate(
            flops=12 * 10**9, transcendentals=0, bytes_accessed=6 << 20
        ),
        name="attn_bwd",
    )(grad_att, qkv, probs, relkq, ints_row, ints_col)


def layer_norm(inputs, gain_vec, bias_vec):
    row_mean = jnp.mean(inputs, axis=-1, keepdims=True)
    centered = inputs - row_mean
    inverse = lax.rsqrt(jnp.mean(centered * centered, axis=-1, keepdims=True) + norm_eps)
    normed = centered * inverse
    return (normed * gain_vec + bias_vec, normed, inverse)


def norm_backward(grad_in, normed, inverse, gain_vec):
    grad_gain = jnp.sum(grad_in * normed, axis=0)
    grad_shift = jnp.sum(grad_in, axis=0)
    scaled = grad_in * gain_vec
    grad_input = inverse * (
        scaled
        - jnp.mean(scaled, axis=-1, keepdims=True)
        - normed * jnp.mean(scaled * normed, axis=-1, keepdims=True)
    )
    return (grad_input, grad_gain, grad_shift)


def bits_of(count):
    assert count & (count - 1) == 0
    return [1 << at for at in range(count.bit_length() - 1)]


def swap(array, axis, by):
    count = lax.axis_size(axis)
    return lax.ppermute(array, axis, [(i, i ^ by) for i in range(count)])


def offsets(count):
    order = [0]
    for bit in reversed(bits_of(count)):
        order = order + [at ^ bit for at in order]
    return order


def spread(shared, pieces):
    count = lax.axis_size("blk")
    got = {0: shared} if shared is not None else {}
    held = {(0, at): piece for at, piece in pieces.items()} if pieces else {}
    for bit in reversed(bits_of(count)):
        out_keys = [key for key in sorted(held) if key[1] & bit]
        out_shared = sorted(got)
        parts = [got[at] for at in out_shared] + [held[key] for key in out_keys]
        if bit == 1:
            came = [swap(part, "blk", bit) for part in parts]
        else:
            came = swap(jnp.concatenate(parts, axis=1), "blk", bit)
            edges = [0]
            for part in parts:
                edges.append(edges[-1] + part.shape[1])
            came = [came[:, a:b] for a, b in zip(edges[:-1], edges[1:])]
        for at, part in zip(out_shared, came):
            got[at ^ bit] = part
        for key, part in zip(out_keys, came[len(out_shared) :]):
            del held[key]
            held[(key[0] ^ bit, key[1] ^ bit)] = part
    return got, {key[0]: part for key, part in held.items()}


def by_place(stacked, place):
    count = len(stacked)
    for bit in bits_of(count):
        turned = (place & bit) != 0
        stacked = [jnp.where(turned, stacked[at ^ bit], stacked[at]) for at in range(count)]
    return stacked


def chunk_order(count):
    order = [0]
    for bit in reversed(bits_of(count)):
        order = order + [at | bit for at in order]
    return order


def for_docs(chunks, doc_place):
    moved = by_place(chunks, doc_place)
    return [moved[at] for at in chunk_order(len(chunks))]


def halve(keep, send, bits):
    count = lax.axis_size("docs")
    first = True
    current = keep
    for bit in bits:
        if not first:
            half = current.shape[0] // 2
            current, send = current[:half], current[half:]
        first = False
        came = swap(send, "docs", bit)
        current = (current.astype(f32) + came.astype(f32)).astype(bf16)
    return current


def shards(
    tokens, lengths, positions, token_boxes, ln1_gain, ln1_bias, w_query, w_key, w_value, w_out,
    rel_table, xbias_table, ybias_table, ln2_gain, ln2_bias, w_in, b_in, w_down, cotangent,
):
    doc_count, row_count, model = tokens.shape
    assert doc_count == 1 and row_count == lanes
    parts = lax.axis_size("blk")
    docs = lax.axis_size("docs")
    place = lax.axis_index("blk")
    doc_place = lax.axis_index("docs")
    heads = xbias_table.shape[1]
    own_heads = heads // parts
    width = model // parts
    buckets = rel_table.shape[0]
    boxes = xbias_table.shape[0]
    hidden_units = w_in.shape[1]
    order = offsets(parts)
    x_own = tokens[0]

    centers_x = jnp.right_shift(token_boxes[0] + token_boxes[2], 1)
    centers_y = jnp.right_shift(token_boxes[1] + token_boxes[3], 1)
    own_ints = jnp.concatenate([positions, centers_x, centers_y], axis=0)
    coded = jnp.concatenate(
        [jnp.right_shift(own_ints, 5), jnp.bitwise_and(own_ints, 31)], axis=0
    ).astype(bf16)
    coded = jnp.pad(coded.reshape(1, -1), ((0, 7), (0, model - coded.size)))
    got, _ = spread(jnp.concatenate([x_own, coded], axis=0), None)
    x_all = jnp.concatenate([got[at][:row_count] for at in order], axis=0)
    decoded = jnp.concatenate(
        [got[at][row_count : row_count + 1, : 6 * row_count].reshape(6, row_count) for at in order], axis=1
    ).astype(jnp.int32)
    ints = decoded[:3] * 32 + decoded[3:]
    slot_ids = jnp.concatenate(
        [
            (place ^ at) * row_count + lax.broadcasted_iota(jnp.int32, (1, row_count), 1)
            for at in order
        ],
        axis=1,
    )
    ints = jnp.concatenate(
        [ints, (slot_ids < lengths[0]).astype(jnp.int32), jnp.zeros((4, ints.shape[1]), jnp.int32)],
        axis=0,
    )
    ints_col = ints.T
    tables = jnp.concatenate([xbias_table.T, ybias_table.T], axis=1).astype(f32)
    tables = tables.reshape(parts, own_heads, 2 * boxes)

    attended_own, probs, qkv, relkq = attn_fwd(
        place.reshape(1), x_all, w_query, w_key, w_value, rel_table, tables, ints, ints_col
    )

    def row_block(array, at):
        t = order.index(at)
        return array[t * row_count : (t + 1) * row_count]

    _, came = spread(None, {at: row_block(attended_own, at) for at in order})
    attended = jnp.concatenate(by_place([came[at] for at in range(parts)], place), axis=1)
    attn_out = jnp.dot(attended, w_out, preferred_element_type=f32)
    hidden, normed1, inverse1 = layer_norm(x_own.astype(f32) + attn_out, ln1_gain, ln1_bias)
    hidden_low = hidden.astype(bf16)
    up_proj = jnp.dot(hidden_low, w_in, preferred_element_type=f32) + b_in
    activated, gelu_back = jax.vjp(lambda inputs: jax.nn.gelu(inputs, approximate=True), up_proj)
    activated_low = activated.astype(bf16)
    ffn_out = jnp.dot(activated_low, w_down, preferred_element_type=f32)
    normed_out, normed2, inverse2 = layer_norm(hidden + ffn_out, ln2_gain, ln2_bias)
    block_out = normed_out.astype(bf16)[None]
    grad_output = cotangent[0].astype(f32)
    grad_mix, grad_ln2_gain, grad_ln2_bias = norm_backward(grad_output, normed2, inverse2, ln2_gain)
    grad_ffn = grad_mix.astype(bf16)
    grad_act = jnp.dot(grad_ffn, w_down.T, preferred_element_type=f32)
    grad_up = gelu_back(grad_act)[0].astype(bf16)
    grad_b_in = jnp.sum(grad_up, axis=0, dtype=f32)
    grad_hidden = grad_mix + jnp.dot(grad_up, w_in.T, preferred_element_type=f32)
    grad_resid, grad_ln1_gain, grad_ln1_bias = norm_backward(
        grad_hidden, normed1, inverse1, ln1_gain
    )
    grad_attn = grad_resid.astype(bf16)
    grad_att = jnp.dot(grad_attn, w_out.T, preferred_element_type=f32).astype(bf16)

    def column_block(array, at, count):
        size = array.shape[1] // count
        return lax.dynamic_slice_in_dim(array, at * size, size, axis=1)

    _, came = spread(None, {at: column_block(grad_att, place ^ at, parts) for at in order})
    grad_att_own = jnp.concatenate([came[at] for at in order], axis=0)
    dqkv, drel, box_sums = attn_bwd(grad_att_own, qkv, probs, relkq, ints, ints_col)

    def docs_columns(array):
        size = array.shape[1] // docs
        chunks = [array[:, at * size : (at + 1) * size] for at in range(docs)]
        return jnp.concatenate(for_docs(chunks, doc_place), axis=1)

    strips = activated_low.reshape(row_count, docs, parts, -1)
    strips = [
        docs_columns(
            lax.dynamic_index_in_dim(strips, place ^ at, axis=2, keepdims=False).reshape(row_count, -1)
        )
        for at in range(parts)
    ]
    got, came = spread(docs_columns(hidden_low), dict(enumerate(strips)))
    hidden_all = jnp.concatenate([got[at] for at in order], axis=0)
    activated_all = jnp.concatenate([came[at] for at in order], axis=0)
    got, came = spread(grad_ffn, {at: column_block(grad_up, place ^ at, parts) for at in order})
    grad_ffn_all = jnp.concatenate([got[at] for at in order], axis=0)
    grad_up_all = jnp.concatenate([came[at] for at in order], axis=0)
    got, came = spread(
        docs_columns(attended), {at: column_block(grad_attn, place ^ at, parts) for at in order}
    )
    attended_all = jnp.concatenate([got[at] for at in order], axis=0)
    grad_attn_all = jnp.concatenate([came[at] for at in order], axis=0)

    def halves(left, right):
        middle = left.shape[1] // 2
        send = dot(left[:, middle:], right, ((0,), (0,))).astype(bf16)
        keep = dot(left[:, :middle], right, ((0,), (0,))).astype(bf16)
        return keep, send

    bits = bits_of(docs)
    down_part = halve(*halves(activated_all, grad_ffn_all), bits)
    in_part = halve(*halves(hidden_all, grad_up_all), bits)
    out_part = halve(*halves(attended_all, grad_attn_all), bits)

    drel_low = drel.astype(bf16)
    left = docs_columns(jnp.concatenate([x_all, rel_table], axis=0))
    right = jnp.concatenate(
        [
            dqkv,
            jnp.concatenate(
                [drel_low[:, width:], drel_low[:, :width], jnp.zeros((buckets, width), bf16)], axis=1
            ),
        ],
        axis=0,
    )
    grad_rel_table = dot(
        drel_low[:, :width], column_block(w_key, place, parts), ((1,), (1,))
    ) + dot(drel_low[:, width:], column_block(w_query, place, parts), ((1,), (1,)))
    plain, less = box_sums[0::2], box_sums[1::2]

    def box_grad(at):
        plain_here, less_here = plain[:, at : at + boxes], less[:, at : at + boxes]
        later = jnp.pad(less_here[:, 1:], ((0, 0), (0, 1)))
        grad = (plain_here - less_here + later).T
        return lax.dynamic_update_slice(jnp.zeros((boxes, heads), f32), grad, (0, place * own_heads))

    small = jnp.concatenate(
        [
            grad_rel_table.reshape(docs, -1),
            grad_ln1_gain.reshape(docs, -1),
            grad_ln1_bias.reshape(docs, -1),
            grad_ln2_gain.reshape(docs, -1),
            grad_ln2_bias.reshape(docs, -1),
            grad_b_in.reshape(docs, -1),
            box_grad(0).reshape(docs, -1),
            box_grad(boxes).reshape(docs, -1),
        ],
        axis=1,
    ).astype(bf16)
    small_width = small.shape[1]
    across = 3 * width
    small = jnp.pad(small, ((0, 0), (0, -small_width % (8 * across))))
    small = for_docs([small[at] for at in range(docs)], doc_place)
    small = jnp.stack(small).reshape(docs, -1, across)
    keep, send = halves(left, right)
    middle = docs // 2
    chunk_rows = model // docs

    def with_small(main, extra):
        main = main.reshape(middle, chunk_rows, across)
        return jnp.concatenate([main, extra], axis=1).reshape(-1, across)

    qkv_part = halve(with_small(keep, small[:middle]), with_small(send, small[middle:]), bits)

    _, came = spread(None, {at: row_block(dqkv, at) for at in order})
    came = by_place([came[at] for at in range(parts)], place)
    grad_tokens = grad_resid
    for at, weight in enumerate((w_query, w_key, w_value)):
        grad = jnp.concatenate([rows[:, at * width : (at + 1) * width] for rows in came], axis=1)
        grad_tokens = grad_tokens + dot(grad, weight, ((1,), (1,)))

    def whole(part):
        got, _ = spread(part, None)
        return by_place([got[at] for at in range(parts)], place)

    grad_w_down = jnp.concatenate(whole(down_part), axis=0).astype(f32)
    grad_w_in = jnp.concatenate(whole(in_part), axis=1).astype(f32)
    grad_w_out = jnp.concatenate(whole(out_part), axis=1).astype(f32)
    pieces = whole(qkv_part)
    grads = [
        jnp.concatenate(
            [piece[:chunk_rows, at * width : (at + 1) * width] for piece in pieces], axis=1
        ).astype(f32)
        for at in range(3)
    ]
    total = sum(piece[chunk_rows:].astype(f32) for piece in pieces).reshape(-1)
    sizes = [
        (buckets // docs, model),
        (model // docs,),
        (model // docs,),
        (model // docs,),
        (model // docs,),
        (hidden_units // docs,),
        (boxes // docs, heads),
        (boxes // docs, heads),
    ]
    small_out = []
    start = 0
    for size in sizes:
        small_out.append(total[start : start + math.prod(size)].reshape(size))
        start += math.prod(size)
    rel_out, ln1g, ln1b, ln2g, ln2b, b_in_out, xb, yb = small_out
    return (
        block_out, grad_tokens[None], ln1g, ln1b, grads[0], grads[1], grads[2], grad_w_out,
        rel_out, xb, yb, ln2g, ln2b, grad_w_in, b_in_out, grad_w_down,
    )


blocks = 4
slots = (0, 2, 1, 3)


def rows_of(handle, tile=None, column=None):
    array, lead = handle if isinstance(handle, tuple) else (handle, None)
    shape = array.shape[-2:] if tile is None else tile
    column = column or (lambda *grid: 0)
    if lead is None:
        return pl.BlockSpec(shape, lambda *grid: (0, column(*grid)))
    return pl.BlockSpec((None,) + shape, lambda *grid: (lead, 0, column(*grid)))


def array_of(handle):
    return handle[0] if isinstance(handle, tuple) else handle


def full(shape):
    return pl.BlockSpec(shape, lambda *grid: (0,) * len(shape))


def params(limit):
    return pltpu.CompilerParams(vmem_limit_bytes=limit << 20)


def gelu_parts(u):
    root = math.sqrt(2.0 / math.pi)
    inner = jnp.tanh(root * (u + 0.044715 * u * u * u))
    value = 0.5 * u * (1.0 + inner)
    slope = 0.5 * (1.0 + inner) + 0.5 * u * (1.0 - inner * inner) * root * (
        1.0 + 3.0 * 0.044715 * u * u
    )
    return value, slope


def scores_kernel(
    at_ref, x0, x1, x2, x3, i0, i1, i2, i3, wq_ref, wk_ref, wv_ref, rel_ref, tab_ref,
    own_ref, core_ref, far_ref, probs_ref, qkv_ref, relkq_ref, row_ref, col_ref, key_rel,
):
    scale = 1.0 / math.sqrt(192.0)
    step = pl.program_id(0)
    rows = blocks * lanes
    width = wq_ref.shape[1]
    heads = tab_ref.shape[1]
    size = width // heads

    @pl.when(step == 0)
    def _():
        for t, (x_ref, i_ref) in enumerate(zip((x0, x1, x2, x3), (i0, i1, i2, i3))):
            span = slice(t * lanes, (t + 1) * lanes)
            for at, w_ref in enumerate((wq_ref, wk_ref, wv_ref)):
                qkv_ref[span, at * width : (at + 1) * width] = dot(
                    x_ref[...], w_ref[...]
                ).astype(bf16)
            first = jnp.bitwise_xor(at_ref[0], slots[t]) * lanes
            slot = first + lax.broadcasted_iota(jnp.int32, (8, lanes), 1)
            kind = lax.broadcasted_iota(jnp.int32, (8, lanes), 0)
            ints = jnp.where(kind == 3, (slot < at_ref[1]).astype(jnp.int32), i_ref[...])
            row_ref[:, span] = ints
            col_ref[span, :] = ints.astype(f32).T.astype(jnp.int32)
        relkq_ref[:, :width] = dot(rel_ref[...], wk_ref[...]).astype(bf16)
        relkq_ref[:, width:] = dot(rel_ref[...], wq_ref[...]).astype(bf16)
        for h in range(heads):
            cols = slice(width + h * size, width + (h + 1) * size)
            key_rel[h] = (
                dot(qkv_ref[:, cols], relkq_ref[:, cols], ((1,), (1,))).astype(bf16).astype(f32)
            )

    here = pl.ds(pl.multiple_of(step * lanes, lanes), lanes)
    pos_i = col_ref[here, 0:1]
    cx_i = col_ref[here, 1:2]
    cy_i = col_ref[here, 2:3]
    own_row = row_ref[0:1, here]
    ahead, mirror, across, vertical = [], [], [], []
    for t in range(blocks):
        span = slice(t * lanes, (t + 1) * lanes)
        ahead.append(ahead_of(pos_i, row_ref[0:1, span]))
        mirror.append(ahead_of(col_ref[span, 0:1], own_row))
        across.append(jnp.clip(jnp.right_shift(cx_i - row_ref[1:2, span], 5), -32, 31) + 32)
        vertical.append(jnp.clip(jnp.right_shift(cy_i - row_ref[2:3, span], 5), -32, 31) + 96)
    valid = row_ref[3:4, :] > 0
    attended = []
    for h in range(heads):
        cols = slice(h * size, (h + 1) * size)
        query = qkv_ref[here, cols]
        rel_scores = (
            dot(query, relkq_ref[:, cols], ((1,), (1,))).astype(bf16).astype(f32)
        )
        table = jnp.broadcast_to(tab_ref[0, h : h + 1, :], (lanes, lanes))
        pieces = []
        for t in range(blocks):
            span = slice(t * lanes, (t + 1) * lanes)
            content = dot(
                query, qkv_ref[span, width + h * size : width + (h + 1) * size], ((1,), (1,))
            )
            mirrored = pick(key_rel[h, span, :], mirror[t]).T
            bias = pick(table, across[t]) + pick(table, vertical[t])
            pieces.append(
                scale * (content + pick(rel_scores, ahead[t]) + mirrored) + bias
            )
        scores = jnp.where(valid, jnp.concatenate(pieces, axis=1), mask_value)
        top = jnp.max(scores, axis=1, keepdims=True)
        raised = jnp.exp(scores - top)
        probs = (raised * (1.0 / jnp.sum(raised, axis=1, keepdims=True))).astype(bf16)
        probs_ref[h] = probs
        attended.append(
            dot(
                probs, qkv_ref[:, 2 * width + h * size : 2 * width + (h + 1) * size]
            ).astype(bf16)
        )
    attended = jnp.concatenate(attended, axis=1)
    for t, target in enumerate((own_ref, far_ref.at[0], core_ref, far_ref.at[1])):

        @pl.when(step == t)
        def _(target=target):
            target[...] = attended


def scores_call(at, xs, ints, w_query, w_key, w_value, rel_table, tables):
    rows, model = blocks * lanes, w_query.shape[0]
    parts, heads, _ = tables.shape
    width = w_query.shape[1] // parts
    buckets = rel_table.shape[0]
    column = pl.BlockSpec((model, width), lambda i, at: (0, at[0]))
    return pl.pallas_call(
        scores_kernel,
        out_shape=(
            jax.ShapeDtypeStruct((lanes, width), bf16),
            jax.ShapeDtypeStruct((lanes, width), bf16),
            jax.ShapeDtypeStruct((2, lanes, width), bf16),
            jax.ShapeDtypeStruct((heads, rows, rows), bf16),
            jax.ShapeDtypeStruct((rows, 3 * width), bf16),
            jax.ShapeDtypeStruct((buckets, 2 * width), bf16),
            jax.ShapeDtypeStruct((8, rows), jnp.int32),
            jax.ShapeDtypeStruct((rows, 8), jnp.int32),
        ),
        grid_spec=pltpu.PrefetchScalarGridSpec(
            num_scalar_prefetch=1,
            grid=(blocks,),
            in_specs=[rows_of(x) for x in xs]
            + [rows_of(i) for i in ints]
            + [
                column,
                column,
                column,
                full((buckets, model)),
                pl.BlockSpec((1, heads, lanes), lambda i, at: (at[0], 0, 0)),
            ],
            out_specs=[
                full((lanes, width)),
                full((lanes, width)),
                full((2, lanes, width)),
                pl.BlockSpec((heads, lanes, rows), lambda i, at: (0, i, 0)),
                full((rows, 3 * width)),
                full((buckets, 2 * width)),
                full((8, rows)),
                full((rows, 8)),
            ],
            scratch_shapes=[pltpu.VMEM((heads, rows, lanes), f32)],
        ),
        compiler_params=params(56),
        cost_estimate=pl.CostEstimate(
            flops=10**10, transcendentals=10**6, bytes_accessed=8 << 20
        ),
        name="scores",
    )(
        at, *map(array_of, xs), *map(array_of, ints), w_query, w_key, w_value, rel_table, tables
    )


def up_kernel(
    at_ref, a0, a1, a2, a3, x_ref, wout_ref, gain_ref, bias_ref, win_ref, bin_ref,
    far_ref, core_ref, own_ref, act_ref, slope_ref, normed_ref, inverse_ref, attended_ref,
    hidden_low,
):
    step = pl.program_id(0)
    width = a0.shape[1]
    tile = win_ref.shape[1]

    @pl.when(step == 0)
    def _():
        total = x_ref[...].astype(f32)
        for t, piece in enumerate((a0, a1, a2, a3)):
            first = pl.multiple_of(jnp.bitwise_xor(at_ref[0], slots[t]) * width, width)
            total = total + dot(piece[...], wout_ref[pl.ds(first, width), :])
            attended_ref[:, pl.ds(first, width)] = piece[...]
        centered = total - jnp.mean(total, axis=1, keepdims=True)
        inverse = lax.rsqrt(jnp.mean(centered * centered, axis=1, keepdims=True) + norm_eps)
        normed = centered * inverse
        normed_ref[...] = normed
        inverse_ref[...] = jnp.broadcast_to(inverse, inverse_ref.shape)
        hidden = (normed * gain_ref[...] + bias_ref[...]).astype(bf16)
        hidden_low[...] = hidden
        far_ref[0] = hidden
        core_ref[0] = hidden

    value, slope = gelu_parts(dot(hidden_low[...], win_ref[...]) + bin_ref[...])
    value = value.astype(bf16)
    act_ref[...] = value
    slope_ref[...] = slope.astype(bf16)
    strip = tile // blocks
    here = pl.ds(pl.multiple_of(step * strip, strip), strip)
    for t, target in enumerate((own_ref, far_ref.at[1], core_ref.at[1], far_ref.at[2])):
        first = pl.multiple_of(jnp.bitwise_xor(at_ref[0], slots[t]) * strip, strip)
        target[:, here] = act_ref[:, pl.ds(first, strip)]


def up_call(at, pieces, x_own, w_out, gain, bias, w_in, b_in, docs):
    rows, model = x_own.shape
    units = w_in.shape[1]
    tile = units // docs
    quarter = units // blocks
    column = lambda i, at: (0, i)
    return pl.pallas_call(
        up_kernel,
        out_shape=(
            jax.ShapeDtypeStruct((3, rows, model), bf16),
            jax.ShapeDtypeStruct((2, rows, model), bf16),
            jax.ShapeDtypeStruct((rows, quarter), bf16),
            jax.ShapeDtypeStruct((rows, units), bf16),
            jax.ShapeDtypeStruct((rows, units), bf16),
            jax.ShapeDtypeStruct((rows, model), f32),
            jax.ShapeDtypeStruct((rows, lanes), f32),
            jax.ShapeDtypeStruct((rows, model), bf16),
        ),
        grid_spec=pltpu.PrefetchScalarGridSpec(
            num_scalar_prefetch=1,
            grid=(docs,),
            in_specs=[rows_of(piece) for piece in pieces]
            + [
                full((rows, model)),
                full((model, model)),
                full((1, model)),
                full((1, model)),
                pl.BlockSpec((model, tile), column),
                pl.BlockSpec((1, tile), column),
            ],
            out_specs=[
                full((3, rows, model)),
                full((2, rows, model)),
                full((rows, quarter)),
                pl.BlockSpec((rows, tile), column),
                pl.BlockSpec((rows, tile), column),
                full((rows, model)),
                full((rows, lanes)),
                full((rows, model)),
            ],
            scratch_shapes=[pltpu.VMEM((rows, model), bf16)],
        ),
        compiler_params=params(40),
        cost_estimate=pl.CostEstimate(
            flops=4 * 10**9, transcendentals=10**6, bytes_accessed=12 << 20
        ),
        name="up",
    )(at, *map(array_of, pieces), x_own, w_out, gain, bias, w_in, b_in)


def down_kernel(
    at_ref, act_ref, wdown_ref, slope_ref, win_ref, wout_ref, normed_ref, inverse_ref,
    cot_ref, attended_ref, gain1_ref, bias1_ref, gain2_ref, bias2_ref,
    block_ref, own_ref, core_ref, far_ref, resid_ref, upfar_ref, upcore_ref, upown_ref,
    outfar_ref, outcore_ref, outown_ref, sums_ref,
    total, grad_ffn, grad_up,
):
    step = pl.program_id(0)
    steps = pl.num_programs(0) // 2
    rows, tile = slope_ref.shape
    model = block_ref.shape[1]
    width = model // blocks

    @pl.when(step == 0)
    def _():
        total[...] = normed_ref[...] * gain1_ref[...] + bias1_ref[...]

    @pl.when(step < steps)
    def _():
        total[...] += dot(act_ref[...], wdown_ref[...])

    def back(grad, normed, inverse, gain):
        scaled = grad * gain
        return inverse * (
            scaled
            - jnp.mean(scaled, axis=1, keepdims=True)
            - normed * jnp.mean(scaled * normed, axis=1, keepdims=True)
        )

    @pl.when(step == steps - 1)
    def _():
        mixed = total[...]
        centered = mixed - jnp.mean(mixed, axis=1, keepdims=True)
        inverse = lax.rsqrt(jnp.mean(centered * centered, axis=1, keepdims=True) + norm_eps)
        normed = centered * inverse
        block_ref[...] = (normed * gain2_ref[...] + bias2_ref[...]).astype(bf16)
        grad = cot_ref[...].astype(f32)
        sums_ref[2:3, :] = jnp.sum(grad * normed, axis=0, keepdims=True)
        sums_ref[3:4, :] = jnp.sum(grad, axis=0, keepdims=True)
        mix = back(grad, normed, inverse, gain2_ref[...])
        total[...] = mix
        grad_ffn[...] = mix.astype(bf16)
        upfar_ref[0] = mix.astype(bf16)
        upcore_ref[0] = mix.astype(bf16)

    @pl.when(step >= steps)
    def _():
        at = step - steps
        grad = dot(grad_ffn[...], wdown_ref[...], ((1,), (1,))) * slope_ref[...].astype(f32)
        low = grad.astype(bf16)
        total[...] += dot(low, win_ref[...], ((1,), (1,)))
        per = model // tile
        part = at // per
        here = pl.ds(pl.multiple_of((at - part * per) * tile, tile), tile)
        grad_up[jnp.bitwise_xor(part, at_ref[0]), :, here] = low
        sums_ref[pl.ds(4 + part, 1), here] = jnp.sum(low.astype(f32), axis=0, keepdims=True)

    @pl.when(step == 2 * steps - 1)
    def _():
        upown_ref[...] = grad_up[0]
        upcore_ref[1] = grad_up[1]
        upfar_ref[1] = grad_up[2]
        upfar_ref[2] = grad_up[3]
        grad = total[...]
        normed = normed_ref[...]
        sums_ref[0:1, :] = jnp.sum(grad * normed, axis=0, keepdims=True)
        sums_ref[1:2, :] = jnp.sum(grad, axis=0, keepdims=True)
        resid = back(grad, normed, inverse_ref[:, 0:1], gain1_ref[...])
        resid_ref[...] = resid
        low = resid.astype(bf16)
        total[...] = low.astype(f32)
        outfar_ref[:, :model] = attended_ref[...]
        outcore_ref[:, :model] = attended_ref[...]
        targets = (own_ref, core_ref, far_ref.at[0], far_ref.at[1])
        wides = (
            outown_ref, outcore_ref.at[:, pl.ds(model, width)],
            outfar_ref.at[:, pl.ds(model, width)], outfar_ref.at[:, pl.ds(model + width, width)],
        )
        for at, (target, wide) in enumerate(zip(targets, wides)):
            first = pl.multiple_of(jnp.bitwise_xor(at_ref[0], at) * width, width)
            target[...] = dot(low, wout_ref[pl.ds(first, width), :], ((1,), (1,))).astype(bf16)
            wide[...] = total[:, pl.ds(first, width)].astype(bf16)


def down_call(
    at, act, w_down, slope, w_in, w_out, normed, inverse, cotangent, attended,
    gain1, bias1, gain2, bias2, tile,
):
    rows, units = act.shape
    model = w_out.shape[0]
    width = model // blocks
    steps = units // tile
    first = lambda i, at: (0, jnp.minimum(i, steps - 1))
    second = lambda i, at: (0, jnp.maximum(i - steps, 0))
    return pl.pallas_call(
        down_kernel,
        out_shape=(
            jax.ShapeDtypeStruct((rows, model), bf16),
            jax.ShapeDtypeStruct((rows, width), bf16),
            jax.ShapeDtypeStruct((rows, width), bf16),
            jax.ShapeDtypeStruct((2, rows, width), bf16),
            jax.ShapeDtypeStruct((rows, model), f32),
            jax.ShapeDtypeStruct((3, rows, model), bf16),
            jax.ShapeDtypeStruct((2, rows, model), bf16),
            jax.ShapeDtypeStruct((rows, model), bf16),
            jax.ShapeDtypeStruct((rows, model + 2 * width), bf16),
            jax.ShapeDtypeStruct((rows, model + width), bf16),
            jax.ShapeDtypeStruct((rows, width), bf16),
            jax.ShapeDtypeStruct((8, model), f32),
        ),
        grid_spec=pltpu.PrefetchScalarGridSpec(
            num_scalar_prefetch=1,
            grid=(2 * steps,),
            in_specs=[
                pl.BlockSpec((rows, tile), first),
                pl.BlockSpec((tile, model), lambda i, at: (lax.rem(i, steps), 0)),
                pl.BlockSpec((rows, tile), second),
                pl.BlockSpec((model, tile), second),
                full((model, model)),
                full((rows, model)),
                full((rows, lanes)),
                full((rows, model)),
                full((rows, model)),
                full((1, model)),
                full((1, model)),
                full((1, model)),
                full((1, model)),
            ],
            out_specs=[
                full((rows, model)),
                full((rows, width)),
                full((rows, width)),
                full((2, rows, width)),
                full((rows, model)),
                full((3, rows, model)),
                full((2, rows, model)),
                full((rows, model)),
                full((rows, model + 2 * width)),
                full((rows, model + width)),
                full((rows, width)),
                full((8, model)),
            ],
            scratch_shapes=[
                pltpu.VMEM((rows, model), f32),
                pltpu.VMEM((rows, model), bf16),
                pltpu.VMEM((blocks, rows, model), bf16),
            ],
        ),
        compiler_params=params(40),
        cost_estimate=pl.CostEstimate(
            flops=8 * 10**9, transcendentals=0, bytes_accessed=28 << 20
        ),
        name="down",
    )(
        at, act, w_down, slope, w_in, w_out, normed, inverse, cotangent, attended,
        gain1, bias1, gain2, bias2,
    )


def scores_grad_kernel(
    at_ref, g0, g1, g2, g3, qkv_ref, probs_ref, relkq_ref, row_ref, col_ref, wq_ref, wk_ref,
    sums_ref,
    dqkv_ref, core_ref, far_ref, small_ref,
    ga_ref, ds_ref, drel, box_sums,
):
    scale = 1.0 / math.sqrt(192.0)
    rows = blocks * lanes
    heads = probs_ref.shape[0]
    width = g0.shape[1]
    size = width // heads
    span_width = 3 * lanes
    for t, piece in enumerate((g0, g1, g2, g3)):
        ga_ref[t * lanes : (t + 1) * lanes, :] = piece[...]
    drel[...] = jnp.zeros_like(drel)
    box_sums[...] = jnp.zeros_like(box_sums)
    window = lax.broadcasted_iota(jnp.int32, (rows, span_width), 1)
    bucket = lax.broadcasted_iota(jnp.int32, (lanes, lanes), 1)
    label = lax.broadcasted_iota(jnp.int32, (rows, lanes), 1)
    all_pos = col_ref[:, 0:1]
    all_x, all_y = col_ref[:, 1:2], col_ref[:, 2:3]
    sector_x, sector_y = jnp.right_shift(all_x, 5), jnp.right_shift(all_y, 5)
    hot_x = (label == sector_x).astype(bf16)
    hot_y = (label == sector_y + 64).astype(bf16)
    hot_both = ((label == sector_x) | (label == sector_y + 64)).astype(bf16)

    def histogram(sums, total, at, base_row):
        first = at - base_row + (lanes - 1) - bucket
        low = jnp.bitwise_and(first, lanes - 1)
        group = jnp.right_shift(first, 7)
        found = jnp.where(
            group == 0,
            pick(sums[:, :lanes], low),
            jnp.where(
                group == 1,
                pick(sums[:, lanes : 2 * lanes], low),
                pick(sums[:, 2 * lanes :], low),
            ),
        )
        found = jnp.where(bucket == 0, total, found)
        later = jnp.where(bucket == lanes - 1, 0.0, pltpu.roll(found, lanes - 1, 1))
        return found - later

    def by_rows(ib, carry):
        here = pl.ds(pl.multiple_of(ib * lanes, lanes), lanes)
        pos_i = col_ref[here, 0:1]
        cx_i, cy_i = col_ref[here, 1:2], col_ref[here, 2:3]
        base = jnp.min(pos_i, axis=0, keepdims=True)
        below = (all_pos <= base - 63 + window).astype(bf16)
        short_x = jnp.bitwise_and(cx_i, 31) < jnp.bitwise_and(row_ref[1:2, :], 31)
        short_y = jnp.bitwise_and(cy_i, 31) < jnp.bitwise_and(row_ref[2:3, :], 31)
        step_x = jnp.right_shift(cx_i, 5) + 32 - bucket
        step_y = jnp.right_shift(cy_i, 5) + 32 - (bucket - 64)
        in_x = (bucket < 64) & (step_x >= 0) & (step_x < 32)
        in_y = (bucket >= 64) & (step_y >= 0) & (step_y < 32)
        seek = jnp.where(in_x, step_x, jnp.where(in_y, step_y + 64, 0))
        inside = in_x | in_y
        for h in range(heads):
            cols = slice(h * size, (h + 1) * size)
            kcols = slice(width + h * size, width + (h + 1) * size)
            vcols = slice(2 * width + h * size, 2 * width + (h + 1) * size)
            probs = probs_ref[h, here, :].astype(f32)
            gained = dot(ga_ref[here, cols], qkv_ref[:, vcols], ((1,), (1,)))
            row_dots = jnp.sum(probs * gained, axis=1, keepdims=True)
            grad = (probs * (gained - row_dots)).astype(bf16)
            ds_ref[h, here, :] = grad
            exact = grad.astype(f32)
            total = jnp.sum(exact, axis=1, keepdims=True)
            rel = histogram(dot(grad, below), total, pos_i, base)
            rel = (scale * rel).astype(bf16)
            dqkv_ref[here, cols] = (
                scale * dot(grad, qkv_ref[:, kcols]) + dot(rel, relkq_ref[:, cols])
            ).astype(bf16)
            drel[:, cols] += dot(rel, qkv_ref[here, cols], ((0,), (0,)))
            grad_x = jnp.where(short_x, exact, 0.0).astype(bf16)
            grad_y = jnp.where(short_y, exact, 0.0).astype(bf16)
            plain = dot(grad, hot_both)
            less = dot(grad_x, hot_x) + dot(grad_y, hot_y)
            plain = jnp.where(inside, pick(plain, seek), 0.0)
            less = jnp.where(inside, pick(less, seek), 0.0)
            box_sums[h : h + 1, :] += jnp.sum(plain, axis=0, keepdims=True)
            box_sums[8 + h : 9 + h, :] += jnp.sum(less, axis=0, keepdims=True)
        return carry

    lax.fori_loop(0, blocks, by_rows, 0)

    def by_columns(jb, carry):
        here = pl.ds(pl.multiple_of(jb * lanes, lanes), lanes)
        pos_j = col_ref[here, 0:1]
        base = jnp.min(pos_j, axis=0, keepdims=True)
        below = (all_pos <= base - 63 + window).astype(bf16)
        for h in range(heads):
            cols = slice(h * size, (h + 1) * size)
            kcols = slice(width + h * size, width + (h + 1) * size)
            vcols = slice(2 * width + h * size, 2 * width + (h + 1) * size)
            grad = ds_ref[h, :, here]
            total = dot(grad, jnp.ones((rows, lanes), bf16), ((0,), (0,)))
            sums = dot(grad, below, ((0,), (0,)))
            mirror = (scale * histogram(sums, total, pos_j, base)).astype(bf16)
            dqkv_ref[here, kcols] = (
                scale * dot(grad, qkv_ref[:, cols], ((0,), (0,)))
                + dot(mirror, relkq_ref[:, kcols])
            ).astype(bf16)
            drel[:, kcols] += dot(mirror, qkv_ref[here, kcols], ((0,), (0,)))
            dqkv_ref[here, vcols] = dot(
                probs_ref[h, :, here], ga_ref[:, cols], ((0,), (0,))
            ).astype(bf16)
        return carry

    lax.fori_loop(0, blocks, by_columns, 0)
    far_ref[0] = dqkv_ref[lanes : 2 * lanes, :]
    core_ref[...] = dqkv_ref[2 * lanes : 3 * lanes, :]
    far_ref[1] = dqkv_ref[3 * lanes : 4 * lanes, :]
    keys, queries = drel[:, :width].astype(bf16), drel[:, width:].astype(bf16)
    dqkv_ref[rows:, :width] = queries
    dqkv_ref[rows:, width : 2 * width] = keys
    dqkv_ref[rows:, 2 * width :] = jnp.zeros((lanes, width), bf16)

    docs, small_rows, small_width = small_ref.shape
    per = lanes // docs
    table = (
        dot(keys, wk_ref[...], ((1,), (1,))) + dot(queries, wq_ref[...], ((1,), (1,)))
    ).astype(bf16)
    plain, less = box_sums[0:8, :], box_sums[8:16, :]
    place_lane = lax.broadcasted_iota(jnp.int32, (8, lanes), 1)
    later = jnp.where(
        jnp.bitwise_and(place_lane, 63) == 63, 0.0, pltpu.roll(less, lanes - 1, 1)
    )
    boxes = (plain - less + later).astype(bf16)
    row_at = lax.broadcasted_iota(jnp.int32, (8, lanes), 0)
    chosen = ((place_lane == at_ref[0] * heads + row_at) & (row_at < heads)).astype(bf16)
    boxes = dot(boxes, chosen, ((0,), (0,)))
    small_ref[...] = jnp.zeros_like(small_ref)
    model = table.shape[1]
    rest = model - small_width
    sums = sums_ref[...]
    share = model // docs
    for chunk in range(docs):
        small_ref[chunk, 0:per, :] = table[chunk * per : (chunk + 1) * per, :small_width].astype(f32)
        small_ref[chunk, per : 2 * per, 0:rest] = (
            table[chunk * per : (chunk + 1) * per, small_width:].astype(f32)
        )
        for at in range(4):
            small_ref[chunk, per + at : per + at + 1, rest : rest + share] = (
                sums[at : at + 1, chunk * share : (chunk + 1) * share]
            )
        bin_at = chunk * blocks * share
        for at in range(blocks):
            first = bin_at + at * share
            line, first = first // model, first % model
            small_ref[chunk, per + at : per + at + 1, rest + share : rest + 2 * share] = (
                sums[4 + line : 5 + line, first : first + share]
            )
        count = lanes // 2 // docs
        for axis in range(2):
            begin = axis * 64 + chunk * count
            lane = rest + (2 + axis) * share
            small_ref[chunk, per : per + count, lane : lane + lanes] = boxes[begin : begin + count, :]


def scores_grad_call(at, pieces, qkv, probs, relkq, row, col, w_query, w_key, sums, docs):
    rows = blocks * lanes
    heads = probs.shape[0]
    model = w_query.shape[0]
    width = model // blocks
    buckets = relkq.shape[0]
    column = pl.BlockSpec((model, width), lambda i, at: (0, at[0]))
    return pl.pallas_call(
        scores_grad_kernel,
        out_shape=(
            jax.ShapeDtypeStruct((rows + buckets, 3 * width), bf16),
            jax.ShapeDtypeStruct((lanes, 3 * width), bf16),
            jax.ShapeDtypeStruct((2, lanes, 3 * width), bf16),
            jax.ShapeDtypeStruct((docs, 2 * buckets // docs, 3 * width), f32),
        ),
        grid_spec=pltpu.PrefetchScalarGridSpec(
            num_scalar_prefetch=1,
            grid=(1,),
            in_specs=[rows_of(piece) for piece in pieces]
            + [
                full((rows, 3 * width)),
                full((heads, rows, rows)),
                full((buckets, 2 * width)),
                full((8, rows)),
                full((rows, 8)),
                column,
                column,
                full((8, model)),
            ],
            out_specs=[
                full((rows + buckets, 3 * width)),
                full((lanes, 3 * width)),
                full((2, lanes, 3 * width)),
                full((docs, 2 * buckets // docs, 3 * width)),
            ],
            scratch_shapes=[
                pltpu.VMEM((rows, width), bf16),
                pltpu.VMEM((heads, rows, rows), bf16),
                pltpu.VMEM((buckets, 2 * width), f32),
                pltpu.VMEM((16, lanes), f32),
            ],
        ),
        compiler_params=params(56),
        cost_estimate=pl.CostEstimate(
            flops=2 * 10**10, transcendentals=0, bytes_accessed=8 << 20
        ),
        name="scores_grad",
    )(at, *map(array_of, pieces), qkv, probs, relkq, row, col, w_query, w_key, sums)


def weight_grad_call(at, lefts, rights, bits, extra=None, right_column=0, right_width=None, name="weight_grad"):
    count = 1 << len(bits)
    model = array_of(lefts[0]).shape[-1]
    chunk = lanes
    width = right_width or array_of(rights[0]).shape[-1]
    pieces = len(lefts)
    tail = 0 if extra is None else extra.shape[1]
    per = 2
    steps = count // per
    half = steps // 2

    def offset(p):
        total = 0
        for place, bit in enumerate(bits):
            total = total + jnp.bitwise_and(jnp.right_shift(p, len(bits) - 1 - place), 1) * bit
        return total

    def chunk_of(i, at, which):
        p = lax.rem(i + half, steps) * per + which
        return jnp.bitwise_xor(at[1], offset(p))

    def kernel(at_ref, *refs):
        left_refs, refs = refs[: pieces * per], refs[pieces * per :]
        right_refs, refs = refs[:pieces], refs[pieces:]
        if extra is not None:
            extra_refs, refs = refs[:per], refs[per:]
        keep_ref, send_ref, right_all = refs
        step = pl.program_id(0)

        @pl.when(step == 0)
        def _():
            for at, ref in enumerate(right_refs):
                right_all[at * lanes : (at + 1) * lanes, :] = ref[...]

        left = jnp.concatenate(
            [
                jnp.concatenate([left_refs[at * per + which][...] for which in range(per)], axis=1)
                for at in range(pieces)
            ],
            axis=0,
        )
        result = dot(left, right_all[...], ((0,), (0,))).astype(bf16)
        for target, mine in ((send_ref, step < half), (keep_ref, step >= half)):

            @pl.when(mine)
            def _(target=target):
                for which in range(per):
                    target[which, :chunk, :] = result[which * chunk : (which + 1) * chunk, :]
                    if extra is not None:
                        target[which, chunk:, :] = extra_refs[which][...].astype(bf16)

    in_specs, operands = [], []
    for handle in lefts:
        for which in range(per):
            in_specs.append(
                rows_of(handle, (lanes, chunk), lambda i, at, which=which: chunk_of(i, at, which))
            )
            operands.append(array_of(handle))
    for handle in rights:
        column = handle[2] if isinstance(handle, tuple) and len(handle) == 3 else right_column
        handle = handle[:2] if isinstance(handle, tuple) and handle[1] is not None else array_of(handle)
        in_specs.append(rows_of(handle, (lanes, width), lambda i, at, column=column: column))
        operands.append(array_of(handle))
    if extra is not None:
        for which in range(per):
            in_specs.append(
                pl.BlockSpec(
                    (None, tail, width), lambda i, at, which=which: (chunk_of(i, at, which), 0, 0)
                )
            )
            operands.append(extra)
    shape = jax.ShapeDtypeStruct((count // 2, chunk + tail, width), bf16)
    block = (per, chunk + tail, width)
    return pl.pallas_call(
        kernel,
        out_shape=(shape, shape),
        grid_spec=pltpu.PrefetchScalarGridSpec(
            num_scalar_prefetch=1,
            grid=(steps,),
            in_specs=in_specs,
            out_specs=[
                pl.BlockSpec(block, lambda i, at: (jnp.maximum(i - half, 0), 0, 0)),
                pl.BlockSpec(block, lambda i, at: (jnp.minimum(i, half - 1), 0, 0)),
            ],
            scratch_shapes=[pltpu.VMEM((pieces * lanes, width), bf16)],
        ),
        compiler_params=params(40),
        cost_estimate=pl.CostEstimate(
            flops=2 * pieces * lanes * model * width,
            transcendentals=0,
            bytes_accessed=2 * (pieces * lanes + model) * (model + width),
        ),
        name=name,
    )(at, *operands)


def tokens_grad_kernel(at_ref, d0, d1, d2, d3, resid_ref, wq_ref, wk_ref, wv_ref, out_ref):
    step = pl.program_id(0)
    width = wq_ref.shape[1]

    @pl.when(step == 0)
    def _():
        out_ref[...] = resid_ref[...]

    for t, piece in enumerate((d0, d1, d2, d3)):

        @pl.when(step == t)
        def _(piece=piece):
            total = out_ref[...]
            for at, w_ref in enumerate((wq_ref, wk_ref, wv_ref)):
                total = total + dot(
                    piece[:, at * width : (at + 1) * width], w_ref[...], ((1,), (1,))
                )
            out_ref[...] = total


def tokens_grad_call(at, pieces, resid, w_query, w_key, w_value):
    rows, model = resid.shape
    width = model // blocks
    tile = (rows, 3 * width)

    def column(i, at):
        offset = jnp.where(i == 1, 2, jnp.where(i == 2, 1, i))
        return (0, jnp.bitwise_xor(at[0], offset))

    weight = pl.BlockSpec((model, width), column)
    return pl.pallas_call(
        tokens_grad_kernel,
        out_shape=jax.ShapeDtypeStruct((rows, model), f32),
        grid_spec=pltpu.PrefetchScalarGridSpec(
            num_scalar_prefetch=1,
            grid=(blocks,),
            in_specs=[rows_of(piece, tile) for piece in pieces]
            + [full((rows, model)), weight, weight, weight],
            out_specs=full((rows, model)),
        ),
        compiler_params=params(40),
        cost_estimate=pl.CostEstimate(
            flops=8 * 10**8, transcendentals=0, bytes_accessed=8 << 20
        ),
        name="tokens_grad",
    )(at, *map(array_of, pieces), resid, w_query, w_key, w_value)


def halve_chunks(keep, send, bits):
    for place, bit in enumerate(bits):
        came = swap(send, "docs", bit)
        total = lambda part: (keep[part].astype(f32) + came[part].astype(f32)).astype(bf16)
        middle = keep.shape[0] // 2
        if place + 1 < len(bits):
            send = total(slice(middle, None))
            keep = total(slice(0, middle))
        else:
            keep = total(slice(None))
    return keep[0]


def across_core(own, core, far):
    came_far = swap(far, "blk", 2)
    return came_far


def shards_tiles(
    tokens, lengths, positions, token_boxes, ln1_gain, ln1_bias, w_query, w_key, w_value, w_out,
    rel_table, xbias_table, ybias_table, ln2_gain, ln2_bias, w_in, b_in, w_down, cotangent,
):
    row_count, model = tokens.shape[1:]
    docs = lax.axis_size("docs")
    place = lax.axis_index("blk")
    doc_place = lax.axis_index("docs")
    heads = xbias_table.shape[1]
    boxes = xbias_table.shape[0]
    units = w_in.shape[1]
    width = model // blocks
    bits = bits_of(docs)
    other = [bits[1], bits[0]] + bits[2:]
    x_own = tokens[0]

    x_far = swap(x_own, "blk", 2)
    own_ints = jnp.concatenate(
        [
            positions,
            jnp.right_shift(token_boxes[0] + token_boxes[2], 1),
            jnp.right_shift(token_boxes[1] + token_boxes[3], 1),
            jnp.zeros((5, row_count), jnp.int32),
        ],
        axis=0,
    )
    ints_far = swap(own_ints, "blk", 2)
    x_core, ints_core = swap(x_own, "blk", 1), swap(own_ints, "blk", 1)
    x_both, ints_both = swap(x_far, "blk", 1), swap(ints_far, "blk", 1)
    xs = (x_own, x_far, x_core, x_both)
    tables = jnp.concatenate([xbias_table.T, ybias_table.T], axis=1).astype(f32)
    tables = tables.reshape(blocks, heads // blocks, 2 * boxes)
    at = jnp.stack([place.astype(jnp.int32), lengths[0]])
    spot = jnp.stack([place, doc_place]).astype(jnp.int32)
    att_own, att_core, att_far, probs, qkv, relkq, row, col = scores_call(
        at, xs, (own_ints, ints_far, ints_core, ints_both), w_query, w_key, w_value, rel_table, tables
    )

    came_far = swap(att_far, "blk", 2)
    came_core = swap(att_core, "blk", 1)
    came_both = swap(came_far, "blk", 1)
    line = lambda vector: vector.reshape(1, -1)
    far1, core1, act_own, act, slope, normed1, inverse1, attended = up_call(
        spot, (att_own, (came_far, 0), came_core, (came_both, 1)), x_own, w_out,
        line(ln1_gain), line(ln1_bias), w_in, line(b_in), docs,
    )
    got_far1 = swap(far1, "blk", 2)
    (
        block_out, ga_own, ga_core, ga_far, grad_resid, far2, core2, up_own,
        far3, core3, gattn_own, sums,
    ) = down_call(
        spot, act, w_down, slope, w_in, w_out, normed1, inverse1, cotangent[0], attended,
        line(ln1_gain), line(ln1_bias), line(ln2_gain), line(ln2_bias), units // docs,
    )
    came_far = swap(ga_far, "blk", 2)
    got_far2 = swap(far2, "blk", 2)
    got_core1, got_both1 = swap(core1, "blk", 1), swap(got_far1, "blk", 1)
    came_core = swap(ga_core, "blk", 1)
    came_both = swap(came_far, "blk", 1)
    dqkv, dq_core, dq_far, small = scores_grad_call(
        spot, (ga_own, (came_far, 0), came_core, (came_both, 1)), qkv, probs, relkq, row, col,
        w_query, w_key, sums, docs,
    )
    got_core2, got_both2 = swap(core2, "blk", 1), swap(got_far2, "blk", 1)
    got_far3 = swap(far3, "blk", 2)
    got_core3, got_both3 = swap(core3, "blk", 1), swap(got_far3, "blk", 1)

    hidden_all = [(far1, 0), (got_far1, 0), (got_core1, 0), (got_both1, 0)]
    act_all = [act_own, (got_far1, 1), (got_core1, 1), (got_both1, 2)]
    gffn_all = [(far2, 0), (got_far2, 0), (got_core2, 0), (got_both2, 0)]
    up_all = [up_own, (got_far2, 1), (got_core2, 1), (got_both2, 2)]
    att_all = [far3, got_far3, got_core3, got_both3]
    per = model // width
    gattn_all = [
        gattn_own, (got_far3, None, per), (got_core3, None, per), (got_both3, None, per + 1),
    ]

    down_part = halve_chunks(*weight_grad_call(spot, act_all, gffn_all, bits, name="grad_down"), bits)
    in_part = halve_chunks(*weight_grad_call(spot, hidden_all, up_all, other, name="grad_in"), other)
    out_part = halve_chunks(
        *weight_grad_call(spot, att_all, gattn_all, bits, right_width=width, name="grad_out"), bits
    )
    dq_rows = dqkv.reshape(blocks + 1, lanes, 3 * width)
    rights = [(dq_rows, t) for t in range(blocks + 1)]
    qkv_part = halve_chunks(
        *weight_grad_call(spot, list(xs) + [rel_table], rights, bits, extra=small, name="grad_qkv"), bits
    )

    came_far = swap(dq_far, "blk", 2)
    came_core = swap(dq_core, "blk", 1)
    came_both = swap(came_far, "blk", 1)
    grad_tokens = tokens_grad_call(
        spot, ((dq_rows, 0), (came_far, 0), came_core, (came_both, 1)), grad_resid, w_query, w_key, w_value
    )

    def whole(part):
        far = swap(part, "blk", 2)
        parts = [part, swap(part, "blk", 1), far, swap(far, "blk", 1)]
        return by_place(parts, place)

    grad_w_down = jnp.concatenate(whole(down_part), axis=0).astype(f32)
    grad_w_in = jnp.concatenate(whole(in_part), axis=1).astype(f32)
    grad_w_out = jnp.concatenate(whole(out_part), axis=1).astype(f32)
    pieces = whole(qkv_part)
    grads = [
        jnp.concatenate(
            [piece[:lanes, at * width : (at + 1) * width] for piece in pieces], axis=1
        ).astype(f32)
        for at in range(3)
    ]
    total = sum(piece[lanes:].astype(f32) for piece in pieces)
    buckets = rel_table.shape[0] // docs
    rest = model - 3 * width
    rel_out = jnp.concatenate([total[:buckets], total[buckets:, :rest]], axis=1)
    norms = [total[buckets + k, rest : rest + lanes] for k in range(4)]
    b_in_out = total[buckets : buckets + blocks, rest + lanes : rest + 2 * lanes].reshape(-1)
    box_rows = boxes // docs
    xb = total[buckets : buckets + box_rows, rest + 2 * lanes : rest + 2 * lanes + heads]
    yb = total[buckets : buckets + box_rows, rest + 3 * lanes : rest + 3 * lanes + heads]
    return (
        block_out[None], grad_tokens[None], norms[0], norms[1], grads[0], grads[1], grads[2], grad_w_out,
        rel_out, xb, yb, norms[2], norms[3], grad_w_in, b_in_out, grad_w_down,
    )


def choose(*args):
    docs, parts = lax.axis_size("docs"), lax.axis_size("blk")
    tokens, w_in = args[0], args[15]
    model, units = w_in.shape
    fits = (
        parts == blocks
        and tokens.shape[1] == lanes
        and model // docs == lanes
        and units // docs == parts * lanes
        and docs & (docs - 1) == 0
        and docs > 2
        and units == blocks * model
    )
    return (shards_tiles if fits else shards)(*args)


def solution(mesh):
    rows = P("docs", "blk", None)
    placed = (
        rows, P("docs"), P("docs", "blk"), P(None, "docs", "blk"),
        *([P()] * 14), rows,
    )
    over_docs, over_docs2 = P("docs"), P("docs", None)
    return jax.shard_map(
        choose,
        mesh=mesh,
        in_specs=placed,
        out_specs=(
            rows, rows, over_docs, over_docs, over_docs2, over_docs2, over_docs2, over_docs2,
            over_docs2, over_docs2, over_docs2, over_docs, over_docs, over_docs2, over_docs, over_docs2,
        ),
        check_vma=False,
    )
```

```python
import functools
import math

import jax
import jax.numpy as jnp
from jax import lax
from jax.experimental import pallas as pl
from jax.experimental.pallas import tpu as pltpu
from jax.sharding import PartitionSpec as P

norm_eps = 1e-05
mask_value = -1e30
f32 = jnp.float32
bf16 = jnp.bfloat16
lanes = 128


def dot(a, b, contract=((1,), (0,))):
    return lax.dot_general(a, b, (contract, ((), ())), preferred_element_type=f32)


def pick(table, index):
    return jnp.take_along_axis(table, index, axis=1, mode="promise_in_bounds")


def ahead_of(first, second):
    return jnp.clip(first - second, -64, 63) + 64


def attn_fwd_kernel(
    place, x_ref, wq_ref, wk_ref, wv_ref, rel_ref, tab_ref, row_ref, col_ref,
    att_ref, probs_ref, qkv_ref, relkq_ref, key_rel,
):
    scale = 1.0 / math.sqrt(192.0)
    step = pl.program_id(0)
    rows = x_ref.shape[0]
    width = wq_ref.shape[1]
    heads = tab_ref.shape[1]
    size = width // heads
    tiles = rows // lanes

    @pl.when(step == 0)
    def _():
        for at, w_ref in enumerate((wq_ref, wk_ref, wv_ref)):
            for t in range(tiles):
                qkv_ref[t * lanes : (t + 1) * lanes, at * width : (at + 1) * width] = dot(
                    x_ref[t * lanes : (t + 1) * lanes, :], w_ref[...]
                ).astype(bf16)
        relkq_ref[:, :width] = dot(rel_ref[...], wk_ref[...]).astype(bf16)
        relkq_ref[:, width:] = dot(rel_ref[...], wq_ref[...]).astype(bf16)
        for h in range(heads):
            key_rel[h] = (
                dot(
                    qkv_ref[:, width + h * size : width + (h + 1) * size],
                    relkq_ref[:, width + h * size : width + (h + 1) * size],
                    ((1,), (1,)),
                )
                .astype(bf16)
                .astype(f32)
            )

    here = pl.ds(pl.multiple_of(step * lanes, lanes), lanes)
    pos_i = col_ref[here, 0:1]
    cx_i = col_ref[here, 1:2]
    cy_i = col_ref[here, 2:3]
    own_row = row_ref[0:1, here]
    ahead, mirror, across, vertical = [], [], [], []
    for t in range(tiles):
        span = slice(t * lanes, (t + 1) * lanes)
        ahead.append(ahead_of(pos_i, row_ref[0:1, span]))
        mirror.append(ahead_of(col_ref[span, 0:1], own_row))
        across.append(jnp.clip(jnp.right_shift(cx_i - row_ref[1:2, span], 5), -32, 31) + 32)
        vertical.append(jnp.clip(jnp.right_shift(cy_i - row_ref[2:3, span], 5), -32, 31) + 96)
    valid = row_ref[3:4, :] > 0
    for h in range(heads):
        cols = slice(h * size, (h + 1) * size)
        query = qkv_ref[here, cols]
        rel_scores = (
            dot(query, relkq_ref[:, cols], ((1,), (1,))).astype(bf16).astype(f32)
        )
        table = jnp.broadcast_to(tab_ref[0, h : h + 1, :], (lanes, lanes))
        pieces = []
        for t in range(tiles):
            span = slice(t * lanes, (t + 1) * lanes)
            content = dot(
                query, qkv_ref[span, width + h * size : width + (h + 1) * size], ((1,), (1,))
            )
            mirrored = pick(key_rel[h, span, :], mirror[t]).T
            bias = pick(table, across[t]) + pick(table, vertical[t])
            pieces.append(
                scale * (content + pick(rel_scores, ahead[t]) + mirrored) + bias
            )
        scores = jnp.where(valid, jnp.concatenate(pieces, axis=1), mask_value)
        top = jnp.max(scores, axis=1, keepdims=True)
        raised = jnp.exp(scores - top)
        probs = (raised * (1.0 / jnp.sum(raised, axis=1, keepdims=True))).astype(bf16)
        probs_ref[h] = probs
        att_ref[:, cols] = dot(
            probs, qkv_ref[:, 2 * width + h * size : 2 * width + (h + 1) * size]
        ).astype(bf16)


def attn_fwd(place, x_all, w_query, w_key, w_value, rel_table, tables, ints_row, ints_col):
    rows, model = x_all.shape
    parts, heads, _ = tables.shape
    width = w_query.shape[1] // parts
    tiles = rows // lanes
    buckets = rel_table.shape[0]
    whole = lambda *shape: pl.BlockSpec(shape, lambda i, at: (0,) * len(shape))
    column = pl.BlockSpec((model, width), lambda i, at: (0, at[0]))
    return pl.pallas_call(
        attn_fwd_kernel,
        out_shape=(
            jax.ShapeDtypeStruct((rows, width), bf16),
            jax.ShapeDtypeStruct((heads, rows, rows), bf16),
            jax.ShapeDtypeStruct((rows, 3 * width), bf16),
            jax.ShapeDtypeStruct((buckets, 2 * width), bf16),
        ),
        grid_spec=pltpu.PrefetchScalarGridSpec(
            num_scalar_prefetch=1,
            grid=(tiles,),
            in_specs=[
                whole(rows, model),
                column,
                column,
                column,
                whole(buckets, model),
                pl.BlockSpec((1, heads, lanes), lambda i, at: (at[0], 0, 0)),
                whole(8, rows),
                whole(rows, 8),
            ],
            out_specs=[
                pl.BlockSpec((lanes, width), lambda i, at: (i, 0)),
                pl.BlockSpec((heads, lanes, rows), lambda i, at: (0, i, 0)),
                whole(rows, 3 * width),
                whole(buckets, 2 * width),
            ],
            scratch_shapes=[pltpu.VMEM((heads, rows, lanes), f32)],
        ),
        compiler_params=pltpu.CompilerParams(vmem_limit_bytes=40 << 20),
        cost_estimate=pl.CostEstimate(
            flops=6 * 10**9, transcendentals=10**6, bytes_accessed=8 << 20
        ),
        name="attn_fwd",
    )(place, x_all, w_query, w_key, w_value, rel_table, tables, ints_row, ints_col)


def attn_bwd_kernel(
    ga_ref, qkv_ref, probs_ref, relkq_ref, row_ref, col_ref,
    dqkv_ref, drel_ref, boxes_ref, ds_ref,
):
    scale = 1.0 / math.sqrt(192.0)
    rows = ga_ref.shape[0]
    heads = probs_ref.shape[0]
    width = ga_ref.shape[1]
    size = width // heads
    tiles = rows // lanes
    span_width = 3 * lanes
    drel_ref[...] = jnp.zeros_like(drel_ref)
    boxes_ref[...] = jnp.zeros_like(boxes_ref)
    window = lax.broadcasted_iota(jnp.int32, (rows, span_width), 1)
    bucket = lax.broadcasted_iota(jnp.int32, (lanes, lanes), 1)
    label = lax.broadcasted_iota(jnp.int32, (rows, lanes), 1)
    all_pos = col_ref[:, 0:1]
    all_x, all_y = col_ref[:, 1:2], col_ref[:, 2:3]
    sector_x, sector_y = jnp.right_shift(all_x, 5), jnp.right_shift(all_y, 5)
    hot_x = (label == sector_x).astype(bf16)
    hot_y = (label == sector_y + 64).astype(bf16)
    hot_both = ((label == sector_x) | (label == sector_y + 64)).astype(bf16)

    def histogram(sums, total, at, base_row):
        first = at - base_row + (2 * lanes // 2 - 1) - bucket
        low = jnp.bitwise_and(first, lanes - 1)
        group = jnp.right_shift(first, 7)
        found = jnp.where(
            group == 0,
            pick(sums[:, :lanes], low),
            jnp.where(
                group == 1,
                pick(sums[:, lanes : 2 * lanes], low),
                pick(sums[:, 2 * lanes :], low),
            ),
        )
        found = jnp.where(bucket == 0, total, found)
        later = jnp.where(bucket == lanes - 1, 0.0, pltpu.roll(found, lanes - 1, 1))
        return found - later

    def by_rows(ib, carry):
        here = pl.ds(pl.multiple_of(ib * lanes, lanes), lanes)
        pos_i = col_ref[here, 0:1]
        cx_i, cy_i = col_ref[here, 1:2], col_ref[here, 2:3]
        base = jnp.min(pos_i, axis=0, keepdims=True)
        below = (all_pos <= base - 63 + window).astype(bf16)
        short_x = jnp.bitwise_and(cx_i, 31) < jnp.bitwise_and(row_ref[1:2, :], 31)
        short_y = jnp.bitwise_and(cy_i, 31) < jnp.bitwise_and(row_ref[2:3, :], 31)
        step_x = jnp.right_shift(cx_i, 5) + 32 - bucket
        step_y = jnp.right_shift(cy_i, 5) + 32 - (bucket - 64)
        in_x = (bucket < 64) & (step_x >= 0) & (step_x < 32)
        in_y = (bucket >= 64) & (step_y >= 0) & (step_y < 32)
        seek = jnp.where(in_x, step_x, jnp.where(in_y, step_y + 64, 0))
        inside = in_x | in_y
        for h in range(heads):
            cols = slice(h * size, (h + 1) * size)
            kcols = slice(width + h * size, width + (h + 1) * size)
            vcols = slice(2 * width + h * size, 2 * width + (h + 1) * size)
            probs = probs_ref[h, here, :].astype(f32)
            gained = dot(ga_ref[here, cols], qkv_ref[:, vcols], ((1,), (1,)))
            row_dots = jnp.sum(probs * gained, axis=1, keepdims=True)
            grad32 = probs * (gained - row_dots)
            grad = grad32.astype(bf16)
            ds_ref[h, here, :] = grad
            exact = grad.astype(f32)
            total = jnp.sum(exact, axis=1, keepdims=True)
            rel = histogram(dot(grad, below), total, pos_i, base)
            rel = (scale * rel).astype(bf16)
            query = qkv_ref[here, cols]
            dqkv_ref[here, cols] = (
                scale * dot(grad, qkv_ref[:, kcols]) + dot(rel, relkq_ref[:, cols])
            ).astype(bf16)
            drel_ref[:, cols] += dot(rel, query, ((0,), (0,)))
            grad_x = jnp.where(short_x, exact, 0.0).astype(bf16)
            grad_y = jnp.where(short_y, exact, 0.0).astype(bf16)
            plain = dot(grad, hot_both)
            less = dot(grad_x, hot_x) + dot(grad_y, hot_y)
            plain = jnp.where(inside, pick(plain, seek), 0.0)
            less = jnp.where(inside, pick(less, seek), 0.0)
            boxes_ref[2 * h : 2 * h + 1, :] += jnp.sum(plain, axis=0, keepdims=True)
            boxes_ref[2 * h + 1 : 2 * h + 2, :] += jnp.sum(less, axis=0, keepdims=True)
        return carry

    lax.fori_loop(0, tiles, by_rows, 0)

    def by_columns(jb, carry):
        here = pl.ds(pl.multiple_of(jb * lanes, lanes), lanes)
        pos_j = col_ref[here, 0:1]
        base = jnp.min(pos_j, axis=0, keepdims=True)
        below = (all_pos <= base - 63 + window).astype(bf16)
        for h in range(heads):
            cols = slice(h * size, (h + 1) * size)
            kcols = slice(width + h * size, width + (h + 1) * size)
            vcols = slice(2 * width + h * size, 2 * width + (h + 1) * size)
            grad = ds_ref[h, :, here]
            total = dot(grad, jnp.ones((rows, lanes), bf16), ((0,), (0,)))
            sums = dot(grad, below, ((0,), (0,)))
            mirror = (scale * histogram(sums, total, pos_j, base)).astype(bf16)
            dqkv_ref[here, kcols] = (
                scale * dot(grad, qkv_ref[:, cols], ((0,), (0,)))
                + dot(mirror, relkq_ref[:, kcols])
            ).astype(bf16)
            drel_ref[:, kcols] += dot(mirror, qkv_ref[here, kcols], ((0,), (0,)))
            dqkv_ref[here, vcols] = dot(
                probs_ref[h, :, here], ga_ref[:, cols], ((0,), (0,))
            ).astype(bf16)
        return carry

    lax.fori_loop(0, tiles, by_columns, 0)


def attn_bwd(grad_att, qkv, probs, relkq, ints_row, ints_col):
    rows, width = grad_att.shape
    heads = probs.shape[0]
    buckets = relkq.shape[0]
    inside = pl.BlockSpec(memory_space=pltpu.VMEM)
    return pl.pallas_call(
        attn_bwd_kernel,
        out_shape=(
            jax.ShapeDtypeStruct((rows, 3 * width), bf16),
            jax.ShapeDtypeStruct((buckets, 2 * width), f32),
            jax.ShapeDtypeStruct((2 * heads, lanes), f32),
        ),
        in_specs=[inside] * 6,
        out_specs=[inside] * 3,
        scratch_shapes=[pltpu.VMEM((heads, rows, rows), bf16)],
        compiler_params=pltpu.CompilerParams(vmem_limit_bytes=40 << 20),
        cost_estimate=pl.CostEstimate(
            flops=12 * 10**9, transcendentals=0, bytes_accessed=6 << 20
        ),
        name="attn_bwd",
    )(grad_att, qkv, probs, relkq, ints_row, ints_col)


def layer_norm(inputs, gain_vec, bias_vec):
    row_mean = jnp.mean(inputs, axis=-1, keepdims=True)
    centered = inputs - row_mean
    inverse = lax.rsqrt(jnp.mean(centered * centered, axis=-1, keepdims=True) + norm_eps)
    normed = centered * inverse
    return (normed * gain_vec + bias_vec, normed, inverse)


def norm_backward(grad_in, normed, inverse, gain_vec):
    grad_gain = jnp.sum(grad_in * normed, axis=0)
    grad_shift = jnp.sum(grad_in, axis=0)
    scaled = grad_in * gain_vec
    grad_input = inverse * (
        scaled
        - jnp.mean(scaled, axis=-1, keepdims=True)
        - normed * jnp.mean(scaled * normed, axis=-1, keepdims=True)
    )
    return (grad_input, grad_gain, grad_shift)


def bits_of(count):
    assert count & (count - 1) == 0
    return [1 << at for at in range(count.bit_length() - 1)]


def swap(array, axis, by):
    count = lax.axis_size(axis)
    return lax.ppermute(array, axis, [(i, i ^ by) for i in range(count)])


def offsets(count):
    order = [0]
    for bit in reversed(bits_of(count)):
        order = order + [at ^ bit for at in order]
    return order


def spread(shared, pieces):
    count = lax.axis_size("blk")
    got = {0: shared} if shared is not None else {}
    held = {(0, at): piece for at, piece in pieces.items()} if pieces else {}
    for bit in reversed(bits_of(count)):
        out_keys = [key for key in sorted(held) if key[1] & bit]
        out_shared = sorted(got)
        parts = [got[at] for at in out_shared] + [held[key] for key in out_keys]
        if bit == 1:
            came = [swap(part, "blk", bit) for part in parts]
        else:
            came = swap(jnp.concatenate(parts, axis=1), "blk", bit)
            edges = [0]
            for part in parts:
                edges.append(edges[-1] + part.shape[1])
            came = [came[:, a:b] for a, b in zip(edges[:-1], edges[1:])]
        for at, part in zip(out_shared, came):
            got[at ^ bit] = part
        for key, part in zip(out_keys, came[len(out_shared) :]):
            del held[key]
            held[(key[0] ^ bit, key[1] ^ bit)] = part
    return got, {key[0]: part for key, part in held.items()}


def by_place(stacked, place):
    count = len(stacked)
    for bit in bits_of(count):
        turned = (place & bit) != 0
        stacked = [jnp.where(turned, stacked[at ^ bit], stacked[at]) for at in range(count)]
    return stacked


def chunk_order(count):
    order = [0]
    for bit in reversed(bits_of(count)):
        order = order + [at | bit for at in order]
    return order


def for_docs(chunks, doc_place):
    moved = by_place(chunks, doc_place)
    return [moved[at] for at in chunk_order(len(chunks))]


def halve(keep, send, bits):
    count = lax.axis_size("docs")
    first = True
    current = keep
    for bit in bits:
        if not first:
            half = current.shape[0] // 2
            current, send = current[:half], current[half:]
        first = False
        came = swap(send, "docs", bit)
        current = (current.astype(f32) + came.astype(f32)).astype(bf16)
    return current


def shards(
    tokens, lengths, positions, token_boxes, ln1_gain, ln1_bias, w_query, w_key, w_value, w_out,
    rel_table, xbias_table, ybias_table, ln2_gain, ln2_bias, w_in, b_in, w_down, cotangent,
):
    doc_count, row_count, model = tokens.shape
    assert doc_count == 1 and row_count == lanes
    parts = lax.axis_size("blk")
    docs = lax.axis_size("docs")
    place = lax.axis_index("blk")
    doc_place = lax.axis_index("docs")
    heads = xbias_table.shape[1]
    own_heads = heads // parts
    width = model // parts
    buckets = rel_table.shape[0]
    boxes = xbias_table.shape[0]
    hidden_units = w_in.shape[1]
    order = offsets(parts)
    x_own = tokens[0]

    centers_x = jnp.right_shift(token_boxes[0] + token_boxes[2], 1)
    centers_y = jnp.right_shift(token_boxes[1] + token_boxes[3], 1)
    own_ints = jnp.concatenate([positions, centers_x, centers_y], axis=0)
    coded = jnp.concatenate(
        [jnp.right_shift(own_ints, 5), jnp.bitwise_and(own_ints, 31)], axis=0
    ).astype(bf16)
    coded = jnp.pad(coded.reshape(1, -1), ((0, 7), (0, model - coded.size)))
    got, _ = spread(jnp.concatenate([x_own, coded], axis=0), None)
    x_all = jnp.concatenate([got[at][:row_count] for at in order], axis=0)
    decoded = jnp.concatenate(
        [got[at][row_count : row_count + 1, : 6 * row_count].reshape(6, row_count) for at in order], axis=1
    ).astype(jnp.int32)
    ints = decoded[:3] * 32 + decoded[3:]
    slot_ids = jnp.concatenate(
        [
            (place ^ at) * row_count + lax.broadcasted_iota(jnp.int32, (1, row_count), 1)
            for at in order
        ],
        axis=1,
    )
    ints = jnp.concatenate(
        [ints, (slot_ids < lengths[0]).astype(jnp.int32), jnp.zeros((4, ints.shape[1]), jnp.int32)],
        axis=0,
    )
    ints_col = ints.T
    tables = jnp.concatenate([xbias_table.T, ybias_table.T], axis=1).astype(f32)
    tables = tables.reshape(parts, own_heads, 2 * boxes)

    attended_own, probs, qkv, relkq = attn_fwd(
        place.reshape(1), x_all, w_query, w_key, w_value, rel_table, tables, ints, ints_col
    )

    def row_block(array, at):
        t = order.index(at)
        return array[t * row_count : (t + 1) * row_count]

    _, came = spread(None, {at: row_block(attended_own, at) for at in order})
    attended = jnp.concatenate(by_place([came[at] for at in range(parts)], place), axis=1)
    attn_out = jnp.dot(attended, w_out, preferred_element_type=f32)
    hidden, normed1, inverse1 = layer_norm(x_own.astype(f32) + attn_out, ln1_gain, ln1_bias)
    hidden_low = hidden.astype(bf16)
    up_proj = jnp.dot(hidden_low, w_in, preferred_element_type=f32) + b_in
    activated, gelu_back = jax.vjp(lambda inputs: jax.nn.gelu(inputs, approximate=True), up_proj)
    activated_low = activated.astype(bf16)
    ffn_out = jnp.dot(activated_low, w_down, preferred_element_type=f32)
    normed_out, normed2, inverse2 = layer_norm(hidden + ffn_out, ln2_gain, ln2_bias)
    block_out = normed_out.astype(bf16)[None]
    grad_output = cotangent[0].astype(f32)
    grad_mix, grad_ln2_gain, grad_ln2_bias = norm_backward(grad_output, normed2, inverse2, ln2_gain)
    grad_ffn = grad_mix.astype(bf16)
    grad_act = jnp.dot(grad_ffn, w_down.T, preferred_element_type=f32)
    grad_up = gelu_back(grad_act)[0].astype(bf16)
    grad_b_in = jnp.sum(grad_up, axis=0, dtype=f32)
    grad_hidden = grad_mix + jnp.dot(grad_up, w_in.T, preferred_element_type=f32)
    grad_resid, grad_ln1_gain, grad_ln1_bias = norm_backward(
        grad_hidden, normed1, inverse1, ln1_gain
    )
    grad_attn = grad_resid.astype(bf16)
    grad_att = jnp.dot(grad_attn, w_out.T, preferred_element_type=f32).astype(bf16)

    def column_block(array, at, count):
        size = array.shape[1] // count
        return lax.dynamic_slice_in_dim(array, at * size, size, axis=1)

    _, came = spread(None, {at: column_block(grad_att, place ^ at, parts) for at in order})
    grad_att_own = jnp.concatenate([came[at] for at in order], axis=0)
    dqkv, drel, box_sums = attn_bwd(grad_att_own, qkv, probs, relkq, ints, ints_col)

    def docs_columns(array):
        size = array.shape[1] // docs
        chunks = [array[:, at * size : (at + 1) * size] for at in range(docs)]
        return jnp.concatenate(for_docs(chunks, doc_place), axis=1)

    strips = activated_low.reshape(row_count, docs, parts, -1)
    strips = [
        docs_columns(
            lax.dynamic_index_in_dim(strips, place ^ at, axis=2, keepdims=False).reshape(row_count, -1)
        )
        for at in range(parts)
    ]
    got, came = spread(docs_columns(hidden_low), dict(enumerate(strips)))
    hidden_all = jnp.concatenate([got[at] for at in order], axis=0)
    activated_all = jnp.concatenate([came[at] for at in order], axis=0)
    got, came = spread(grad_ffn, {at: column_block(grad_up, place ^ at, parts) for at in order})
    grad_ffn_all = jnp.concatenate([got[at] for at in order], axis=0)
    grad_up_all = jnp.concatenate([came[at] for at in order], axis=0)
    got, came = spread(
        docs_columns(attended), {at: column_block(grad_attn, place ^ at, parts) for at in order}
    )
    attended_all = jnp.concatenate([got[at] for at in order], axis=0)
    grad_attn_all = jnp.concatenate([came[at] for at in order], axis=0)

    def halves(left, right):
        middle = left.shape[1] // 2
        send = dot(left[:, middle:], right, ((0,), (0,))).astype(bf16)
        keep = dot(left[:, :middle], right, ((0,), (0,))).astype(bf16)
        return keep, send

    bits = bits_of(docs)
    down_part = halve(*halves(activated_all, grad_ffn_all), bits)
    in_part = halve(*halves(hidden_all, grad_up_all), bits)
    out_part = halve(*halves(attended_all, grad_attn_all), bits)

    drel_low = drel.astype(bf16)
    left = docs_columns(jnp.concatenate([x_all, rel_table], axis=0))
    right = jnp.concatenate(
        [
            dqkv,
            jnp.concatenate(
                [drel_low[:, width:], drel_low[:, :width], jnp.zeros((buckets, width), bf16)], axis=1
            ),
        ],
        axis=0,
    )
    grad_rel_table = dot(
        drel_low[:, :width], column_block(w_key, place, parts), ((1,), (1,))
    ) + dot(drel_low[:, width:], column_block(w_query, place, parts), ((1,), (1,)))
    plain, less = box_sums[0::2], box_sums[1::2]

    def box_grad(at):
        plain_here, less_here = plain[:, at : at + boxes], less[:, at : at + boxes]
        later = jnp.pad(less_here[:, 1:], ((0, 0), (0, 1)))
        grad = (plain_here - less_here + later).T
        return lax.dynamic_update_slice(jnp.zeros((boxes, heads), f32), grad, (0, place * own_heads))

    small = jnp.concatenate(
        [
            grad_rel_table.reshape(docs, -1),
            grad_ln1_gain.reshape(docs, -1),
            grad_ln1_bias.reshape(docs, -1),
            grad_ln2_gain.reshape(docs, -1),
            grad_ln2_bias.reshape(docs, -1),
            grad_b_in.reshape(docs, -1),
            box_grad(0).reshape(docs, -1),
            box_grad(boxes).reshape(docs, -1),
        ],
        axis=1,
    ).astype(bf16)
    small_width = small.shape[1]
    across = 3 * width
    small = jnp.pad(small, ((0, 0), (0, -small_width % (8 * across))))
    small = for_docs([small[at] for at in range(docs)], doc_place)
    small = jnp.stack(small).reshape(docs, -1, across)
    keep, send = halves(left, right)
    middle = docs // 2
    chunk_rows = model // docs

    def with_small(main, extra):
        main = main.reshape(middle, chunk_rows, across)
        return jnp.concatenate([main, extra], axis=1).reshape(-1, across)

    qkv_part = halve(with_small(keep, small[:middle]), with_small(send, small[middle:]), bits)

    _, came = spread(None, {at: row_block(dqkv, at) for at in order})
    came = by_place([came[at] for at in range(parts)], place)
    grad_tokens = grad_resid
    for at, weight in enumerate((w_query, w_key, w_value)):
        grad = jnp.concatenate([rows[:, at * width : (at + 1) * width] for rows in came], axis=1)
        grad_tokens = grad_tokens + dot(grad, weight, ((1,), (1,)))

    def whole(part):
        got, _ = spread(part, None)
        return by_place([got[at] for at in range(parts)], place)

    grad_w_down = jnp.concatenate(whole(down_part), axis=0).astype(f32)
    grad_w_in = jnp.concatenate(whole(in_part), axis=1).astype(f32)
    grad_w_out = jnp.concatenate(whole(out_part), axis=1).astype(f32)
    pieces = whole(qkv_part)
    grads = [
        jnp.concatenate(
            [piece[:chunk_rows, at * width : (at + 1) * width] for piece in pieces], axis=1
        ).astype(f32)
        for at in range(3)
    ]
    total = sum(piece[chunk_rows:].astype(f32) for piece in pieces).reshape(-1)
    sizes = [
        (buckets // docs, model),
        (model // docs,),
        (model // docs,),
        (model // docs,),
        (model // docs,),
        (hidden_units // docs,),
        (boxes // docs, heads),
        (boxes // docs, heads),
    ]
    small_out = []
    start = 0
    for size in sizes:
        small_out.append(total[start : start + math.prod(size)].reshape(size))
        start += math.prod(size)
    rel_out, ln1g, ln1b, ln2g, ln2b, b_in_out, xb, yb = small_out
    return (
        block_out, grad_tokens[None], ln1g, ln1b, grads[0], grads[1], grads[2], grad_w_out,
        rel_out, xb, yb, ln2g, ln2b, grad_w_in, b_in_out, grad_w_down,
    )


blocks = 4
slots = (0, 2, 1, 3)


def rows_of(handle, tile=None, column=None):
    array, lead = handle if isinstance(handle, tuple) else (handle, None)
    shape = array.shape[-2:] if tile is None else tile
    column = column or (lambda *grid: 0)
    if lead is None:
        return pl.BlockSpec(shape, lambda *grid: (0, column(*grid)))
    return pl.BlockSpec((None,) + shape, lambda *grid: (lead, 0, column(*grid)))


def array_of(handle):
    return handle[0] if isinstance(handle, tuple) else handle


def full(shape):
    return pl.BlockSpec(shape, lambda *grid: (0,) * len(shape))


def cost(us):
    return pl.CostEstimate(flops=int(us * 3 * 10**8), transcendentals=0, bytes_accessed=0)


def ordered(array, *before):
    return lax.optimization_barrier((array,) + before)[0]


def params(limit):
    return pltpu.CompilerParams(vmem_limit_bytes=limit << 20)


def gelu_parts(u):
    root = math.sqrt(2.0 / math.pi)
    inner = jnp.tanh(root * (u + 0.044715 * u * u * u))
    value = 0.5 * u * (1.0 + inner)
    slope = 0.5 * (1.0 + inner) + 0.5 * u * (1.0 - inner * inner) * root * (
        1.0 + 3.0 * 0.044715 * u * u
    )
    return value, slope


def scores_kernel(
    at_ref, x0, x1, x2, x3, i0, i1, i2, i3, wq_ref, wk_ref, wv_ref, rel_ref, tab_ref,
    own_ref, core_ref, far_ref, probs_ref, qkv_ref, relkq_ref, row_ref, col_ref, key_rel,
):
    scale = 1.0 / math.sqrt(192.0)
    step = pl.program_id(0)
    rows = blocks * lanes
    width = wq_ref.shape[1]
    heads = tab_ref.shape[1]
    size = width // heads

    @pl.when(step == 0)
    def _():
        for t, (x_ref, i_ref) in enumerate(zip((x0, x1, x2, x3), (i0, i1, i2, i3))):
            span = slice(t * lanes, (t + 1) * lanes)
            for at, w_ref in enumerate((wq_ref, wk_ref, wv_ref)):
                qkv_ref[span, at * width : (at + 1) * width] = dot(
                    x_ref[...], w_ref[...]
                ).astype(bf16)
            first = jnp.bitwise_xor(at_ref[0], slots[t]) * lanes
            slot = first + lax.broadcasted_iota(jnp.int32, (8, lanes), 1)
            kind = lax.broadcasted_iota(jnp.int32, (8, lanes), 0)
            ints = jnp.where(kind == 3, (slot < at_ref[1]).astype(jnp.int32), i_ref[...])
            row_ref[:, span] = ints
            col_ref[span, :] = ints.astype(f32).T.astype(jnp.int32)
        relkq_ref[:, :width] = dot(rel_ref[...], wk_ref[...]).astype(bf16)
        relkq_ref[:, width:] = dot(rel_ref[...], wq_ref[...]).astype(bf16)
        for h in range(heads):
            cols = slice(width + h * size, width + (h + 1) * size)
            key_rel[h] = (
                dot(qkv_ref[:, cols], relkq_ref[:, cols], ((1,), (1,))).astype(bf16).astype(f32)
            )

    here = pl.ds(pl.multiple_of(step * lanes, lanes), lanes)
    pos_i = col_ref[here, 0:1]
    cx_i = col_ref[here, 1:2]
    cy_i = col_ref[here, 2:3]
    own_row = row_ref[0:1, here]
    ahead, mirror, across, vertical = [], [], [], []
    for t in range(blocks):
        span = slice(t * lanes, (t + 1) * lanes)
        ahead.append(ahead_of(pos_i, row_ref[0:1, span]))
        mirror.append(ahead_of(col_ref[span, 0:1], own_row))
        across.append(jnp.clip(jnp.right_shift(cx_i - row_ref[1:2, span], 5), -32, 31) + 32)
        vertical.append(jnp.clip(jnp.right_shift(cy_i - row_ref[2:3, span], 5), -32, 31) + 96)
    valid = row_ref[3:4, :] > 0
    attended = []
    for h in range(heads):
        cols = slice(h * size, (h + 1) * size)
        query = qkv_ref[here, cols]
        rel_scores = (
            dot(query, relkq_ref[:, cols], ((1,), (1,))).astype(bf16).astype(f32)
        )
        table = jnp.broadcast_to(tab_ref[0, h : h + 1, :], (lanes, lanes))
        pieces = []
        for t in range(blocks):
            span = slice(t * lanes, (t + 1) * lanes)
            content = dot(
                query, qkv_ref[span, width + h * size : width + (h + 1) * size], ((1,), (1,))
            )
            mirrored = pick(key_rel[h, span, :], mirror[t]).T
            bias = pick(table, across[t]) + pick(table, vertical[t])
            pieces.append(
                scale * (content + pick(rel_scores, ahead[t]) + mirrored) + bias
            )
        scores = jnp.where(valid, jnp.concatenate(pieces, axis=1), mask_value)
        top = jnp.max(scores, axis=1, keepdims=True)
        raised = jnp.exp(scores - top)
        probs = (raised * (1.0 / jnp.sum(raised, axis=1, keepdims=True))).astype(bf16)
        probs_ref[h] = probs
        attended.append(
            dot(
                probs, qkv_ref[:, 2 * width + h * size : 2 * width + (h + 1) * size]
            ).astype(bf16)
        )
    attended = jnp.concatenate(attended, axis=1)
    for t, target in enumerate((own_ref, far_ref.at[0], core_ref, far_ref.at[1])):

        @pl.when(step == t)
        def _(target=target):
            target[...] = attended


def scores_call(at, xs, ints, w_query, w_key, w_value, rel_table, tables):
    rows, model = blocks * lanes, w_query.shape[0]
    parts, heads, _ = tables.shape
    width = w_query.shape[1] // parts
    buckets = rel_table.shape[0]
    column = pl.BlockSpec((model, width), lambda i, at: (0, at[0]))
    return pl.pallas_call(
        scores_kernel,
        out_shape=(
            jax.ShapeDtypeStruct((lanes, width), bf16),
            jax.ShapeDtypeStruct((lanes, width), bf16),
            jax.ShapeDtypeStruct((2, lanes, width), bf16),
            jax.ShapeDtypeStruct((heads, rows, rows), bf16),
            jax.ShapeDtypeStruct((rows, 3 * width), bf16),
            jax.ShapeDtypeStruct((buckets, 2 * width), bf16),
            jax.ShapeDtypeStruct((8, rows), jnp.int32),
            jax.ShapeDtypeStruct((rows, 8), jnp.int32),
        ),
        grid_spec=pltpu.PrefetchScalarGridSpec(
            num_scalar_prefetch=1,
            grid=(blocks,),
            in_specs=[rows_of(x) for x in xs]
            + [rows_of(i) for i in ints]
            + [
                column,
                column,
                column,
                full((buckets, model)),
                pl.BlockSpec((1, heads, lanes), lambda i, at: (at[0], 0, 0)),
            ],
            out_specs=[
                full((lanes, width)),
                full((lanes, width)),
                full((2, lanes, width)),
                pl.BlockSpec((heads, lanes, rows), lambda i, at: (0, i, 0)),
                full((rows, 3 * width)),
                full((buckets, 2 * width)),
                full((8, rows)),
                full((rows, 8)),
            ],
            scratch_shapes=[pltpu.VMEM((heads, rows, lanes), f32)],
        ),
        compiler_params=params(56),
        cost_estimate=cost(25),
        name="scores",
    )(
        at, *map(array_of, xs), *map(array_of, ints), w_query, w_key, w_value, rel_table, tables
    )


def up_kernel(
    at_ref, a0, a1, a2, a3, x_ref, wout_ref, gain_ref, bias_ref, win_ref, bin_ref,
    far_ref, core_ref, own_ref, act_ref, slope_ref, normed_ref, inverse_ref, attended_ref,
    hidden_low,
):
    step = pl.program_id(0)
    width = a0.shape[1]
    tile = win_ref.shape[1]

    @pl.when(step == 0)
    def _():
        total = x_ref[...].astype(f32)
        for t, piece in enumerate((a0, a1, a2, a3)):
            first = pl.multiple_of(jnp.bitwise_xor(at_ref[0], slots[t]) * width, width)
            total = total + dot(piece[...], wout_ref[pl.ds(first, width), :])
            attended_ref[:, pl.ds(first, width)] = piece[...]
        centered = total - jnp.mean(total, axis=1, keepdims=True)
        inverse = lax.rsqrt(jnp.mean(centered * centered, axis=1, keepdims=True) + norm_eps)
        normed = centered * inverse
        normed_ref[...] = normed
        inverse_ref[...] = jnp.broadcast_to(inverse, inverse_ref.shape)
        hidden = (normed * gain_ref[...] + bias_ref[...]).astype(bf16)
        hidden_low[...] = hidden
        far_ref[0] = hidden
        core_ref[0] = hidden

    value, slope = gelu_parts(dot(hidden_low[...], win_ref[...]) + bin_ref[...])
    value = value.astype(bf16)
    act_ref[...] = value
    slope_ref[...] = slope.astype(bf16)
    strip = tile // blocks
    here = pl.ds(pl.multiple_of(step * strip, strip), strip)
    for t, target in enumerate((own_ref, far_ref.at[1], core_ref.at[1], far_ref.at[2])):
        first = pl.multiple_of(jnp.bitwise_xor(at_ref[0], slots[t]) * strip, strip)
        target[:, here] = act_ref[:, pl.ds(first, strip)]


def up_call(at, pieces, x_own, w_out, gain, bias, w_in, b_in, docs):
    rows, model = x_own.shape
    units = w_in.shape[1]
    tile = units // docs
    quarter = units // blocks
    column = lambda i, at: (0, i)
    return pl.pallas_call(
        up_kernel,
        out_shape=(
            jax.ShapeDtypeStruct((3, rows, model), bf16),
            jax.ShapeDtypeStruct((2, rows, model), bf16),
            jax.ShapeDtypeStruct((rows, quarter), bf16),
            jax.ShapeDtypeStruct((rows, units), bf16),
            jax.ShapeDtypeStruct((rows, units), bf16),
            jax.ShapeDtypeStruct((rows, model), f32),
            jax.ShapeDtypeStruct((rows, lanes), f32),
            jax.ShapeDtypeStruct((rows, model), bf16),
        ),
        grid_spec=pltpu.PrefetchScalarGridSpec(
            num_scalar_prefetch=1,
            grid=(docs,),
            in_specs=[rows_of(piece) for piece in pieces]
            + [
                full((rows, model)),
                full((model, model)),
                full((1, model)),
                full((1, model)),
                pl.BlockSpec((model, tile), column),
                pl.BlockSpec((1, tile), column),
            ],
            out_specs=[
                full((3, rows, model)),
                full((2, rows, model)),
                full((rows, quarter)),
                pl.BlockSpec((rows, tile), column),
                pl.BlockSpec((rows, tile), column),
                full((rows, model)),
                full((rows, lanes)),
                full((rows, model)),
            ],
            scratch_shapes=[pltpu.VMEM((rows, model), bf16)],
        ),
        compiler_params=params(40),
        cost_estimate=cost(9),
        name="up",
    )(at, *map(array_of, pieces), x_own, w_out, gain, bias, w_in, b_in)


def norm_back(grad, normed, inverse, gain):
    scaled = grad * gain
    return inverse * (
        scaled
        - jnp.mean(scaled, axis=1, keepdims=True)
        - normed * jnp.mean(scaled * normed, axis=1, keepdims=True)
    )


def down_kernel(
    act_ref, wdown_ref, normed_ref, cot_ref, gain1_ref, bias1_ref, gain2_ref, bias2_ref,
    block_ref, mix_ref, low_ref, sums_ref,
):
    step = pl.program_id(0)

    @pl.when(step == 0)
    def _():
        mix_ref[...] = normed_ref[...] * gain1_ref[...] + bias1_ref[...]

    mix_ref[...] += dot(act_ref[...], wdown_ref[...])

    @pl.when(step == pl.num_programs(0) - 1)
    def _():
        mixed = mix_ref[...]
        centered = mixed - jnp.mean(mixed, axis=1, keepdims=True)
        inverse = lax.rsqrt(jnp.mean(centered * centered, axis=1, keepdims=True) + norm_eps)
        normed = centered * inverse
        block_ref[...] = (normed * gain2_ref[...] + bias2_ref[...]).astype(bf16)
        grad = cot_ref[...].astype(f32)
        sums_ref[0:1, :] = jnp.sum(grad * normed, axis=0, keepdims=True)
        sums_ref[1:2, :] = jnp.sum(grad, axis=0, keepdims=True)
        mix = norm_back(grad, normed, inverse, gain2_ref[...])
        mix_ref[...] = mix
        low_ref[...] = mix.astype(bf16)


def down_call(act, w_down, normed, cotangent, gain1, bias1, gain2, bias2, tile):
    rows, units = act.shape
    model = w_down.shape[1]
    return pl.pallas_call(
        down_kernel,
        out_shape=(
            jax.ShapeDtypeStruct((rows, model), bf16),
            jax.ShapeDtypeStruct((rows, model), f32),
            jax.ShapeDtypeStruct((rows, model), bf16),
            jax.ShapeDtypeStruct((8, model), f32),
        ),
        grid=(units // tile,),
        in_specs=[
            pl.BlockSpec((rows, tile), lambda i: (0, i)),
            pl.BlockSpec((tile, model), lambda i: (i, 0)),
            full((rows, model)),
            full((rows, model)),
        ]
        + [full((1, model))] * 4,
        out_specs=[full((rows, model))] * 3 + [full((8, model))],
        compiler_params=params(40),
        cost_estimate=cost(8),
        name="down",
    )(act, w_down, normed, cotangent, gain1, bias1, gain2, bias2)


def back_kernel(
    at_ref, wdown_ref, slope_ref, win_ref, wout_ref, normed_ref, inverse_ref, mix_ref, ffn_ref,
    attended_ref, gain1_ref, above_ref,
    own_ref, core_ref, far_ref, resid_ref, upfar_ref, upcore_ref, upown_ref,
    outfar_ref, outcore_ref, outown_ref, sums_ref,
    total, grad_up,
):
    step = pl.program_id(0)
    steps = pl.num_programs(0)
    rows, tile = slope_ref.shape
    model = mix_ref.shape[1]
    width = model // blocks

    @pl.when(step == 0)
    def _():
        total[...] = mix_ref[...]

    grad = dot(ffn_ref[...], wdown_ref[...], ((1,), (1,))) * slope_ref[...].astype(f32)
    low = grad.astype(bf16)
    total[...] += dot(low, win_ref[...], ((1,), (1,)))
    per = model // tile
    part = step // per
    here = pl.ds(pl.multiple_of((step - part * per) * tile, tile), tile)
    grad_up[jnp.bitwise_xor(part, at_ref[0]), :, here] = low
    sums_ref[pl.ds(4 + part, 1), here] = jnp.sum(low.astype(f32), axis=0, keepdims=True)

    @pl.when(step == steps - 1)
    def _():
        upown_ref[...] = grad_up[0]
        upcore_ref[...] = grad_up[1]
        upfar_ref[0] = grad_up[2]
        upfar_ref[1] = grad_up[3]
        grad = total[...]
        normed = normed_ref[...]
        sums_ref[0:1, :] = jnp.sum(grad * normed, axis=0, keepdims=True)
        sums_ref[1:2, :] = jnp.sum(grad, axis=0, keepdims=True)
        sums_ref[2:4, :] = above_ref[0:2, :]
        resid = norm_back(grad, normed, inverse_ref[:, 0:1], gain1_ref[...])
        resid_ref[...] = resid
        low = resid.astype(bf16)
        total[...] = low.astype(f32)
        outfar_ref[:, :model] = attended_ref[...]
        outcore_ref[:, :model] = attended_ref[...]
        targets = (own_ref, core_ref, far_ref.at[0], far_ref.at[1])
        wides = (
            outown_ref, outcore_ref.at[:, pl.ds(model, width)],
            outfar_ref.at[:, pl.ds(model, width)], outfar_ref.at[:, pl.ds(model + width, width)],
        )
        for at, (target, wide) in enumerate(zip(targets, wides)):
            first = pl.multiple_of(jnp.bitwise_xor(at_ref[0], at) * width, width)
            target[...] = dot(low, wout_ref[pl.ds(first, width), :], ((1,), (1,))).astype(bf16)
            wide[...] = total[:, pl.ds(first, width)].astype(bf16)


def back_call(
    at, w_down, slope, w_in, w_out, normed, inverse, mix, grad_ffn, attended, gain1, above, tile,
):
    rows, units = slope.shape
    model = w_out.shape[0]
    width = model // blocks
    return pl.pallas_call(
        back_kernel,
        out_shape=(
            jax.ShapeDtypeStruct((rows, width), bf16),
            jax.ShapeDtypeStruct((rows, width), bf16),
            jax.ShapeDtypeStruct((2, rows, width), bf16),
            jax.ShapeDtypeStruct((rows, model), f32),
            jax.ShapeDtypeStruct((2, rows, model), bf16),
            jax.ShapeDtypeStruct((rows, model), bf16),
            jax.ShapeDtypeStruct((rows, model), bf16),
            jax.ShapeDtypeStruct((rows, model + 2 * width), bf16),
            jax.ShapeDtypeStruct((rows, model + width), bf16),
            jax.ShapeDtypeStruct((rows, width), bf16),
            jax.ShapeDtypeStruct((8, model), f32),
        ),
        grid_spec=pltpu.PrefetchScalarGridSpec(
            num_scalar_prefetch=1,
            grid=(units // tile,),
            in_specs=[
                pl.BlockSpec((tile, model), lambda i, at: (i, 0)),
                pl.BlockSpec((rows, tile), lambda i, at: (0, i)),
                pl.BlockSpec((model, tile), lambda i, at: (0, i)),
                full((model, model)),
                full((rows, model)),
                full((rows, lanes)),
                full((rows, model)),
                full((rows, model)),
                full((rows, model)),
                full((1, model)),
                full((8, model)),
            ],
            out_specs=[
                full((rows, width)),
                full((rows, width)),
                full((2, rows, width)),
                full((rows, model)),
                full((2, rows, model)),
                full((rows, model)),
                full((rows, model)),
                full((rows, model + 2 * width)),
                full((rows, model + width)),
                full((rows, width)),
                full((8, model)),
            ],
            scratch_shapes=[
                pltpu.VMEM((rows, model), f32),
                pltpu.VMEM((blocks, rows, model), bf16),
            ],
        ),
        compiler_params=params(40),
        cost_estimate=cost(12),
        name="back",
    )(at, w_down, slope, w_in, w_out, normed, inverse, mix, grad_ffn, attended, gain1, above)


def scores_grad_kernel(half, held, *refs):
    at_ref, g0, g1, g2, g3, qkv_ref, probs_ref, relkq_ref, row_ref, col_ref = refs[:10]
    refs = refs[10:]
    last = half == 1
    if last:
        wq_ref, wk_ref, sums_ref, before_ref, boxes_before = refs[:5]
        refs = refs[5:]
    refs = refs[held:]
    if last:
        dqkv_ref, own_ref, core_ref, far_ref, small_ref, ga_ref, ds_ref, drel, box_sums = refs
    else:
        dqkv_ref, box_sums, ga_ref, ds_ref, drel = refs
    scale = 1.0 / math.sqrt(192.0)
    rows = blocks * lanes
    width = qkv_ref.shape[1] // 3
    part = width // 2
    heads = probs_ref.shape[0]
    size = part // heads
    span_width = 3 * lanes
    for t, piece in enumerate((g0, g1, g2, g3)):
        ga_ref[t * lanes : (t + 1) * lanes, :] = piece[...]
    drel[...] = jnp.zeros_like(drel)
    box_sums[...] = jnp.zeros_like(box_sums)
    window = lax.broadcasted_iota(jnp.int32, (rows, span_width), 1)
    bucket = lax.broadcasted_iota(jnp.int32, (lanes, lanes), 1)
    label = lax.broadcasted_iota(jnp.int32, (rows, lanes), 1)
    all_pos = col_ref[:, 0:1]
    all_x, all_y = col_ref[:, 1:2], col_ref[:, 2:3]
    sector_x, sector_y = jnp.right_shift(all_x, 5), jnp.right_shift(all_y, 5)
    hot_x = (label == sector_x).astype(bf16)
    hot_y = (label == sector_y + 64).astype(bf16)
    hot_both = ((label == sector_x) | (label == sector_y + 64)).astype(bf16)

    def histogram(sums, total, at, base_row):
        first = at - base_row + (lanes - 1) - bucket
        low = jnp.bitwise_and(first, lanes - 1)
        group = jnp.right_shift(first, 7)
        found = jnp.where(
            group == 0,
            pick(sums[:, :lanes], low),
            jnp.where(
                group == 1,
                pick(sums[:, lanes : 2 * lanes], low),
                pick(sums[:, 2 * lanes :], low),
            ),
        )
        found = jnp.where(bucket == 0, total, found)
        later = jnp.where(bucket == lanes - 1, 0.0, pltpu.roll(found, lanes - 1, 1))
        return found - later

    def by_rows(ib, carry):
        here = pl.ds(pl.multiple_of(ib * lanes, lanes), lanes)
        pos_i = col_ref[here, 0:1]
        cx_i, cy_i = col_ref[here, 1:2], col_ref[here, 2:3]
        base = jnp.min(pos_i, axis=0, keepdims=True)
        below = (all_pos <= base - 63 + window).astype(bf16)
        short_x = jnp.bitwise_and(cx_i, 31) < jnp.bitwise_and(row_ref[1:2, :], 31)
        short_y = jnp.bitwise_and(cy_i, 31) < jnp.bitwise_and(row_ref[2:3, :], 31)
        step_x = jnp.right_shift(cx_i, 5) + 32 - bucket
        step_y = jnp.right_shift(cy_i, 5) + 32 - (bucket - 64)
        in_x = (bucket < 64) & (step_x >= 0) & (step_x < 32)
        in_y = (bucket >= 64) & (step_y >= 0) & (step_y < 32)
        seek = jnp.where(in_x, step_x, jnp.where(in_y, step_y + 64, 0))
        inside = in_x | in_y
        for h in range(heads):
            gcols = slice(h * size, (h + 1) * size)
            kgcols = slice(part + h * size, part + (h + 1) * size)
            vgcols = slice(2 * part + h * size, 2 * part + (h + 1) * size)
            cols, kcols, vcols = (
                slice(k * width + half * part + h * size, k * width + half * part + (h + 1) * size)
                for k in range(3)
            )
            probs = probs_ref[h, here, :].astype(f32)
            gained = dot(ga_ref[here, gcols], qkv_ref[:, vcols], ((1,), (1,)))
            row_dots = jnp.sum(probs * gained, axis=1, keepdims=True)
            grad = (probs * (gained - row_dots)).astype(bf16)
            ds_ref[h, here, :] = grad
            exact = grad.astype(f32)
            total = jnp.sum(exact, axis=1, keepdims=True)
            rel = histogram(dot(grad, below), total, pos_i, base)
            rel = (scale * rel).astype(bf16)
            dqkv_ref[here, gcols] = (
                scale * dot(grad, qkv_ref[:, kcols]) + dot(rel, relkq_ref[:, cols])
            ).astype(bf16)
            drel[:, gcols] += dot(rel, qkv_ref[here, cols], ((0,), (0,)))
            grad_x = jnp.where(short_x, exact, 0.0).astype(bf16)
            grad_y = jnp.where(short_y, exact, 0.0).astype(bf16)
            plain = dot(grad, hot_both)
            less = dot(grad_x, hot_x) + dot(grad_y, hot_y)
            plain = jnp.where(inside, pick(plain, seek), 0.0)
            less = jnp.where(inside, pick(less, seek), 0.0)
            box_sums[h : h + 1, :] += jnp.sum(plain, axis=0, keepdims=True)
            box_sums[8 + h : 9 + h, :] += jnp.sum(less, axis=0, keepdims=True)
        return carry

    lax.fori_loop(0, blocks, by_rows, 0)

    def by_columns(jb, carry):
        here = pl.ds(pl.multiple_of(jb * lanes, lanes), lanes)
        pos_j = col_ref[here, 0:1]
        base = jnp.min(pos_j, axis=0, keepdims=True)
        below = (all_pos <= base - 63 + window).astype(bf16)
        for h in range(heads):
            gcols = slice(h * size, (h + 1) * size)
            kgcols = slice(part + h * size, part + (h + 1) * size)
            vgcols = slice(2 * part + h * size, 2 * part + (h + 1) * size)
            cols, kcols, vcols = (
                slice(k * width + half * part + h * size, k * width + half * part + (h + 1) * size)
                for k in range(3)
            )
            grad = ds_ref[h, :, here]
            total = dot(grad, jnp.ones((rows, lanes), bf16), ((0,), (0,)))
            sums = dot(grad, below, ((0,), (0,)))
            mirror = (scale * histogram(sums, total, pos_j, base)).astype(bf16)
            dqkv_ref[here, kgcols] = (
                scale * dot(grad, qkv_ref[:, cols], ((0,), (0,)))
                + dot(mirror, relkq_ref[:, kcols])
            ).astype(bf16)
            drel[:, kgcols] += dot(mirror, qkv_ref[here, kcols], ((0,), (0,)))
            dqkv_ref[here, vgcols] = dot(
                probs_ref[h, :, here], ga_ref[:, gcols], ((0,), (0,))
            ).astype(bf16)
        return carry

    lax.fori_loop(0, blocks, by_columns, 0)
    keys, queries = drel[:, :part].astype(bf16), drel[:, part:].astype(bf16)
    dqkv_ref[rows:, :part] = queries
    dqkv_ref[rows:, part : 2 * part] = keys
    dqkv_ref[rows:, 2 * part :] = jnp.zeros((lanes, part), bf16)
    if not last:
        return
    for t, target in enumerate((own_ref, far_ref.at[0], core_ref, far_ref.at[1])):
        span = slice(t * lanes, (t + 1) * lanes)
        for k in range(3):
            first = k * width
            target[:, first : first + part] = before_ref[span, k * part : (k + 1) * part]
            target[:, first + part : first + width] = dqkv_ref[span, k * part : (k + 1) * part]
    queries = jnp.concatenate([before_ref[rows:, :part], queries], axis=1)
    keys = jnp.concatenate([before_ref[rows:, part : 2 * part], keys], axis=1)

    docs, small_rows, small_width = small_ref.shape
    per = lanes // docs
    table = (
        dot(keys, wk_ref[...], ((1,), (1,))) + dot(queries, wq_ref[...], ((1,), (1,)))
    ).astype(bf16)
    plain = jnp.concatenate([boxes_before[0:heads], box_sums[0:heads], box_sums[heads + heads : 8]], axis=0)
    less = jnp.concatenate(
        [boxes_before[8 : 8 + heads], box_sums[8 : 8 + heads], box_sums[8 + 2 * heads : 16]], axis=0
    )
    heads = 2 * heads
    place_lane = lax.broadcasted_iota(jnp.int32, (8, lanes), 1)
    later = jnp.where(
        jnp.bitwise_and(place_lane, 63) == 63, 0.0, pltpu.roll(less, lanes - 1, 1)
    )
    boxes = (plain - less + later).astype(bf16)
    row_at = lax.broadcasted_iota(jnp.int32, (8, lanes), 0)
    head_at = at_ref[0] * heads + row_at
    by_head = [
        dot(boxes, ((place_lane == head_at + k * 64) & (row_at < heads)).astype(bf16), ((0,), (0,)))
        for k in range(2)
    ]
    model = table.shape[1]
    edges = list(range(0, model, small_width)) + [model]
    rest = edges[-1] - edges[-2]
    lane = slice(rest, rest + lanes)
    line = (len(edges) - 2) * per
    count = lanes // 2 // docs
    for chunk in range(docs):
        own = slice(chunk * per, (chunk + 1) * per)
        for k, (first, end) in enumerate(zip(edges[:-1], edges[1:])):
            small_ref[chunk, k * per : (k + 1) * per, : end - first] = table[own, first:end].astype(f32)
        for k in range(4):
            small_ref[chunk, line + k : line + k + 1, lane] = (
                sums_ref[k : k + 1, chunk * lanes : (chunk + 1) * lanes]
            )
            first = (chunk * blocks + k) * lanes
            where = first // model
            small_ref[chunk, line + 4 + k : line + 5 + k, lane] = (
                sums_ref[4 + where : 5 + where, first - where * model : first - where * model + lanes]
            )
        begin = chunk * count
        small_ref[chunk, line + 8 : line + 8 + count, lane] = (
            by_head[0][begin : begin + count, :] + by_head[1][64 + begin : 64 + begin + count, :]
        )


def scores_grad_call(half, at, pieces, qkv, probs, relkq, row, col, after, docs=0, extra=()):
    rows = blocks * lanes
    heads = probs.shape[0] // 2
    width = qkv.shape[1] // 3
    part = width // 2
    model = width * blocks
    buckets = relkq.shape[0]
    column = pl.BlockSpec((model, width), lambda i, at: (0, at[0]))
    grads = jax.ShapeDtypeStruct((rows + buckets, 3 * part), bf16)
    box_shape = (16, lanes)
    scratch = [
        pltpu.VMEM((rows, part), bf16),
        pltpu.VMEM((heads, rows, rows), bf16),
        pltpu.VMEM((buckets, 2 * part), f32),
    ]
    extra_specs = []
    if half == 1:
        shapes = (
            grads,
            jax.ShapeDtypeStruct((lanes, 3 * width), bf16),
            jax.ShapeDtypeStruct((lanes, 3 * width), bf16),
            jax.ShapeDtypeStruct((2, lanes, 3 * width), bf16),
            jax.ShapeDtypeStruct((docs, 3 * buckets // docs, 3 * part), f32),
        )
        extra_specs = [column, column, full((8, model)), full(grads.shape), full(box_shape)]
        scratch = scratch + [pltpu.VMEM(box_shape, f32)]
    else:
        shapes = (grads, jax.ShapeDtypeStruct(box_shape, f32))
    return pl.pallas_call(
        functools.partial(scores_grad_kernel, half, len(after)),
        out_shape=shapes,
        grid_spec=pltpu.PrefetchScalarGridSpec(
            num_scalar_prefetch=1,
            grid=(1,),
            in_specs=[rows_of(piece, (lanes, part), lambda i, at: half) for piece in pieces]
            + [
                full((rows, 3 * width)),
                pl.BlockSpec((heads, rows, rows), lambda i, at: (half, 0, 0)),
                full((buckets, 2 * width)),
                full((8, rows)),
                full((rows, 8)),
            ]
            + extra_specs
            + [pl.BlockSpec(memory_space=pl.ANY)] * len(after),
            out_specs=[full(shape.shape) for shape in shapes],
            scratch_shapes=scratch,
        ),
        compiler_params=params(56),
        cost_estimate=cost(15),
        name="scores_grad",
    )(at, *map(array_of, pieces), qkv, probs, relkq, row, col, *extra, *after)


def weight_grad_call(at, lefts, rights, bits, extra=None, after=(), right_width=None, name="weight_grad"):
    count = 1 << len(bits)
    model = array_of(lefts[0]).shape[-1]
    chunk = lanes
    width = right_width or array_of(rights[0]).shape[-1]
    pieces = len(lefts)
    tail = 0 if extra is None else extra.shape[1]
    per = 2
    steps = count // per
    half = steps // 2

    def offset(p):
        total = 0
        for place, bit in enumerate(bits):
            total = total + jnp.bitwise_and(jnp.right_shift(p, len(bits) - 1 - place), 1) * bit
        return total

    def chunk_of(i, at, which):
        p = lax.rem(i + half, steps) * per + which
        return jnp.bitwise_xor(at[1], offset(p))

    def kernel(at_ref, *refs):
        left_refs, refs = refs[: pieces * per], refs[pieces * per :]
        right_refs, refs = refs[:pieces], refs[pieces:]
        if extra is not None:
            extra_refs, refs = refs[:per], refs[per:]
        keep_ref, send_ref, right_all = refs[len(after) :]
        step = pl.program_id(0)

        @pl.when(step == 0)
        def _():
            for at, ref in enumerate(right_refs):
                right_all[at * lanes : (at + 1) * lanes, :] = ref[...]

        left = jnp.concatenate(
            [
                jnp.concatenate([left_refs[at * per + which][...] for which in range(per)], axis=1)
                for at in range(pieces)
            ],
            axis=0,
        )
        result = dot(left, right_all[...], ((0,), (0,))).astype(bf16)
        for target, mine in ((send_ref, step < half), (keep_ref, step >= half)):

            @pl.when(mine)
            def _(target=target):
                for which in range(per):
                    target[which, :chunk, :] = result[which * chunk : (which + 1) * chunk, :]
                    if extra is not None:
                        target[which, chunk:, :] = extra_refs[which][...].astype(bf16)

    in_specs, operands = [], []
    for handle in lefts:
        for which in range(per):
            in_specs.append(
                rows_of(handle, (lanes, chunk), lambda i, at, which=which: chunk_of(i, at, which))
            )
            operands.append(array_of(handle))
    for handle in rights:
        column = handle[2] if isinstance(handle, tuple) and len(handle) == 3 else 0
        handle = handle[:2] if isinstance(handle, tuple) and handle[1] is not None else array_of(handle)
        in_specs.append(rows_of(handle, (lanes, width), lambda i, at, column=column: column))
        operands.append(array_of(handle))
    if extra is not None:
        for which in range(per):
            in_specs.append(
                pl.BlockSpec(
                    (None, tail, width), lambda i, at, which=which: (chunk_of(i, at, which), 0, 0)
                )
            )
            operands.append(extra)
    in_specs += [pl.BlockSpec(memory_space=pl.ANY)] * len(after)
    operands += list(after)
    shape = jax.ShapeDtypeStruct((count // 2, chunk + tail, width), bf16)
    block = (per, chunk + tail, width)
    return pl.pallas_call(
        kernel,
        out_shape=(shape, shape),
        grid_spec=pltpu.PrefetchScalarGridSpec(
            num_scalar_prefetch=1,
            grid=(steps,),
            in_specs=in_specs,
            out_specs=[
                pl.BlockSpec(block, lambda i, at: (jnp.maximum(i - half, 0), 0, 0)),
                pl.BlockSpec(block, lambda i, at: (jnp.minimum(i, half - 1), 0, 0)),
            ],
            scratch_shapes=[pltpu.VMEM((pieces * lanes, width), bf16)],
        ),
        compiler_params=params(40),
        cost_estimate=cost(4),
        name=name,
    )(at, *operands)


def tokens_grad_kernel(at_ref, d0, d1, d2, d3, resid_ref, wq_ref, wk_ref, wv_ref, *refs):
    out_ref = refs[-1]
    step = pl.program_id(0)
    width = wq_ref.shape[1]

    @pl.when(step == 0)
    def _():
        out_ref[...] = resid_ref[...]

    for t, piece in enumerate((d0, d1, d2, d3)):

        @pl.when(step == t)
        def _(piece=piece):
            total = out_ref[...]
            for at, w_ref in enumerate((wq_ref, wk_ref, wv_ref)):
                total = total + dot(
                    piece[:, at * width : (at + 1) * width], w_ref[...], ((1,), (1,))
                )
            out_ref[...] = total


def tokens_grad_call(at, pieces, resid, w_query, w_key, w_value, after):
    rows, model = resid.shape
    width = model // blocks
    tile = (rows, 3 * width)

    def column(i, at):
        offset = jnp.where(i == 1, 2, jnp.where(i == 2, 1, i))
        return (0, jnp.bitwise_xor(at[0], offset))

    weight = pl.BlockSpec((model, width), column)
    return pl.pallas_call(
        tokens_grad_kernel,
        out_shape=jax.ShapeDtypeStruct((rows, model), f32),
        grid_spec=pltpu.PrefetchScalarGridSpec(
            num_scalar_prefetch=1,
            grid=(blocks,),
            in_specs=[rows_of(piece, tile) for piece in pieces]
            + [full((rows, model)), weight, weight, weight]
            + [pl.BlockSpec(memory_space=pl.ANY)] * len(after),
            out_specs=full((rows, model)),
        ),
        compiler_params=params(40),
        cost_estimate=cost(4),
        name="tokens_grad",
    )(at, *map(array_of, pieces), resid, w_query, w_key, w_value, *after)


def parts_kernel(fields, at_ref, *refs):
    step = pl.program_id(0)
    parts, outs = refs[: blocks * fields], refs[blocks * fields :]
    for field in range(fields):
        for at in range(blocks):

            @pl.when(step == at)
            def _(part=parts[field * blocks + at], out=outs[field]):
                out[...] = part[...].astype(f32)


def parts_call(at, fields, name):
    in_specs, operands, shapes, out_specs = [], [], [], []
    for parts, axis in fields:
        rows, width = parts[0].shape
        in_specs += [full((rows, width))] * blocks
        operands += list(parts)
        shape = (rows * blocks, width) if axis == 0 else (rows, width * blocks)
        shapes.append(jax.ShapeDtypeStruct(shape, f32))

        def index(i, at, axis=axis):
            spot = jnp.bitwise_xor(at[0], i)
            return (spot, 0) if axis == 0 else (0, spot)

        out_specs.append(pl.BlockSpec((rows, width), index))
    return pl.pallas_call(
        functools.partial(parts_kernel, len(fields)),
        out_shape=tuple(shapes),
        grid_spec=pltpu.PrefetchScalarGridSpec(
            num_scalar_prefetch=1, grid=(blocks,), in_specs=in_specs, out_specs=out_specs
        ),
        compiler_params=params(40),
        cost_estimate=cost(2),
        name=name,
    )(at, *operands)


def last_kernel(at_ref, *refs):
    step = pl.program_id(0)
    firsts, seconds, outs = refs[:blocks], refs[blocks : 2 * blocks], refs[2 * blocks : 2 * blocks + 3]
    rel_ref, norm_ref, bin_ref, box_ref = refs[2 * blocks + 3 :]
    for at in range(blocks):

        @pl.when(step == at)
        def _(first=firsts[at], second=seconds[at]):
            for k, out in enumerate(outs):
                span = slice(k * lanes, (k + 1) * lanes)
                out[:, :lanes] = first[:, span].astype(f32)
                out[:, lanes:] = second[:lanes, span].astype(f32)

    @pl.when(step == 0)
    def _():
        total = seconds[0][lanes:, :].astype(f32)
        for second in seconds[1:]:
            total = total + second[lanes:, :].astype(f32)
        rows = rel_ref.shape[0]
        width = total.shape[1]
        for k in range(3):
            end = min((k + 1) * width, rel_ref.shape[1])
            rel_ref[:, k * width : end] = total[k * rows : (k + 1) * rows, : end - k * width]
        rest = total[2 * rows :, width - lanes :]
        norm_ref[...] = rest[:4]
        bin_ref[...] = rest[4:8]
        box_ref[...] = rest[8:16]


def last_call(at, firsts, seconds, buckets, model):
    rows = blocks * lanes // blocks
    wide = jax.ShapeDtypeStruct((lanes, model), f32)
    column = pl.BlockSpec((lanes, model // blocks), lambda i, at: (0, jnp.bitwise_xor(at[0], i)))
    return pl.pallas_call(
        last_kernel,
        out_shape=(wide, wide, wide)
        + tuple(jax.ShapeDtypeStruct(shape, f32) for shape in ((buckets, model), (4, lanes), (4, lanes), (8, lanes))),
        grid_spec=pltpu.PrefetchScalarGridSpec(
            num_scalar_prefetch=1,
            grid=(blocks,),
            in_specs=[full(part.shape) for part in firsts + seconds],
            out_specs=[column] * 3 + [full((buckets, model)), full((4, lanes)), full((4, lanes)), full((8, lanes))],
        ),
        compiler_params=params(40),
        cost_estimate=cost(2),
        name="last",
    )(at, *firsts, *seconds)


class Halving:
    def __init__(self, halves, bits):
        self.keep, self.send = halves
        self.bits = list(bits)
        self.step()

    def step(self):
        self.came = swap(self.send, "docs", self.bits.pop(0))

    def add(self):
        keep, came = self.keep, self.came
        total = lambda part: (keep[part].astype(f32) + came[part].astype(f32)).astype(bf16)
        if not self.bits:
            self.keep = self.send = total(slice(None))[0]
            return self.keep
        middle = keep.shape[0] // 2
        self.send = total(slice(middle, None))
        self.keep = total(slice(0, middle))
        sent = self.send
        self.step()
        return sent

    def finish(self):
        while self.keep.ndim == 3:
            self.add()
        return self.keep


def shards_tiles(
    tokens, lengths, positions, token_boxes, ln1_gain, ln1_bias, w_query, w_key, w_value, w_out,
    rel_table, xbias_table, ybias_table, ln2_gain, ln2_bias, w_in, b_in, w_down, cotangent,
):
    row_count, model = tokens.shape[1:]
    docs = lax.axis_size("docs")
    place = lax.axis_index("blk")
    doc_place = lax.axis_index("docs")
    heads = xbias_table.shape[1]
    boxes = xbias_table.shape[0]
    units = w_in.shape[1]
    width = model // blocks
    bits = bits_of(docs)
    other = [bits[1], bits[0]] + bits[2:]
    x_own = tokens[0]

    x_far = swap(x_own, "blk", 2)
    own_ints = jnp.concatenate(
        [
            positions,
            jnp.right_shift(token_boxes[0] + token_boxes[2], 1),
            jnp.right_shift(token_boxes[1] + token_boxes[3], 1),
            jnp.zeros((5, row_count), jnp.int32),
        ],
        axis=0,
    )
    ints_far = swap(own_ints, "blk", 2)
    x_core, ints_core = swap(x_own, "blk", 1), swap(own_ints, "blk", 1)
    x_both, ints_both = swap(x_far, "blk", 1), swap(ints_far, "blk", 1)
    xs = (x_own, x_far, x_core, x_both)
    tables = jnp.concatenate([xbias_table.T, ybias_table.T], axis=1).astype(f32)
    tables = tables.reshape(blocks, heads // blocks, 2 * boxes)
    at = jnp.stack([place.astype(jnp.int32), lengths[0]])
    spot = jnp.stack([place, doc_place]).astype(jnp.int32)
    att_own, att_core, att_far, probs, qkv, relkq, row, col = scores_call(
        at, xs, (own_ints, ints_far, ints_core, ints_both), w_query, w_key, w_value, rel_table, tables
    )

    came_far = swap(att_far, "blk", 2)
    came_core = swap(att_core, "blk", 1)
    came_both = swap(came_far, "blk", 1)
    line = lambda vector: vector.reshape(1, -1)
    far1, core1, act_own, act, slope, normed1, inverse1, attended = up_call(
        spot, (att_own, (came_far, 0), came_core, (came_both, 1)), x_own, w_out,
        line(ln1_gain), line(ln1_bias), w_in, line(b_in), docs,
    )
    got_far1 = swap(far1, "blk", 2)
    block_out, mix, grad_ffn, above = down_call(
        act, w_down, normed1, cotangent[0],
        line(ln1_gain), line(ln1_bias), line(ln2_gain), line(ln2_bias), units // docs,
    )
    ffn_far = swap(grad_ffn, "blk", 2)
    (
        ga_own, ga_core, ga_far, grad_resid, up_far, up_core, up_own, far3, core3, gattn_own, sums,
    ) = back_call(
        spot, w_down, slope, w_in, w_out, normed1, inverse1, mix, grad_ffn, attended,
        line(ln1_gain), above, units // docs,
    )
    came_far = swap(ordered(ga_far, ffn_far), "blk", 2)
    got_core1, got_both1 = swap(core1, "blk", 1), swap(ordered(got_far1, ga_own), "blk", 1)
    ffn_core, ffn_both = swap(grad_ffn, "blk", 1), swap(ordered(ffn_far, ga_own), "blk", 1)
    act_all = [act_own, (got_far1, 1), (got_core1, 1), (got_both1, 2)]
    gffn_all = [grad_ffn, ffn_far, ffn_core, ffn_both]
    down_halves = weight_grad_call(spot, act_all, gffn_all, bits, after=[ga_own], name="grad_down")
    down_sum = Halving(down_halves, bits)

    came_core = swap(ga_core, "blk", 1)
    came_both = swap(came_far, "blk", 1)
    ga_all = (ga_own, (came_far, 0), came_core, (came_both, 1))
    up_far_got = swap(ordered(up_far, came_far), "blk", 2)
    first_grads, first_boxes = scores_grad_call(
        0, spot, ga_all, qkv, probs, relkq, row, col, [down_halves[0]]
    )

    up_core_got, up_both_got = swap(up_core, "blk", 1), swap(ordered(up_far_got, first_grads), "blk", 1)
    hidden_all = [(far1, 0), (got_far1, 0), (got_core1, 0), (got_both1, 0)]
    up_all = [up_own, (up_far_got, 0), up_core_got, (up_both_got, 1)]
    got_far3 = swap(ordered(far3, first_grads), "blk", 2)
    in_halves = weight_grad_call(spot, hidden_all, up_all, other, after=[first_grads], name="grad_in")
    in_sum = Halving(in_halves, other)
    down_sent = down_sum.add()
    lefts = list(xs) + [rel_table]

    def rows_by_piece(grads):
        return [(grads.reshape(blocks + 1, lanes, -1), t) for t in range(blocks + 1)]

    first_halves = weight_grad_call(
        spot, lefts, rows_by_piece(first_grads), bits, after=[in_halves[0], down_sent], name="grad_qkv"
    )
    first_sum = Halving(first_halves, bits)
    second_grads, dq_own, dq_core, dq_far, small = scores_grad_call(
        1, spot, ga_all, qkv, probs, relkq, row, col, [first_halves[0]], docs,
        (w_query, w_key, sums, first_grads, first_boxes),
    )
    down_sent = down_sum.add()
    second_halves = weight_grad_call(
        spot, lefts, rows_by_piece(second_grads), other, extra=small, after=[down_sent],
        name="grad_qkv",
    )
    second_sum = Halving(second_halves, other)
    got_core3, got_both3 = swap(core3, "blk", 1), swap(ordered(got_far3, second_grads), "blk", 1)
    att_all = [far3, got_far3, got_core3, got_both3]
    per = model // width
    gattn_all = [
        gattn_own, (got_far3, None, per), (got_core3, None, per), (got_both3, None, per + 1),
    ]
    out_halves = weight_grad_call(
        spot, att_all, gattn_all, bits, right_width=width, after=[second_halves[0]], name="grad_out"
    )
    out_sum = Halving(out_halves, bits)
    dq_far_got = swap(dq_far, "blk", 2)
    dq_core_got, dq_both_got = swap(dq_core, "blk", 1), swap(dq_far_got, "blk", 1)
    in_sent = in_sum.add()
    first_sent = first_sum.add()
    out_sent = out_sum.add()
    down_part = down_sum.finish()
    grad_tokens = tokens_grad_call(
        spot, (dq_own, (dq_far_got, 0), dq_core_got, (dq_both_got, 1)), grad_resid,
        w_query, w_key, w_value, [out_halves[0], in_sent, first_sent, out_sent, down_part],
    )
    in_part = in_sum.finish()
    first_part = first_sum.finish()
    out_part = out_sum.finish()
    second_part = second_sum.finish()

    def whole(part):
        far = swap(part, "blk", 2)
        return (part, swap(part, "blk", 1), far, swap(far, "blk", 1))

    grad_w_down, grad_w_in, grad_w_out = parts_call(
        spot, ((whole(down_part), 0), (whole(in_part), 1), (whole(out_part), 1)), "gather_parts"
    )
    *grads, rel_out, norms, b_in_out, both_boxes = last_call(
        spot, whole(first_part), whole(second_part), rel_table.shape[0] // docs, model
    )
    b_in_out = b_in_out.reshape(-1)
    xb, yb = both_boxes[:, :heads], both_boxes[:, 64 : 64 + heads]
    return (
        block_out[None], grad_tokens[None], norms[0], norms[1], grads[0], grads[1], grads[2], grad_w_out,
        rel_out, xb, yb, norms[2], norms[3], grad_w_in, b_in_out, grad_w_down,
    )


def choose(*args):
    docs, parts = lax.axis_size("docs"), lax.axis_size("blk")
    tokens, w_in = args[0], args[15]
    model, units = w_in.shape
    fits = (
        parts == blocks
        and tokens.shape[1] == lanes
        and model // docs == lanes
        and units // docs == parts * lanes
        and docs & (docs - 1) == 0
        and docs > 2
        and units == blocks * model
    )
    return (shards_tiles if fits else shards)(*args)


def solution(mesh):
    rows = P("docs", "blk", None)
    placed = (
        rows, P("docs"), P("docs", "blk"), P(None, "docs", "blk"),
        *([P()] * 14), rows,
    )
    over_docs, over_docs2 = P("docs"), P("docs", None)
    return jax.shard_map(
        choose,
        mesh=mesh,
        in_specs=placed,
        out_specs=(
            rows, rows, over_docs, over_docs, over_docs2, over_docs2, over_docs2, over_docs2,
            over_docs2, over_docs2, over_docs2, over_docs, over_docs, over_docs2, over_docs, over_docs2,
        ),
        check_vma=False,
    )
```

```python
import functools
import math

import jax
import jax.numpy as jnp
from jax import lax
from jax.experimental import pallas as pl
from jax.experimental.pallas import tpu as pltpu
from jax.sharding import PartitionSpec as P

norm_eps = 1e-05
mask_value = -1e30
f32 = jnp.float32
bf16 = jnp.bfloat16
lanes = 128


def dot(a, b, contract=((1,), (0,))):
    return lax.dot_general(a, b, (contract, ((), ())), preferred_element_type=f32)


def pick(table, index):
    return jnp.take_along_axis(table, index, axis=1, mode="promise_in_bounds")


def ahead_of(first, second):
    return jnp.clip(first - second, -64, 63) + 64


def attn_fwd_kernel(
    place, x_ref, wq_ref, wk_ref, wv_ref, rel_ref, tab_ref, row_ref, col_ref,
    att_ref, probs_ref, qkv_ref, relkq_ref, key_rel,
):
    scale = 1.0 / math.sqrt(192.0)
    step = pl.program_id(0)
    rows = x_ref.shape[0]
    width = wq_ref.shape[1]
    heads = tab_ref.shape[1]
    size = width // heads
    tiles = rows // lanes

    @pl.when(step == 0)
    def _():
        for at, w_ref in enumerate((wq_ref, wk_ref, wv_ref)):
            for t in range(tiles):
                qkv_ref[t * lanes : (t + 1) * lanes, at * width : (at + 1) * width] = dot(
                    x_ref[t * lanes : (t + 1) * lanes, :], w_ref[...]
                ).astype(bf16)
        relkq_ref[:, :width] = dot(rel_ref[...], wk_ref[...]).astype(bf16)
        relkq_ref[:, width:] = dot(rel_ref[...], wq_ref[...]).astype(bf16)
        for h in range(heads):
            key_rel[h] = (
                dot(
                    qkv_ref[:, width + h * size : width + (h + 1) * size],
                    relkq_ref[:, width + h * size : width + (h + 1) * size],
                    ((1,), (1,)),
                )
                .astype(bf16)
                .astype(f32)
            )

    here = pl.ds(pl.multiple_of(step * lanes, lanes), lanes)
    pos_i = col_ref[here, 0:1]
    cx_i = col_ref[here, 1:2]
    cy_i = col_ref[here, 2:3]
    own_row = row_ref[0:1, here]
    ahead, mirror, across, vertical = [], [], [], []
    for t in range(tiles):
        span = slice(t * lanes, (t + 1) * lanes)
        ahead.append(ahead_of(pos_i, row_ref[0:1, span]))
        mirror.append(ahead_of(col_ref[span, 0:1], own_row))
        across.append(jnp.clip(jnp.right_shift(cx_i - row_ref[1:2, span], 5), -32, 31) + 32)
        vertical.append(jnp.clip(jnp.right_shift(cy_i - row_ref[2:3, span], 5), -32, 31) + 96)
    valid = row_ref[3:4, :] > 0
    for h in range(heads):
        cols = slice(h * size, (h + 1) * size)
        query = qkv_ref[here, cols]
        rel_scores = (
            dot(query, relkq_ref[:, cols], ((1,), (1,))).astype(bf16).astype(f32)
        )
        table = jnp.broadcast_to(tab_ref[0, h : h + 1, :], (lanes, lanes))
        pieces = []
        for t in range(tiles):
            span = slice(t * lanes, (t + 1) * lanes)
            content = dot(
                query, qkv_ref[span, width + h * size : width + (h + 1) * size], ((1,), (1,))
            )
            mirrored = pick(key_rel[h, span, :], mirror[t]).T
            bias = pick(table, across[t]) + pick(table, vertical[t])
            pieces.append(
                scale * (content + pick(rel_scores, ahead[t]) + mirrored) + bias
            )
        scores = jnp.where(valid, jnp.concatenate(pieces, axis=1), mask_value)
        top = jnp.max(scores, axis=1, keepdims=True)
        raised = jnp.exp(scores - top)
        probs = (raised * (1.0 / jnp.sum(raised, axis=1, keepdims=True))).astype(bf16)
        probs_ref[h] = probs
        att_ref[:, cols] = dot(
            probs, qkv_ref[:, 2 * width + h * size : 2 * width + (h + 1) * size]
        ).astype(bf16)


def attn_fwd(place, x_all, w_query, w_key, w_value, rel_table, tables, ints_row, ints_col):
    rows, model = x_all.shape
    parts, heads, _ = tables.shape
    width = w_query.shape[1] // parts
    tiles = rows // lanes
    buckets = rel_table.shape[0]
    whole = lambda *shape: pl.BlockSpec(shape, lambda i, at: (0,) * len(shape))
    column = pl.BlockSpec((model, width), lambda i, at: (0, at[0]))
    return pl.pallas_call(
        attn_fwd_kernel,
        out_shape=(
            jax.ShapeDtypeStruct((rows, width), bf16),
            jax.ShapeDtypeStruct((heads, rows, rows), bf16),
            jax.ShapeDtypeStruct((rows, 3 * width), bf16),
            jax.ShapeDtypeStruct((buckets, 2 * width), bf16),
        ),
        grid_spec=pltpu.PrefetchScalarGridSpec(
            num_scalar_prefetch=1,
            grid=(tiles,),
            in_specs=[
                whole(rows, model),
                column,
                column,
                column,
                whole(buckets, model),
                pl.BlockSpec((1, heads, lanes), lambda i, at: (at[0], 0, 0)),
                whole(8, rows),
                whole(rows, 8),
            ],
            out_specs=[
                pl.BlockSpec((lanes, width), lambda i, at: (i, 0)),
                pl.BlockSpec((heads, lanes, rows), lambda i, at: (0, i, 0)),
                whole(rows, 3 * width),
                whole(buckets, 2 * width),
            ],
            scratch_shapes=[pltpu.VMEM((heads, rows, lanes), f32)],
        ),
        compiler_params=pltpu.CompilerParams(vmem_limit_bytes=40 << 20),
        cost_estimate=pl.CostEstimate(
            flops=6 * 10**9, transcendentals=10**6, bytes_accessed=8 << 20
        ),
        name="attn_fwd",
    )(place, x_all, w_query, w_key, w_value, rel_table, tables, ints_row, ints_col)


def attn_bwd_kernel(
    ga_ref, qkv_ref, probs_ref, relkq_ref, row_ref, col_ref,
    dqkv_ref, drel_ref, boxes_ref, ds_ref,
):
    scale = 1.0 / math.sqrt(192.0)
    rows = ga_ref.shape[0]
    heads = probs_ref.shape[0]
    width = ga_ref.shape[1]
    size = width // heads
    tiles = rows // lanes
    span_width = 3 * lanes
    drel_ref[...] = jnp.zeros_like(drel_ref)
    boxes_ref[...] = jnp.zeros_like(boxes_ref)
    window = lax.broadcasted_iota(jnp.int32, (rows, span_width), 1)
    bucket = lax.broadcasted_iota(jnp.int32, (lanes, lanes), 1)
    label = lax.broadcasted_iota(jnp.int32, (rows, lanes), 1)
    all_pos = col_ref[:, 0:1]
    all_x, all_y = col_ref[:, 1:2], col_ref[:, 2:3]
    sector_x, sector_y = jnp.right_shift(all_x, 5), jnp.right_shift(all_y, 5)
    hot_x = (label == sector_x).astype(bf16)
    hot_y = (label == sector_y + 64).astype(bf16)
    hot_both = ((label == sector_x) | (label == sector_y + 64)).astype(bf16)

    def histogram(sums, total, at, base_row):
        first = at - base_row + (2 * lanes // 2 - 1) - bucket
        low = jnp.bitwise_and(first, lanes - 1)
        group = jnp.right_shift(first, 7)
        found = jnp.where(
            group == 0,
            pick(sums[:, :lanes], low),
            jnp.where(
                group == 1,
                pick(sums[:, lanes : 2 * lanes], low),
                pick(sums[:, 2 * lanes :], low),
            ),
        )
        found = jnp.where(bucket == 0, total, found)
        later = jnp.where(bucket == lanes - 1, 0.0, pltpu.roll(found, lanes - 1, 1))
        return found - later

    def by_rows(ib, carry):
        here = pl.ds(pl.multiple_of(ib * lanes, lanes), lanes)
        pos_i = col_ref[here, 0:1]
        cx_i, cy_i = col_ref[here, 1:2], col_ref[here, 2:3]
        base = jnp.min(pos_i, axis=0, keepdims=True)
        below = (all_pos <= base - 63 + window).astype(bf16)
        short_x = jnp.bitwise_and(cx_i, 31) < jnp.bitwise_and(row_ref[1:2, :], 31)
        short_y = jnp.bitwise_and(cy_i, 31) < jnp.bitwise_and(row_ref[2:3, :], 31)
        step_x = jnp.right_shift(cx_i, 5) + 32 - bucket
        step_y = jnp.right_shift(cy_i, 5) + 32 - (bucket - 64)
        in_x = (bucket < 64) & (step_x >= 0) & (step_x < 32)
        in_y = (bucket >= 64) & (step_y >= 0) & (step_y < 32)
        seek = jnp.where(in_x, step_x, jnp.where(in_y, step_y + 64, 0))
        inside = in_x | in_y
        for h in range(heads):
            cols = slice(h * size, (h + 1) * size)
            kcols = slice(width + h * size, width + (h + 1) * size)
            vcols = slice(2 * width + h * size, 2 * width + (h + 1) * size)
            probs = probs_ref[h, here, :].astype(f32)
            gained = dot(ga_ref[here, cols], qkv_ref[:, vcols], ((1,), (1,)))
            row_dots = jnp.sum(probs * gained, axis=1, keepdims=True)
            grad32 = probs * (gained - row_dots)
            grad = grad32.astype(bf16)
            ds_ref[h, here, :] = grad
            exact = grad.astype(f32)
            total = jnp.sum(exact, axis=1, keepdims=True)
            rel = histogram(dot(grad, below), total, pos_i, base)
            rel = (scale * rel).astype(bf16)
            query = qkv_ref[here, cols]
            dqkv_ref[here, cols] = (
                scale * dot(grad, qkv_ref[:, kcols]) + dot(rel, relkq_ref[:, cols])
            ).astype(bf16)
            drel_ref[:, cols] += dot(rel, query, ((0,), (0,)))
            grad_x = jnp.where(short_x, exact, 0.0).astype(bf16)
            grad_y = jnp.where(short_y, exact, 0.0).astype(bf16)
            plain = dot(grad, hot_both)
            less = dot(grad_x, hot_x) + dot(grad_y, hot_y)
            plain = jnp.where(inside, pick(plain, seek), 0.0)
            less = jnp.where(inside, pick(less, seek), 0.0)
            boxes_ref[2 * h : 2 * h + 1, :] += jnp.sum(plain, axis=0, keepdims=True)
            boxes_ref[2 * h + 1 : 2 * h + 2, :] += jnp.sum(less, axis=0, keepdims=True)
        return carry

    lax.fori_loop(0, tiles, by_rows, 0)

    def by_columns(jb, carry):
        here = pl.ds(pl.multiple_of(jb * lanes, lanes), lanes)
        pos_j = col_ref[here, 0:1]
        base = jnp.min(pos_j, axis=0, keepdims=True)
        below = (all_pos <= base - 63 + window).astype(bf16)
        for h in range(heads):
            cols = slice(h * size, (h + 1) * size)
            kcols = slice(width + h * size, width + (h + 1) * size)
            vcols = slice(2 * width + h * size, 2 * width + (h + 1) * size)
            grad = ds_ref[h, :, here]
            total = dot(grad, jnp.ones((rows, lanes), bf16), ((0,), (0,)))
            sums = dot(grad, below, ((0,), (0,)))
            mirror = (scale * histogram(sums, total, pos_j, base)).astype(bf16)
            dqkv_ref[here, kcols] = (
                scale * dot(grad, qkv_ref[:, cols], ((0,), (0,)))
                + dot(mirror, relkq_ref[:, kcols])
            ).astype(bf16)
            drel_ref[:, kcols] += dot(mirror, qkv_ref[here, kcols], ((0,), (0,)))
            dqkv_ref[here, vcols] = dot(
                probs_ref[h, :, here], ga_ref[:, cols], ((0,), (0,))
            ).astype(bf16)
        return carry

    lax.fori_loop(0, tiles, by_columns, 0)


def attn_bwd(grad_att, qkv, probs, relkq, ints_row, ints_col):
    rows, width = grad_att.shape
    heads = probs.shape[0]
    buckets = relkq.shape[0]
    inside = pl.BlockSpec(memory_space=pltpu.VMEM)
    return pl.pallas_call(
        attn_bwd_kernel,
        out_shape=(
            jax.ShapeDtypeStruct((rows, 3 * width), bf16),
            jax.ShapeDtypeStruct((buckets, 2 * width), f32),
            jax.ShapeDtypeStruct((2 * heads, lanes), f32),
        ),
        in_specs=[inside] * 6,
        out_specs=[inside] * 3,
        scratch_shapes=[pltpu.VMEM((heads, rows, rows), bf16)],
        compiler_params=pltpu.CompilerParams(vmem_limit_bytes=40 << 20),
        cost_estimate=pl.CostEstimate(
            flops=12 * 10**9, transcendentals=0, bytes_accessed=6 << 20
        ),
        name="attn_bwd",
    )(grad_att, qkv, probs, relkq, ints_row, ints_col)


def layer_norm(inputs, gain_vec, bias_vec):
    row_mean = jnp.mean(inputs, axis=-1, keepdims=True)
    centered = inputs - row_mean
    inverse = lax.rsqrt(jnp.mean(centered * centered, axis=-1, keepdims=True) + norm_eps)
    normed = centered * inverse
    return (normed * gain_vec + bias_vec, normed, inverse)


def norm_backward(grad_in, normed, inverse, gain_vec):
    grad_gain = jnp.sum(grad_in * normed, axis=0)
    grad_shift = jnp.sum(grad_in, axis=0)
    scaled = grad_in * gain_vec
    grad_input = inverse * (
        scaled
        - jnp.mean(scaled, axis=-1, keepdims=True)
        - normed * jnp.mean(scaled * normed, axis=-1, keepdims=True)
    )
    return (grad_input, grad_gain, grad_shift)


def bits_of(count):
    assert count & (count - 1) == 0
    return [1 << at for at in range(count.bit_length() - 1)]


def swap(array, axis, by):
    count = lax.axis_size(axis)
    return lax.ppermute(array, axis, [(i, i ^ by) for i in range(count)])


def offsets(count):
    order = [0]
    for bit in reversed(bits_of(count)):
        order = order + [at ^ bit for at in order]
    return order


def spread(shared, pieces):
    count = lax.axis_size("blk")
    got = {0: shared} if shared is not None else {}
    held = {(0, at): piece for at, piece in pieces.items()} if pieces else {}
    for bit in reversed(bits_of(count)):
        out_keys = [key for key in sorted(held) if key[1] & bit]
        out_shared = sorted(got)
        parts = [got[at] for at in out_shared] + [held[key] for key in out_keys]
        if bit == 1:
            came = [swap(part, "blk", bit) for part in parts]
        else:
            came = swap(jnp.concatenate(parts, axis=1), "blk", bit)
            edges = [0]
            for part in parts:
                edges.append(edges[-1] + part.shape[1])
            came = [came[:, a:b] for a, b in zip(edges[:-1], edges[1:])]
        for at, part in zip(out_shared, came):
            got[at ^ bit] = part
        for key, part in zip(out_keys, came[len(out_shared) :]):
            del held[key]
            held[(key[0] ^ bit, key[1] ^ bit)] = part
    return got, {key[0]: part for key, part in held.items()}


def by_place(stacked, place):
    count = len(stacked)
    for bit in bits_of(count):
        turned = (place & bit) != 0
        stacked = [jnp.where(turned, stacked[at ^ bit], stacked[at]) for at in range(count)]
    return stacked


def chunk_order(count):
    order = [0]
    for bit in reversed(bits_of(count)):
        order = order + [at | bit for at in order]
    return order


def for_docs(chunks, doc_place):
    moved = by_place(chunks, doc_place)
    return [moved[at] for at in chunk_order(len(chunks))]


def halve(keep, send, bits):
    count = lax.axis_size("docs")
    first = True
    current = keep
    for bit in bits:
        if not first:
            half = current.shape[0] // 2
            current, send = current[:half], current[half:]
        first = False
        came = swap(send, "docs", bit)
        current = (current.astype(f32) + came.astype(f32)).astype(bf16)
    return current


def shards(
    tokens, lengths, positions, token_boxes, ln1_gain, ln1_bias, w_query, w_key, w_value, w_out,
    rel_table, xbias_table, ybias_table, ln2_gain, ln2_bias, w_in, b_in, w_down, cotangent,
):
    doc_count, row_count, model = tokens.shape
    assert doc_count == 1 and row_count == lanes
    parts = lax.axis_size("blk")
    docs = lax.axis_size("docs")
    place = lax.axis_index("blk")
    doc_place = lax.axis_index("docs")
    heads = xbias_table.shape[1]
    own_heads = heads // parts
    width = model // parts
    buckets = rel_table.shape[0]
    boxes = xbias_table.shape[0]
    hidden_units = w_in.shape[1]
    order = offsets(parts)
    x_own = tokens[0]

    centers_x = jnp.right_shift(token_boxes[0] + token_boxes[2], 1)
    centers_y = jnp.right_shift(token_boxes[1] + token_boxes[3], 1)
    own_ints = jnp.concatenate([positions, centers_x, centers_y], axis=0)
    coded = jnp.concatenate(
        [jnp.right_shift(own_ints, 5), jnp.bitwise_and(own_ints, 31)], axis=0
    ).astype(bf16)
    coded = jnp.pad(coded.reshape(1, -1), ((0, 7), (0, model - coded.size)))
    got, _ = spread(jnp.concatenate([x_own, coded], axis=0), None)
    x_all = jnp.concatenate([got[at][:row_count] for at in order], axis=0)
    decoded = jnp.concatenate(
        [got[at][row_count : row_count + 1, : 6 * row_count].reshape(6, row_count) for at in order], axis=1
    ).astype(jnp.int32)
    ints = decoded[:3] * 32 + decoded[3:]
    slot_ids = jnp.concatenate(
        [
            (place ^ at) * row_count + lax.broadcasted_iota(jnp.int32, (1, row_count), 1)
            for at in order
        ],
        axis=1,
    )
    ints = jnp.concatenate(
        [ints, (slot_ids < lengths[0]).astype(jnp.int32), jnp.zeros((4, ints.shape[1]), jnp.int32)],
        axis=0,
    )
    ints_col = ints.T
    tables = jnp.concatenate([xbias_table.T, ybias_table.T], axis=1).astype(f32)
    tables = tables.reshape(parts, own_heads, 2 * boxes)

    attended_own, probs, qkv, relkq = attn_fwd(
        place.reshape(1), x_all, w_query, w_key, w_value, rel_table, tables, ints, ints_col
    )

    def row_block(array, at):
        t = order.index(at)
        return array[t * row_count : (t + 1) * row_count]

    _, came = spread(None, {at: row_block(attended_own, at) for at in order})
    attended = jnp.concatenate(by_place([came[at] for at in range(parts)], place), axis=1)
    attn_out = jnp.dot(attended, w_out, preferred_element_type=f32)
    hidden, normed1, inverse1 = layer_norm(x_own.astype(f32) + attn_out, ln1_gain, ln1_bias)
    hidden_low = hidden.astype(bf16)
    up_proj = jnp.dot(hidden_low, w_in, preferred_element_type=f32) + b_in
    activated, gelu_back = jax.vjp(lambda inputs: jax.nn.gelu(inputs, approximate=True), up_proj)
    activated_low = activated.astype(bf16)
    ffn_out = jnp.dot(activated_low, w_down, preferred_element_type=f32)
    normed_out, normed2, inverse2 = layer_norm(hidden + ffn_out, ln2_gain, ln2_bias)
    block_out = normed_out.astype(bf16)[None]
    grad_output = cotangent[0].astype(f32)
    grad_mix, grad_ln2_gain, grad_ln2_bias = norm_backward(grad_output, normed2, inverse2, ln2_gain)
    grad_ffn = grad_mix.astype(bf16)
    grad_act = jnp.dot(grad_ffn, w_down.T, preferred_element_type=f32)
    grad_up = gelu_back(grad_act)[0].astype(bf16)
    grad_b_in = jnp.sum(grad_up, axis=0, dtype=f32)
    grad_hidden = grad_mix + jnp.dot(grad_up, w_in.T, preferred_element_type=f32)
    grad_resid, grad_ln1_gain, grad_ln1_bias = norm_backward(
        grad_hidden, normed1, inverse1, ln1_gain
    )
    grad_attn = grad_resid.astype(bf16)
    grad_att = jnp.dot(grad_attn, w_out.T, preferred_element_type=f32).astype(bf16)

    def column_block(array, at, count):
        size = array.shape[1] // count
        return lax.dynamic_slice_in_dim(array, at * size, size, axis=1)

    _, came = spread(None, {at: column_block(grad_att, place ^ at, parts) for at in order})
    grad_att_own = jnp.concatenate([came[at] for at in order], axis=0)
    dqkv, drel, box_sums = attn_bwd(grad_att_own, qkv, probs, relkq, ints, ints_col)

    def docs_columns(array):
        size = array.shape[1] // docs
        chunks = [array[:, at * size : (at + 1) * size] for at in range(docs)]
        return jnp.concatenate(for_docs(chunks, doc_place), axis=1)

    strips = activated_low.reshape(row_count, docs, parts, -1)
    strips = [
        docs_columns(
            lax.dynamic_index_in_dim(strips, place ^ at, axis=2, keepdims=False).reshape(row_count, -1)
        )
        for at in range(parts)
    ]
    got, came = spread(docs_columns(hidden_low), dict(enumerate(strips)))
    hidden_all = jnp.concatenate([got[at] for at in order], axis=0)
    activated_all = jnp.concatenate([came[at] for at in order], axis=0)
    got, came = spread(grad_ffn, {at: column_block(grad_up, place ^ at, parts) for at in order})
    grad_ffn_all = jnp.concatenate([got[at] for at in order], axis=0)
    grad_up_all = jnp.concatenate([came[at] for at in order], axis=0)
    got, came = spread(
        docs_columns(attended), {at: column_block(grad_attn, place ^ at, parts) for at in order}
    )
    attended_all = jnp.concatenate([got[at] for at in order], axis=0)
    grad_attn_all = jnp.concatenate([came[at] for at in order], axis=0)

    def halves(left, right):
        middle = left.shape[1] // 2
        send = dot(left[:, middle:], right, ((0,), (0,))).astype(bf16)
        keep = dot(left[:, :middle], right, ((0,), (0,))).astype(bf16)
        return keep, send

    bits = bits_of(docs)
    down_part = halve(*halves(activated_all, grad_ffn_all), bits)
    in_part = halve(*halves(hidden_all, grad_up_all), bits)
    out_part = halve(*halves(attended_all, grad_attn_all), bits)

    drel_low = drel.astype(bf16)
    left = docs_columns(jnp.concatenate([x_all, rel_table], axis=0))
    right = jnp.concatenate(
        [
            dqkv,
            jnp.concatenate(
                [drel_low[:, width:], drel_low[:, :width], jnp.zeros((buckets, width), bf16)], axis=1
            ),
        ],
        axis=0,
    )
    grad_rel_table = dot(
        drel_low[:, :width], column_block(w_key, place, parts), ((1,), (1,))
    ) + dot(drel_low[:, width:], column_block(w_query, place, parts), ((1,), (1,)))
    plain, less = box_sums[0::2], box_sums[1::2]

    def box_grad(at):
        plain_here, less_here = plain[:, at : at + boxes], less[:, at : at + boxes]
        later = jnp.pad(less_here[:, 1:], ((0, 0), (0, 1)))
        grad = (plain_here - less_here + later).T
        return lax.dynamic_update_slice(jnp.zeros((boxes, heads), f32), grad, (0, place * own_heads))

    small = jnp.concatenate(
        [
            grad_rel_table.reshape(docs, -1),
            grad_ln1_gain.reshape(docs, -1),
            grad_ln1_bias.reshape(docs, -1),
            grad_ln2_gain.reshape(docs, -1),
            grad_ln2_bias.reshape(docs, -1),
            grad_b_in.reshape(docs, -1),
            box_grad(0).reshape(docs, -1),
            box_grad(boxes).reshape(docs, -1),
        ],
        axis=1,
    ).astype(bf16)
    small_width = small.shape[1]
    across = 3 * width
    small = jnp.pad(small, ((0, 0), (0, -small_width % (8 * across))))
    small = for_docs([small[at] for at in range(docs)], doc_place)
    small = jnp.stack(small).reshape(docs, -1, across)
    keep, send = halves(left, right)
    middle = docs // 2
    chunk_rows = model // docs

    def with_small(main, extra):
        main = main.reshape(middle, chunk_rows, across)
        return jnp.concatenate([main, extra], axis=1).reshape(-1, across)

    qkv_part = halve(with_small(keep, small[:middle]), with_small(send, small[middle:]), bits)

    _, came = spread(None, {at: row_block(dqkv, at) for at in order})
    came = by_place([came[at] for at in range(parts)], place)
    grad_tokens = grad_resid
    for at, weight in enumerate((w_query, w_key, w_value)):
        grad = jnp.concatenate([rows[:, at * width : (at + 1) * width] for rows in came], axis=1)
        grad_tokens = grad_tokens + dot(grad, weight, ((1,), (1,)))

    def whole(part):
        got, _ = spread(part, None)
        return by_place([got[at] for at in range(parts)], place)

    grad_w_down = jnp.concatenate(whole(down_part), axis=0).astype(f32)
    grad_w_in = jnp.concatenate(whole(in_part), axis=1).astype(f32)
    grad_w_out = jnp.concatenate(whole(out_part), axis=1).astype(f32)
    pieces = whole(qkv_part)
    grads = [
        jnp.concatenate(
            [piece[:chunk_rows, at * width : (at + 1) * width] for piece in pieces], axis=1
        ).astype(f32)
        for at in range(3)
    ]
    total = sum(piece[chunk_rows:].astype(f32) for piece in pieces).reshape(-1)
    sizes = [
        (buckets // docs, model),
        (model // docs,),
        (model // docs,),
        (model // docs,),
        (model // docs,),
        (hidden_units // docs,),
        (boxes // docs, heads),
        (boxes // docs, heads),
    ]
    small_out = []
    start = 0
    for size in sizes:
        small_out.append(total[start : start + math.prod(size)].reshape(size))
        start += math.prod(size)
    rel_out, ln1g, ln1b, ln2g, ln2b, b_in_out, xb, yb = small_out
    return (
        block_out, grad_tokens[None], ln1g, ln1b, grads[0], grads[1], grads[2], grad_w_out,
        rel_out, xb, yb, ln2g, ln2b, grad_w_in, b_in_out, grad_w_down,
    )


blocks = 4
slots = (0, 2, 1, 3)


def rows_of(handle, tile=None, column=None):
    array, lead = handle if isinstance(handle, tuple) else (handle, None)
    shape = array.shape[-2:] if tile is None else tile
    column = column or (lambda *grid: 0)
    if lead is None:
        return pl.BlockSpec(shape, lambda *grid: (0, column(*grid)))
    return pl.BlockSpec((None,) + shape, lambda *grid: (lead, 0, column(*grid)))


def array_of(handle):
    return handle[0] if isinstance(handle, tuple) else handle


def full(shape):
    return pl.BlockSpec(shape, lambda *grid: (0,) * len(shape))


def cost(us):
    return pl.CostEstimate(flops=int(us * 3 * 10**8), transcendentals=0, bytes_accessed=0)


def ordered(array, *before):
    return lax.optimization_barrier((array,) + before)[0]


def params(limit):
    return pltpu.CompilerParams(vmem_limit_bytes=limit << 20)


def gelu_parts(u):
    root = math.sqrt(2.0 / math.pi)
    inner = jnp.tanh(root * (u + 0.044715 * u * u * u))
    value = 0.5 * u * (1.0 + inner)
    slope = 0.5 * (1.0 + inner) + 0.5 * u * (1.0 - inner * inner) * root * (
        1.0 + 3.0 * 0.044715 * u * u
    )
    return value, slope


def scores_kernel(
    at_ref, x0, x1, x2, x3, i0, i1, i2, i3, wq_ref, wk_ref, wv_ref, rel_ref, tab_ref,
    own_ref, core_ref, far_ref, probs_ref, qkv_ref, relkq_ref, row_ref, col_ref,
    key_rel, queries, keys_t, values, rel_keys_t, sector_hot,
):
    scale = 1.0 / math.sqrt(192.0)
    step = pl.program_id(0)
    rows = blocks * lanes
    width = wq_ref.shape[1]
    heads = tab_ref.shape[1]
    size = width // heads

    @pl.when(step == 0)
    def _():
        for t, (x_ref, i_ref) in enumerate(zip((x0, x1, x2, x3), (i0, i1, i2, i3))):
            span = slice(t * lanes, (t + 1) * lanes)
            for at, w_ref in enumerate((wq_ref, wk_ref, wv_ref)):
                part = dot(x_ref[...], w_ref[...]).astype(bf16)
                qkv_ref[span, at * width : (at + 1) * width] = part
                if at == 1:
                    keys_t[:, span] = part.astype(f32).T.astype(bf16)
                else:
                    for h in range(heads):
                        (queries, None, values)[at][h, span, :] = part[:, h * size : (h + 1) * size]
            first = jnp.bitwise_xor(at_ref[0], slots[t]) * lanes
            slot = first + lax.broadcasted_iota(jnp.int32, (8, lanes), 1)
            kind = lax.broadcasted_iota(jnp.int32, (8, lanes), 0)
            ints = jnp.where(kind == 3, (slot < at_ref[1]).astype(jnp.int32), i_ref[...])
            row_ref[:, span] = ints
            col_ref[span, :] = ints.astype(f32).T.astype(jnp.int32)
        sector = lax.broadcasted_iota(jnp.int32, (32, rows), 0)
        for k in range(2):
            hot = (jnp.right_shift(row_ref[1 + k : 2 + k, :], 5) == sector).astype(f32).astype(bf16)
            sector_hot[k * 32 : (k + 1) * 32, :] = hot
        rel_keys = dot(rel_ref[...], wk_ref[...])
        relkq_ref[:, :width] = rel_keys.astype(bf16)
        rel_keys_t[...] = rel_keys.T.astype(bf16)
        relkq_ref[:, width:] = dot(rel_ref[...], wq_ref[...]).astype(bf16)
        for h in range(heads):
            cols = slice(width + h * size, width + (h + 1) * size)
            key_rel[h] = (
                dot(qkv_ref[:, cols], relkq_ref[:, cols], ((1,), (1,))).astype(bf16).astype(f32)
            )

    here = pl.ds(pl.multiple_of(step * lanes, lanes), lanes)
    pos_i = col_ref[here, 0:1]
    cx_i = col_ref[here, 1:2]
    cy_i = col_ref[here, 2:3]
    own_row = row_ref[0:1, here]
    lane = lax.broadcasted_iota(jnp.int32, (lanes, lanes), 1)
    on_x = jnp.bitwise_and(jnp.right_shift(lane, 5), 1) == 0
    seek = (
        jnp.where(on_x, jnp.right_shift(cx_i, 5), jnp.right_shift(cy_i, 5) + 64)
        + 32
        - jnp.bitwise_and(lane, 31)
        - (lane >= 64).astype(jnp.int32)
    )
    short_x = jnp.bitwise_and(cx_i, 31) < jnp.bitwise_and(row_ref[1:2, :], 31)
    short_y = jnp.bitwise_and(cy_i, 31) < jnp.bitwise_and(row_ref[2:3, :], 31)
    ahead, mirror = [], []
    for t in range(blocks):
        span = slice(t * lanes, (t + 1) * lanes)
        ahead.append(ahead_of(pos_i, row_ref[0:1, span]))
        mirror.append(ahead_of(col_ref[span, 0:1], own_row))
    valid = row_ref[3:4, :] > 0
    attended = []
    for h in range(heads):
        cols = slice(h * size, (h + 1) * size)
        query = queries[h, here, :]
        rel_scores = dot(query, rel_keys_t[cols, :]).astype(bf16).astype(f32)
        table = jnp.broadcast_to(tab_ref[0, h : h + 1, :], (lanes, lanes))
        by_sector = pick(table, seek).astype(bf16)
        content = dot(query, keys_t[cols, :])
        plain_x = dot(by_sector[:, 0:32], sector_hot[0:32, :])
        plain_y = dot(by_sector[:, 32:64], sector_hot[32:64, :])
        less_x = dot(by_sector[:, 64:96], sector_hot[0:32, :])
        less_y = dot(by_sector[:, 96:128], sector_hot[32:64, :])
        bias = jnp.where(short_x, less_x, plain_x) + jnp.where(short_y, less_y, plain_y)
        moved = []
        for t in range(blocks):
            span = slice(t * lanes, (t + 1) * lanes)
            moved.append(pick(rel_scores, ahead[t]) + pick(key_rel[h, span, :], mirror[t]).T)
        scores = scale * (content + jnp.concatenate(moved, axis=1)) + bias
        scores = jnp.where(valid, scores, mask_value)
        top = jnp.max(scores, axis=1, keepdims=True)
        raised = jnp.exp(scores - top)
        probs = (raised * (1.0 / jnp.sum(raised, axis=1, keepdims=True))).astype(bf16)
        probs_ref[h] = probs
        attended.append(dot(probs, values[h]).astype(bf16))
    attended = jnp.concatenate(attended, axis=1)
    for t, target in enumerate((own_ref, far_ref.at[0], core_ref, far_ref.at[1])):

        @pl.when(step == t)
        def _(target=target):
            target[...] = attended


def scores_call(at, xs, ints, w_query, w_key, w_value, rel_table, tables):
    rows, model = blocks * lanes, w_query.shape[0]
    parts, heads, _ = tables.shape
    width = w_query.shape[1] // parts
    buckets = rel_table.shape[0]
    column = pl.BlockSpec((model, width), lambda i, at: (0, at[0]))
    return pl.pallas_call(
        scores_kernel,
        out_shape=(
            jax.ShapeDtypeStruct((lanes, width), bf16),
            jax.ShapeDtypeStruct((lanes, width), bf16),
            jax.ShapeDtypeStruct((2, lanes, width), bf16),
            jax.ShapeDtypeStruct((heads, rows, rows), bf16),
            jax.ShapeDtypeStruct((rows, 3 * width), bf16),
            jax.ShapeDtypeStruct((buckets, 2 * width), bf16),
            jax.ShapeDtypeStruct((8, rows), jnp.int32),
            jax.ShapeDtypeStruct((rows, 8), jnp.int32),
        ),
        grid_spec=pltpu.PrefetchScalarGridSpec(
            num_scalar_prefetch=1,
            grid=(blocks,),
            in_specs=[rows_of(x) for x in xs]
            + [rows_of(i) for i in ints]
            + [
                column,
                column,
                column,
                full((buckets, model)),
                pl.BlockSpec((1, heads, lanes), lambda i, at: (at[0], 0, 0)),
            ],
            out_specs=[
                full((lanes, width)),
                full((lanes, width)),
                full((2, lanes, width)),
                pl.BlockSpec((heads, lanes, rows), lambda i, at: (0, i, 0)),
                full((rows, 3 * width)),
                full((buckets, 2 * width)),
                full((8, rows)),
                full((rows, 8)),
            ],
            scratch_shapes=[
                pltpu.VMEM((heads, rows, lanes), f32),
                pltpu.VMEM((heads, rows, width // heads), bf16),
                pltpu.VMEM((width, rows), bf16),
                pltpu.VMEM((heads, rows, width // heads), bf16),
                pltpu.VMEM((width, buckets), bf16),
                pltpu.VMEM((64, rows), bf16),
            ],
        ),
        compiler_params=params(56),
        cost_estimate=cost(25),
        name="scores",
    )(
        at, *map(array_of, xs), *map(array_of, ints), w_query, w_key, w_value, rel_table, tables
    )


def up_kernel(
    at_ref, a0, a1, a2, a3, x_ref, wout_ref, gain_ref, bias_ref, win_ref, bin_ref,
    far_ref, core_ref, own_ref, act_ref, slope_ref, normed_ref, inverse_ref, attended_ref,
    hidden_low,
):
    step = pl.program_id(0)
    width = a0.shape[1]
    tile = win_ref.shape[1]

    @pl.when(step == 0)
    def _():
        total = x_ref[...].astype(f32)
        for t, piece in enumerate((a0, a1, a2, a3)):
            first = pl.multiple_of(jnp.bitwise_xor(at_ref[0], slots[t]) * width, width)
            total = total + dot(piece[...], wout_ref[pl.ds(first, width), :])
            attended_ref[:, pl.ds(first, width)] = piece[...]
        centered = total - jnp.mean(total, axis=1, keepdims=True)
        inverse = lax.rsqrt(jnp.mean(centered * centered, axis=1, keepdims=True) + norm_eps)
        normed = centered * inverse
        normed_ref[...] = normed
        inverse_ref[...] = jnp.broadcast_to(inverse, inverse_ref.shape)
        hidden = (normed * gain_ref[...] + bias_ref[...]).astype(bf16)
        hidden_low[...] = hidden
        far_ref[0] = hidden
        core_ref[0] = hidden

    value, slope = gelu_parts(dot(hidden_low[...], win_ref[...]) + bin_ref[...])
    value = value.astype(bf16)
    act_ref[...] = value
    slope_ref[...] = slope.astype(bf16)
    strip = tile // blocks
    here = pl.ds(pl.multiple_of(step * strip, strip), strip)
    for t, target in enumerate((own_ref, far_ref.at[1], core_ref.at[1], far_ref.at[2])):
        first = pl.multiple_of(jnp.bitwise_xor(at_ref[0], slots[t]) * strip, strip)
        target[:, here] = act_ref[:, pl.ds(first, strip)]


def up_call(at, pieces, x_own, w_out, gain, bias, w_in, b_in, docs):
    rows, model = x_own.shape
    units = w_in.shape[1]
    tile = units // docs
    quarter = units // blocks
    column = lambda i, at: (0, i)
    return pl.pallas_call(
        up_kernel,
        out_shape=(
            jax.ShapeDtypeStruct((3, rows, model), bf16),
            jax.ShapeDtypeStruct((2, rows, model), bf16),
            jax.ShapeDtypeStruct((rows, quarter), bf16),
            jax.ShapeDtypeStruct((rows, units), bf16),
            jax.ShapeDtypeStruct((rows, units), bf16),
            jax.ShapeDtypeStruct((rows, model), f32),
            jax.ShapeDtypeStruct((rows, lanes), f32),
            jax.ShapeDtypeStruct((rows, model), bf16),
        ),
        grid_spec=pltpu.PrefetchScalarGridSpec(
            num_scalar_prefetch=1,
            grid=(docs,),
            in_specs=[rows_of(piece) for piece in pieces]
            + [
                full((rows, model)),
                full((model, model)),
                full((1, model)),
                full((1, model)),
                pl.BlockSpec((model, tile), column),
                pl.BlockSpec((1, tile), column),
            ],
            out_specs=[
                full((3, rows, model)),
                full((2, rows, model)),
                full((rows, quarter)),
                pl.BlockSpec((rows, tile), column),
                pl.BlockSpec((rows, tile), column),
                full((rows, model)),
                full((rows, lanes)),
                full((rows, model)),
            ],
            scratch_shapes=[pltpu.VMEM((rows, model), bf16)],
        ),
        compiler_params=params(40),
        cost_estimate=cost(9),
        name="up",
    )(at, *map(array_of, pieces), x_own, w_out, gain, bias, w_in, b_in)


def norm_back(grad, normed, inverse, gain):
    scaled = grad * gain
    return inverse * (
        scaled
        - jnp.mean(scaled, axis=1, keepdims=True)
        - normed * jnp.mean(scaled * normed, axis=1, keepdims=True)
    )


def down_kernel(
    act_ref, wdown_ref, normed_ref, cot_ref, gain1_ref, bias1_ref, gain2_ref, bias2_ref,
    block_ref, mix_ref, low_ref, sums_ref,
):
    step = pl.program_id(0)

    @pl.when(step == 0)
    def _():
        mix_ref[...] = normed_ref[...] * gain1_ref[...] + bias1_ref[...]

    mix_ref[...] += dot(act_ref[...], wdown_ref[...])

    @pl.when(step == pl.num_programs(0) - 1)
    def _():
        mixed = mix_ref[...]
        centered = mixed - jnp.mean(mixed, axis=1, keepdims=True)
        inverse = lax.rsqrt(jnp.mean(centered * centered, axis=1, keepdims=True) + norm_eps)
        normed = centered * inverse
        block_ref[...] = (normed * gain2_ref[...] + bias2_ref[...]).astype(bf16)
        grad = cot_ref[...].astype(f32)
        sums_ref[0:1, :] = jnp.sum(grad * normed, axis=0, keepdims=True)
        sums_ref[1:2, :] = jnp.sum(grad, axis=0, keepdims=True)
        mix = norm_back(grad, normed, inverse, gain2_ref[...])
        mix_ref[...] = mix
        low_ref[...] = mix.astype(bf16)


def down_call(act, w_down, normed, cotangent, gain1, bias1, gain2, bias2, tile):
    rows, units = act.shape
    model = w_down.shape[1]
    return pl.pallas_call(
        down_kernel,
        out_shape=(
            jax.ShapeDtypeStruct((rows, model), bf16),
            jax.ShapeDtypeStruct((rows, model), f32),
            jax.ShapeDtypeStruct((rows, model), bf16),
            jax.ShapeDtypeStruct((8, model), f32),
        ),
        grid=(units // tile,),
        in_specs=[
            pl.BlockSpec((rows, tile), lambda i: (0, i)),
            pl.BlockSpec((tile, model), lambda i: (i, 0)),
            full((rows, model)),
            full((rows, model)),
        ]
        + [full((1, model))] * 4,
        out_specs=[full((rows, model))] * 3 + [full((8, model))],
        compiler_params=params(40),
        cost_estimate=cost(8),
        name="down",
    )(act, w_down, normed, cotangent, gain1, bias1, gain2, bias2)


def back_kernel(
    at_ref, wdown_ref, slope_ref, win_ref, wout_ref, normed_ref, inverse_ref, mix_ref, ffn_ref,
    attended_ref, gain1_ref, above_ref,
    own_ref, core_ref, far_ref, resid_ref, upfar_ref, upcore_ref, upown_ref,
    outfar_ref, outcore_ref, outown_ref, sums_ref,
    total, grad_up,
):
    step = pl.program_id(0)
    steps = pl.num_programs(0)
    rows, tile = slope_ref.shape
    model = mix_ref.shape[1]
    width = model // blocks

    @pl.when(step == 0)
    def _():
        total[...] = mix_ref[...]

    grad = dot(ffn_ref[...], wdown_ref[...], ((1,), (1,))) * slope_ref[...].astype(f32)
    low = grad.astype(bf16)
    total[...] += dot(low, win_ref[...], ((1,), (1,)))
    per = model // tile
    part = step // per
    here = pl.ds(pl.multiple_of((step - part * per) * tile, tile), tile)
    grad_up[jnp.bitwise_xor(part, at_ref[0]), :, here] = low
    sums_ref[pl.ds(4 + part, 1), here] = jnp.sum(low.astype(f32), axis=0, keepdims=True)

    @pl.when(step == steps - 1)
    def _():
        upown_ref[...] = grad_up[0]
        upcore_ref[0] = ffn_ref[...]
        upcore_ref[1] = grad_up[1]
        upfar_ref[0] = ffn_ref[...]
        upfar_ref[1] = grad_up[2]
        upfar_ref[2] = grad_up[3]
        grad = total[...]
        normed = normed_ref[...]
        sums_ref[0:1, :] = jnp.sum(grad * normed, axis=0, keepdims=True)
        sums_ref[1:2, :] = jnp.sum(grad, axis=0, keepdims=True)
        sums_ref[2:4, :] = above_ref[0:2, :]
        resid = norm_back(grad, normed, inverse_ref[:, 0:1], gain1_ref[...])
        resid_ref[...] = resid
        low = resid.astype(bf16)
        total[...] = low.astype(f32)
        outfar_ref[:, :model] = attended_ref[...]
        outcore_ref[:, :model] = attended_ref[...]
        targets = (own_ref, core_ref, far_ref.at[0], far_ref.at[1])
        wides = (
            outown_ref, outcore_ref.at[:, pl.ds(model, width)],
            outfar_ref.at[:, pl.ds(model, width)], outfar_ref.at[:, pl.ds(model + width, width)],
        )
        for at, (target, wide) in enumerate(zip(targets, wides)):
            first = pl.multiple_of(jnp.bitwise_xor(at_ref[0], at) * width, width)
            target[...] = dot(low, wout_ref[pl.ds(first, width), :], ((1,), (1,))).astype(bf16)
            wide[...] = total[:, pl.ds(first, width)].astype(bf16)


def back_call(
    at, w_down, slope, w_in, w_out, normed, inverse, mix, grad_ffn, attended, gain1, above, tile,
):
    rows, units = slope.shape
    model = w_out.shape[0]
    width = model // blocks
    return pl.pallas_call(
        back_kernel,
        out_shape=(
            jax.ShapeDtypeStruct((rows, width), bf16),
            jax.ShapeDtypeStruct((rows, width), bf16),
            jax.ShapeDtypeStruct((2, rows, width), bf16),
            jax.ShapeDtypeStruct((rows, model), f32),
            jax.ShapeDtypeStruct((3, rows, model), bf16),
            jax.ShapeDtypeStruct((2, rows, model), bf16),
            jax.ShapeDtypeStruct((rows, model), bf16),
            jax.ShapeDtypeStruct((rows, model + 2 * width), bf16),
            jax.ShapeDtypeStruct((rows, model + width), bf16),
            jax.ShapeDtypeStruct((rows, width), bf16),
            jax.ShapeDtypeStruct((8, model), f32),
        ),
        grid_spec=pltpu.PrefetchScalarGridSpec(
            num_scalar_prefetch=1,
            grid=(units // tile,),
            in_specs=[
                pl.BlockSpec((tile, model), lambda i, at: (i, 0)),
                pl.BlockSpec((rows, tile), lambda i, at: (0, i)),
                pl.BlockSpec((model, tile), lambda i, at: (0, i)),
                full((model, model)),
                full((rows, model)),
                full((rows, lanes)),
                full((rows, model)),
                full((rows, model)),
                full((rows, model)),
                full((1, model)),
                full((8, model)),
            ],
            out_specs=[
                full((rows, width)),
                full((rows, width)),
                full((2, rows, width)),
                full((rows, model)),
                full((3, rows, model)),
                full((2, rows, model)),
                full((rows, model)),
                full((rows, model + 2 * width)),
                full((rows, model + width)),
                full((rows, width)),
                full((8, model)),
            ],
            scratch_shapes=[
                pltpu.VMEM((rows, model), f32),
                pltpu.VMEM((blocks, rows, model), bf16),
            ],
        ),
        compiler_params=params(40),
        cost_estimate=cost(12),
        name="back",
    )(at, w_down, slope, w_in, w_out, normed, inverse, mix, grad_ffn, attended, gain1, above)


def scores_grad_kernel(half, held, *refs):
    at_ref, g0, g1, g2, g3, qkv_ref, probs_ref, relkq_ref, row_ref, col_ref = refs[:10]
    refs = refs[10:]
    last = half == 1
    if last:
        wq_ref, wk_ref, sums_ref, before_ref, boxes_before = refs[:5]
        refs = refs[5:]
    refs = refs[held:]
    if last:
        dqkv_ref, own_ref, core_ref, far_ref, small_ref, ga_ref, ds_ref, drel, box_sums = refs
    else:
        dqkv_ref, box_sums, ga_ref, ds_ref, drel = refs
    scale = 1.0 / math.sqrt(192.0)
    rows = blocks * lanes
    width = qkv_ref.shape[1] // 3
    part = width // 2
    heads = probs_ref.shape[0]
    size = part // heads
    span_width = 3 * lanes
    for t, piece in enumerate((g0, g1, g2, g3)):
        ga_ref[t * lanes : (t + 1) * lanes, :] = piece[...]
    drel[...] = jnp.zeros_like(drel)
    box_sums[...] = jnp.zeros_like(box_sums)
    window = lax.broadcasted_iota(jnp.int32, (rows, span_width), 1)
    bucket = lax.broadcasted_iota(jnp.int32, (lanes, lanes), 1)
    label = lax.broadcasted_iota(jnp.int32, (rows, lanes), 1)
    all_pos = col_ref[:, 0:1]
    all_x, all_y = col_ref[:, 1:2], col_ref[:, 2:3]
    sector_x, sector_y = jnp.right_shift(all_x, 5), jnp.right_shift(all_y, 5)
    hot_x = (label == sector_x).astype(bf16)
    hot_y = (label == sector_y + 64).astype(bf16)
    hot_both = ((label == sector_x) | (label == sector_y + 64)).astype(bf16)

    def histogram(sums, total, at, base_row):
        first = at - base_row + (lanes - 1) - bucket
        low = jnp.bitwise_and(first, lanes - 1)
        group = jnp.right_shift(first, 7)
        found = jnp.where(
            group == 0,
            pick(sums[:, :lanes], low),
            jnp.where(
                group == 1,
                pick(sums[:, lanes : 2 * lanes], low),
                pick(sums[:, 2 * lanes :], low),
            ),
        )
        found = jnp.where(bucket == 0, total, found)
        later = jnp.where(bucket == lanes - 1, 0.0, pltpu.roll(found, lanes - 1, 1))
        return found - later

    def by_rows(ib, carry):
        here = pl.ds(pl.multiple_of(ib * lanes, lanes), lanes)
        pos_i = col_ref[here, 0:1]
        cx_i, cy_i = col_ref[here, 1:2], col_ref[here, 2:3]
        base = jnp.min(pos_i, axis=0, keepdims=True)
        below = (all_pos <= base - 63 + window).astype(bf16)
        short_x = jnp.bitwise_and(cx_i, 31) < jnp.bitwise_and(row_ref[1:2, :], 31)
        short_y = jnp.bitwise_and(cy_i, 31) < jnp.bitwise_and(row_ref[2:3, :], 31)
        step_x = jnp.right_shift(cx_i, 5) + 32 - bucket
        step_y = jnp.right_shift(cy_i, 5) + 32 - (bucket - 64)
        in_x = (bucket < 64) & (step_x >= 0) & (step_x < 32)
        in_y = (bucket >= 64) & (step_y >= 0) & (step_y < 32)
        seek = jnp.where(in_x, step_x, jnp.where(in_y, step_y + 64, 0))
        inside = in_x | in_y
        for h in range(heads):
            gcols = slice(h * size, (h + 1) * size)
            kgcols = slice(part + h * size, part + (h + 1) * size)
            vgcols = slice(2 * part + h * size, 2 * part + (h + 1) * size)
            cols, kcols, vcols = (
                slice(k * width + half * part + h * size, k * width + half * part + (h + 1) * size)
                for k in range(3)
            )
            probs = probs_ref[h, here, :].astype(f32)
            gained = dot(ga_ref[here, gcols], qkv_ref[:, vcols], ((1,), (1,)))
            row_dots = jnp.sum(probs * gained, axis=1, keepdims=True)
            grad = (probs * (gained - row_dots)).astype(bf16)
            ds_ref[h, here, :] = grad
            exact = grad.astype(f32)
            total = jnp.sum(exact, axis=1, keepdims=True)
            rel = histogram(dot(grad, below), total, pos_i, base)
            rel = (scale * rel).astype(bf16)
            dqkv_ref[here, gcols] = (
                scale * dot(grad, qkv_ref[:, kcols]) + dot(rel, relkq_ref[:, cols])
            ).astype(bf16)
            drel[:, gcols] += dot(rel, qkv_ref[here, cols], ((0,), (0,)))
            grad_x = jnp.where(short_x, exact, 0.0).astype(bf16)
            grad_y = jnp.where(short_y, exact, 0.0).astype(bf16)
            plain = dot(grad, hot_both)
            less = dot(grad_x, hot_x) + dot(grad_y, hot_y)
            plain = jnp.where(inside, pick(plain, seek), 0.0)
            less = jnp.where(inside, pick(less, seek), 0.0)
            box_sums[h : h + 1, :] += jnp.sum(plain, axis=0, keepdims=True)
            box_sums[8 + h : 9 + h, :] += jnp.sum(less, axis=0, keepdims=True)
        return carry

    lax.fori_loop(0, blocks, by_rows, 0)

    def by_columns(jb, carry):
        here = pl.ds(pl.multiple_of(jb * lanes, lanes), lanes)
        pos_j = col_ref[here, 0:1]
        base = jnp.min(pos_j, axis=0, keepdims=True)
        below = (all_pos <= base - 63 + window).astype(bf16)
        for h in range(heads):
            gcols = slice(h * size, (h + 1) * size)
            kgcols = slice(part + h * size, part + (h + 1) * size)
            vgcols = slice(2 * part + h * size, 2 * part + (h + 1) * size)
            cols, kcols, vcols = (
                slice(k * width + half * part + h * size, k * width + half * part + (h + 1) * size)
                for k in range(3)
            )
            grad = ds_ref[h, :, here]
            total = dot(grad, jnp.ones((rows, lanes), bf16), ((0,), (0,)))
            sums = dot(grad, below, ((0,), (0,)))
            mirror = (scale * histogram(sums, total, pos_j, base)).astype(bf16)
            dqkv_ref[here, kgcols] = (
                scale * dot(grad, qkv_ref[:, cols], ((0,), (0,)))
                + dot(mirror, relkq_ref[:, kcols])
            ).astype(bf16)
            drel[:, kgcols] += dot(mirror, qkv_ref[here, kcols], ((0,), (0,)))
            dqkv_ref[here, vgcols] = dot(
                probs_ref[h, :, here], ga_ref[:, gcols], ((0,), (0,))
            ).astype(bf16)
        return carry

    lax.fori_loop(0, blocks, by_columns, 0)
    keys, queries = drel[:, :part].astype(bf16), drel[:, part:].astype(bf16)
    dqkv_ref[rows:, :part] = queries
    dqkv_ref[rows:, part : 2 * part] = keys
    dqkv_ref[rows:, 2 * part :] = jnp.zeros((lanes, part), bf16)
    if not last:
        return
    for t, target in enumerate((own_ref, far_ref.at[0], core_ref, far_ref.at[1])):
        span = slice(t * lanes, (t + 1) * lanes)
        for k in range(3):
            first = k * width
            target[:, first : first + part] = before_ref[span, k * part : (k + 1) * part]
            target[:, first + part : first + width] = dqkv_ref[span, k * part : (k + 1) * part]
    queries = jnp.concatenate([before_ref[rows:, :part], queries], axis=1)
    keys = jnp.concatenate([before_ref[rows:, part : 2 * part], keys], axis=1)

    docs, small_rows, small_width = small_ref.shape
    per = lanes // docs
    table = (
        dot(keys, wk_ref[...], ((1,), (1,))) + dot(queries, wq_ref[...], ((1,), (1,)))
    ).astype(bf16)
    plain = jnp.concatenate([boxes_before[0:heads], box_sums[0:heads], box_sums[heads + heads : 8]], axis=0)
    less = jnp.concatenate(
        [boxes_before[8 : 8 + heads], box_sums[8 : 8 + heads], box_sums[8 + 2 * heads : 16]], axis=0
    )
    heads = 2 * heads
    place_lane = lax.broadcasted_iota(jnp.int32, (8, lanes), 1)
    later = jnp.where(
        jnp.bitwise_and(place_lane, 63) == 63, 0.0, pltpu.roll(less, lanes - 1, 1)
    )
    boxes = (plain - less + later).astype(bf16)
    row_at = lax.broadcasted_iota(jnp.int32, (8, lanes), 0)
    head_at = at_ref[0] * heads + row_at
    by_head = [
        dot(boxes, ((place_lane == head_at + k * 64) & (row_at < heads)).astype(bf16), ((0,), (0,)))
        for k in range(2)
    ]
    model = table.shape[1]
    edges = list(range(0, model, small_width)) + [model]
    rest = edges[-1] - edges[-2]
    lane = slice(rest, rest + lanes)
    line = (len(edges) - 2) * per
    count = lanes // 2 // docs
    for chunk in range(docs):
        own = slice(chunk * per, (chunk + 1) * per)
        for k, (first, end) in enumerate(zip(edges[:-1], edges[1:])):
            small_ref[chunk, k * per : (k + 1) * per, : end - first] = table[own, first:end].astype(f32)
        for k in range(4):
            small_ref[chunk, line + k : line + k + 1, lane] = (
                sums_ref[k : k + 1, chunk * lanes : (chunk + 1) * lanes]
            )
            first = (chunk * blocks + k) * lanes
            where = first // model
            small_ref[chunk, line + 4 + k : line + 5 + k, lane] = (
                sums_ref[4 + where : 5 + where, first - where * model : first - where * model + lanes]
            )
        begin = chunk * count
        small_ref[chunk, line + 8 : line + 8 + count, lane] = (
            by_head[0][begin : begin + count, :] + by_head[1][64 + begin : 64 + begin + count, :]
        )


def scores_grad_call(half, at, pieces, qkv, probs, relkq, row, col, after, docs=0, extra=()):
    rows = blocks * lanes
    heads = probs.shape[0] // 2
    width = qkv.shape[1] // 3
    part = width // 2
    model = width * blocks
    buckets = relkq.shape[0]
    column = pl.BlockSpec((model, width), lambda i, at: (0, at[0]))
    grads = jax.ShapeDtypeStruct((rows + buckets, 3 * part), bf16)
    box_shape = (16, lanes)
    scratch = [
        pltpu.VMEM((rows, part), bf16),
        pltpu.VMEM((heads, rows, rows), bf16),
        pltpu.VMEM((buckets, 2 * part), f32),
    ]
    extra_specs = []
    if half == 1:
        shapes = (
            grads,
            jax.ShapeDtypeStruct((lanes, 3 * width), bf16),
            jax.ShapeDtypeStruct((lanes, 3 * width), bf16),
            jax.ShapeDtypeStruct((2, lanes, 3 * width), bf16),
            jax.ShapeDtypeStruct((docs, 3 * buckets // docs, 3 * part), f32),
        )
        extra_specs = [column, column, full((8, model)), full(grads.shape), full(box_shape)]
        scratch = scratch + [pltpu.VMEM(box_shape, f32)]
    else:
        shapes = (grads, jax.ShapeDtypeStruct(box_shape, f32))
    return pl.pallas_call(
        functools.partial(scores_grad_kernel, half, len(after)),
        out_shape=shapes,
        grid_spec=pltpu.PrefetchScalarGridSpec(
            num_scalar_prefetch=1,
            grid=(1,),
            in_specs=[rows_of(piece, (lanes, part), lambda i, at: half) for piece in pieces]
            + [
                full((rows, 3 * width)),
                pl.BlockSpec((heads, rows, rows), lambda i, at: (half, 0, 0)),
                full((buckets, 2 * width)),
                full((8, rows)),
                full((rows, 8)),
            ]
            + extra_specs
            + [pl.BlockSpec(memory_space=pl.ANY)] * len(after),
            out_specs=[full(shape.shape) for shape in shapes],
            scratch_shapes=scratch,
        ),
        compiler_params=params(56),
        cost_estimate=cost(15),
        name="scores_grad",
    )(at, *map(array_of, pieces), qkv, probs, relkq, row, col, *extra, *after)


def weight_grads_call(at, wholes, after=(), name="weight_grads"):
    count = 1 << len(wholes[0][1])
    chunk = lanes
    per = 2
    steps = count // per
    half = steps // 2

    def chunk_of(bits, which):
        def index(i, at):
            p = lax.rem(i + half, steps) * per + which
            total = 0
            for place, bit in enumerate(bits):
                total = total + jnp.bitwise_and(jnp.right_shift(p, len(bits) - 1 - place), 1) * bit
            return jnp.bitwise_xor(at[1], total)

        return index

    def kernel(at_ref, *refs):
        refs = list(refs)
        take = lambda number: [refs.pop(0) for _ in range(number)]
        ins = []
        for groups, bits, extra in wholes:
            sides = [(take(len(lefts) * per), take(len(rights))) for lefts, rights, _ in groups]
            ins.append((sides, take(per) if extra is not None else []))
        take(len(after))
        outs = [take(2) for _ in wholes]
        step = pl.program_id(0)
        for (sides, extras), (keep_ref, send_ref) in zip(ins, outs):
            results = []
            for own, right_refs in sides:
                right_all = refs.pop(0)

                @pl.when(step == 0)
                def _(right_refs=right_refs, right_all=right_all):
                    for k, ref in enumerate(right_refs):
                        right_all[k * lanes : (k + 1) * lanes, :] = ref[...]

                left = jnp.concatenate(
                    [
                        jnp.concatenate([own[k + which][...] for which in range(per)], axis=1)
                        for k in range(0, len(own), per)
                    ],
                    axis=0,
                )
                results.append(dot(left, right_all[...], ((0,), (0,))).astype(bf16))
            for target, mine in ((send_ref, step < half), (keep_ref, step >= half)):

                @pl.when(mine)
                def _(target=target, results=results, extras=extras):
                    for which in range(per):
                        first = 0
                        for result in results:
                            end = first + result.shape[1]
                            target[which, :chunk, first:end] = (
                                result[which * chunk : (which + 1) * chunk, :]
                            )
                            first = end
                        if extras:
                            target[which, chunk:, :] = extras[which][...].astype(bf16)

    in_specs, operands, scratch, shapes, out_specs = [], [], [], [], []
    for groups, bits, extra in wholes:
        total_width = sum(width for _, _, width in groups)
        tail = 0 if extra is None else extra.shape[1]
        for lefts, rights, width in groups:
            for handle in lefts:
                for which in range(per):
                    in_specs.append(rows_of(handle, (lanes, chunk), chunk_of(bits, which)))
                    operands.append(array_of(handle))
            for handle in rights:
                column = handle[2] if isinstance(handle, tuple) and len(handle) == 3 else 0
                handle = (
                    handle[:2] if isinstance(handle, tuple) and handle[1] is not None else array_of(handle)
                )
                in_specs.append(rows_of(handle, (lanes, width), lambda i, at, column=column: column))
                operands.append(array_of(handle))
            scratch.append(pltpu.VMEM((len(rights) * lanes, width), bf16))
        for which in range(per if extra is not None else 0):
            index = chunk_of(bits, which)
            in_specs.append(
                pl.BlockSpec(
                    (None, tail, total_width), lambda i, at, index=index: (index(i, at), 0, 0)
                )
            )
            operands.append(extra)
        shapes += [jax.ShapeDtypeStruct((count // 2, chunk + tail, total_width), bf16)] * 2
        block = (per, chunk + tail, total_width)
        out_specs += [
            pl.BlockSpec(block, lambda i, at: (jnp.maximum(i - half, 0), 0, 0)),
            pl.BlockSpec(block, lambda i, at: (jnp.minimum(i, half - 1), 0, 0)),
        ]
    in_specs += [pl.BlockSpec(memory_space=pl.ANY)] * len(after)
    operands += list(after)
    out = pl.pallas_call(
        kernel,
        out_shape=tuple(shapes),
        grid_spec=pltpu.PrefetchScalarGridSpec(
            num_scalar_prefetch=1,
            grid=(steps,),
            in_specs=in_specs,
            out_specs=out_specs,
            scratch_shapes=scratch,
        ),
        compiler_params=params(48),
        cost_estimate=cost(4 * len(wholes)),
        name=name,
    )(at, *operands)
    return [tuple(out[k : k + 2]) for k in range(0, len(out), 2)]


def tokens_grad_kernel(at_ref, d0, d1, d2, d3, resid_ref, wq_ref, wk_ref, wv_ref, *refs):
    out_ref = refs[-1]
    step = pl.program_id(0)
    width = wq_ref.shape[1]

    @pl.when(step == 0)
    def _():
        out_ref[...] = resid_ref[...]

    for t, piece in enumerate((d0, d1, d2, d3)):

        @pl.when(step == t)
        def _(piece=piece):
            total = out_ref[...]
            for at, w_ref in enumerate((wq_ref, wk_ref, wv_ref)):
                total = total + dot(
                    piece[:, at * width : (at + 1) * width], w_ref[...], ((1,), (1,))
                )
            out_ref[...] = total


def tokens_grad_call(at, pieces, resid, w_query, w_key, w_value, after):
    rows, model = resid.shape
    width = model // blocks
    tile = (rows, 3 * width)

    def column(i, at):
        offset = jnp.where(i == 1, 2, jnp.where(i == 2, 1, i))
        return (0, jnp.bitwise_xor(at[0], offset))

    weight = pl.BlockSpec((model, width), column)
    return pl.pallas_call(
        tokens_grad_kernel,
        out_shape=jax.ShapeDtypeStruct((rows, model), f32),
        grid_spec=pltpu.PrefetchScalarGridSpec(
            num_scalar_prefetch=1,
            grid=(blocks,),
            in_specs=[rows_of(piece, tile) for piece in pieces]
            + [full((rows, model)), weight, weight, weight]
            + [pl.BlockSpec(memory_space=pl.ANY)] * len(after),
            out_specs=full((rows, model)),
        ),
        compiler_params=params(40),
        cost_estimate=cost(4),
        name="tokens_grad",
    )(at, *map(array_of, pieces), resid, w_query, w_key, w_value, *after)


def parts_kernel(fields, at_ref, *refs):
    step = pl.program_id(0)
    parts, outs = refs[: blocks * fields], refs[blocks * fields :]
    for field in range(fields):
        for at in range(blocks):

            @pl.when(step == at)
            def _(part=parts[field * blocks + at], out=outs[field]):
                out[...] = part[...].astype(f32)


def parts_call(at, fields, name):
    in_specs, operands, shapes, out_specs = [], [], [], []
    for parts, axis in fields:
        rows, width = parts[0].shape
        in_specs += [full((rows, width))] * blocks
        operands += list(parts)
        shape = (rows * blocks, width) if axis == 0 else (rows, width * blocks)
        shapes.append(jax.ShapeDtypeStruct(shape, f32))

        def index(i, at, axis=axis):
            spot = jnp.bitwise_xor(at[0], i)
            return (spot, 0) if axis == 0 else (0, spot)

        out_specs.append(pl.BlockSpec((rows, width), index))
    return pl.pallas_call(
        functools.partial(parts_kernel, len(fields)),
        out_shape=tuple(shapes),
        grid_spec=pltpu.PrefetchScalarGridSpec(
            num_scalar_prefetch=1, grid=(blocks,), in_specs=in_specs, out_specs=out_specs
        ),
        compiler_params=params(40),
        cost_estimate=cost(2),
        name=name,
    )(at, *operands)


def last_kernel(at_ref, *refs):
    step = pl.program_id(0)
    firsts, seconds, outs = refs[:blocks], refs[blocks : 2 * blocks], refs[2 * blocks : 2 * blocks + 3]
    wout_ref, rel_ref, norm_ref, bin_ref, box_ref = refs[2 * blocks + 3 :]
    for at in range(blocks):

        @pl.when(step == at)
        def _(first=firsts[at], second=seconds[at]):
            for k, out in enumerate(outs):
                span = slice(k * lanes, (k + 1) * lanes)
                out[:, :lanes] = first[:, span].astype(f32)
                out[:, lanes:] = second[:lanes, span].astype(f32)
            wout_ref[...] = first[:, 3 * lanes :].astype(f32)

    @pl.when(step == 0)
    def _():
        total = seconds[0][lanes:, :].astype(f32)
        for second in seconds[1:]:
            total = total + second[lanes:, :].astype(f32)
        rows = rel_ref.shape[0]
        width = total.shape[1]
        for k in range(3):
            end = min((k + 1) * width, rel_ref.shape[1])
            rel_ref[:, k * width : end] = total[k * rows : (k + 1) * rows, : end - k * width]
        rest = total[2 * rows :, width - lanes :]
        norm_ref[...] = rest[:4]
        bin_ref[...] = rest[4:8]
        box_ref[...] = rest[8:16]


def last_call(at, firsts, seconds, buckets, model):
    wide = jax.ShapeDtypeStruct((lanes, model), f32)
    column = pl.BlockSpec((lanes, model // blocks), lambda i, at: (0, jnp.bitwise_xor(at[0], i)))
    return pl.pallas_call(
        last_kernel,
        out_shape=(wide, wide, wide, wide)
        + tuple(jax.ShapeDtypeStruct(shape, f32) for shape in ((buckets, model), (4, lanes), (4, lanes), (8, lanes))),
        grid_spec=pltpu.PrefetchScalarGridSpec(
            num_scalar_prefetch=1,
            grid=(blocks,),
            in_specs=[full(part.shape) for part in firsts + seconds],
            out_specs=[column] * 4 + [full((buckets, model)), full((4, lanes)), full((4, lanes)), full((8, lanes))],
        ),
        compiler_params=params(40),
        cost_estimate=cost(2),
        name="last",
    )(at, *firsts, *seconds)


class Halving:
    def __init__(self, halves, bits):
        self.keep, self.send = halves
        self.bits = list(bits)
        self.step()

    def step(self):
        self.came = swap(self.send, "docs", self.bits.pop(0))

    def add(self, *before):
        keep, came = self.keep, self.came
        if before:
            came = ordered(came, *before)
        total = lambda part: (keep[part].astype(f32) + came[part].astype(f32)).astype(bf16)
        if not self.bits:
            self.keep = self.send = total(slice(None))[0]
            return self.keep
        middle = keep.shape[0] // 2
        self.send = total(slice(middle, None))
        self.keep = total(slice(0, middle))
        sent = self.send
        self.step()
        return sent


def shards_tiles(
    tokens, lengths, positions, token_boxes, ln1_gain, ln1_bias, w_query, w_key, w_value, w_out,
    rel_table, xbias_table, ybias_table, ln2_gain, ln2_bias, w_in, b_in, w_down, cotangent,
):
    row_count, model = tokens.shape[1:]
    docs = lax.axis_size("docs")
    place = lax.axis_index("blk")
    doc_place = lax.axis_index("docs")
    heads = xbias_table.shape[1]
    boxes = xbias_table.shape[0]
    units = w_in.shape[1]
    width = model // blocks
    bits = bits_of(docs)
    other = [bits[1], bits[0]] + bits[2:]
    x_own = tokens[0]

    x_far = swap(x_own, "blk", 2)
    own_ints = jnp.concatenate(
        [
            positions,
            jnp.right_shift(token_boxes[0] + token_boxes[2], 1),
            jnp.right_shift(token_boxes[1] + token_boxes[3], 1),
            jnp.zeros((5, row_count), jnp.int32),
        ],
        axis=0,
    )
    ints_far = swap(own_ints, "blk", 2)
    x_core, ints_core = swap(x_own, "blk", 1), swap(own_ints, "blk", 1)
    x_both, ints_both = swap(ordered(x_far, ints_far), "blk", 1), swap(ints_far, "blk", 1)
    xs = (x_own, x_far, x_core, x_both)
    tables = jnp.concatenate([xbias_table.T, ybias_table.T], axis=1).astype(f32)
    tables = tables.reshape(blocks, heads // blocks, 2 * boxes)
    at = jnp.stack([place.astype(jnp.int32), lengths[0]])
    spot = jnp.stack([place, doc_place]).astype(jnp.int32)
    att_own, att_core, att_far, probs, qkv, relkq, row, col = scores_call(
        at, xs, (own_ints, ints_far, ints_core, ints_both), w_query, w_key, w_value, rel_table, tables
    )

    came_far = swap(att_far, "blk", 2)
    came_core = swap(att_core, "blk", 1)
    came_both = swap(came_far, "blk", 1)
    line = lambda vector: vector.reshape(1, -1)
    far1, core1, act_own, act, slope, normed1, inverse1, attended = up_call(
        spot, (att_own, (came_far, 0), came_core, (came_both, 1)), x_own, w_out,
        line(ln1_gain), line(ln1_bias), w_in, line(b_in), docs,
    )
    got_far1 = swap(far1, "blk", 2)
    block_out, mix, grad_ffn, above = down_call(
        act, w_down, normed1, cotangent[0],
        line(ln1_gain), line(ln1_bias), line(ln2_gain), line(ln2_bias), units // docs,
    )
    (
        ga_own, ga_core, ga_far, grad_resid, up_far, up_core, up_own, far3, core3, gattn_own, sums,
    ) = back_call(
        spot, w_down, slope, w_in, w_out, normed1, inverse1, mix, grad_ffn, attended,
        line(ln1_gain), above, units // docs,
    )
    came_far = swap(ordered(ga_far, got_far1), "blk", 2)
    came_core = swap(ga_core, "blk", 1)
    came_both = swap(came_far, "blk", 1)
    ga_all = (ga_own, (came_far, 0), came_core, (came_both, 1))
    got_far2 = swap(ordered(up_far, came_far), "blk", 2)
    first_grads, first_boxes = scores_grad_call(
        0, spot, ga_all, qkv, probs, relkq, row, col, []
    )

    got_core1, got_both1 = swap(core1, "blk", 1), swap(ordered(got_far1, came_far), "blk", 1)
    got_core2, got_both2 = swap(up_core, "blk", 1), swap(ordered(got_far2, first_grads), "blk", 1)
    got_far3 = swap(ordered(far3, got_far2), "blk", 2)
    hidden_all = [(far1, 0), (got_far1, 0), (got_core1, 0), (got_both1, 0)]
    act_all = [act_own, (got_far1, 1), (got_core1, 1), (got_both1, 2)]
    gffn_all = [grad_ffn, (got_far2, 0), (got_core2, 0), (got_both2, 0)]
    up_all = [up_own, (got_far2, 1), (got_core2, 1), (got_both2, 2)]
    down_halves, in_halves = weight_grads_call(
        spot,
        [([(act_all, gffn_all, model)], bits, None), ([(hidden_all, up_all, model)], other, None)],
        after=[first_grads], name="grad_down_in",
    )
    down_sum, in_sum = Halving(down_halves, bits), Halving(in_halves, other)
    lefts = list(xs) + [rel_table]

    def rows_by_piece(grads):
        return [(grads.reshape(blocks + 1, lanes, -1), t) for t in range(blocks + 1)]

    got_core3, got_both3 = swap(core3, "blk", 1), swap(ordered(got_far3, in_halves[0]), "blk", 1)
    att_all = [far3, got_far3, got_core3, got_both3]
    per = model // width
    gattn_all = [
        gattn_own, (got_far3, None, per), (got_core3, None, per), (got_both3, None, per + 1),
    ]
    first_groups = [(lefts, rows_by_piece(first_grads), 3 * width // 2), (att_all, gattn_all, width)]
    (first_halves,) = weight_grads_call(
        spot, [(first_groups, other, None)], after=[in_halves[0]], name="grad_qkv_out"
    )
    first_sum = Halving(first_halves, other)
    second_grads, dq_own, dq_core, dq_far, small = scores_grad_call(
        1, spot, ga_all, qkv, probs, relkq, row, col, [first_halves[0]], docs,
        (w_query, w_key, sums, first_grads, first_boxes),
    )
    done = down_sum.add(second_grads)
    done = in_sum.add(done)
    second_groups = [(lefts, rows_by_piece(second_grads), 3 * width // 2)]
    (second_halves,) = weight_grads_call(
        spot, [(second_groups, bits, small)], after=[done], name="grad_qkv"
    )
    second_sum = Halving(second_halves, bits)
    dq_far_got = ordered(swap(dq_far, "blk", 2), second_halves[0])
    dq_core_got, dq_both_got = swap(dq_core, "blk", 1), swap(dq_far_got, "blk", 1)
    grad_tokens = tokens_grad_call(
        spot, (dq_own, (dq_far_got, 0), dq_core_got, (dq_both_got, 1)), grad_resid,
        w_query, w_key, w_value, [second_halves[0]],
    )

    def whole(part):
        far = swap(part, "blk", 2)
        return [part, swap(part, "blk", 1), far, far]

    def both(parts, *before):
        far = ordered(parts[2], *before)
        return (parts[0], parts[1], far, swap(far, "blk", 1))

    done = down_sum.add(grad_tokens)
    done = in_sum.add(done)
    done = second_sum.add(done)
    done = first_sum.add(done)
    done = down_sum.add(done)
    down_all = whole(done)
    done = second_sum.add(done)
    done = in_sum.add(done)
    in_all = whole(done)
    done = first_sum.add(done)
    done = second_sum.add(done)
    second_all = whole(done)
    done = first_sum.add(done)
    first_all = whole(done)
    down_all, in_all = both(down_all, done), both(in_all, done)
    second_all, first_all = both(second_all, done), both(first_all, done)
    grad_w_down, grad_w_in = parts_call(
        spot, ((down_all, 0), (in_all, 1)), "gather_parts"
    )
    *grads, grad_w_out, rel_out, norms, b_in_out, both_boxes = last_call(
        spot, first_all, second_all, rel_table.shape[0] // docs, model
    )
    b_in_out = b_in_out.reshape(-1)
    xb, yb = both_boxes[:, :heads], both_boxes[:, 64 : 64 + heads]
    return (
        block_out[None], grad_tokens[None], norms[0], norms[1], grads[0], grads[1], grads[2], grad_w_out,
        rel_out, xb, yb, norms[2], norms[3], grad_w_in, b_in_out, grad_w_down,
    )


def choose(*args):
    docs, parts = lax.axis_size("docs"), lax.axis_size("blk")
    tokens, w_in = args[0], args[15]
    model, units = w_in.shape
    fits = (
        parts == blocks
        and tokens.shape[1] == lanes
        and model // docs == lanes
        and units // docs == parts * lanes
        and docs & (docs - 1) == 0
        and docs > 2
        and units == blocks * model
    )
    return (shards_tiles if fits else shards)(*args)


def solution(mesh):
    rows = P("docs", "blk", None)
    placed = (
        rows, P("docs"), P("docs", "blk"), P(None, "docs", "blk"),
        *([P()] * 14), rows,
    )
    over_docs, over_docs2 = P("docs"), P("docs", None)
    return jax.shard_map(
        choose,
        mesh=mesh,
        in_specs=placed,
        out_specs=(
            rows, rows, over_docs, over_docs, over_docs2, over_docs2, over_docs2, over_docs2,
            over_docs2, over_docs2, over_docs2, over_docs, over_docs, over_docs2, over_docs, over_docs2,
        ),
        check_vma=False,
    )
```

```python
import functools
import math

import jax
import jax.numpy as jnp
from jax import lax
from jax.experimental import pallas as pl
from jax.experimental.pallas import tpu as pltpu
from jax.sharding import PartitionSpec as P

norm_eps = 1e-05
mask_value = -1e30
f32 = jnp.float32
bf16 = jnp.bfloat16
lanes = 128


def dot(a, b, contract=((1,), (0,))):
    return lax.dot_general(a, b, (contract, ((), ())), preferred_element_type=f32)


def pick(table, index):
    return jnp.take_along_axis(table, index, axis=1, mode="promise_in_bounds")


def ahead_of(first, second):
    return jnp.clip(first - second, -64, 63) + 64


def attn_fwd_kernel(
    place, x_ref, wq_ref, wk_ref, wv_ref, rel_ref, tab_ref, row_ref, col_ref,
    att_ref, probs_ref, qkv_ref, relkq_ref, key_rel,
):
    scale = 1.0 / math.sqrt(192.0)
    step = pl.program_id(0)
    rows = x_ref.shape[0]
    width = wq_ref.shape[1]
    heads = tab_ref.shape[1]
    size = width // heads
    tiles = rows // lanes

    @pl.when(step == 0)
    def _():
        for at, w_ref in enumerate((wq_ref, wk_ref, wv_ref)):
            for t in range(tiles):
                qkv_ref[t * lanes : (t + 1) * lanes, at * width : (at + 1) * width] = dot(
                    x_ref[t * lanes : (t + 1) * lanes, :], w_ref[...]
                ).astype(bf16)
        relkq_ref[:, :width] = dot(rel_ref[...], wk_ref[...]).astype(bf16)
        relkq_ref[:, width:] = dot(rel_ref[...], wq_ref[...]).astype(bf16)
        for h in range(heads):
            key_rel[h] = (
                dot(
                    qkv_ref[:, width + h * size : width + (h + 1) * size],
                    relkq_ref[:, width + h * size : width + (h + 1) * size],
                    ((1,), (1,)),
                )
                .astype(bf16)
                .astype(f32)
            )

    here = pl.ds(pl.multiple_of(step * lanes, lanes), lanes)
    pos_i = col_ref[here, 0:1]
    cx_i = col_ref[here, 1:2]
    cy_i = col_ref[here, 2:3]
    own_row = row_ref[0:1, here]
    ahead, mirror, across, vertical = [], [], [], []
    for t in range(tiles):
        span = slice(t * lanes, (t + 1) * lanes)
        ahead.append(ahead_of(pos_i, row_ref[0:1, span]))
        mirror.append(ahead_of(col_ref[span, 0:1], own_row))
        across.append(jnp.clip(jnp.right_shift(cx_i - row_ref[1:2, span], 5), -32, 31) + 32)
        vertical.append(jnp.clip(jnp.right_shift(cy_i - row_ref[2:3, span], 5), -32, 31) + 96)
    valid = row_ref[3:4, :] > 0
    for h in range(heads):
        cols = slice(h * size, (h + 1) * size)
        query = qkv_ref[here, cols]
        rel_scores = (
            dot(query, relkq_ref[:, cols], ((1,), (1,))).astype(bf16).astype(f32)
        )
        table = jnp.broadcast_to(tab_ref[0, h : h + 1, :], (lanes, lanes))
        pieces = []
        for t in range(tiles):
            span = slice(t * lanes, (t + 1) * lanes)
            content = dot(
                query, qkv_ref[span, width + h * size : width + (h + 1) * size], ((1,), (1,))
            )
            mirrored = pick(key_rel[h, span, :], mirror[t]).T
            bias = pick(table, across[t]) + pick(table, vertical[t])
            pieces.append(
                scale * (content + pick(rel_scores, ahead[t]) + mirrored) + bias
            )
        scores = jnp.where(valid, jnp.concatenate(pieces, axis=1), mask_value)
        top = jnp.max(scores, axis=1, keepdims=True)
        raised = jnp.exp(scores - top)
        probs = (raised * (1.0 / jnp.sum(raised, axis=1, keepdims=True))).astype(bf16)
        probs_ref[h] = probs
        att_ref[:, cols] = dot(
            probs, qkv_ref[:, 2 * width + h * size : 2 * width + (h + 1) * size]
        ).astype(bf16)


def attn_fwd(place, x_all, w_query, w_key, w_value, rel_table, tables, ints_row, ints_col):
    rows, model = x_all.shape
    parts, heads, _ = tables.shape
    width = w_query.shape[1] // parts
    tiles = rows // lanes
    buckets = rel_table.shape[0]
    whole = lambda *shape: pl.BlockSpec(shape, lambda i, at: (0,) * len(shape))
    column = pl.BlockSpec((model, width), lambda i, at: (0, at[0]))
    return pl.pallas_call(
        attn_fwd_kernel,
        out_shape=(
            jax.ShapeDtypeStruct((rows, width), bf16),
            jax.ShapeDtypeStruct((heads, rows, rows), bf16),
            jax.ShapeDtypeStruct((rows, 3 * width), bf16),
            jax.ShapeDtypeStruct((buckets, 2 * width), bf16),
        ),
        grid_spec=pltpu.PrefetchScalarGridSpec(
            num_scalar_prefetch=1,
            grid=(tiles,),
            in_specs=[
                whole(rows, model),
                column,
                column,
                column,
                whole(buckets, model),
                pl.BlockSpec((1, heads, lanes), lambda i, at: (at[0], 0, 0)),
                whole(8, rows),
                whole(rows, 8),
            ],
            out_specs=[
                pl.BlockSpec((lanes, width), lambda i, at: (i, 0)),
                pl.BlockSpec((heads, lanes, rows), lambda i, at: (0, i, 0)),
                whole(rows, 3 * width),
                whole(buckets, 2 * width),
            ],
            scratch_shapes=[pltpu.VMEM((heads, rows, lanes), f32)],
        ),
        compiler_params=pltpu.CompilerParams(vmem_limit_bytes=40 << 20),
        cost_estimate=pl.CostEstimate(
            flops=6 * 10**9, transcendentals=10**6, bytes_accessed=8 << 20
        ),
        name="attn_fwd",
    )(place, x_all, w_query, w_key, w_value, rel_table, tables, ints_row, ints_col)


def attn_bwd_kernel(
    ga_ref, qkv_ref, probs_ref, relkq_ref, row_ref, col_ref,
    dqkv_ref, drel_ref, boxes_ref, ds_ref,
):
    scale = 1.0 / math.sqrt(192.0)
    rows = ga_ref.shape[0]
    heads = probs_ref.shape[0]
    width = ga_ref.shape[1]
    size = width // heads
    tiles = rows // lanes
    span_width = 3 * lanes
    drel_ref[...] = jnp.zeros_like(drel_ref)
    boxes_ref[...] = jnp.zeros_like(boxes_ref)
    window = lax.broadcasted_iota(jnp.int32, (rows, span_width), 1)
    bucket = lax.broadcasted_iota(jnp.int32, (lanes, lanes), 1)
    label = lax.broadcasted_iota(jnp.int32, (rows, lanes), 1)
    all_pos = col_ref[:, 0:1]
    all_x, all_y = col_ref[:, 1:2], col_ref[:, 2:3]
    sector_x, sector_y = jnp.right_shift(all_x, 5), jnp.right_shift(all_y, 5)
    hot_x = (label == sector_x).astype(bf16)
    hot_y = (label == sector_y + 64).astype(bf16)
    hot_both = ((label == sector_x) | (label == sector_y + 64)).astype(bf16)

    def histogram(sums, total, at, base_row):
        first = at - base_row + (2 * lanes // 2 - 1) - bucket
        low = jnp.bitwise_and(first, lanes - 1)
        group = jnp.right_shift(first, 7)
        found = jnp.where(
            group == 0,
            pick(sums[:, :lanes], low),
            jnp.where(
                group == 1,
                pick(sums[:, lanes : 2 * lanes], low),
                pick(sums[:, 2 * lanes :], low),
            ),
        )
        found = jnp.where(bucket == 0, total, found)
        later = jnp.where(bucket == lanes - 1, 0.0, pltpu.roll(found, lanes - 1, 1))
        return found - later

    def by_rows(ib, carry):
        here = pl.ds(pl.multiple_of(ib * lanes, lanes), lanes)
        pos_i = col_ref[here, 0:1]
        cx_i, cy_i = col_ref[here, 1:2], col_ref[here, 2:3]
        base = jnp.min(pos_i, axis=0, keepdims=True)
        below = (all_pos <= base - 63 + window).astype(bf16)
        short_x = jnp.bitwise_and(cx_i, 31) < jnp.bitwise_and(row_ref[1:2, :], 31)
        short_y = jnp.bitwise_and(cy_i, 31) < jnp.bitwise_and(row_ref[2:3, :], 31)
        step_x = jnp.right_shift(cx_i, 5) + 32 - bucket
        step_y = jnp.right_shift(cy_i, 5) + 32 - (bucket - 64)
        in_x = (bucket < 64) & (step_x >= 0) & (step_x < 32)
        in_y = (bucket >= 64) & (step_y >= 0) & (step_y < 32)
        seek = jnp.where(in_x, step_x, jnp.where(in_y, step_y + 64, 0))
        inside = in_x | in_y
        for h in range(heads):
            cols = slice(h * size, (h + 1) * size)
            kcols = slice(width + h * size, width + (h + 1) * size)
            vcols = slice(2 * width + h * size, 2 * width + (h + 1) * size)
            probs = probs_ref[h, here, :].astype(f32)
            gained = dot(ga_ref[here, cols], qkv_ref[:, vcols], ((1,), (1,)))
            row_dots = jnp.sum(probs * gained, axis=1, keepdims=True)
            grad32 = probs * (gained - row_dots)
            grad = grad32.astype(bf16)
            ds_ref[h, here, :] = grad
            exact = grad.astype(f32)
            total = jnp.sum(exact, axis=1, keepdims=True)
            rel = histogram(dot(grad, below), total, pos_i, base)
            rel = (scale * rel).astype(bf16)
            query = qkv_ref[here, cols]
            dqkv_ref[here, cols] = (
                scale * dot(grad, qkv_ref[:, kcols]) + dot(rel, relkq_ref[:, cols])
            ).astype(bf16)
            drel_ref[:, cols] += dot(rel, query, ((0,), (0,)))
            grad_x = jnp.where(short_x, exact, 0.0).astype(bf16)
            grad_y = jnp.where(short_y, exact, 0.0).astype(bf16)
            plain = dot(grad, hot_both)
            less = dot(grad_x, hot_x) + dot(grad_y, hot_y)
            plain = jnp.where(inside, pick(plain, seek), 0.0)
            less = jnp.where(inside, pick(less, seek), 0.0)
            boxes_ref[2 * h : 2 * h + 1, :] += jnp.sum(plain, axis=0, keepdims=True)
            boxes_ref[2 * h + 1 : 2 * h + 2, :] += jnp.sum(less, axis=0, keepdims=True)
        return carry

    lax.fori_loop(0, tiles, by_rows, 0)

    def by_columns(jb, carry):
        here = pl.ds(pl.multiple_of(jb * lanes, lanes), lanes)
        pos_j = col_ref[here, 0:1]
        base = jnp.min(pos_j, axis=0, keepdims=True)
        below = (all_pos <= base - 63 + window).astype(bf16)
        for h in range(heads):
            cols = slice(h * size, (h + 1) * size)
            kcols = slice(width + h * size, width + (h + 1) * size)
            vcols = slice(2 * width + h * size, 2 * width + (h + 1) * size)
            grad = ds_ref[h, :, here]
            total = dot(grad, jnp.ones((rows, lanes), bf16), ((0,), (0,)))
            sums = dot(grad, below, ((0,), (0,)))
            mirror = (scale * histogram(sums, total, pos_j, base)).astype(bf16)
            dqkv_ref[here, kcols] = (
                scale * dot(grad, qkv_ref[:, cols], ((0,), (0,)))
                + dot(mirror, relkq_ref[:, kcols])
            ).astype(bf16)
            drel_ref[:, kcols] += dot(mirror, qkv_ref[here, kcols], ((0,), (0,)))
            dqkv_ref[here, vcols] = dot(
                probs_ref[h, :, here], ga_ref[:, cols], ((0,), (0,))
            ).astype(bf16)
        return carry

    lax.fori_loop(0, tiles, by_columns, 0)


def attn_bwd(grad_att, qkv, probs, relkq, ints_row, ints_col):
    rows, width = grad_att.shape
    heads = probs.shape[0]
    buckets = relkq.shape[0]
    inside = pl.BlockSpec(memory_space=pltpu.VMEM)
    return pl.pallas_call(
        attn_bwd_kernel,
        out_shape=(
            jax.ShapeDtypeStruct((rows, 3 * width), bf16),
            jax.ShapeDtypeStruct((buckets, 2 * width), f32),
            jax.ShapeDtypeStruct((2 * heads, lanes), f32),
        ),
        in_specs=[inside] * 6,
        out_specs=[inside] * 3,
        scratch_shapes=[pltpu.VMEM((heads, rows, rows), bf16)],
        compiler_params=pltpu.CompilerParams(vmem_limit_bytes=40 << 20),
        cost_estimate=pl.CostEstimate(
            flops=12 * 10**9, transcendentals=0, bytes_accessed=6 << 20
        ),
        name="attn_bwd",
    )(grad_att, qkv, probs, relkq, ints_row, ints_col)


def layer_norm(inputs, gain_vec, bias_vec):
    row_mean = jnp.mean(inputs, axis=-1, keepdims=True)
    centered = inputs - row_mean
    inverse = lax.rsqrt(jnp.mean(centered * centered, axis=-1, keepdims=True) + norm_eps)
    normed = centered * inverse
    return (normed * gain_vec + bias_vec, normed, inverse)


def norm_backward(grad_in, normed, inverse, gain_vec):
    grad_gain = jnp.sum(grad_in * normed, axis=0)
    grad_shift = jnp.sum(grad_in, axis=0)
    scaled = grad_in * gain_vec
    grad_input = inverse * (
        scaled
        - jnp.mean(scaled, axis=-1, keepdims=True)
        - normed * jnp.mean(scaled * normed, axis=-1, keepdims=True)
    )
    return (grad_input, grad_gain, grad_shift)


def bits_of(count):
    assert count & (count - 1) == 0
    return [1 << at for at in range(count.bit_length() - 1)]


def swap(array, axis, by):
    count = lax.axis_size(axis)
    return lax.ppermute(array, axis, [(i, i ^ by) for i in range(count)])


def offsets(count):
    order = [0]
    for bit in reversed(bits_of(count)):
        order = order + [at ^ bit for at in order]
    return order


def spread(shared, pieces):
    count = lax.axis_size("blk")
    got = {0: shared} if shared is not None else {}
    held = {(0, at): piece for at, piece in pieces.items()} if pieces else {}
    for bit in reversed(bits_of(count)):
        out_keys = [key for key in sorted(held) if key[1] & bit]
        out_shared = sorted(got)
        parts = [got[at] for at in out_shared] + [held[key] for key in out_keys]
        if bit == 1:
            came = [swap(part, "blk", bit) for part in parts]
        else:
            came = swap(jnp.concatenate(parts, axis=1), "blk", bit)
            edges = [0]
            for part in parts:
                edges.append(edges[-1] + part.shape[1])
            came = [came[:, a:b] for a, b in zip(edges[:-1], edges[1:])]
        for at, part in zip(out_shared, came):
            got[at ^ bit] = part
        for key, part in zip(out_keys, came[len(out_shared) :]):
            del held[key]
            held[(key[0] ^ bit, key[1] ^ bit)] = part
    return got, {key[0]: part for key, part in held.items()}


def by_place(stacked, place):
    count = len(stacked)
    for bit in bits_of(count):
        turned = (place & bit) != 0
        stacked = [jnp.where(turned, stacked[at ^ bit], stacked[at]) for at in range(count)]
    return stacked


def chunk_order(count):
    order = [0]
    for bit in reversed(bits_of(count)):
        order = order + [at | bit for at in order]
    return order


def for_docs(chunks, doc_place):
    moved = by_place(chunks, doc_place)
    return [moved[at] for at in chunk_order(len(chunks))]


def halve(keep, send, bits):
    count = lax.axis_size("docs")
    first = True
    current = keep
    for bit in bits:
        if not first:
            half = current.shape[0] // 2
            current, send = current[:half], current[half:]
        first = False
        came = swap(send, "docs", bit)
        current = (current.astype(f32) + came.astype(f32)).astype(bf16)
    return current


def shards(
    tokens, lengths, positions, token_boxes, ln1_gain, ln1_bias, w_query, w_key, w_value, w_out,
    rel_table, xbias_table, ybias_table, ln2_gain, ln2_bias, w_in, b_in, w_down, cotangent,
):
    doc_count, row_count, model = tokens.shape
    assert doc_count == 1 and row_count == lanes
    parts = lax.axis_size("blk")
    docs = lax.axis_size("docs")
    place = lax.axis_index("blk")
    doc_place = lax.axis_index("docs")
    heads = xbias_table.shape[1]
    own_heads = heads // parts
    width = model // parts
    buckets = rel_table.shape[0]
    boxes = xbias_table.shape[0]
    hidden_units = w_in.shape[1]
    order = offsets(parts)
    x_own = tokens[0]

    centers_x = jnp.right_shift(token_boxes[0] + token_boxes[2], 1)
    centers_y = jnp.right_shift(token_boxes[1] + token_boxes[3], 1)
    own_ints = jnp.concatenate([positions, centers_x, centers_y], axis=0)
    coded = jnp.concatenate(
        [jnp.right_shift(own_ints, 5), jnp.bitwise_and(own_ints, 31)], axis=0
    ).astype(bf16)
    coded = jnp.pad(coded.reshape(1, -1), ((0, 7), (0, model - coded.size)))
    got, _ = spread(jnp.concatenate([x_own, coded], axis=0), None)
    x_all = jnp.concatenate([got[at][:row_count] for at in order], axis=0)
    decoded = jnp.concatenate(
        [got[at][row_count : row_count + 1, : 6 * row_count].reshape(6, row_count) for at in order], axis=1
    ).astype(jnp.int32)
    ints = decoded[:3] * 32 + decoded[3:]
    slot_ids = jnp.concatenate(
        [
            (place ^ at) * row_count + lax.broadcasted_iota(jnp.int32, (1, row_count), 1)
            for at in order
        ],
        axis=1,
    )
    ints = jnp.concatenate(
        [ints, (slot_ids < lengths[0]).astype(jnp.int32), jnp.zeros((4, ints.shape[1]), jnp.int32)],
        axis=0,
    )
    ints_col = ints.T
    tables = jnp.concatenate([xbias_table.T, ybias_table.T], axis=1).astype(f32)
    tables = tables.reshape(parts, own_heads, 2 * boxes)

    attended_own, probs, qkv, relkq = attn_fwd(
        place.reshape(1), x_all, w_query, w_key, w_value, rel_table, tables, ints, ints_col
    )

    def row_block(array, at):
        t = order.index(at)
        return array[t * row_count : (t + 1) * row_count]

    _, came = spread(None, {at: row_block(attended_own, at) for at in order})
    attended = jnp.concatenate(by_place([came[at] for at in range(parts)], place), axis=1)
    attn_out = jnp.dot(attended, w_out, preferred_element_type=f32)
    hidden, normed1, inverse1 = layer_norm(x_own.astype(f32) + attn_out, ln1_gain, ln1_bias)
    hidden_low = hidden.astype(bf16)
    up_proj = jnp.dot(hidden_low, w_in, preferred_element_type=f32) + b_in
    activated, gelu_back = jax.vjp(lambda inputs: jax.nn.gelu(inputs, approximate=True), up_proj)
    activated_low = activated.astype(bf16)
    ffn_out = jnp.dot(activated_low, w_down, preferred_element_type=f32)
    normed_out, normed2, inverse2 = layer_norm(hidden + ffn_out, ln2_gain, ln2_bias)
    block_out = normed_out.astype(bf16)[None]
    grad_output = cotangent[0].astype(f32)
    grad_mix, grad_ln2_gain, grad_ln2_bias = norm_backward(grad_output, normed2, inverse2, ln2_gain)
    grad_ffn = grad_mix.astype(bf16)
    grad_act = jnp.dot(grad_ffn, w_down.T, preferred_element_type=f32)
    grad_up = gelu_back(grad_act)[0].astype(bf16)
    grad_b_in = jnp.sum(grad_up, axis=0, dtype=f32)
    grad_hidden = grad_mix + jnp.dot(grad_up, w_in.T, preferred_element_type=f32)
    grad_resid, grad_ln1_gain, grad_ln1_bias = norm_backward(
        grad_hidden, normed1, inverse1, ln1_gain
    )
    grad_attn = grad_resid.astype(bf16)
    grad_att = jnp.dot(grad_attn, w_out.T, preferred_element_type=f32).astype(bf16)

    def column_block(array, at, count):
        size = array.shape[1] // count
        return lax.dynamic_slice_in_dim(array, at * size, size, axis=1)

    _, came = spread(None, {at: column_block(grad_att, place ^ at, parts) for at in order})
    grad_att_own = jnp.concatenate([came[at] for at in order], axis=0)
    dqkv, drel, box_sums = attn_bwd(grad_att_own, qkv, probs, relkq, ints, ints_col)

    def docs_columns(array):
        size = array.shape[1] // docs
        chunks = [array[:, at * size : (at + 1) * size] for at in range(docs)]
        return jnp.concatenate(for_docs(chunks, doc_place), axis=1)

    strips = activated_low.reshape(row_count, docs, parts, -1)
    strips = [
        docs_columns(
            lax.dynamic_index_in_dim(strips, place ^ at, axis=2, keepdims=False).reshape(row_count, -1)
        )
        for at in range(parts)
    ]
    got, came = spread(docs_columns(hidden_low), dict(enumerate(strips)))
    hidden_all = jnp.concatenate([got[at] for at in order], axis=0)
    activated_all = jnp.concatenate([came[at] for at in order], axis=0)
    got, came = spread(grad_ffn, {at: column_block(grad_up, place ^ at, parts) for at in order})
    grad_ffn_all = jnp.concatenate([got[at] for at in order], axis=0)
    grad_up_all = jnp.concatenate([came[at] for at in order], axis=0)
    got, came = spread(
        docs_columns(attended), {at: column_block(grad_attn, place ^ at, parts) for at in order}
    )
    attended_all = jnp.concatenate([got[at] for at in order], axis=0)
    grad_attn_all = jnp.concatenate([came[at] for at in order], axis=0)

    def halves(left, right):
        middle = left.shape[1] // 2
        send = dot(left[:, middle:], right, ((0,), (0,))).astype(bf16)
        keep = dot(left[:, :middle], right, ((0,), (0,))).astype(bf16)
        return keep, send

    bits = bits_of(docs)
    down_part = halve(*halves(activated_all, grad_ffn_all), bits)
    in_part = halve(*halves(hidden_all, grad_up_all), bits)
    out_part = halve(*halves(attended_all, grad_attn_all), bits)

    drel_low = drel.astype(bf16)
    left = docs_columns(jnp.concatenate([x_all, rel_table], axis=0))
    right = jnp.concatenate(
        [
            dqkv,
            jnp.concatenate(
                [drel_low[:, width:], drel_low[:, :width], jnp.zeros((buckets, width), bf16)], axis=1
            ),
        ],
        axis=0,
    )
    grad_rel_table = dot(
        drel_low[:, :width], column_block(w_key, place, parts), ((1,), (1,))
    ) + dot(drel_low[:, width:], column_block(w_query, place, parts), ((1,), (1,)))
    plain, less = box_sums[0::2], box_sums[1::2]

    def box_grad(at):
        plain_here, less_here = plain[:, at : at + boxes], less[:, at : at + boxes]
        later = jnp.pad(less_here[:, 1:], ((0, 0), (0, 1)))
        grad = (plain_here - less_here + later).T
        return lax.dynamic_update_slice(jnp.zeros((boxes, heads), f32), grad, (0, place * own_heads))

    small = jnp.concatenate(
        [
            grad_rel_table.reshape(docs, -1),
            grad_ln1_gain.reshape(docs, -1),
            grad_ln1_bias.reshape(docs, -1),
            grad_ln2_gain.reshape(docs, -1),
            grad_ln2_bias.reshape(docs, -1),
            grad_b_in.reshape(docs, -1),
            box_grad(0).reshape(docs, -1),
            box_grad(boxes).reshape(docs, -1),
        ],
        axis=1,
    ).astype(bf16)
    small_width = small.shape[1]
    across = 3 * width
    small = jnp.pad(small, ((0, 0), (0, -small_width % (8 * across))))
    small = for_docs([small[at] for at in range(docs)], doc_place)
    small = jnp.stack(small).reshape(docs, -1, across)
    keep, send = halves(left, right)
    middle = docs // 2
    chunk_rows = model // docs

    def with_small(main, extra):
        main = main.reshape(middle, chunk_rows, across)
        return jnp.concatenate([main, extra], axis=1).reshape(-1, across)

    qkv_part = halve(with_small(keep, small[:middle]), with_small(send, small[middle:]), bits)

    _, came = spread(None, {at: row_block(dqkv, at) for at in order})
    came = by_place([came[at] for at in range(parts)], place)
    grad_tokens = grad_resid
    for at, weight in enumerate((w_query, w_key, w_value)):
        grad = jnp.concatenate([rows[:, at * width : (at + 1) * width] for rows in came], axis=1)
        grad_tokens = grad_tokens + dot(grad, weight, ((1,), (1,)))

    def whole(part):
        got, _ = spread(part, None)
        return by_place([got[at] for at in range(parts)], place)

    grad_w_down = jnp.concatenate(whole(down_part), axis=0).astype(f32)
    grad_w_in = jnp.concatenate(whole(in_part), axis=1).astype(f32)
    grad_w_out = jnp.concatenate(whole(out_part), axis=1).astype(f32)
    pieces = whole(qkv_part)
    grads = [
        jnp.concatenate(
            [piece[:chunk_rows, at * width : (at + 1) * width] for piece in pieces], axis=1
        ).astype(f32)
        for at in range(3)
    ]
    total = sum(piece[chunk_rows:].astype(f32) for piece in pieces).reshape(-1)
    sizes = [
        (buckets // docs, model),
        (model // docs,),
        (model // docs,),
        (model // docs,),
        (model // docs,),
        (hidden_units // docs,),
        (boxes // docs, heads),
        (boxes // docs, heads),
    ]
    small_out = []
    start = 0
    for size in sizes:
        small_out.append(total[start : start + math.prod(size)].reshape(size))
        start += math.prod(size)
    rel_out, ln1g, ln1b, ln2g, ln2b, b_in_out, xb, yb = small_out
    return (
        block_out, grad_tokens[None], ln1g, ln1b, grads[0], grads[1], grads[2], grad_w_out,
        rel_out, xb, yb, ln2g, ln2b, grad_w_in, b_in_out, grad_w_down,
    )


blocks = 4
slots = (0, 2, 1, 3)


def rows_of(handle, tile=None, column=None):
    array, lead = handle if isinstance(handle, tuple) else (handle, None)
    shape = array.shape[-2:] if tile is None else tile
    column = column or (lambda *grid: 0)
    if lead is None:
        return pl.BlockSpec(shape, lambda *grid: (0, column(*grid)))
    return pl.BlockSpec((None,) + shape, lambda *grid: (lead, 0, column(*grid)))


def array_of(handle):
    return handle[0] if isinstance(handle, tuple) else handle


def full(shape):
    return pl.BlockSpec(shape, lambda *grid: (0,) * len(shape))


def cost(us):
    return pl.CostEstimate(flops=int(us * 3 * 10**8), transcendentals=0, bytes_accessed=0)


def ordered(array, *before):
    return lax.optimization_barrier((array,) + before)[0]


def in_hbm(array):
    return pltpu.with_memory_space_constraint(array, pltpu.HBM)


def params(limit):
    return pltpu.CompilerParams(vmem_limit_bytes=limit << 20)


def gelu_parts(u):
    root = math.sqrt(2.0 / math.pi)
    inner = jnp.tanh(root * (u + 0.044715 * u * u * u))
    value = 0.5 * u * (1.0 + inner)
    slope = 0.5 * (1.0 + inner) + 0.5 * u * (1.0 - inner * inner) * root * (
        1.0 + 3.0 * 0.044715 * u * u
    )
    return value, slope


def scores_kernel(
    at_ref, x0, x1, x2, x3, i0, i1, i2, i3, wq_ref, wk_ref, wv_ref, rel_ref, tab_ref,
    own_ref, core_ref, far_ref, probs_ref, qkv_ref, relkq_ref, row_ref, col_ref,
    key_rel, queries, keys_t, values, rel_keys_t, sector_hot,
):
    scale = 1.0 / math.sqrt(192.0)
    step = pl.program_id(0)
    rows = blocks * lanes
    width = wq_ref.shape[1]
    heads = tab_ref.shape[1]
    size = width // heads

    @pl.when(step == 0)
    def _():
        for t, (x_ref, i_ref) in enumerate(zip((x0, x1, x2, x3), (i0, i1, i2, i3))):
            span = slice(t * lanes, (t + 1) * lanes)
            for at, w_ref in enumerate((wq_ref, wk_ref, wv_ref)):
                part = dot(x_ref[...], w_ref[...]).astype(bf16)
                qkv_ref[span, at * width : (at + 1) * width] = part
                if at == 1:
                    keys_t[:, span] = part.astype(f32).T.astype(bf16)
                else:
                    for h in range(heads):
                        (queries, None, values)[at][h, span, :] = part[:, h * size : (h + 1) * size]
            first = jnp.bitwise_xor(at_ref[0], slots[t]) * lanes
            slot = first + lax.broadcasted_iota(jnp.int32, (8, lanes), 1)
            kind = lax.broadcasted_iota(jnp.int32, (8, lanes), 0)
            ints = jnp.where(kind == 3, (slot < at_ref[1]).astype(jnp.int32), i_ref[...])
            row_ref[:, span] = ints
            col_ref[span, :] = ints.astype(f32).T.astype(jnp.int32)
        sector = lax.broadcasted_iota(jnp.int32, (32, rows), 0)
        for k in range(2):
            hot = (jnp.right_shift(row_ref[1 + k : 2 + k, :], 5) == sector).astype(f32).astype(bf16)
            sector_hot[k * 32 : (k + 1) * 32, :] = hot
        rel_keys = dot(rel_ref[...], wk_ref[...])
        relkq_ref[:, :width] = rel_keys.astype(bf16)
        rel_keys_t[...] = rel_keys.T.astype(bf16)
        relkq_ref[:, width:] = dot(rel_ref[...], wq_ref[...]).astype(bf16)
        for h in range(heads):
            cols = slice(width + h * size, width + (h + 1) * size)
            key_rel[h] = (
                dot(qkv_ref[:, cols], relkq_ref[:, cols], ((1,), (1,))).astype(bf16).astype(f32)
            )

    here = pl.ds(pl.multiple_of(step * lanes, lanes), lanes)
    pos_i = col_ref[here, 0:1]
    cx_i = col_ref[here, 1:2]
    cy_i = col_ref[here, 2:3]
    own_row = row_ref[0:1, here]
    lane = lax.broadcasted_iota(jnp.int32, (lanes, lanes), 1)
    on_x = jnp.bitwise_and(jnp.right_shift(lane, 5), 1) == 0
    seek = (
        jnp.where(on_x, jnp.right_shift(cx_i, 5), jnp.right_shift(cy_i, 5) + 64)
        + 32
        - jnp.bitwise_and(lane, 31)
        - (lane >= 64).astype(jnp.int32)
    )
    short_x = jnp.bitwise_and(cx_i, 31) < jnp.bitwise_and(row_ref[1:2, :], 31)
    short_y = jnp.bitwise_and(cy_i, 31) < jnp.bitwise_and(row_ref[2:3, :], 31)
    ahead, mirror = [], []
    for t in range(blocks):
        span = slice(t * lanes, (t + 1) * lanes)
        ahead.append(ahead_of(pos_i, row_ref[0:1, span]))
        mirror.append(ahead_of(col_ref[span, 0:1], own_row))
    valid = row_ref[3:4, :] > 0
    attended = []
    for h in range(heads):
        cols = slice(h * size, (h + 1) * size)
        query = queries[h, here, :]
        rel_scores = dot(query, rel_keys_t[cols, :]).astype(bf16).astype(f32)
        table = jnp.broadcast_to(tab_ref[0, h : h + 1, :], (lanes, lanes))
        by_sector = pick(table, seek).astype(bf16)
        content = dot(query, keys_t[cols, :])
        plain_x = dot(by_sector[:, 0:32], sector_hot[0:32, :])
        plain_y = dot(by_sector[:, 32:64], sector_hot[32:64, :])
        less_x = dot(by_sector[:, 64:96], sector_hot[0:32, :])
        less_y = dot(by_sector[:, 96:128], sector_hot[32:64, :])
        bias = jnp.where(short_x, less_x, plain_x) + jnp.where(short_y, less_y, plain_y)
        moved = []
        for t in range(blocks):
            span = slice(t * lanes, (t + 1) * lanes)
            moved.append(pick(rel_scores, ahead[t]) + pick(key_rel[h, span, :], mirror[t]).T)
        scores = scale * (content + jnp.concatenate(moved, axis=1)) + bias
        scores = jnp.where(valid, scores, mask_value)
        top = jnp.max(scores, axis=1, keepdims=True)
        raised = jnp.exp(scores - top)
        probs = (raised * (1.0 / jnp.sum(raised, axis=1, keepdims=True))).astype(bf16)
        probs_ref[h] = probs
        attended.append(dot(probs, values[h]).astype(bf16))
    attended = jnp.concatenate(attended, axis=1)
    for t, target in enumerate((own_ref, far_ref.at[0], core_ref, far_ref.at[1])):

        @pl.when(step == t)
        def _(target=target):
            target[...] = attended


def scores_call(at, xs, ints, w_query, w_key, w_value, rel_table, tables):
    rows, model = blocks * lanes, w_query.shape[0]
    parts, heads, _ = tables.shape
    width = w_query.shape[1] // parts
    buckets = rel_table.shape[0]
    column = pl.BlockSpec((model, width), lambda i, at: (0, at[0]))
    return pl.pallas_call(
        scores_kernel,
        out_shape=(
            jax.ShapeDtypeStruct((lanes, width), bf16),
            jax.ShapeDtypeStruct((lanes, width), bf16),
            jax.ShapeDtypeStruct((2, lanes, width), bf16),
            pltpu.HBM((heads, rows, rows), bf16),
            pltpu.HBM((rows, 3 * width), bf16),
            pltpu.HBM((buckets, 2 * width), bf16),
            pltpu.HBM((8, rows), jnp.int32),
            pltpu.HBM((rows, 8), jnp.int32),
        ),
        grid_spec=pltpu.PrefetchScalarGridSpec(
            num_scalar_prefetch=1,
            grid=(blocks,),
            in_specs=[rows_of(x) for x in xs]
            + [rows_of(i) for i in ints]
            + [
                column,
                column,
                column,
                full((buckets, model)),
                pl.BlockSpec((1, heads, lanes), lambda i, at: (at[0], 0, 0)),
            ],
            out_specs=[
                full((lanes, width)),
                full((lanes, width)),
                full((2, lanes, width)),
                pl.BlockSpec((heads, lanes, rows), lambda i, at: (0, i, 0)),
                full((rows, 3 * width)),
                full((buckets, 2 * width)),
                full((8, rows)),
                full((rows, 8)),
            ],
            scratch_shapes=[
                pltpu.VMEM((heads, rows, lanes), f32),
                pltpu.VMEM((heads, rows, width // heads), bf16),
                pltpu.VMEM((width, rows), bf16),
                pltpu.VMEM((heads, rows, width // heads), bf16),
                pltpu.VMEM((width, buckets), bf16),
                pltpu.VMEM((64, rows), bf16),
            ],
        ),
        compiler_params=params(18),
        cost_estimate=cost(25),
        name="scores",
    )(
        at, *map(array_of, xs), *map(array_of, ints), w_query, w_key, w_value, rel_table, tables
    )


def up_kernel(
    at_ref, a0, a1, a2, a3, x_ref, wout_ref, gain_ref, bias_ref, win_ref, bin_ref,
    far_ref, core_ref, own_ref, act_ref, slope_ref, normed_ref, inverse_ref, attended_ref,
    hidden_low,
):
    step = pl.program_id(0)
    width = a0.shape[1]
    tile = win_ref.shape[1]

    @pl.when(step == 0)
    def _():
        total = x_ref[...].astype(f32)
        for t, piece in enumerate((a0, a1, a2, a3)):
            first = pl.multiple_of(jnp.bitwise_xor(at_ref[0], slots[t]) * width, width)
            total = total + dot(piece[...], wout_ref[pl.ds(first, width), :])
            attended_ref[:, pl.ds(first, width)] = piece[...]
        centered = total - jnp.mean(total, axis=1, keepdims=True)
        inverse = lax.rsqrt(jnp.mean(centered * centered, axis=1, keepdims=True) + norm_eps)
        normed = centered * inverse
        normed_ref[...] = normed
        inverse_ref[...] = jnp.broadcast_to(inverse, inverse_ref.shape)
        hidden = (normed * gain_ref[...] + bias_ref[...]).astype(bf16)
        hidden_low[...] = hidden

    value, slope = gelu_parts(dot(hidden_low[...], win_ref[...]) + bin_ref[...])
    value = value.astype(bf16)
    act_ref[...] = value
    slope_ref[...] = slope.astype(bf16)
    strip = tile // blocks
    here = pl.ds(pl.multiple_of(step * strip, strip), strip)
    for t, target in enumerate((own_ref, far_ref.at[0], core_ref, far_ref.at[1])):
        first = pl.multiple_of(jnp.bitwise_xor(at_ref[0], slots[t]) * strip, strip)
        target[:, here] = act_ref[:, pl.ds(first, strip)]


def up_call(at, pieces, x_own, w_out, gain, bias, w_in, b_in, docs):
    rows, model = x_own.shape
    units = w_in.shape[1]
    tile = units // docs
    quarter = units // blocks
    column = lambda i, at: (0, i)
    return pl.pallas_call(
        up_kernel,
        out_shape=(
            jax.ShapeDtypeStruct((2, rows, quarter), bf16),
            jax.ShapeDtypeStruct((rows, quarter), bf16),
            jax.ShapeDtypeStruct((rows, quarter), bf16),
            jax.ShapeDtypeStruct((rows, units), bf16),
            jax.ShapeDtypeStruct((rows, units), bf16),
            jax.ShapeDtypeStruct((rows, model), f32),
            jax.ShapeDtypeStruct((rows, lanes), f32),
            jax.ShapeDtypeStruct((rows, model), bf16),
            jax.ShapeDtypeStruct((rows, model), bf16),
        ),
        grid_spec=pltpu.PrefetchScalarGridSpec(
            num_scalar_prefetch=1,
            grid=(docs,),
            in_specs=[rows_of(piece) for piece in pieces]
            + [
                full((rows, model)),
                full((model, model)),
                full((1, model)),
                full((1, model)),
                pl.BlockSpec((model, tile), column),
                pl.BlockSpec((1, tile), column),
            ],
            out_specs=[
                full((2, rows, quarter)),
                full((rows, quarter)),
                full((rows, quarter)),
                pl.BlockSpec((rows, tile), column),
                pl.BlockSpec((rows, tile), column),
                full((rows, model)),
                full((rows, lanes)),
                full((rows, model)),
                full((rows, model)),
            ],
        ),
        compiler_params=params(18),
        cost_estimate=cost(9),
        name="up",
    )(at, *map(array_of, pieces), x_own, w_out, gain, bias, w_in, b_in)


def norm_back(grad, normed, inverse, gain):
    scaled = grad * gain
    return inverse * (
        scaled
        - jnp.mean(scaled, axis=1, keepdims=True)
        - normed * jnp.mean(scaled * normed, axis=1, keepdims=True)
    )


def down_kernel(
    act_ref, wdown_ref, normed_ref, cot_ref, gain1_ref, bias1_ref, gain2_ref, bias2_ref,
    block_ref, mix_ref, low_ref, sums_ref,
):
    step = pl.program_id(0)

    @pl.when(step == 0)
    def _():
        mix_ref[...] = normed_ref[...] * gain1_ref[...] + bias1_ref[...]

    mix_ref[...] += dot(act_ref[...], wdown_ref[...])

    @pl.when(step == pl.num_programs(0) - 1)
    def _():
        mixed = mix_ref[...]
        centered = mixed - jnp.mean(mixed, axis=1, keepdims=True)
        inverse = lax.rsqrt(jnp.mean(centered * centered, axis=1, keepdims=True) + norm_eps)
        normed = centered * inverse
        block_ref[...] = (normed * gain2_ref[...] + bias2_ref[...]).astype(bf16)
        grad = cot_ref[...].astype(f32)
        sums_ref[0:1, :] = jnp.sum(grad * normed, axis=0, keepdims=True)
        sums_ref[1:2, :] = jnp.sum(grad, axis=0, keepdims=True)
        mix = norm_back(grad, normed, inverse, gain2_ref[...])
        mix_ref[...] = mix
        low_ref[...] = mix.astype(bf16)


def down_call(act, w_down, normed, cotangent, gain1, bias1, gain2, bias2, tile):
    rows, units = act.shape
    model = w_down.shape[1]
    return pl.pallas_call(
        down_kernel,
        out_shape=(
            jax.ShapeDtypeStruct((rows, model), bf16),
            jax.ShapeDtypeStruct((rows, model), f32),
            jax.ShapeDtypeStruct((rows, model), bf16),
            jax.ShapeDtypeStruct((8, model), f32),
        ),
        grid=(units // tile,),
        in_specs=[
            pl.BlockSpec((rows, tile), lambda i: (0, i)),
            pl.BlockSpec((tile, model), lambda i: (i, 0)),
            full((rows, model)),
            full((rows, model)),
        ]
        + [full((1, model))] * 4,
        out_specs=[full((rows, model))] * 3 + [full((8, model))],
        compiler_params=params(18),
        cost_estimate=cost(8),
        name="down",
    )(act, w_down, normed, cotangent, gain1, bias1, gain2, bias2)


def back_kernel(
    at_ref, wdown_ref, slope_ref, win_ref, wout_ref, normed_ref, inverse_ref, mix_ref, ffn_ref,
    attended_ref, gain1_ref, above_ref, hidden_ref,
    own_ref, core_ref, far_ref, resid_ref, upfar_ref, upcore_ref, upown_ref,
    outfar_ref, outcore_ref, outown_ref, sums_ref,
    total, grad_up,
):
    step = pl.program_id(0)
    steps = pl.num_programs(0)
    rows, tile = slope_ref.shape
    model = mix_ref.shape[1]
    width = model // blocks

    @pl.when(step == 0)
    def _():
        total[...] = mix_ref[...]

    grad = dot(ffn_ref[...], wdown_ref[...], ((1,), (1,))) * slope_ref[...].astype(f32)
    low = grad.astype(bf16)
    total[...] += dot(low, win_ref[...], ((1,), (1,)))
    per = model // tile
    part = step // per
    here = pl.ds(pl.multiple_of((step - part * per) * tile, tile), tile)
    grad_up[jnp.bitwise_xor(part, at_ref[0]), :, here] = low
    sums_ref[pl.ds(4 + part, 1), here] = jnp.sum(low.astype(f32), axis=0, keepdims=True)

    @pl.when(step == steps - 1)
    def _():
        upown_ref[...] = grad_up[0]
        upcore_ref[0] = hidden_ref[...]
        upcore_ref[1] = grad_up[1]
        upfar_ref[0] = hidden_ref[...]
        upfar_ref[1] = grad_up[2]
        upfar_ref[2] = grad_up[3]
        grad = total[...]
        normed = normed_ref[...]
        sums_ref[0:1, :] = jnp.sum(grad * normed, axis=0, keepdims=True)
        sums_ref[1:2, :] = jnp.sum(grad, axis=0, keepdims=True)
        sums_ref[2:4, :] = above_ref[0:2, :]
        resid = norm_back(grad, normed, inverse_ref[:, 0:1], gain1_ref[...])
        resid_ref[...] = resid
        low = resid.astype(bf16)
        total[...] = low.astype(f32)
        outfar_ref[:, :model] = attended_ref[...]
        outcore_ref[:, :model] = attended_ref[...]
        targets = (own_ref, core_ref, far_ref.at[0], far_ref.at[1])
        wides = (
            outown_ref, outcore_ref.at[:, pl.ds(model, width)],
            outfar_ref.at[:, pl.ds(model, width)], outfar_ref.at[:, pl.ds(model + width, width)],
        )
        for at, (target, wide) in enumerate(zip(targets, wides)):
            first = pl.multiple_of(jnp.bitwise_xor(at_ref[0], at) * width, width)
            target[...] = dot(low, wout_ref[pl.ds(first, width), :], ((1,), (1,))).astype(bf16)
            wide[...] = total[:, pl.ds(first, width)].astype(bf16)


def back_call(
    at, w_down, slope, w_in, w_out, normed, inverse, mix, grad_ffn, attended, gain1, above, hidden, tile,
):
    rows, units = slope.shape
    model = w_out.shape[0]
    width = model // blocks
    return pl.pallas_call(
        back_kernel,
        out_shape=(
            jax.ShapeDtypeStruct((rows, width), bf16),
            jax.ShapeDtypeStruct((rows, width), bf16),
            jax.ShapeDtypeStruct((2, rows, width), bf16),
            jax.ShapeDtypeStruct((rows, model), f32),
            jax.ShapeDtypeStruct((3, rows, model), bf16),
            jax.ShapeDtypeStruct((2, rows, model), bf16),
            jax.ShapeDtypeStruct((rows, model), bf16),
            jax.ShapeDtypeStruct((rows, model + 2 * width), bf16),
            jax.ShapeDtypeStruct((rows, model + width), bf16),
            jax.ShapeDtypeStruct((rows, width), bf16),
            jax.ShapeDtypeStruct((8, model), f32),
        ),
        grid_spec=pltpu.PrefetchScalarGridSpec(
            num_scalar_prefetch=1,
            grid=(units // tile,),
            in_specs=[
                pl.BlockSpec((tile, model), lambda i, at: (i, 0)),
                pl.BlockSpec((rows, tile), lambda i, at: (0, i)),
                pl.BlockSpec((model, tile), lambda i, at: (0, i)),
                full((model, model)),
                full((rows, model)),
                full((rows, lanes)),
                full((rows, model)),
                full((rows, model)),
                full((rows, model)),
                full((1, model)),
                full((8, model)),
                full((rows, model)),
            ],
            out_specs=[
                full((rows, width)),
                full((rows, width)),
                full((2, rows, width)),
                full((rows, model)),
                full((3, rows, model)),
                full((2, rows, model)),
                full((rows, model)),
                full((rows, model + 2 * width)),
                full((rows, model + width)),
                full((rows, width)),
                full((8, model)),
            ],
            scratch_shapes=[
                pltpu.VMEM((rows, model), f32),
                pltpu.VMEM((blocks, rows, model), bf16),
            ],
        ),
        compiler_params=params(18),
        cost_estimate=cost(12),
        name="back",
    )(at, w_down, slope, w_in, w_out, normed, inverse, mix, grad_ffn, attended, gain1, above, hidden)


def scores_grad_kernel(half, held, *refs):
    at_ref, g0, g1, g2, g3, qkv_ref, probs_ref, relkq_ref, row_ref, col_ref = refs[:10]
    refs = refs[10:]
    last = half == 1
    if last:
        wq_ref, wk_ref, sums_ref, before_ref, boxes_before = refs[:5]
        refs = refs[5:]
    refs = refs[held:]
    if last:
        dqkv_ref, own_ref, core_ref, far_ref, small_ref, ga_ref, ds_ref, drel, box_sums = refs
    else:
        dqkv_ref, box_sums, ga_ref, ds_ref, drel = refs
    scale = 1.0 / math.sqrt(192.0)
    rows = blocks * lanes
    width = qkv_ref.shape[1] // 3
    part = width // 2
    heads = probs_ref.shape[0]
    size = part // heads
    span_width = 3 * lanes
    for t, piece in enumerate((g0, g1, g2, g3)):
        ga_ref[t * lanes : (t + 1) * lanes, :] = piece[...]
    drel[...] = jnp.zeros_like(drel)
    box_sums[...] = jnp.zeros_like(box_sums)
    window = lax.broadcasted_iota(jnp.int32, (rows, span_width), 1)
    bucket = lax.broadcasted_iota(jnp.int32, (lanes, lanes), 1)
    label = lax.broadcasted_iota(jnp.int32, (rows, lanes), 1)
    all_pos = col_ref[:, 0:1]
    all_x, all_y = col_ref[:, 1:2], col_ref[:, 2:3]
    sector_x, sector_y = jnp.right_shift(all_x, 5), jnp.right_shift(all_y, 5)
    hot_x = (label == sector_x).astype(bf16)
    hot_y = (label == sector_y + 64).astype(bf16)
    hot_both = ((label == sector_x) | (label == sector_y + 64)).astype(bf16)

    def histogram(sums, total, at, base_row):
        first = at - base_row + (lanes - 1) - bucket
        low = jnp.bitwise_and(first, lanes - 1)
        group = jnp.right_shift(first, 7)
        found = jnp.where(
            group == 0,
            pick(sums[:, :lanes], low),
            jnp.where(
                group == 1,
                pick(sums[:, lanes : 2 * lanes], low),
                pick(sums[:, 2 * lanes :], low),
            ),
        )
        found = jnp.where(bucket == 0, total, found)
        later = jnp.where(bucket == lanes - 1, 0.0, pltpu.roll(found, lanes - 1, 1))
        return found - later

    def by_rows(ib, carry):
        here = pl.ds(pl.multiple_of(ib * lanes, lanes), lanes)
        pos_i = col_ref[here, 0:1]
        cx_i, cy_i = col_ref[here, 1:2], col_ref[here, 2:3]
        base = jnp.min(pos_i, axis=0, keepdims=True)
        below = (all_pos <= base - 63 + window).astype(bf16)
        short_x = jnp.bitwise_and(cx_i, 31) < jnp.bitwise_and(row_ref[1:2, :], 31)
        short_y = jnp.bitwise_and(cy_i, 31) < jnp.bitwise_and(row_ref[2:3, :], 31)
        step_x = jnp.right_shift(cx_i, 5) + 32 - bucket
        step_y = jnp.right_shift(cy_i, 5) + 32 - (bucket - 64)
        in_x = (bucket < 64) & (step_x >= 0) & (step_x < 32)
        in_y = (bucket >= 64) & (step_y >= 0) & (step_y < 32)
        seek = jnp.where(in_x, step_x, jnp.where(in_y, step_y + 64, 0))
        inside = in_x | in_y
        for h in range(heads):
            gcols = slice(h * size, (h + 1) * size)
            kgcols = slice(part + h * size, part + (h + 1) * size)
            vgcols = slice(2 * part + h * size, 2 * part + (h + 1) * size)
            cols, kcols, vcols = (
                slice(k * width + half * part + h * size, k * width + half * part + (h + 1) * size)
                for k in range(3)
            )
            probs = probs_ref[h, here, :].astype(f32)
            gained = dot(ga_ref[here, gcols], qkv_ref[:, vcols], ((1,), (1,)))
            row_dots = jnp.sum(probs * gained, axis=1, keepdims=True)
            grad = (probs * (gained - row_dots)).astype(bf16)
            ds_ref[h, here, :] = grad
            exact = grad.astype(f32)
            total = jnp.sum(exact, axis=1, keepdims=True)
            rel = histogram(dot(grad, below), total, pos_i, base)
            rel = (scale * rel).astype(bf16)
            dqkv_ref[here, gcols] = (
                scale * dot(grad, qkv_ref[:, kcols]) + dot(rel, relkq_ref[:, cols])
            ).astype(bf16)
            drel[:, gcols] += dot(rel, qkv_ref[here, cols], ((0,), (0,)))
            grad_x = jnp.where(short_x, exact, 0.0).astype(bf16)
            grad_y = jnp.where(short_y, exact, 0.0).astype(bf16)
            plain = dot(grad, hot_both)
            less = dot(grad_x, hot_x) + dot(grad_y, hot_y)
            plain = jnp.where(inside, pick(plain, seek), 0.0)
            less = jnp.where(inside, pick(less, seek), 0.0)
            box_sums[h : h + 1, :] += jnp.sum(plain, axis=0, keepdims=True)
            box_sums[8 + h : 9 + h, :] += jnp.sum(less, axis=0, keepdims=True)
        return carry

    lax.fori_loop(0, blocks, by_rows, 0)

    def by_columns(jb, carry):
        here = pl.ds(pl.multiple_of(jb * lanes, lanes), lanes)
        pos_j = col_ref[here, 0:1]
        base = jnp.min(pos_j, axis=0, keepdims=True)
        below = (all_pos <= base - 63 + window).astype(bf16)
        for h in range(heads):
            gcols = slice(h * size, (h + 1) * size)
            kgcols = slice(part + h * size, part + (h + 1) * size)
            vgcols = slice(2 * part + h * size, 2 * part + (h + 1) * size)
            cols, kcols, vcols = (
                slice(k * width + half * part + h * size, k * width + half * part + (h + 1) * size)
                for k in range(3)
            )
            grad = ds_ref[h, :, here]
            total = dot(grad, jnp.ones((rows, lanes), bf16), ((0,), (0,)))
            sums = dot(grad, below, ((0,), (0,)))
            mirror = (scale * histogram(sums, total, pos_j, base)).astype(bf16)
            dqkv_ref[here, kgcols] = (
                scale * dot(grad, qkv_ref[:, cols], ((0,), (0,)))
                + dot(mirror, relkq_ref[:, kcols])
            ).astype(bf16)
            drel[:, kgcols] += dot(mirror, qkv_ref[here, kcols], ((0,), (0,)))
            dqkv_ref[here, vgcols] = dot(
                probs_ref[h, :, here], ga_ref[:, gcols], ((0,), (0,))
            ).astype(bf16)
        return carry

    lax.fori_loop(0, blocks, by_columns, 0)
    keys, queries = drel[:, :part].astype(bf16), drel[:, part:].astype(bf16)
    dqkv_ref[rows:, :part] = queries
    dqkv_ref[rows:, part : 2 * part] = keys
    dqkv_ref[rows:, 2 * part :] = jnp.zeros((lanes, part), bf16)
    if not last:
        return
    for t, target in enumerate((own_ref, far_ref.at[0], core_ref, far_ref.at[1])):
        span = slice(t * lanes, (t + 1) * lanes)
        for k in range(3):
            first = k * width
            target[:, first : first + part] = before_ref[span, k * part : (k + 1) * part]
            target[:, first + part : first + width] = dqkv_ref[span, k * part : (k + 1) * part]
    queries = jnp.concatenate([before_ref[rows:, :part], queries], axis=1)
    keys = jnp.concatenate([before_ref[rows:, part : 2 * part], keys], axis=1)

    docs, small_rows, small_width = small_ref.shape
    per = lanes // docs
    table = (
        dot(keys, wk_ref[...], ((1,), (1,))) + dot(queries, wq_ref[...], ((1,), (1,)))
    ).astype(bf16)
    plain = jnp.concatenate([boxes_before[0:heads], box_sums[0:heads], box_sums[heads + heads : 8]], axis=0)
    less = jnp.concatenate(
        [boxes_before[8 : 8 + heads], box_sums[8 : 8 + heads], box_sums[8 + 2 * heads : 16]], axis=0
    )
    heads = 2 * heads
    place_lane = lax.broadcasted_iota(jnp.int32, (8, lanes), 1)
    later = jnp.where(
        jnp.bitwise_and(place_lane, 63) == 63, 0.0, pltpu.roll(less, lanes - 1, 1)
    )
    boxes = (plain - less + later).astype(bf16)
    row_at = lax.broadcasted_iota(jnp.int32, (8, lanes), 0)
    head_at = at_ref[0] * heads + row_at
    by_head = [
        dot(boxes, ((place_lane == head_at + k * 64) & (row_at < heads)).astype(bf16), ((0,), (0,)))
        for k in range(2)
    ]
    model = table.shape[1]
    edges = list(range(0, model, small_width)) + [model]
    rest = edges[-1] - edges[-2]
    lane = slice(rest, rest + lanes)
    line = (len(edges) - 2) * per
    count = lanes // 2 // docs
    for chunk in range(docs):
        own = slice(chunk * per, (chunk + 1) * per)
        for k, (first, end) in enumerate(zip(edges[:-1], edges[1:])):
            small_ref[chunk, k * per : (k + 1) * per, : end - first] = table[own, first:end].astype(f32)
        for k in range(4):
            small_ref[chunk, line + k : line + k + 1, lane] = (
                sums_ref[k : k + 1, chunk * lanes : (chunk + 1) * lanes]
            )
            first = (chunk * blocks + k) * lanes
            where = first // model
            small_ref[chunk, line + 4 + k : line + 5 + k, lane] = (
                sums_ref[4 + where : 5 + where, first - where * model : first - where * model + lanes]
            )
        begin = chunk * count
        small_ref[chunk, line + 8 : line + 8 + count, lane] = (
            by_head[0][begin : begin + count, :] + by_head[1][64 + begin : 64 + begin + count, :]
        )


def scores_grad_call(half, at, pieces, qkv, probs, relkq, row, col, after, docs=0, extra=()):
    rows = blocks * lanes
    heads = probs.shape[0] // 2
    width = qkv.shape[1] // 3
    part = width // 2
    model = width * blocks
    buckets = relkq.shape[0]
    column = pl.BlockSpec((model, width), lambda i, at: (0, at[0]))
    grads = jax.ShapeDtypeStruct((rows + buckets, 3 * part), bf16)
    box_shape = (16, lanes)
    scratch = [
        pltpu.VMEM((rows, part), bf16),
        pltpu.VMEM((heads, rows, rows), bf16),
        pltpu.VMEM((buckets, 2 * part), f32),
    ]
    extra_specs = []
    if half == 1:
        shapes = (
            grads,
            jax.ShapeDtypeStruct((lanes, 3 * width), bf16),
            jax.ShapeDtypeStruct((lanes, 3 * width), bf16),
            jax.ShapeDtypeStruct((2, lanes, 3 * width), bf16),
            jax.ShapeDtypeStruct((docs, 3 * buckets // docs, 3 * part), f32),
        )
        extra_specs = [column, column, full((8, model)), full(grads.shape), full(box_shape)]
        scratch = scratch + [pltpu.VMEM(box_shape, f32)]
    else:
        shapes = (grads, jax.ShapeDtypeStruct(box_shape, f32))
    at = ordered(at, *after) if after else at
    return pl.pallas_call(
        functools.partial(scores_grad_kernel, half, 0),
        out_shape=shapes,
        grid_spec=pltpu.PrefetchScalarGridSpec(
            num_scalar_prefetch=1,
            grid=(1,),
            in_specs=[rows_of(piece, (lanes, part), lambda i, at: half) for piece in pieces]
            + [
                full((rows, 3 * width)),
                pl.BlockSpec((heads, rows, rows), lambda i, at: (half, 0, 0)),
                full((buckets, 2 * width)),
                full((8, rows)),
                full((rows, 8)),
            ]
            + extra_specs,
            out_specs=[full(shape.shape) for shape in shapes],
            scratch_shapes=scratch,
        ),
        compiler_params=params(18),
        cost_estimate=cost(15),
        name="scores_grad",
    )(at, *map(array_of, pieces), qkv, probs, relkq, row, col, *extra)


def weight_grads_call(at, wholes, after=(), name="weight_grads"):
    count = 1 << len(wholes[0][1])
    chunk = lanes
    per = 2
    steps = count // per
    half = steps // 2

    def chunk_of(bits, which):
        def index(i, at):
            p = lax.rem(i + half, steps) * per + which
            total = 0
            for place, bit in enumerate(bits):
                total = total + jnp.bitwise_and(jnp.right_shift(p, len(bits) - 1 - place), 1) * bit
            return jnp.bitwise_xor(at[1], total)

        return index

    def kernel(at_ref, *refs):
        refs = list(refs)
        take = lambda number: [refs.pop(0) for _ in range(number)]
        ins = []
        for groups, bits, extra in wholes:
            sides = [(take(len(lefts) * per), take(len(rights))) for lefts, rights, _ in groups]
            ins.append((sides, take(per) if extra is not None else []))
        outs = [take(2) for _ in wholes]
        step = pl.program_id(0)
        for (sides, extras), (keep_ref, send_ref) in zip(ins, outs):
            results = []
            for own, right_refs in sides:
                right_all = refs.pop(0)

                @pl.when(step == 0)
                def _(right_refs=right_refs, right_all=right_all):
                    for k, ref in enumerate(right_refs):
                        right_all[k * lanes : (k + 1) * lanes, :] = ref[...]

                left = jnp.concatenate(
                    [
                        jnp.concatenate([own[k + which][...] for which in range(per)], axis=1)
                        for k in range(0, len(own), per)
                    ],
                    axis=0,
                )
                results.append(dot(left, right_all[...], ((0,), (0,))).astype(bf16))
            for target, mine in ((send_ref, step < half), (keep_ref, step >= half)):

                @pl.when(mine)
                def _(target=target, results=results, extras=extras):
                    for which in range(per):
                        first = 0
                        for result in results:
                            end = first + result.shape[1]
                            target[which, :chunk, first:end] = (
                                result[which * chunk : (which + 1) * chunk, :]
                            )
                            first = end
                        if extras:
                            target[which, chunk:, :] = extras[which][...].astype(bf16)

    in_specs, operands, scratch, shapes, out_specs = [], [], [], [], []
    for groups, bits, extra in wholes:
        total_width = sum(width for _, _, width in groups)
        tail = 0 if extra is None else extra.shape[1]
        for lefts, rights, width in groups:
            for handle in lefts:
                for which in range(per):
                    in_specs.append(rows_of(handle, (lanes, chunk), chunk_of(bits, which)))
                    operands.append(array_of(handle))
            for handle in rights:
                column = handle[2] if isinstance(handle, tuple) and len(handle) == 3 else 0
                handle = (
                    handle[:2] if isinstance(handle, tuple) and handle[1] is not None else array_of(handle)
                )
                in_specs.append(rows_of(handle, (lanes, width), lambda i, at, column=column: column))
                operands.append(array_of(handle))
            scratch.append(pltpu.VMEM((len(rights) * lanes, width), bf16))
        for which in range(per if extra is not None else 0):
            index = chunk_of(bits, which)
            in_specs.append(
                pl.BlockSpec(
                    (None, tail, total_width), lambda i, at, index=index: (index(i, at), 0, 0)
                )
            )
            operands.append(extra)
        shapes += [jax.ShapeDtypeStruct((count // 2, chunk + tail, total_width), bf16)] * 2
        block = (per, chunk + tail, total_width)
        out_specs += [
            pl.BlockSpec(block, lambda i, at: (jnp.maximum(i - half, 0), 0, 0)),
            pl.BlockSpec(block, lambda i, at: (jnp.minimum(i, half - 1), 0, 0)),
        ]
    at = ordered(at, *after) if after else at
    out = pl.pallas_call(
        kernel,
        out_shape=tuple(shapes),
        grid_spec=pltpu.PrefetchScalarGridSpec(
            num_scalar_prefetch=1,
            grid=(steps,),
            in_specs=in_specs,
            out_specs=out_specs,
            scratch_shapes=scratch,
        ),
        compiler_params=params(18),
        cost_estimate=cost(0.01),
        name=name,
    )(at, *operands)
    return [tuple(out[k : k + 2]) for k in range(0, len(out), 2)]


def tokens_grad_kernel(at_ref, d0, d1, d2, d3, resid_ref, wq_ref, wk_ref, wv_ref, *refs):
    out_ref = refs[-1]
    step = pl.program_id(0)
    width = wq_ref.shape[1]

    @pl.when(step == 0)
    def _():
        out_ref[...] = resid_ref[...]

    for t, piece in enumerate((d0, d1, d2, d3)):

        @pl.when(step == t)
        def _(piece=piece):
            total = out_ref[...]
            for at, w_ref in enumerate((wq_ref, wk_ref, wv_ref)):
                total = total + dot(
                    piece[:, at * width : (at + 1) * width], w_ref[...], ((1,), (1,))
                )
            out_ref[...] = total


def tokens_grad_call(at, pieces, resid, w_query, w_key, w_value, after):
    rows, model = resid.shape
    width = model // blocks
    tile = (rows, 3 * width)

    def column(i, at):
        offset = jnp.where(i == 1, 2, jnp.where(i == 2, 1, i))
        return (0, jnp.bitwise_xor(at[0], offset))

    weight = pl.BlockSpec((model, width), column)
    at = ordered(at, *after) if after else at
    return pl.pallas_call(
        tokens_grad_kernel,
        out_shape=jax.ShapeDtypeStruct((rows, model), f32),
        grid_spec=pltpu.PrefetchScalarGridSpec(
            num_scalar_prefetch=1,
            grid=(blocks,),
            in_specs=[rows_of(piece, tile) for piece in pieces]
            + [full((rows, model)), weight, weight, weight],
            out_specs=full((rows, model)),
        ),
        compiler_params=params(18),
        cost_estimate=cost(4),
        name="tokens_grad",
    )(at, *map(array_of, pieces), resid, w_query, w_key, w_value)


def parts_kernel(fields, at_ref, *refs):
    step = pl.program_id(0)
    parts, outs = refs[: blocks * fields], refs[blocks * fields :]
    for field in range(fields):
        for at in range(blocks):

            @pl.when(step == at)
            def _(part=parts[field * blocks + at], out=outs[field]):
                out[...] = part[...].astype(f32)


def parts_call(at, fields, name):
    in_specs, operands, shapes, out_specs = [], [], [], []
    for parts, axis in fields:
        rows, width = parts[0].shape
        in_specs += [full((rows, width))] * blocks
        operands += list(parts)
        shape = (rows * blocks, width) if axis == 0 else (rows, width * blocks)
        shapes.append(jax.ShapeDtypeStruct(shape, f32))

        def index(i, at, axis=axis):
            spot = jnp.bitwise_xor(at[0], i)
            return (spot, 0) if axis == 0 else (0, spot)

        out_specs.append(pl.BlockSpec((rows, width), index))
    return pl.pallas_call(
        functools.partial(parts_kernel, len(fields)),
        out_shape=tuple(shapes),
        grid_spec=pltpu.PrefetchScalarGridSpec(
            num_scalar_prefetch=1, grid=(blocks,), in_specs=in_specs, out_specs=out_specs
        ),
        compiler_params=params(18),
        cost_estimate=cost(2),
        name=name,
    )(at, *operands)


def last_kernel(at_ref, *refs):
    step = pl.program_id(0)
    firsts, seconds, outs = refs[:blocks], refs[blocks : 2 * blocks], refs[2 * blocks : 2 * blocks + 3]
    wout_ref, rel_ref, norm_ref, bin_ref, box_ref = refs[2 * blocks + 3 :]
    for at in range(blocks):

        @pl.when(step == at)
        def _(first=firsts[at], second=seconds[at]):
            for k, out in enumerate(outs):
                span = slice(k * lanes, (k + 1) * lanes)
                out[:, :lanes] = first[:, span].astype(f32)
                out[:, lanes:] = second[:lanes, span].astype(f32)
            wout_ref[...] = first[:, 3 * lanes :].astype(f32)

    @pl.when(step == 0)
    def _():
        total = seconds[0][lanes:, :].astype(f32)
        for second in seconds[1:]:
            total = total + second[lanes:, :].astype(f32)
        rows = rel_ref.shape[0]
        width = total.shape[1]
        for k in range(3):
            end = min((k + 1) * width, rel_ref.shape[1])
            rel_ref[:, k * width : end] = total[k * rows : (k + 1) * rows, : end - k * width]
        rest = total[2 * rows :, width - lanes :]
        norm_ref[...] = rest[:4]
        bin_ref[...] = rest[4:8]
        box_ref[...] = rest[8:16]


def last_call(at, firsts, seconds, buckets, model):
    wide = jax.ShapeDtypeStruct((lanes, model), f32)
    column = pl.BlockSpec((lanes, model // blocks), lambda i, at: (0, jnp.bitwise_xor(at[0], i)))
    return pl.pallas_call(
        last_kernel,
        out_shape=(wide, wide, wide, wide)
        + tuple(jax.ShapeDtypeStruct(shape, f32) for shape in ((buckets, model), (4, lanes), (4, lanes), (8, lanes))),
        grid_spec=pltpu.PrefetchScalarGridSpec(
            num_scalar_prefetch=1,
            grid=(blocks,),
            in_specs=[full(part.shape) for part in firsts + seconds],
            out_specs=[column] * 4 + [full((buckets, model)), full((4, lanes)), full((4, lanes)), full((8, lanes))],
        ),
        compiler_params=params(18),
        cost_estimate=cost(2),
        name="last",
    )(at, *firsts, *seconds)


class Halving:
    def __init__(self, halves, bits):
        self.keep, self.send = halves
        self.bits = list(bits)
        self.step()

    def step(self):
        self.came = swap(self.send, "docs", self.bits.pop(0))

    def add(self, *before):
        keep, came = self.keep, self.came
        if before:
            came = ordered(came, *before)
        total = lambda part: (keep[part].astype(f32) + came[part].astype(f32)).astype(bf16)
        if not self.bits:
            self.keep = self.send = total(slice(None))[0]
            return self.keep
        middle = keep.shape[0] // 2
        self.send = total(slice(middle, None))
        self.keep = total(slice(0, middle))
        sent = self.send
        self.step()
        return sent


def shards_tiles(
    tokens, lengths, positions, token_boxes, ln1_gain, ln1_bias, w_query, w_key, w_value, w_out,
    rel_table, xbias_table, ybias_table, ln2_gain, ln2_bias, w_in, b_in, w_down, cotangent,
):
    row_count, model = tokens.shape[1:]
    docs = lax.axis_size("docs")
    place = lax.axis_index("blk")
    doc_place = lax.axis_index("docs")
    heads = xbias_table.shape[1]
    boxes = xbias_table.shape[0]
    units = w_in.shape[1]
    width = model // blocks
    bits = bits_of(docs)
    other = [bits[1], bits[0]] + bits[2:]
    x_own = tokens[0]
    w_query, w_key, w_value = in_hbm(w_query), in_hbm(w_key), in_hbm(w_value)

    x_far = swap(x_own, "blk", 2)
    own_ints = jnp.concatenate(
        [
            positions,
            jnp.right_shift(token_boxes[0] + token_boxes[2], 1),
            jnp.right_shift(token_boxes[1] + token_boxes[3], 1),
            jnp.zeros((5, row_count), jnp.int32),
        ],
        axis=0,
    )
    ints_far = swap(own_ints, "blk", 2)
    x_core, ints_core = swap(x_own, "blk", 1), swap(own_ints, "blk", 1)
    x_both, ints_both = swap(ordered(x_far, ints_far), "blk", 1), swap(ints_far, "blk", 1)
    xs = tuple(map(in_hbm, (x_own, x_far, x_core, x_both)))
    tables = jnp.concatenate([xbias_table.T, ybias_table.T], axis=1).astype(f32)
    tables = tables.reshape(blocks, heads // blocks, 2 * boxes)
    at = jnp.stack([place.astype(jnp.int32), lengths[0]])
    spot = jnp.stack([place, doc_place]).astype(jnp.int32)
    att_own, att_core, att_far, probs, qkv, relkq, row, col = scores_call(
        at, xs, (own_ints, ints_far, ints_core, ints_both), w_query, w_key, w_value, rel_table, tables
    )

    came_far = swap(att_far, "blk", 2)
    came_core = swap(att_core, "blk", 1)
    came_both = swap(came_far, "blk", 1)
    line = lambda vector: vector.reshape(1, -1)
    far1, core1, act_own, act, slope, normed1, inverse1, attended, hidden = up_call(
        spot, (att_own, (came_far, 0), came_core, (came_both, 1)), x_own, w_out,
        line(ln1_gain), line(ln1_bias), w_in, line(b_in), docs,
    )
    got_far1 = swap(far1, "blk", 2)
    block_out, mix, grad_ffn, above = down_call(
        act, w_down, normed1, cotangent[0],
        line(ln1_gain), line(ln1_bias), line(ln2_gain), line(ln2_bias), units // docs,
    )
    (
        ga_own, ga_core, ga_far, grad_resid, up_far, up_core, up_own, far3, core3, gattn_own, sums,
    ) = back_call(
        spot, w_down, slope, w_in, w_out, normed1, inverse1, mix, grad_ffn, attended,
        line(ln1_gain), above, hidden, units // docs,
    )
    came_far = swap(ga_far, "blk", 2)
    came_core = swap(ga_core, "blk", 1)
    came_both = swap(came_far, "blk", 1)
    ga_all = (ga_own, (came_far, 0), came_core, (came_both, 1))
    ffn_far = swap(grad_ffn, "blk", 2)
    got_core1, got_both1 = swap(core1, "blk", 1), swap(ordered(got_far1, ga_own), "blk", 1)
    ffn_core, ffn_both = swap(grad_ffn, "blk", 1), swap(ordered(ffn_far, ga_own), "blk", 1)
    act_all = [act_own, (got_far1, 0), got_core1, (got_both1, 1)]
    gffn_all = [grad_ffn, ffn_far, ffn_core, ffn_both]
    (down_halves,) = weight_grads_call(
        spot, [([(act_all, gffn_all, model)], bits, None)], after=[ga_own], name="grad_down"
    )
    down_sum = Halving(down_halves, bits)
    got_far2 = swap(ordered(up_far, came_far), "blk", 2)
    first_grads, first_boxes = scores_grad_call(
        0, spot, ga_all, qkv, probs, relkq, row, col, [down_halves[0]]
    )
    got_core2, got_both2 = swap(up_core, "blk", 1), swap(ordered(got_far2, first_grads), "blk", 1)
    got_far3 = swap(ordered(far3, got_far2), "blk", 2)
    hidden_all = [hidden, (got_far2, 0), (got_core2, 0), (got_both2, 0)]
    up_all = [up_own, (got_far2, 1), (got_core2, 1), (got_both2, 2)]
    (in_halves,) = weight_grads_call(
        spot, [([(hidden_all, up_all, model)], bits, None)], after=[first_grads], name="grad_in"
    )
    in_sum = Halving(in_halves, bits)
    lefts = list(xs) + [rel_table]

    def rows_by_piece(grads):
        return [(grads.reshape(blocks + 1, lanes, -1), t) for t in range(blocks + 1)]

    got_core3, got_both3 = swap(core3, "blk", 1), swap(ordered(got_far3, in_halves[0]), "blk", 1)
    att_all = [far3, got_far3, got_core3, got_both3]
    per = model // width
    gattn_all = [
        gattn_own, (got_far3, None, per), (got_core3, None, per), (got_both3, None, per + 1),
    ]
    done = down_sum.add(in_halves[0])
    first_groups = [(lefts, rows_by_piece(first_grads), 3 * width // 2), (att_all, gattn_all, width)]
    (first_halves,) = weight_grads_call(
        spot, [(first_groups, other, None)], after=[in_halves[0], done], name="grad_qkv_out"
    )
    first_sum = Halving(first_halves, other)
    second_grads, dq_own, dq_core, dq_far, small = scores_grad_call(
        1, spot, ga_all, qkv, probs, relkq, row, col, [first_halves[0]], docs,
        (w_query, w_key, sums, first_grads, first_boxes),
    )
    done = down_sum.add(second_grads)
    done = in_sum.add(done)
    second_groups = [(lefts, rows_by_piece(second_grads), 3 * width // 2)]
    (second_halves,) = weight_grads_call(
        spot, [(second_groups, bits, small)], after=[done], name="grad_qkv"
    )
    second_sum = Halving(second_halves, bits)
    dq_far_got = ordered(swap(dq_far, "blk", 2), second_halves[0])
    dq_core_got, dq_both_got = swap(dq_core, "blk", 1), swap(dq_far_got, "blk", 1)
    done = first_sum.add(second_halves[0])
    grad_tokens = tokens_grad_call(
        spot, (dq_own, (dq_far_got, 0), dq_core_got, (dq_both_got, 1)), grad_resid,
        w_query, w_key, w_value, [done],
    )

    def whole(part, *before):
        far = swap(part, "blk", 2)
        held = ordered(far, *before) if before else far
        return (part, swap(part, "blk", 1), far, swap(held, "blk", 1))

    done = in_sum.add(grad_tokens)
    done = second_sum.add(done)
    done = down_sum.add(done)
    down_part = done
    done = first_sum.add(done)
    done = second_sum.add(done)
    done = in_sum.add(done)
    in_part = done
    done = first_sum.add(done)
    first_part = done
    done = second_sum.add(done)
    second_part = done
    grad_w_down, grad_w_in = parts_call(
        spot, ((whole(down_part, done), 0), (whole(in_part, done), 1)), "gather_parts"
    )
    *grads, grad_w_out, rel_out, norms, b_in_out, both_boxes = last_call(
        spot, whole(first_part, grad_w_down), whole(second_part, grad_w_down), rel_table.shape[0] // docs, model
    )
    b_in_out = b_in_out.reshape(-1)
    xb, yb = both_boxes[:, :heads], both_boxes[:, 64 : 64 + heads]
    return (
        block_out[None], grad_tokens[None], norms[0], norms[1], grads[0], grads[1], grads[2], grad_w_out,
        rel_out, xb, yb, norms[2], norms[3], grad_w_in, b_in_out, grad_w_down,
    )


def choose(*args):
    docs, parts = lax.axis_size("docs"), lax.axis_size("blk")
    tokens, w_in = args[0], args[15]
    model, units = w_in.shape
    fits = (
        parts == blocks
        and tokens.shape[1] == lanes
        and model // docs == lanes
        and units // docs == parts * lanes
        and docs & (docs - 1) == 0
        and docs > 2
        and units == blocks * model
    )
    return (shards_tiles if fits else shards)(*args)


def solution(mesh):
    rows = P("docs", "blk", None)
    placed = (
        rows, P("docs"), P("docs", "blk"), P(None, "docs", "blk"),
        *([P()] * 14), rows,
    )
    over_docs, over_docs2 = P("docs"), P("docs", None)
    return jax.shard_map(
        choose,
        mesh=mesh,
        in_specs=placed,
        out_specs=(
            rows, rows, over_docs, over_docs, over_docs2, over_docs2, over_docs2, over_docs2,
            over_docs2, over_docs2, over_docs2, over_docs, over_docs, over_docs2, over_docs, over_docs2,
        ),
        check_vma=False,
    )
```

```python
import functools
import math

import jax
import jax.numpy as jnp
from jax import lax
from jax.experimental import pallas as pl
from jax.experimental.pallas import tpu as pltpu
from jax.sharding import PartitionSpec as P

norm_eps = 1e-05
mask_value = -1e30
f32 = jnp.float32
bf16 = jnp.bfloat16
lanes = 128


def dot(a, b, contract=((1,), (0,))):
    return lax.dot_general(a, b, (contract, ((), ())), preferred_element_type=f32)


def pick(table, index):
    return jnp.take_along_axis(table, index, axis=1, mode="promise_in_bounds")


def ahead_of(first, second):
    return jnp.clip(first - second, -64, 63) + 64


def attn_fwd_kernel(
    place, x_ref, wq_ref, wk_ref, wv_ref, rel_ref, tab_ref, row_ref, col_ref,
    att_ref, probs_ref, qkv_ref, relkq_ref, key_rel,
):
    scale = 1.0 / math.sqrt(192.0)
    step = pl.program_id(0)
    rows = x_ref.shape[0]
    width = wq_ref.shape[1]
    heads = tab_ref.shape[1]
    size = width // heads
    tiles = rows // lanes

    @pl.when(step == 0)
    def _():
        for at, w_ref in enumerate((wq_ref, wk_ref, wv_ref)):
            for t in range(tiles):
                qkv_ref[t * lanes : (t + 1) * lanes, at * width : (at + 1) * width] = dot(
                    x_ref[t * lanes : (t + 1) * lanes, :], w_ref[...]
                ).astype(bf16)
        relkq_ref[:, :width] = dot(rel_ref[...], wk_ref[...]).astype(bf16)
        relkq_ref[:, width:] = dot(rel_ref[...], wq_ref[...]).astype(bf16)
        for h in range(heads):
            key_rel[h] = (
                dot(
                    qkv_ref[:, width + h * size : width + (h + 1) * size],
                    relkq_ref[:, width + h * size : width + (h + 1) * size],
                    ((1,), (1,)),
                )
                .astype(bf16)
                .astype(f32)
            )

    here = pl.ds(pl.multiple_of(step * lanes, lanes), lanes)
    pos_i = col_ref[here, 0:1]
    cx_i = col_ref[here, 1:2]
    cy_i = col_ref[here, 2:3]
    own_row = row_ref[0:1, here]
    ahead, mirror, across, vertical = [], [], [], []
    for t in range(tiles):
        span = slice(t * lanes, (t + 1) * lanes)
        ahead.append(ahead_of(pos_i, row_ref[0:1, span]))
        mirror.append(ahead_of(col_ref[span, 0:1], own_row))
        across.append(jnp.clip(jnp.right_shift(cx_i - row_ref[1:2, span], 5), -32, 31) + 32)
        vertical.append(jnp.clip(jnp.right_shift(cy_i - row_ref[2:3, span], 5), -32, 31) + 96)
    valid = row_ref[3:4, :] > 0
    for h in range(heads):
        cols = slice(h * size, (h + 1) * size)
        query = qkv_ref[here, cols]
        rel_scores = (
            dot(query, relkq_ref[:, cols], ((1,), (1,))).astype(bf16).astype(f32)
        )
        table = jnp.broadcast_to(tab_ref[0, h : h + 1, :], (lanes, lanes))
        pieces = []
        for t in range(tiles):
            span = slice(t * lanes, (t + 1) * lanes)
            content = dot(
                query, qkv_ref[span, width + h * size : width + (h + 1) * size], ((1,), (1,))
            )
            mirrored = pick(key_rel[h, span, :], mirror[t]).T
            bias = pick(table, across[t]) + pick(table, vertical[t])
            pieces.append(
                scale * (content + pick(rel_scores, ahead[t]) + mirrored) + bias
            )
        scores = jnp.where(valid, jnp.concatenate(pieces, axis=1), mask_value)
        top = jnp.max(scores, axis=1, keepdims=True)
        raised = jnp.exp(scores - top)
        probs = (raised * (1.0 / jnp.sum(raised, axis=1, keepdims=True))).astype(bf16)
        probs_ref[h] = probs
        att_ref[:, cols] = dot(
            probs, qkv_ref[:, 2 * width + h * size : 2 * width + (h + 1) * size]
        ).astype(bf16)


def attn_fwd(place, x_all, w_query, w_key, w_value, rel_table, tables, ints_row, ints_col):
    rows, model = x_all.shape
    parts, heads, _ = tables.shape
    width = w_query.shape[1] // parts
    tiles = rows // lanes
    buckets = rel_table.shape[0]
    whole = lambda *shape: pl.BlockSpec(shape, lambda i, at: (0,) * len(shape))
    column = pl.BlockSpec((model, width), lambda i, at: (0, at[0]))
    return pl.pallas_call(
        attn_fwd_kernel,
        out_shape=(
            jax.ShapeDtypeStruct((rows, width), bf16),
            jax.ShapeDtypeStruct((heads, rows, rows), bf16),
            jax.ShapeDtypeStruct((rows, 3 * width), bf16),
            jax.ShapeDtypeStruct((buckets, 2 * width), bf16),
        ),
        grid_spec=pltpu.PrefetchScalarGridSpec(
            num_scalar_prefetch=1,
            grid=(tiles,),
            in_specs=[
                whole(rows, model),
                column,
                column,
                column,
                whole(buckets, model),
                pl.BlockSpec((1, heads, lanes), lambda i, at: (at[0], 0, 0)),
                whole(8, rows),
                whole(rows, 8),
            ],
            out_specs=[
                pl.BlockSpec((lanes, width), lambda i, at: (i, 0)),
                pl.BlockSpec((heads, lanes, rows), lambda i, at: (0, i, 0)),
                whole(rows, 3 * width),
                whole(buckets, 2 * width),
            ],
            scratch_shapes=[pltpu.VMEM((heads, rows, lanes), f32)],
        ),
        compiler_params=pltpu.CompilerParams(vmem_limit_bytes=40 << 20),
        cost_estimate=pl.CostEstimate(
            flops=6 * 10**9, transcendentals=10**6, bytes_accessed=8 << 20
        ),
        name="attn_fwd",
    )(place, x_all, w_query, w_key, w_value, rel_table, tables, ints_row, ints_col)


def attn_bwd_kernel(
    ga_ref, qkv_ref, probs_ref, relkq_ref, row_ref, col_ref,
    dqkv_ref, drel_ref, boxes_ref, ds_ref,
):
    scale = 1.0 / math.sqrt(192.0)
    rows = ga_ref.shape[0]
    heads = probs_ref.shape[0]
    width = ga_ref.shape[1]
    size = width // heads
    tiles = rows // lanes
    span_width = 3 * lanes
    drel_ref[...] = jnp.zeros_like(drel_ref)
    boxes_ref[...] = jnp.zeros_like(boxes_ref)
    window = lax.broadcasted_iota(jnp.int32, (rows, span_width), 1)
    bucket = lax.broadcasted_iota(jnp.int32, (lanes, lanes), 1)
    label = lax.broadcasted_iota(jnp.int32, (rows, lanes), 1)
    all_pos = col_ref[:, 0:1]
    all_x, all_y = col_ref[:, 1:2], col_ref[:, 2:3]
    sector_x, sector_y = jnp.right_shift(all_x, 5), jnp.right_shift(all_y, 5)
    hot_x = (label == sector_x).astype(bf16)
    hot_y = (label == sector_y + 64).astype(bf16)
    hot_both = ((label == sector_x) | (label == sector_y + 64)).astype(bf16)

    def histogram(sums, total, at, base_row):
        first = at - base_row + (2 * lanes // 2 - 1) - bucket
        low = jnp.bitwise_and(first, lanes - 1)
        group = jnp.right_shift(first, 7)
        found = jnp.where(
            group == 0,
            pick(sums[:, :lanes], low),
            jnp.where(
                group == 1,
                pick(sums[:, lanes : 2 * lanes], low),
                pick(sums[:, 2 * lanes :], low),
            ),
        )
        found = jnp.where(bucket == 0, total, found)
        later = jnp.where(bucket == lanes - 1, 0.0, pltpu.roll(found, lanes - 1, 1))
        return found - later

    def by_rows(ib, carry):
        here = pl.ds(pl.multiple_of(ib * lanes, lanes), lanes)
        pos_i = col_ref[here, 0:1]
        cx_i, cy_i = col_ref[here, 1:2], col_ref[here, 2:3]
        base = jnp.min(pos_i, axis=0, keepdims=True)
        below = (all_pos <= base - 63 + window).astype(bf16)
        short_x = jnp.bitwise_and(cx_i, 31) < jnp.bitwise_and(row_ref[1:2, :], 31)
        short_y = jnp.bitwise_and(cy_i, 31) < jnp.bitwise_and(row_ref[2:3, :], 31)
        step_x = jnp.right_shift(cx_i, 5) + 32 - bucket
        step_y = jnp.right_shift(cy_i, 5) + 32 - (bucket - 64)
        in_x = (bucket < 64) & (step_x >= 0) & (step_x < 32)
        in_y = (bucket >= 64) & (step_y >= 0) & (step_y < 32)
        seek = jnp.where(in_x, step_x, jnp.where(in_y, step_y + 64, 0))
        inside = in_x | in_y
        for h in range(heads):
            cols = slice(h * size, (h + 1) * size)
            kcols = slice(width + h * size, width + (h + 1) * size)
            vcols = slice(2 * width + h * size, 2 * width + (h + 1) * size)
            probs = probs_ref[h, here, :].astype(f32)
            gained = dot(ga_ref[here, cols], qkv_ref[:, vcols], ((1,), (1,)))
            row_dots = jnp.sum(probs * gained, axis=1, keepdims=True)
            grad32 = probs * (gained - row_dots)
            grad = grad32.astype(bf16)
            ds_ref[h, here, :] = grad
            exact = grad.astype(f32)
            total = jnp.sum(exact, axis=1, keepdims=True)
            rel = histogram(dot(grad, below), total, pos_i, base)
            rel = (scale * rel).astype(bf16)
            query = qkv_ref[here, cols]
            dqkv_ref[here, cols] = (
                scale * dot(grad, qkv_ref[:, kcols]) + dot(rel, relkq_ref[:, cols])
            ).astype(bf16)
            drel_ref[:, cols] += dot(rel, query, ((0,), (0,)))
            grad_x = jnp.where(short_x, exact, 0.0).astype(bf16)
            grad_y = jnp.where(short_y, exact, 0.0).astype(bf16)
            plain = dot(grad, hot_both)
            less = dot(grad_x, hot_x) + dot(grad_y, hot_y)
            plain = jnp.where(inside, pick(plain, seek), 0.0)
            less = jnp.where(inside, pick(less, seek), 0.0)
            boxes_ref[2 * h : 2 * h + 1, :] += jnp.sum(plain, axis=0, keepdims=True)
            boxes_ref[2 * h + 1 : 2 * h + 2, :] += jnp.sum(less, axis=0, keepdims=True)
        return carry

    lax.fori_loop(0, tiles, by_rows, 0)

    def by_columns(jb, carry):
        here = pl.ds(pl.multiple_of(jb * lanes, lanes), lanes)
        pos_j = col_ref[here, 0:1]
        base = jnp.min(pos_j, axis=0, keepdims=True)
        below = (all_pos <= base - 63 + window).astype(bf16)
        for h in range(heads):
            cols = slice(h * size, (h + 1) * size)
            kcols = slice(width + h * size, width + (h + 1) * size)
            vcols = slice(2 * width + h * size, 2 * width + (h + 1) * size)
            grad = ds_ref[h, :, here]
            total = dot(grad, jnp.ones((rows, lanes), bf16), ((0,), (0,)))
            sums = dot(grad, below, ((0,), (0,)))
            mirror = (scale * histogram(sums, total, pos_j, base)).astype(bf16)
            dqkv_ref[here, kcols] = (
                scale * dot(grad, qkv_ref[:, cols], ((0,), (0,)))
                + dot(mirror, relkq_ref[:, kcols])
            ).astype(bf16)
            drel_ref[:, kcols] += dot(mirror, qkv_ref[here, kcols], ((0,), (0,)))
            dqkv_ref[here, vcols] = dot(
                probs_ref[h, :, here], ga_ref[:, cols], ((0,), (0,))
            ).astype(bf16)
        return carry

    lax.fori_loop(0, tiles, by_columns, 0)


def attn_bwd(grad_att, qkv, probs, relkq, ints_row, ints_col):
    rows, width = grad_att.shape
    heads = probs.shape[0]
    buckets = relkq.shape[0]
    inside = pl.BlockSpec(memory_space=pltpu.VMEM)
    return pl.pallas_call(
        attn_bwd_kernel,
        out_shape=(
            jax.ShapeDtypeStruct((rows, 3 * width), bf16),
            jax.ShapeDtypeStruct((buckets, 2 * width), f32),
            jax.ShapeDtypeStruct((2 * heads, lanes), f32),
        ),
        in_specs=[inside] * 6,
        out_specs=[inside] * 3,
        scratch_shapes=[pltpu.VMEM((heads, rows, rows), bf16)],
        compiler_params=pltpu.CompilerParams(vmem_limit_bytes=40 << 20),
        cost_estimate=pl.CostEstimate(
            flops=12 * 10**9, transcendentals=0, bytes_accessed=6 << 20
        ),
        name="attn_bwd",
    )(grad_att, qkv, probs, relkq, ints_row, ints_col)


def layer_norm(inputs, gain_vec, bias_vec):
    row_mean = jnp.mean(inputs, axis=-1, keepdims=True)
    centered = inputs - row_mean
    inverse = lax.rsqrt(jnp.mean(centered * centered, axis=-1, keepdims=True) + norm_eps)
    normed = centered * inverse
    return (normed * gain_vec + bias_vec, normed, inverse)


def norm_backward(grad_in, normed, inverse, gain_vec):
    grad_gain = jnp.sum(grad_in * normed, axis=0)
    grad_shift = jnp.sum(grad_in, axis=0)
    scaled = grad_in * gain_vec
    grad_input = inverse * (
        scaled
        - jnp.mean(scaled, axis=-1, keepdims=True)
        - normed * jnp.mean(scaled * normed, axis=-1, keepdims=True)
    )
    return (grad_input, grad_gain, grad_shift)


def bits_of(count):
    assert count & (count - 1) == 0
    return [1 << at for at in range(count.bit_length() - 1)]


def swap(array, axis, by):
    count = lax.axis_size(axis)
    return lax.ppermute(array, axis, [(i, i ^ by) for i in range(count)])


def offsets(count):
    order = [0]
    for bit in reversed(bits_of(count)):
        order = order + [at ^ bit for at in order]
    return order


def spread(shared, pieces):
    count = lax.axis_size("blk")
    got = {0: shared} if shared is not None else {}
    held = {(0, at): piece for at, piece in pieces.items()} if pieces else {}
    for bit in reversed(bits_of(count)):
        out_keys = [key for key in sorted(held) if key[1] & bit]
        out_shared = sorted(got)
        parts = [got[at] for at in out_shared] + [held[key] for key in out_keys]
        if bit == 1:
            came = [swap(part, "blk", bit) for part in parts]
        else:
            came = swap(jnp.concatenate(parts, axis=1), "blk", bit)
            edges = [0]
            for part in parts:
                edges.append(edges[-1] + part.shape[1])
            came = [came[:, a:b] for a, b in zip(edges[:-1], edges[1:])]
        for at, part in zip(out_shared, came):
            got[at ^ bit] = part
        for key, part in zip(out_keys, came[len(out_shared) :]):
            del held[key]
            held[(key[0] ^ bit, key[1] ^ bit)] = part
    return got, {key[0]: part for key, part in held.items()}


def by_place(stacked, place):
    count = len(stacked)
    for bit in bits_of(count):
        turned = (place & bit) != 0
        stacked = [jnp.where(turned, stacked[at ^ bit], stacked[at]) for at in range(count)]
    return stacked


def chunk_order(count):
    order = [0]
    for bit in reversed(bits_of(count)):
        order = order + [at | bit for at in order]
    return order


def for_docs(chunks, doc_place):
    moved = by_place(chunks, doc_place)
    return [moved[at] for at in chunk_order(len(chunks))]


def halve(keep, send, bits):
    count = lax.axis_size("docs")
    first = True
    current = keep
    for bit in bits:
        if not first:
            half = current.shape[0] // 2
            current, send = current[:half], current[half:]
        first = False
        came = swap(send, "docs", bit)
        current = (current.astype(f32) + came.astype(f32)).astype(bf16)
    return current


def shards(
    tokens, lengths, positions, token_boxes, ln1_gain, ln1_bias, w_query, w_key, w_value, w_out,
    rel_table, xbias_table, ybias_table, ln2_gain, ln2_bias, w_in, b_in, w_down, cotangent,
):
    doc_count, row_count, model = tokens.shape
    assert doc_count == 1 and row_count == lanes
    parts = lax.axis_size("blk")
    docs = lax.axis_size("docs")
    place = lax.axis_index("blk")
    doc_place = lax.axis_index("docs")
    heads = xbias_table.shape[1]
    own_heads = heads // parts
    width = model // parts
    buckets = rel_table.shape[0]
    boxes = xbias_table.shape[0]
    hidden_units = w_in.shape[1]
    order = offsets(parts)
    x_own = tokens[0]

    centers_x = jnp.right_shift(token_boxes[0] + token_boxes[2], 1)
    centers_y = jnp.right_shift(token_boxes[1] + token_boxes[3], 1)
    own_ints = jnp.concatenate([positions, centers_x, centers_y], axis=0)
    coded = jnp.concatenate(
        [jnp.right_shift(own_ints, 5), jnp.bitwise_and(own_ints, 31)], axis=0
    ).astype(bf16)
    coded = jnp.pad(coded.reshape(1, -1), ((0, 7), (0, model - coded.size)))
    got, _ = spread(jnp.concatenate([x_own, coded], axis=0), None)
    x_all = jnp.concatenate([got[at][:row_count] for at in order], axis=0)
    decoded = jnp.concatenate(
        [got[at][row_count : row_count + 1, : 6 * row_count].reshape(6, row_count) for at in order], axis=1
    ).astype(jnp.int32)
    ints = decoded[:3] * 32 + decoded[3:]
    slot_ids = jnp.concatenate(
        [
            (place ^ at) * row_count + lax.broadcasted_iota(jnp.int32, (1, row_count), 1)
            for at in order
        ],
        axis=1,
    )
    ints = jnp.concatenate(
        [ints, (slot_ids < lengths[0]).astype(jnp.int32), jnp.zeros((4, ints.shape[1]), jnp.int32)],
        axis=0,
    )
    ints_col = ints.T
    tables = jnp.concatenate([xbias_table.T, ybias_table.T], axis=1).astype(f32)
    tables = tables.reshape(parts, own_heads, 2 * boxes)

    attended_own, probs, qkv, relkq = attn_fwd(
        place.reshape(1), x_all, w_query, w_key, w_value, rel_table, tables, ints, ints_col
    )

    def row_block(array, at):
        t = order.index(at)
        return array[t * row_count : (t + 1) * row_count]

    _, came = spread(None, {at: row_block(attended_own, at) for at in order})
    attended = jnp.concatenate(by_place([came[at] for at in range(parts)], place), axis=1)
    attn_out = jnp.dot(attended, w_out, preferred_element_type=f32)
    hidden, normed1, inverse1 = layer_norm(x_own.astype(f32) + attn_out, ln1_gain, ln1_bias)
    hidden_low = hidden.astype(bf16)
    up_proj = jnp.dot(hidden_low, w_in, preferred_element_type=f32) + b_in
    activated, gelu_back = jax.vjp(lambda inputs: jax.nn.gelu(inputs, approximate=True), up_proj)
    activated_low = activated.astype(bf16)
    ffn_out = jnp.dot(activated_low, w_down, preferred_element_type=f32)
    normed_out, normed2, inverse2 = layer_norm(hidden + ffn_out, ln2_gain, ln2_bias)
    block_out = normed_out.astype(bf16)[None]
    grad_output = cotangent[0].astype(f32)
    grad_mix, grad_ln2_gain, grad_ln2_bias = norm_backward(grad_output, normed2, inverse2, ln2_gain)
    grad_ffn = grad_mix.astype(bf16)
    grad_act = jnp.dot(grad_ffn, w_down.T, preferred_element_type=f32)
    grad_up = gelu_back(grad_act)[0].astype(bf16)
    grad_b_in = jnp.sum(grad_up, axis=0, dtype=f32)
    grad_hidden = grad_mix + jnp.dot(grad_up, w_in.T, preferred_element_type=f32)
    grad_resid, grad_ln1_gain, grad_ln1_bias = norm_backward(
        grad_hidden, normed1, inverse1, ln1_gain
    )
    grad_attn = grad_resid.astype(bf16)
    grad_att = jnp.dot(grad_attn, w_out.T, preferred_element_type=f32).astype(bf16)

    def column_block(array, at, count):
        size = array.shape[1] // count
        return lax.dynamic_slice_in_dim(array, at * size, size, axis=1)

    _, came = spread(None, {at: column_block(grad_att, place ^ at, parts) for at in order})
    grad_att_own = jnp.concatenate([came[at] for at in order], axis=0)
    dqkv, drel, box_sums = attn_bwd(grad_att_own, qkv, probs, relkq, ints, ints_col)

    def docs_columns(array):
        size = array.shape[1] // docs
        chunks = [array[:, at * size : (at + 1) * size] for at in range(docs)]
        return jnp.concatenate(for_docs(chunks, doc_place), axis=1)

    strips = activated_low.reshape(row_count, docs, parts, -1)
    strips = [
        docs_columns(
            lax.dynamic_index_in_dim(strips, place ^ at, axis=2, keepdims=False).reshape(row_count, -1)
        )
        for at in range(parts)
    ]
    got, came = spread(docs_columns(hidden_low), dict(enumerate(strips)))
    hidden_all = jnp.concatenate([got[at] for at in order], axis=0)
    activated_all = jnp.concatenate([came[at] for at in order], axis=0)
    got, came = spread(grad_ffn, {at: column_block(grad_up, place ^ at, parts) for at in order})
    grad_ffn_all = jnp.concatenate([got[at] for at in order], axis=0)
    grad_up_all = jnp.concatenate([came[at] for at in order], axis=0)
    got, came = spread(
        docs_columns(attended), {at: column_block(grad_attn, place ^ at, parts) for at in order}
    )
    attended_all = jnp.concatenate([got[at] for at in order], axis=0)
    grad_attn_all = jnp.concatenate([came[at] for at in order], axis=0)

    def halves(left, right):
        middle = left.shape[1] // 2
        send = dot(left[:, middle:], right, ((0,), (0,))).astype(bf16)
        keep = dot(left[:, :middle], right, ((0,), (0,))).astype(bf16)
        return keep, send

    bits = bits_of(docs)
    down_part = halve(*halves(activated_all, grad_ffn_all), bits)
    in_part = halve(*halves(hidden_all, grad_up_all), bits)
    out_part = halve(*halves(attended_all, grad_attn_all), bits)

    drel_low = drel.astype(bf16)
    left = docs_columns(jnp.concatenate([x_all, rel_table], axis=0))
    right = jnp.concatenate(
        [
            dqkv,
            jnp.concatenate(
                [drel_low[:, width:], drel_low[:, :width], jnp.zeros((buckets, width), bf16)], axis=1
            ),
        ],
        axis=0,
    )
    grad_rel_table = dot(
        drel_low[:, :width], column_block(w_key, place, parts), ((1,), (1,))
    ) + dot(drel_low[:, width:], column_block(w_query, place, parts), ((1,), (1,)))
    plain, less = box_sums[0::2], box_sums[1::2]

    def box_grad(at):
        plain_here, less_here = plain[:, at : at + boxes], less[:, at : at + boxes]
        later = jnp.pad(less_here[:, 1:], ((0, 0), (0, 1)))
        grad = (plain_here - less_here + later).T
        return lax.dynamic_update_slice(jnp.zeros((boxes, heads), f32), grad, (0, place * own_heads))

    small = jnp.concatenate(
        [
            grad_rel_table.reshape(docs, -1),
            grad_ln1_gain.reshape(docs, -1),
            grad_ln1_bias.reshape(docs, -1),
            grad_ln2_gain.reshape(docs, -1),
            grad_ln2_bias.reshape(docs, -1),
            grad_b_in.reshape(docs, -1),
            box_grad(0).reshape(docs, -1),
            box_grad(boxes).reshape(docs, -1),
        ],
        axis=1,
    ).astype(bf16)
    small_width = small.shape[1]
    across = 3 * width
    small = jnp.pad(small, ((0, 0), (0, -small_width % (8 * across))))
    small = for_docs([small[at] for at in range(docs)], doc_place)
    small = jnp.stack(small).reshape(docs, -1, across)
    keep, send = halves(left, right)
    middle = docs // 2
    chunk_rows = model // docs

    def with_small(main, extra):
        main = main.reshape(middle, chunk_rows, across)
        return jnp.concatenate([main, extra], axis=1).reshape(-1, across)

    qkv_part = halve(with_small(keep, small[:middle]), with_small(send, small[middle:]), bits)

    _, came = spread(None, {at: row_block(dqkv, at) for at in order})
    came = by_place([came[at] for at in range(parts)], place)
    grad_tokens = grad_resid
    for at, weight in enumerate((w_query, w_key, w_value)):
        grad = jnp.concatenate([rows[:, at * width : (at + 1) * width] for rows in came], axis=1)
        grad_tokens = grad_tokens + dot(grad, weight, ((1,), (1,)))

    def whole(part):
        got, _ = spread(part, None)
        return by_place([got[at] for at in range(parts)], place)

    grad_w_down = jnp.concatenate(whole(down_part), axis=0).astype(f32)
    grad_w_in = jnp.concatenate(whole(in_part), axis=1).astype(f32)
    grad_w_out = jnp.concatenate(whole(out_part), axis=1).astype(f32)
    pieces = whole(qkv_part)
    grads = [
        jnp.concatenate(
            [piece[:chunk_rows, at * width : (at + 1) * width] for piece in pieces], axis=1
        ).astype(f32)
        for at in range(3)
    ]
    total = sum(piece[chunk_rows:].astype(f32) for piece in pieces).reshape(-1)
    sizes = [
        (buckets // docs, model),
        (model // docs,),
        (model // docs,),
        (model // docs,),
        (model // docs,),
        (hidden_units // docs,),
        (boxes // docs, heads),
        (boxes // docs, heads),
    ]
    small_out = []
    start = 0
    for size in sizes:
        small_out.append(total[start : start + math.prod(size)].reshape(size))
        start += math.prod(size)
    rel_out, ln1g, ln1b, ln2g, ln2b, b_in_out, xb, yb = small_out
    return (
        block_out, grad_tokens[None], ln1g, ln1b, grads[0], grads[1], grads[2], grad_w_out,
        rel_out, xb, yb, ln2g, ln2b, grad_w_in, b_in_out, grad_w_down,
    )


blocks = 4
slots = (0, 2, 1, 3)


def rows_of(handle, tile=None, column=None):
    array, lead = handle if isinstance(handle, tuple) else (handle, None)
    shape = array.shape[-2:] if tile is None else tile
    column = column or (lambda *grid: 0)
    if lead is None:
        return pl.BlockSpec(shape, lambda *grid: (0, column(*grid)))
    return pl.BlockSpec((None,) + shape, lambda *grid: (lead, 0, column(*grid)))


def array_of(handle):
    return handle[0] if isinstance(handle, tuple) else handle


def full(shape):
    return pl.BlockSpec(shape, lambda *grid: (0,) * len(shape))


def cost(us):
    return pl.CostEstimate(flops=int(us * 3 * 10**8), transcendentals=0, bytes_accessed=0)


def ordered(array, *before):
    return lax.optimization_barrier((array,) + before)[0]


def in_hbm(array):
    return pltpu.with_memory_space_constraint(array, pltpu.HBM)


def params(limit):
    return pltpu.CompilerParams(vmem_limit_bytes=limit << 20)


def gelu_parts(u):
    root = math.sqrt(2.0 / math.pi)
    inner = jnp.tanh(root * (u + 0.044715 * u * u * u))
    value = 0.5 * u * (1.0 + inner)
    slope = 0.5 * (1.0 + inner) + 0.5 * u * (1.0 - inner * inner) * root * (
        1.0 + 3.0 * 0.044715 * u * u
    )
    return value, slope


def scores_kernel(
    at_ref, x0, x1, x2, x3, i0, i1, i2, i3, wq_ref, wk_ref, wv_ref, rel_ref, tab_ref,
    own_ref, core_ref, far_ref, probs_ref, qkv_ref, relkq_ref, row_ref, col_ref,
    key_rel, queries, keys_t, values, rel_keys_t, sector_hot,
):
    scale = 1.0 / math.sqrt(192.0)
    step = pl.program_id(0)
    rows = blocks * lanes
    width = wq_ref.shape[1]
    heads = tab_ref.shape[1]
    size = width // heads

    @pl.when(step == 0)
    def _():
        for t, (x_ref, i_ref) in enumerate(zip((x0, x1, x2, x3), (i0, i1, i2, i3))):
            span = slice(t * lanes, (t + 1) * lanes)
            for at, w_ref in enumerate((wq_ref, wk_ref, wv_ref)):
                part = dot(x_ref[...], w_ref[...]).astype(bf16)
                qkv_ref[span, at * width : (at + 1) * width] = part
                if at == 1:
                    keys_t[:, span] = part.astype(f32).T.astype(bf16)
                else:
                    for h in range(heads):
                        (queries, None, values)[at][h, span, :] = part[:, h * size : (h + 1) * size]
            first = jnp.bitwise_xor(at_ref[0], slots[t]) * lanes
            slot = first + lax.broadcasted_iota(jnp.int32, (8, lanes), 1)
            kind = lax.broadcasted_iota(jnp.int32, (8, lanes), 0)
            ints = jnp.where(kind == 3, (slot < at_ref[1]).astype(jnp.int32), i_ref[...])
            row_ref[:, span] = ints
            col_ref[span, :] = ints.astype(f32).T.astype(jnp.int32)
        sector = lax.broadcasted_iota(jnp.int32, (32, rows), 0)
        for k in range(2):
            hot = (jnp.right_shift(row_ref[1 + k : 2 + k, :], 5) == sector).astype(f32).astype(bf16)
            sector_hot[k * 32 : (k + 1) * 32, :] = hot
        rel_keys = dot(rel_ref[...], wk_ref[...])
        relkq_ref[:, :width] = rel_keys.astype(bf16)
        rel_keys_t[...] = rel_keys.T.astype(bf16)
        relkq_ref[:, width:] = dot(rel_ref[...], wq_ref[...]).astype(bf16)
        for h in range(heads):
            cols = slice(width + h * size, width + (h + 1) * size)
            key_rel[h] = (
                dot(qkv_ref[:, cols], relkq_ref[:, cols], ((1,), (1,))).astype(bf16).astype(f32)
            )

    here = pl.ds(pl.multiple_of(step * lanes, lanes), lanes)
    pos_i = col_ref[here, 0:1]
    cx_i = col_ref[here, 1:2]
    cy_i = col_ref[here, 2:3]
    own_row = row_ref[0:1, here]
    lane = lax.broadcasted_iota(jnp.int32, (lanes, lanes), 1)
    on_x = jnp.bitwise_and(jnp.right_shift(lane, 5), 1) == 0
    seek = (
        jnp.where(on_x, jnp.right_shift(cx_i, 5), jnp.right_shift(cy_i, 5) + 64)
        + 32
        - jnp.bitwise_and(lane, 31)
        - (lane >= 64).astype(jnp.int32)
    )
    short_x = jnp.bitwise_and(cx_i, 31) < jnp.bitwise_and(row_ref[1:2, :], 31)
    short_y = jnp.bitwise_and(cy_i, 31) < jnp.bitwise_and(row_ref[2:3, :], 31)
    ahead, mirror = [], []
    for t in range(blocks):
        span = slice(t * lanes, (t + 1) * lanes)
        ahead.append(ahead_of(pos_i, row_ref[0:1, span]))
        mirror.append(ahead_of(col_ref[span, 0:1], own_row))
    valid = row_ref[3:4, :] > 0
    attended = []
    for h in range(heads):
        cols = slice(h * size, (h + 1) * size)
        query = queries[h, here, :]
        rel_scores = dot(query, rel_keys_t[cols, :]).astype(bf16).astype(f32)
        table = jnp.broadcast_to(tab_ref[0, h : h + 1, :], (lanes, lanes))
        by_sector = pick(table, seek).astype(bf16)
        content = dot(query, keys_t[cols, :])
        plain_x = dot(by_sector[:, 0:32], sector_hot[0:32, :])
        plain_y = dot(by_sector[:, 32:64], sector_hot[32:64, :])
        less_x = dot(by_sector[:, 64:96], sector_hot[0:32, :])
        less_y = dot(by_sector[:, 96:128], sector_hot[32:64, :])
        bias = jnp.where(short_x, less_x, plain_x) + jnp.where(short_y, less_y, plain_y)
        moved = []
        for t in range(blocks):
            span = slice(t * lanes, (t + 1) * lanes)
            moved.append(pick(rel_scores, ahead[t]) + pick(key_rel[h, span, :], mirror[t]).T)
        scores = scale * (content + jnp.concatenate(moved, axis=1)) + bias
        scores = jnp.where(valid, scores, mask_value)
        top = jnp.max(scores, axis=1, keepdims=True)
        raised = jnp.exp(scores - top)
        probs = (raised * (1.0 / jnp.sum(raised, axis=1, keepdims=True))).astype(bf16)
        probs_ref[h] = probs
        attended.append(dot(probs, values[h]).astype(bf16))
    attended = jnp.concatenate(attended, axis=1)
    for t, target in enumerate((own_ref, far_ref.at[0], core_ref, far_ref.at[1])):

        @pl.when(step == t)
        def _(target=target):
            target[...] = attended


def scores_call(at, xs, ints, w_query, w_key, w_value, rel_table, tables):
    rows, model = blocks * lanes, w_query.shape[0]
    parts, heads, _ = tables.shape
    width = w_query.shape[1] // parts
    buckets = rel_table.shape[0]
    column = pl.BlockSpec((model, width), lambda i, at: (0, at[0]))
    return pl.pallas_call(
        scores_kernel,
        out_shape=(
            jax.ShapeDtypeStruct((lanes, width), bf16),
            jax.ShapeDtypeStruct((lanes, width), bf16),
            jax.ShapeDtypeStruct((2, lanes, width), bf16),
            pltpu.HBM((heads, rows, rows), bf16),
            pltpu.HBM((rows, 3 * width), bf16),
            pltpu.HBM((buckets, 2 * width), bf16),
            pltpu.HBM((8, rows), jnp.int32),
            pltpu.HBM((rows, 8), jnp.int32),
        ),
        grid_spec=pltpu.PrefetchScalarGridSpec(
            num_scalar_prefetch=1,
            grid=(blocks,),
            in_specs=[rows_of(x) for x in xs]
            + [rows_of(i) for i in ints]
            + [
                column,
                column,
                column,
                full((buckets, model)),
                pl.BlockSpec((1, heads, lanes), lambda i, at: (at[0], 0, 0)),
            ],
            out_specs=[
                full((lanes, width)),
                full((lanes, width)),
                full((2, lanes, width)),
                pl.BlockSpec((heads, lanes, rows), lambda i, at: (0, i, 0)),
                full((rows, 3 * width)),
                full((buckets, 2 * width)),
                full((8, rows)),
                full((rows, 8)),
            ],
            scratch_shapes=[
                pltpu.VMEM((heads, rows, lanes), f32),
                pltpu.VMEM((heads, rows, width // heads), bf16),
                pltpu.VMEM((width, rows), bf16),
                pltpu.VMEM((heads, rows, width // heads), bf16),
                pltpu.VMEM((width, buckets), bf16),
                pltpu.VMEM((64, rows), bf16),
            ],
        ),
        compiler_params=params(18),
        cost_estimate=cost(25),
        name="scores",
    )(
        at, *map(array_of, xs), *map(array_of, ints), w_query, w_key, w_value, rel_table, tables
    )


def up_kernel(
    at_ref, a0, a1, a2, a3, x_ref, wout_ref, gain_ref, bias_ref, win_ref, bin_ref,
    far_ref, core_ref, own_ref, act_ref, slope_ref, normed_ref, inverse_ref, attended_ref,
    hidden_low,
):
    step = pl.program_id(0)
    width = a0.shape[1]
    tile = win_ref.shape[1]

    @pl.when(step == 0)
    def _():
        total = x_ref[...].astype(f32)
        for t, piece in enumerate((a0, a1, a2, a3)):
            first = pl.multiple_of(jnp.bitwise_xor(at_ref[0], slots[t]) * width, width)
            total = total + dot(piece[...], wout_ref[pl.ds(first, width), :])
            attended_ref[:, pl.ds(first, width)] = piece[...]
        centered = total - jnp.mean(total, axis=1, keepdims=True)
        inverse = lax.rsqrt(jnp.mean(centered * centered, axis=1, keepdims=True) + norm_eps)
        normed = centered * inverse
        normed_ref[...] = normed
        inverse_ref[...] = jnp.broadcast_to(inverse, inverse_ref.shape)
        hidden = (normed * gain_ref[...] + bias_ref[...]).astype(bf16)
        hidden_low[...] = hidden

    value, slope = gelu_parts(dot(hidden_low[...], win_ref[...]) + bin_ref[...])
    value = value.astype(bf16)
    act_ref[...] = value
    slope_ref[...] = slope.astype(bf16)
    strip = tile // blocks
    here = pl.ds(pl.multiple_of(step * strip, strip), strip)
    for t, target in enumerate((own_ref, far_ref.at[0], core_ref, far_ref.at[1])):
        first = pl.multiple_of(jnp.bitwise_xor(at_ref[0], slots[t]) * strip, strip)
        target[:, here] = act_ref[:, pl.ds(first, strip)]


def up_call(at, pieces, x_own, w_out, gain, bias, w_in, b_in, docs):
    rows, model = x_own.shape
    units = w_in.shape[1]
    tile = units // docs
    quarter = units // blocks
    column = lambda i, at: (0, i)
    return pl.pallas_call(
        up_kernel,
        out_shape=(
            jax.ShapeDtypeStruct((2, rows, quarter), bf16),
            jax.ShapeDtypeStruct((rows, quarter), bf16),
            jax.ShapeDtypeStruct((rows, quarter), bf16),
            jax.ShapeDtypeStruct((rows, units), bf16),
            jax.ShapeDtypeStruct((rows, units), bf16),
            jax.ShapeDtypeStruct((rows, model), f32),
            jax.ShapeDtypeStruct((rows, lanes), f32),
            jax.ShapeDtypeStruct((rows, model), bf16),
            jax.ShapeDtypeStruct((rows, model), bf16),
        ),
        grid_spec=pltpu.PrefetchScalarGridSpec(
            num_scalar_prefetch=1,
            grid=(docs,),
            in_specs=[rows_of(piece) for piece in pieces]
            + [
                full((rows, model)),
                full((model, model)),
                full((1, model)),
                full((1, model)),
                pl.BlockSpec((model, tile), column),
                pl.BlockSpec((1, tile), column),
            ],
            out_specs=[
                full((2, rows, quarter)),
                full((rows, quarter)),
                full((rows, quarter)),
                pl.BlockSpec((rows, tile), column),
                pl.BlockSpec((rows, tile), column),
                full((rows, model)),
                full((rows, lanes)),
                full((rows, model)),
                full((rows, model)),
            ],
        ),
        compiler_params=params(18),
        cost_estimate=cost(9),
        name="up",
    )(at, *map(array_of, pieces), x_own, w_out, gain, bias, w_in, b_in)


def norm_back(grad, normed, inverse, gain):
    scaled = grad * gain
    return inverse * (
        scaled
        - jnp.mean(scaled, axis=1, keepdims=True)
        - normed * jnp.mean(scaled * normed, axis=1, keepdims=True)
    )


def down_kernel(
    act_ref, wdown_ref, normed_ref, cot_ref, gain1_ref, bias1_ref, gain2_ref, bias2_ref,
    block_ref, mix_ref, low_ref, sums_ref,
):
    step = pl.program_id(0)

    @pl.when(step == 0)
    def _():
        mix_ref[...] = normed_ref[...] * gain1_ref[...] + bias1_ref[...]

    mix_ref[...] += dot(act_ref[...], wdown_ref[...])

    @pl.when(step == pl.num_programs(0) - 1)
    def _():
        mixed = mix_ref[...]
        centered = mixed - jnp.mean(mixed, axis=1, keepdims=True)
        inverse = lax.rsqrt(jnp.mean(centered * centered, axis=1, keepdims=True) + norm_eps)
        normed = centered * inverse
        block_ref[...] = (normed * gain2_ref[...] + bias2_ref[...]).astype(bf16)
        grad = cot_ref[...].astype(f32)
        sums_ref[0:1, :] = jnp.sum(grad * normed, axis=0, keepdims=True)
        sums_ref[1:2, :] = jnp.sum(grad, axis=0, keepdims=True)
        mix = norm_back(grad, normed, inverse, gain2_ref[...])
        mix_ref[...] = mix
        low_ref[...] = mix.astype(bf16)


def down_call(act, w_down, normed, cotangent, gain1, bias1, gain2, bias2, tile):
    rows, units = act.shape
    model = w_down.shape[1]
    return pl.pallas_call(
        down_kernel,
        out_shape=(
            jax.ShapeDtypeStruct((rows, model), bf16),
            jax.ShapeDtypeStruct((rows, model), f32),
            jax.ShapeDtypeStruct((rows, model), bf16),
            jax.ShapeDtypeStruct((8, model), f32),
        ),
        grid=(units // tile,),
        in_specs=[
            pl.BlockSpec((rows, tile), lambda i: (0, i)),
            pl.BlockSpec((tile, model), lambda i: (i, 0)),
            full((rows, model)),
            full((rows, model)),
        ]
        + [full((1, model))] * 4,
        out_specs=[full((rows, model))] * 3 + [full((8, model))],
        compiler_params=params(18),
        cost_estimate=cost(8),
        name="down",
    )(act, w_down, normed, cotangent, gain1, bias1, gain2, bias2)


def back_kernel(
    at_ref, wdown_ref, slope_ref, win_ref, wout_ref, normed_ref, inverse_ref, mix_ref, ffn_ref,
    attended_ref, gain1_ref, above_ref, hidden_ref,
    own_ref, core_ref, far_ref, resid_ref, upfar_ref, upcore_ref, upown_ref,
    outfar_ref, outcore_ref, outown_ref, sums_ref,
    total, grad_up,
):
    step = pl.program_id(0)
    steps = pl.num_programs(0)
    rows, tile = slope_ref.shape
    model = mix_ref.shape[1]
    width = model // blocks

    @pl.when(step == 0)
    def _():
        total[...] = mix_ref[...]

    grad = dot(ffn_ref[...], wdown_ref[...], ((1,), (1,))) * slope_ref[...].astype(f32)
    low = grad.astype(bf16)
    total[...] += dot(low, win_ref[...], ((1,), (1,)))
    per = model // tile
    part = step // per
    here = pl.ds(pl.multiple_of((step - part * per) * tile, tile), tile)
    grad_up[jnp.bitwise_xor(part, at_ref[0]), :, here] = low
    sums_ref[pl.ds(4 + part, 1), here] = jnp.sum(low.astype(f32), axis=0, keepdims=True)

    @pl.when(step == steps - 1)
    def _():
        upown_ref[...] = grad_up[0]
        upcore_ref[0] = hidden_ref[...]
        upcore_ref[1] = grad_up[1]
        upfar_ref[0] = hidden_ref[...]
        upfar_ref[1] = grad_up[2]
        upfar_ref[2] = grad_up[3]
        grad = total[...]
        normed = normed_ref[...]
        sums_ref[0:1, :] = jnp.sum(grad * normed, axis=0, keepdims=True)
        sums_ref[1:2, :] = jnp.sum(grad, axis=0, keepdims=True)
        sums_ref[2:4, :] = above_ref[0:2, :]
        resid = norm_back(grad, normed, inverse_ref[:, 0:1], gain1_ref[...])
        resid_ref[...] = resid
        low = resid.astype(bf16)
        total[...] = low.astype(f32)
        outfar_ref[:, :model] = attended_ref[...]
        outcore_ref[:, :model] = attended_ref[...]
        targets = (own_ref, core_ref, far_ref.at[0], far_ref.at[1])
        wides = (
            outown_ref, outcore_ref.at[:, pl.ds(model, width)],
            outfar_ref.at[:, pl.ds(model, width)], outfar_ref.at[:, pl.ds(model + width, width)],
        )
        for at, (target, wide) in enumerate(zip(targets, wides)):
            first = pl.multiple_of(jnp.bitwise_xor(at_ref[0], at) * width, width)
            target[...] = dot(low, wout_ref[pl.ds(first, width), :], ((1,), (1,))).astype(bf16)
            wide[...] = total[:, pl.ds(first, width)].astype(bf16)


def back_call(
    at, w_down, slope, w_in, w_out, normed, inverse, mix, grad_ffn, attended, gain1, above, hidden, tile,
):
    rows, units = slope.shape
    model = w_out.shape[0]
    width = model // blocks
    return pl.pallas_call(
        back_kernel,
        out_shape=(
            jax.ShapeDtypeStruct((rows, width), bf16),
            jax.ShapeDtypeStruct((rows, width), bf16),
            jax.ShapeDtypeStruct((2, rows, width), bf16),
            jax.ShapeDtypeStruct((rows, model), f32),
            jax.ShapeDtypeStruct((3, rows, model), bf16),
            jax.ShapeDtypeStruct((2, rows, model), bf16),
            jax.ShapeDtypeStruct((rows, model), bf16),
            jax.ShapeDtypeStruct((rows, model + 2 * width), bf16),
            jax.ShapeDtypeStruct((rows, model + width), bf16),
            jax.ShapeDtypeStruct((rows, width), bf16),
            jax.ShapeDtypeStruct((8, model), f32),
        ),
        grid_spec=pltpu.PrefetchScalarGridSpec(
            num_scalar_prefetch=1,
            grid=(units // tile,),
            in_specs=[
                pl.BlockSpec((tile, model), lambda i, at: (i, 0)),
                pl.BlockSpec((rows, tile), lambda i, at: (0, i)),
                pl.BlockSpec((model, tile), lambda i, at: (0, i)),
                full((model, model)),
                full((rows, model)),
                full((rows, lanes)),
                full((rows, model)),
                full((rows, model)),
                full((rows, model)),
                full((1, model)),
                full((8, model)),
                full((rows, model)),
            ],
            out_specs=[
                full((rows, width)),
                full((rows, width)),
                full((2, rows, width)),
                full((rows, model)),
                full((3, rows, model)),
                full((2, rows, model)),
                full((rows, model)),
                full((rows, model + 2 * width)),
                full((rows, model + width)),
                full((rows, width)),
                full((8, model)),
            ],
            scratch_shapes=[
                pltpu.VMEM((rows, model), f32),
                pltpu.VMEM((blocks, rows, model), bf16),
            ],
        ),
        compiler_params=params(18),
        cost_estimate=cost(12),
        name="back",
    )(at, w_down, slope, w_in, w_out, normed, inverse, mix, grad_ffn, attended, gain1, above, hidden)


def scores_grad_kernel(half, held, *refs):
    at_ref, g0, g1, g2, g3, qkv_ref, probs_ref, relkq_ref, row_ref, col_ref = refs[:10]
    refs = refs[10:]
    last = half == 1
    if last:
        wq_ref, wk_ref, sums_ref, before_ref, boxes_before = refs[:5]
        refs = refs[5:]
    refs = refs[held:]
    if last:
        dqkv_ref, own_ref, core_ref, far_ref, small_ref, ga_ref, ds_ref, drel, own_qkv, box_sums = refs
    else:
        dqkv_ref, box_sums, ga_ref, ds_ref, drel, own_qkv = refs
    scale = 1.0 / math.sqrt(192.0)
    rows = blocks * lanes
    width = qkv_ref.shape[1] // 3
    part = width // 2
    heads = probs_ref.shape[0]
    size = part // heads
    short = lanes // 2
    for t, piece in enumerate((g0, g1, g2, g3)):
        ga_ref[t * lanes : (t + 1) * lanes, :] = piece[...]
    for k in range(3):
        for h in range(heads):
            first = k * width + half * part + h * size
            own_qkv[k * heads + h] = qkv_ref[:, first : first + size]
    drel[...] = jnp.zeros_like(drel)
    box_sums[...] = jnp.zeros_like(box_sums)
    window = lax.broadcasted_iota(jnp.int32, (rows, 2 * lanes), 1)
    bucket = lax.broadcasted_iota(jnp.int32, (lanes, lanes), 1)
    label = lax.broadcasted_iota(jnp.int32, (rows, lanes), 1)
    all_pos = col_ref[:, 0:1]
    all_x, all_y = col_ref[:, 1:2], col_ref[:, 2:3]
    sector_x, sector_y = jnp.right_shift(all_x, 5), jnp.right_shift(all_y, 5)
    hot_x = (label == sector_x).astype(f32).astype(bf16)
    hot_y = (label == sector_y + 64).astype(f32).astype(bf16)
    hot_both = hot_x + hot_y

    def shares(grads, start):
        found = []
        for u in range(2):
            at = col_ref[pl.ds(pl.multiple_of(start + u * short, short), short), 0:1]
            base = jnp.min(at, axis=0, keepdims=True)
            below = (all_pos <= base - 63 + window) | (window == 2 * lanes - 1)
            stacked = jnp.concatenate([g[u * short : (u + 1) * short, :] for g in grads], axis=0)
            sums = dot(stacked, below.astype(f32).astype(bf16))
            first = at - base + (lanes - 1) - bucket[:short]
            first = jnp.concatenate([first] * heads, axis=0)
            low = jnp.bitwise_and(first, lanes - 1)
            value = jnp.where(
                first < lanes, pick(sums[:, :lanes], low), pick(sums[:, lanes:], low)
            )
            value = jnp.where(bucket == 0, sums[:, 2 * lanes - 1 :], value)
            later = jnp.where(bucket == lanes - 1, 0.0, pltpu.roll(value, lanes - 1, 1))
            found.append(scale * (value - later))
        return [
            jnp.concatenate([f[h * short : (h + 1) * short, :] for f in found], axis=0).astype(bf16)
            for h in range(heads)
        ]

    def by_rows(ib, carry):
        start = ib * lanes
        here = pl.ds(pl.multiple_of(start, lanes), lanes)
        cx_i, cy_i = col_ref[here, 1:2], col_ref[here, 2:3]
        short_x = jnp.bitwise_and(cx_i, 31) < jnp.bitwise_and(row_ref[1:2, :], 31)
        short_y = jnp.bitwise_and(cy_i, 31) < jnp.bitwise_and(row_ref[2:3, :], 31)
        short_x = short_x.astype(f32).astype(bf16)
        short_y = short_y.astype(f32).astype(bf16)
        step_x = jnp.right_shift(cx_i, 5) + 32 - bucket
        step_y = jnp.right_shift(cy_i, 5) + 32 - (bucket - 64)
        in_x = (bucket < 64) & (step_x >= 0) & (step_x < 32)
        in_y = (bucket >= 64) & (step_y >= 0) & (step_y < 32)
        seek = jnp.where(in_x, step_x, jnp.where(in_y, step_y + 64, 0))
        inside = in_x | in_y
        grads = []
        for h in range(heads):
            probs = probs_ref[h, here, :].astype(f32)
            gained = dot(ga_ref[here, h * size : (h + 1) * size], own_qkv[2 * heads + h], ((1,), (1,)))
            row_dots = jnp.sum(probs * gained, axis=1, keepdims=True)
            grad = (probs * (gained - row_dots)).astype(bf16)
            ds_ref[h, here, :] = grad
            grads.append(grad)
        rels = shares(grads, start)
        for h, (grad, rel) in enumerate(zip(grads, rels)):
            gcols = slice(h * size, (h + 1) * size)
            kgcols = slice(half * part + h * size, half * part + (h + 1) * size)
            dqkv_ref[here, gcols] = (
                scale * dot(grad, own_qkv[heads + h]) + dot(rel, relkq_ref[:, kgcols])
            ).astype(bf16)
            drel[:, gcols] += dot(rel, own_qkv[h, here, :], ((0,), (0,)))
        stacked = jnp.concatenate(grads, axis=0)
        plain = dot(stacked, hot_both)
        less = dot(jnp.concatenate([g * short_x for g in grads], axis=0), hot_x) + dot(
            jnp.concatenate([g * short_y for g in grads], axis=0), hot_y
        )
        for h in range(heads):
            span = slice(h * lanes, (h + 1) * lanes)
            own_plain = jnp.where(inside, pick(plain[span, :], seek), 0.0)
            own_less = jnp.where(inside, pick(less[span, :], seek), 0.0)
            box_sums[h : h + 1, :] += jnp.sum(own_plain, axis=0, keepdims=True)
            box_sums[8 + h : 9 + h, :] += jnp.sum(own_less, axis=0, keepdims=True)
        return carry

    lax.fori_loop(0, blocks, by_rows, 0)

    def by_columns(jb, carry):
        start = jb * lanes
        here = pl.ds(pl.multiple_of(start, lanes), lanes)
        grads = [ds_ref[h, :, here].T for h in range(heads)]
        mirrors = shares(grads, start)
        for h, (grad, mirror) in enumerate(zip(grads, mirrors)):
            gcols = slice(h * size, (h + 1) * size)
            kgcols = slice(part + h * size, part + (h + 1) * size)
            vgcols = slice(2 * part + h * size, 2 * part + (h + 1) * size)
            kcols = slice(width + half * part + h * size, width + half * part + (h + 1) * size)
            dqkv_ref[here, kgcols] = (
                scale * dot(grad, own_qkv[h]) + dot(mirror, relkq_ref[:, kcols])
            ).astype(bf16)
            drel[:, kgcols] += dot(mirror, own_qkv[heads + h, here, :], ((0,), (0,)))
            dqkv_ref[here, vgcols] = dot(
                probs_ref[h, :, here], ga_ref[:, gcols], ((0,), (0,))
            ).astype(bf16)
        return carry

    lax.fori_loop(0, blocks, by_columns, 0)
    keys, queries = drel[:, :part].astype(bf16), drel[:, part:].astype(bf16)
    dqkv_ref[rows:, :part] = queries
    dqkv_ref[rows:, part : 2 * part] = keys
    dqkv_ref[rows:, 2 * part :] = jnp.zeros((lanes, part), bf16)
    if not last:
        return
    for t, target in enumerate((own_ref, far_ref.at[0], core_ref, far_ref.at[1])):
        span = slice(t * lanes, (t + 1) * lanes)
        for k in range(3):
            first = k * width
            target[:, first : first + part] = before_ref[span, k * part : (k + 1) * part]
            target[:, first + part : first + width] = dqkv_ref[span, k * part : (k + 1) * part]
    queries = jnp.concatenate([before_ref[rows:, :part], queries], axis=1)
    keys = jnp.concatenate([before_ref[rows:, part : 2 * part], keys], axis=1)

    docs, small_rows, small_width = small_ref.shape
    per = lanes // docs
    table = (
        dot(keys, wk_ref[...], ((1,), (1,))) + dot(queries, wq_ref[...], ((1,), (1,)))
    ).astype(bf16)
    plain = jnp.concatenate([boxes_before[0:heads], box_sums[0:heads], box_sums[heads + heads : 8]], axis=0)
    less = jnp.concatenate(
        [boxes_before[8 : 8 + heads], box_sums[8 : 8 + heads], box_sums[8 + 2 * heads : 16]], axis=0
    )
    heads = 2 * heads
    place_lane = lax.broadcasted_iota(jnp.int32, (8, lanes), 1)
    later = jnp.where(
        jnp.bitwise_and(place_lane, 63) == 63, 0.0, pltpu.roll(less, lanes - 1, 1)
    )
    boxes = (plain - less + later).astype(bf16)
    row_at = lax.broadcasted_iota(jnp.int32, (8, lanes), 0)
    head_at = at_ref[0] * heads + row_at
    by_head = [
        dot(boxes, ((place_lane == head_at + k * 64) & (row_at < heads)).astype(bf16), ((0,), (0,)))
        for k in range(2)
    ]
    model = table.shape[1]
    edges = list(range(0, model, small_width)) + [model]
    rest = edges[-1] - edges[-2]
    lane = slice(rest, rest + lanes)
    line = (len(edges) - 2) * per
    count = lanes // 2 // docs
    for chunk in range(docs):
        own = slice(chunk * per, (chunk + 1) * per)
        for k, (first, end) in enumerate(zip(edges[:-1], edges[1:])):
            small_ref[chunk, k * per : (k + 1) * per, : end - first] = table[own, first:end].astype(f32)
        for k in range(4):
            small_ref[chunk, line + k : line + k + 1, lane] = (
                sums_ref[k : k + 1, chunk * lanes : (chunk + 1) * lanes]
            )
            first = (chunk * blocks + k) * lanes
            where = first // model
            small_ref[chunk, line + 4 + k : line + 5 + k, lane] = (
                sums_ref[4 + where : 5 + where, first - where * model : first - where * model + lanes]
            )
        begin = chunk * count
        small_ref[chunk, line + 8 : line + 8 + count, lane] = (
            by_head[0][begin : begin + count, :] + by_head[1][64 + begin : 64 + begin + count, :]
        )


def scores_grad_call(half, at, pieces, qkv, probs, relkq, row, col, after, docs=0, extra=()):
    rows = blocks * lanes
    heads = probs.shape[0] // 2
    width = qkv.shape[1] // 3
    part = width // 2
    model = width * blocks
    buckets = relkq.shape[0]
    column = pl.BlockSpec((model, width), lambda i, at: (0, at[0]))
    grads = jax.ShapeDtypeStruct((rows + buckets, 3 * part), bf16)
    box_shape = (16, lanes)
    scratch = [
        pltpu.VMEM((rows, part), bf16),
        pltpu.VMEM((heads, rows, rows), bf16),
        pltpu.VMEM((buckets, 2 * part), f32),
        pltpu.VMEM((3 * heads, rows, part // heads), bf16),
    ]
    extra_specs = []
    if half == 1:
        shapes = (
            grads,
            jax.ShapeDtypeStruct((lanes, 3 * width), bf16),
            jax.ShapeDtypeStruct((lanes, 3 * width), bf16),
            jax.ShapeDtypeStruct((2, lanes, 3 * width), bf16),
            jax.ShapeDtypeStruct((docs, 3 * buckets // docs, 3 * part), f32),
        )
        extra_specs = [column, column, full((8, model)), full(grads.shape), full(box_shape)]
        scratch = scratch + [pltpu.VMEM(box_shape, f32)]
    else:
        shapes = (grads, jax.ShapeDtypeStruct(box_shape, f32))
    at = ordered(at, *after) if after else at
    return pl.pallas_call(
        functools.partial(scores_grad_kernel, half, 0),
        out_shape=shapes,
        grid_spec=pltpu.PrefetchScalarGridSpec(
            num_scalar_prefetch=1,
            grid=(1,),
            in_specs=[rows_of(piece, (lanes, part), lambda i, at: half) for piece in pieces]
            + [
                full((rows, 3 * width)),
                pl.BlockSpec((heads, rows, rows), lambda i, at: (half, 0, 0)),
                full((buckets, 2 * width)),
                full((8, rows)),
                full((rows, 8)),
            ]
            + extra_specs,
            out_specs=[full(shape.shape) for shape in shapes],
            scratch_shapes=scratch,
        ),
        compiler_params=params(18),
        cost_estimate=cost(15),
        name="scores_grad",
    )(at, *map(array_of, pieces), qkv, probs, relkq, row, col, *extra)


def weight_grads_call(at, wholes, after=(), name="weight_grads"):
    count = 1 << len(wholes[0][1])
    chunk = lanes
    per = 2
    steps = count // per
    half = steps // 2

    def chunk_of(bits, which):
        def index(i, at):
            p = lax.rem(i + half, steps) * per + which
            total = 0
            for place, bit in enumerate(bits):
                total = total + jnp.bitwise_and(jnp.right_shift(p, len(bits) - 1 - place), 1) * bit
            return jnp.bitwise_xor(at[1], total)

        return index

    def kernel(at_ref, *refs):
        refs = list(refs)
        take = lambda number: [refs.pop(0) for _ in range(number)]
        ins = []
        for groups, bits, extra in wholes:
            sides = [(take(len(lefts) * per), take(len(rights))) for lefts, rights, _ in groups]
            ins.append((sides, take(per) if extra is not None else []))
        outs = [take(2) for _ in wholes]
        step = pl.program_id(0)
        for (sides, extras), (keep_ref, send_ref) in zip(ins, outs):
            results = []
            for own, right_refs in sides:
                right_all = refs.pop(0)

                @pl.when(step == 0)
                def _(right_refs=right_refs, right_all=right_all):
                    for k, ref in enumerate(right_refs):
                        right_all[k * lanes : (k + 1) * lanes, :] = ref[...]

                left = jnp.concatenate(
                    [
                        jnp.concatenate([own[k + which][...] for which in range(per)], axis=1)
                        for k in range(0, len(own), per)
                    ],
                    axis=0,
                )
                results.append(dot(left, right_all[...], ((0,), (0,))).astype(bf16))
            for target, mine in ((send_ref, step < half), (keep_ref, step >= half)):

                @pl.when(mine)
                def _(target=target, results=results, extras=extras):
                    for which in range(per):
                        first = 0
                        for result in results:
                            end = first + result.shape[1]
                            target[which, :chunk, first:end] = (
                                result[which * chunk : (which + 1) * chunk, :]
                            )
                            first = end
                        if extras:
                            target[which, chunk:, :] = extras[which][...].astype(bf16)

    in_specs, operands, scratch, shapes, out_specs = [], [], [], [], []
    for groups, bits, extra in wholes:
        total_width = sum(width for _, _, width in groups)
        tail = 0 if extra is None else extra.shape[1]
        for lefts, rights, width in groups:
            for handle in lefts:
                for which in range(per):
                    in_specs.append(rows_of(handle, (lanes, chunk), chunk_of(bits, which)))
                    operands.append(array_of(handle))
            for handle in rights:
                column = handle[2] if isinstance(handle, tuple) and len(handle) == 3 else 0
                handle = (
                    handle[:2] if isinstance(handle, tuple) and handle[1] is not None else array_of(handle)
                )
                in_specs.append(rows_of(handle, (lanes, width), lambda i, at, column=column: column))
                operands.append(array_of(handle))
            scratch.append(pltpu.VMEM((len(rights) * lanes, width), bf16))
        for which in range(per if extra is not None else 0):
            index = chunk_of(bits, which)
            in_specs.append(
                pl.BlockSpec(
                    (None, tail, total_width), lambda i, at, index=index: (index(i, at), 0, 0)
                )
            )
            operands.append(extra)
        shapes += [jax.ShapeDtypeStruct((count // 2, chunk + tail, total_width), bf16)] * 2
        block = (per, chunk + tail, total_width)
        out_specs += [
            pl.BlockSpec(block, lambda i, at: (jnp.maximum(i - half, 0), 0, 0)),
            pl.BlockSpec(block, lambda i, at: (jnp.minimum(i, half - 1), 0, 0)),
        ]
    at = ordered(at, *after) if after else at
    out = pl.pallas_call(
        kernel,
        out_shape=tuple(shapes),
        grid_spec=pltpu.PrefetchScalarGridSpec(
            num_scalar_prefetch=1,
            grid=(steps,),
            in_specs=in_specs,
            out_specs=out_specs,
            scratch_shapes=scratch,
        ),
        compiler_params=params(18),
        cost_estimate=cost(0.01),
        name=name,
    )(at, *operands)
    return [tuple(out[k : k + 2]) for k in range(0, len(out), 2)]


def tokens_grad_kernel(at_ref, d0, d1, d2, d3, resid_ref, wq_ref, wk_ref, wv_ref, *refs):
    out_ref = refs[-1]
    step = pl.program_id(0)
    width = wq_ref.shape[1]

    @pl.when(step == 0)
    def _():
        out_ref[...] = resid_ref[...]

    for t, piece in enumerate((d0, d1, d2, d3)):

        @pl.when(step == t)
        def _(piece=piece):
            total = out_ref[...]
            for at, w_ref in enumerate((wq_ref, wk_ref, wv_ref)):
                total = total + dot(
                    piece[:, at * width : (at + 1) * width], w_ref[...], ((1,), (1,))
                )
            out_ref[...] = total


def tokens_grad_call(at, pieces, resid, w_query, w_key, w_value, after):
    rows, model = resid.shape
    width = model // blocks
    tile = (rows, 3 * width)

    def column(i, at):
        offset = jnp.where(i == 1, 2, jnp.where(i == 2, 1, i))
        return (0, jnp.bitwise_xor(at[0], offset))

    weight = pl.BlockSpec((model, width), column)
    at = ordered(at, *after) if after else at
    return pl.pallas_call(
        tokens_grad_kernel,
        out_shape=jax.ShapeDtypeStruct((rows, model), f32),
        grid_spec=pltpu.PrefetchScalarGridSpec(
            num_scalar_prefetch=1,
            grid=(blocks,),
            in_specs=[rows_of(piece, tile) for piece in pieces]
            + [full((rows, model)), weight, weight, weight],
            out_specs=full((rows, model)),
        ),
        compiler_params=params(18),
        cost_estimate=cost(4),
        name="tokens_grad",
    )(at, *map(array_of, pieces), resid, w_query, w_key, w_value)


def parts_kernel(fields, at_ref, *refs):
    step = pl.program_id(0)
    parts, outs = refs[: blocks * fields], refs[blocks * fields :]
    for field in range(fields):
        for at in range(blocks):

            @pl.when(step == at)
            def _(part=parts[field * blocks + at], out=outs[field]):
                out[...] = part[...].astype(f32)


def parts_call(at, fields, name):
    in_specs, operands, shapes, out_specs = [], [], [], []
    for parts, axis in fields:
        rows, width = parts[0].shape
        in_specs += [full((rows, width))] * blocks
        operands += list(parts)
        shape = (rows * blocks, width) if axis == 0 else (rows, width * blocks)
        shapes.append(jax.ShapeDtypeStruct(shape, f32))

        def index(i, at, axis=axis):
            spot = jnp.bitwise_xor(at[0], i)
            return (spot, 0) if axis == 0 else (0, spot)

        out_specs.append(pl.BlockSpec((rows, width), index))
    return pl.pallas_call(
        functools.partial(parts_kernel, len(fields)),
        out_shape=tuple(shapes),
        grid_spec=pltpu.PrefetchScalarGridSpec(
            num_scalar_prefetch=1, grid=(blocks,), in_specs=in_specs, out_specs=out_specs
        ),
        compiler_params=params(18),
        cost_estimate=cost(2),
        name=name,
    )(at, *operands)


def last_kernel(at_ref, *refs):
    step = pl.program_id(0)
    firsts, seconds, outs = refs[:blocks], refs[blocks : 2 * blocks], refs[2 * blocks : 2 * blocks + 3]
    wout_ref, rel_ref, *small_refs = refs[2 * blocks + 3 :]
    norm_refs, (bin_ref, xbox_ref, ybox_ref) = small_refs[:4], small_refs[4:]
    for at in range(blocks):

        @pl.when(step == at)
        def _(first=firsts[at], second=seconds[at]):
            for k, out in enumerate(outs):
                span = slice(k * lanes, (k + 1) * lanes)
                out[:, :lanes] = first[:, span].astype(f32)
                out[:, lanes:] = second[:lanes, span].astype(f32)
            wout_ref[...] = first[:, 3 * lanes :].astype(f32)

    @pl.when(step == 0)
    def _():
        total = seconds[0][lanes:, :].astype(f32)
        for second in seconds[1:]:
            total = total + second[lanes:, :].astype(f32)
        rows = rel_ref.shape[0]
        width = total.shape[1]
        for k in range(3):
            end = min((k + 1) * width, rel_ref.shape[1])
            rel_ref[:, k * width : end] = total[k * rows : (k + 1) * rows, : end - k * width]
        rest = total[2 * rows :, width - lanes :]
        for k in range(4):
            norm_refs[k][...] = rest[k]
            bin_ref[k * lanes : (k + 1) * lanes] = rest[4 + k]
        heads = xbox_ref.shape[1]
        xbox_ref[...] = rest[8:16, :heads]
        ybox_ref[...] = rest[8:16, 64 : 64 + heads]


def last_call(at, firsts, seconds, buckets, model, heads):
    wide = jax.ShapeDtypeStruct((lanes, model), f32)
    small_shapes = ((buckets, model),) + ((lanes,),) * 4 + ((blocks * lanes,), (8, heads), (8, heads))
    column = pl.BlockSpec((lanes, model // blocks), lambda i, at: (0, jnp.bitwise_xor(at[0], i)))
    return pl.pallas_call(
        last_kernel,
        out_shape=(wide, wide, wide, wide)
        + tuple(jax.ShapeDtypeStruct(shape, f32) for shape in small_shapes),
        grid_spec=pltpu.PrefetchScalarGridSpec(
            num_scalar_prefetch=1,
            grid=(blocks,),
            in_specs=[full(part.shape) for part in firsts + seconds],
            out_specs=[column] * 4 + [full(shape) for shape in small_shapes],
        ),
        compiler_params=params(18),
        cost_estimate=cost(2),
        name="last",
    )(at, *firsts, *seconds)


class Halving:
    def __init__(self, halves, bits):
        self.keep, self.send = halves
        self.bits = list(bits)
        self.step()

    def step(self):
        self.came = swap(self.send, "docs", self.bits.pop(0))

    def add(self, *before):
        keep, came = self.keep, self.came
        if before:
            came = ordered(came, *before)
        total = lambda part: (keep[part].astype(f32) + came[part].astype(f32)).astype(bf16)
        if not self.bits:
            self.keep = self.send = total(slice(None))[0]
            return self.keep
        middle = keep.shape[0] // 2
        self.send = total(slice(middle, None))
        self.keep = total(slice(0, middle))
        sent = self.send
        self.step()
        return sent


def shards_tiles(
    tokens, lengths, positions, token_boxes, ln1_gain, ln1_bias, w_query, w_key, w_value, w_out,
    rel_table, xbias_table, ybias_table, ln2_gain, ln2_bias, w_in, b_in, w_down, cotangent,
):
    row_count, model = tokens.shape[1:]
    docs = lax.axis_size("docs")
    place = lax.axis_index("blk")
    doc_place = lax.axis_index("docs")
    heads = xbias_table.shape[1]
    boxes = xbias_table.shape[0]
    units = w_in.shape[1]
    width = model // blocks
    bits = bits_of(docs)
    other = [bits[1], bits[0]] + bits[2:]
    x_own = tokens[0]
    w_query, w_key, w_value = in_hbm(w_query), in_hbm(w_key), in_hbm(w_value)

    x_far = swap(x_own, "blk", 2)
    own_ints = jnp.concatenate(
        [
            positions,
            jnp.right_shift(token_boxes[0] + token_boxes[2], 1),
            jnp.right_shift(token_boxes[1] + token_boxes[3], 1),
            jnp.zeros((5, row_count), jnp.int32),
        ],
        axis=0,
    )
    ints_far = swap(own_ints, "blk", 2)
    x_core, ints_core = swap(x_own, "blk", 1), swap(own_ints, "blk", 1)
    x_both, ints_both = swap(ordered(x_far, ints_far), "blk", 1), swap(ints_far, "blk", 1)
    xs = tuple(map(in_hbm, (x_own, x_far, x_core, x_both)))
    tables = jnp.concatenate([xbias_table.T, ybias_table.T], axis=1).astype(f32)
    tables = tables.reshape(blocks, heads // blocks, 2 * boxes)
    at = jnp.stack([place.astype(jnp.int32), lengths[0]])
    spot = jnp.stack([place, doc_place]).astype(jnp.int32)
    att_own, att_core, att_far, probs, qkv, relkq, row, col = scores_call(
        at, xs, (own_ints, ints_far, ints_core, ints_both), w_query, w_key, w_value, rel_table, tables
    )

    came_far = swap(att_far, "blk", 2)
    came_core = swap(att_core, "blk", 1)
    came_both = swap(came_far, "blk", 1)
    line = lambda vector: vector.reshape(1, -1)
    far1, core1, act_own, act, slope, normed1, inverse1, attended, hidden = up_call(
        spot, (att_own, (came_far, 0), came_core, (came_both, 1)), x_own, w_out,
        line(ln1_gain), line(ln1_bias), in_hbm(w_in), line(b_in), docs,
    )
    got_far1 = swap(far1, "blk", 2)
    block_out, mix, grad_ffn, above = down_call(
        act, w_down, normed1, cotangent[0],
        line(ln1_gain), line(ln1_bias), line(ln2_gain), line(ln2_bias), units // docs,
    )
    (
        ga_own, ga_core, ga_far, grad_resid, up_far, up_core, up_own, far3, core3, gattn_own, sums,
    ) = back_call(
        spot, w_down, slope, w_in, w_out, normed1, inverse1, mix, grad_ffn, attended,
        line(ln1_gain), above, hidden, units // docs,
    )
    came_far = swap(ga_far, "blk", 2)
    came_core = swap(ga_core, "blk", 1)
    came_both = swap(came_far, "blk", 1)
    ga_all = (ga_own, (came_far, 0), came_core, (came_both, 1))
    ffn_far = swap(grad_ffn, "blk", 2)
    got_core1, got_both1 = swap(core1, "blk", 1), swap(ordered(got_far1, ga_own), "blk", 1)
    ffn_core, ffn_both = swap(grad_ffn, "blk", 1), swap(ordered(ffn_far, ga_own), "blk", 1)
    act_all = [act_own, (got_far1, 0), got_core1, (got_both1, 1)]
    gffn_all = [grad_ffn, ffn_far, ffn_core, ffn_both]
    (down_halves,) = weight_grads_call(
        spot, [([(act_all, gffn_all, model)], bits, None)], after=[ga_own], name="grad_down"
    )
    down_sum = Halving(down_halves, bits)
    got_far2 = swap(ordered(up_far, came_far), "blk", 2)
    first_grads, first_boxes = scores_grad_call(
        0, spot, ga_all, qkv, probs, relkq, row, col, [down_halves[0]]
    )
    got_core2, got_both2 = swap(up_core, "blk", 1), swap(ordered(got_far2, first_grads), "blk", 1)
    got_far3 = swap(ordered(far3, got_far2), "blk", 2)
    hidden_all = [hidden, (got_far2, 0), (got_core2, 0), (got_both2, 0)]
    up_all = [up_own, (got_far2, 1), (got_core2, 1), (got_both2, 2)]
    (in_halves,) = weight_grads_call(
        spot, [([(hidden_all, up_all, model)], bits, None)], after=[first_grads], name="grad_in"
    )
    in_sum = Halving(in_halves, bits)
    lefts = list(xs) + [rel_table]

    def rows_by_piece(grads):
        return [(grads.reshape(blocks + 1, lanes, -1), t) for t in range(blocks + 1)]

    got_core3, got_both3 = swap(core3, "blk", 1), swap(ordered(got_far3, in_halves[0]), "blk", 1)
    att_all = [far3, got_far3, got_core3, got_both3]
    per = model // width
    gattn_all = [
        gattn_own, (got_far3, None, per), (got_core3, None, per), (got_both3, None, per + 1),
    ]
    done = down_sum.add(in_halves[0])
    early = [done]
    first_groups = [(lefts, rows_by_piece(first_grads), 3 * width // 2), (att_all, gattn_all, width)]
    (first_halves,) = weight_grads_call(
        spot, [(first_groups, other, None)], after=[in_halves[0]] + early, name="grad_qkv_out"
    )
    first_sum = Halving(first_halves, other)
    second_grads, dq_own, dq_core, dq_far, small = scores_grad_call(
        1, spot, ga_all, qkv, probs, relkq, row, col, [first_halves[0]], docs,
        (w_query, w_key, sums, first_grads, first_boxes),
    )
    done = down_sum.add(second_grads)
    done = in_sum.add(done)
    second_groups = [(lefts, rows_by_piece(second_grads), 3 * width // 2)]
    (second_halves,) = weight_grads_call(
        spot, [(second_groups, bits, small)], after=[done], name="grad_qkv"
    )
    second_sum = Halving(second_halves, bits)
    done = first_sum.add(second_halves[0])
    dq_far_got = ordered(swap(dq_far, "blk", 2), second_halves[0])
    dq_core_got, dq_both_got = swap(dq_core, "blk", 1), swap(dq_far_got, "blk", 1)
    grad_tokens = tokens_grad_call(
        spot, (dq_own, (dq_far_got, 0), dq_core_got, (dq_both_got, 1)), grad_resid,
        w_query, w_key, w_value, [done],
    )

    def whole(part, *before):
        far = swap(part, "blk", 2)
        held = ordered(far, *before) if before else far
        return (part, swap(part, "blk", 1), far, swap(held, "blk", 1))

    done = in_sum.add(grad_tokens)
    done = second_sum.add(done)
    done = down_sum.add(done)
    down_part = done
    done = first_sum.add(done)
    done = second_sum.add(done)
    done = in_sum.add(done)
    in_part = done
    done = first_sum.add(done)
    first_part = done
    done = second_sum.add(done)
    second_part = done
    grad_w_down, grad_w_in = parts_call(
        spot, ((whole(down_part, done), 0), (whole(in_part, done), 1)), "gather_parts"
    )
    *grads, grad_w_out, rel_out, n0, n1, n2, n3, b_in_out, xb, yb = last_call(
        spot, whole(first_part, grad_w_down), whole(second_part, grad_w_down), rel_table.shape[0] // docs, model, heads
    )
    norms = (n0, n1, n2, n3)
    return (
        block_out[None], grad_tokens[None], norms[0], norms[1], grads[0], grads[1], grads[2], grad_w_out,
        rel_out, xb, yb, norms[2], norms[3], grad_w_in, b_in_out, grad_w_down,
    )


def choose(*args):
    docs, parts = lax.axis_size("docs"), lax.axis_size("blk")
    tokens, w_in = args[0], args[15]
    model, units = w_in.shape
    fits = (
        parts == blocks
        and tokens.shape[1] == lanes
        and model // docs == lanes
        and units // docs == parts * lanes
        and docs & (docs - 1) == 0
        and docs > 2
        and units == blocks * model
    )
    return (shards_tiles if fits else shards)(*args)


def solution(mesh):
    rows = P("docs", "blk", None)
    placed = (
        rows, P("docs"), P("docs", "blk"), P(None, "docs", "blk"),
        *([P()] * 14), rows,
    )
    over_docs, over_docs2 = P("docs"), P("docs", None)
    return jax.shard_map(
        choose,
        mesh=mesh,
        in_specs=placed,
        out_specs=(
            rows, rows, over_docs, over_docs, over_docs2, over_docs2, over_docs2, over_docs2,
            over_docs2, over_docs2, over_docs2, over_docs, over_docs, over_docs2, over_docs, over_docs2,
        ),
        check_vma=False,
    )
```

```python
import functools
import math

import jax
import jax.numpy as jnp
from jax import lax
from jax.experimental import pallas as pl
from jax.experimental.pallas import tpu as pltpu
from jax.sharding import PartitionSpec as P

norm_eps = 1e-05
mask_value = -1e30
f32 = jnp.float32
bf16 = jnp.bfloat16
lanes = 128


def dot(a, b, contract=((1,), (0,))):
    return lax.dot_general(a, b, (contract, ((), ())), preferred_element_type=f32)


def pick(table, index):
    return jnp.take_along_axis(table, index, axis=1, mode="promise_in_bounds")


def ahead_of(first, second):
    return jnp.clip(first - second, -64, 63) + 64


def attn_fwd_kernel(
    place, x_ref, wq_ref, wk_ref, wv_ref, rel_ref, tab_ref, row_ref, col_ref,
    att_ref, probs_ref, qkv_ref, relkq_ref, key_rel,
):
    scale = 1.0 / math.sqrt(192.0)
    step = pl.program_id(0)
    rows = x_ref.shape[0]
    width = wq_ref.shape[1]
    heads = tab_ref.shape[1]
    size = width // heads
    tiles = rows // lanes

    @pl.when(step == 0)
    def _():
        for at, w_ref in enumerate((wq_ref, wk_ref, wv_ref)):
            for t in range(tiles):
                qkv_ref[t * lanes : (t + 1) * lanes, at * width : (at + 1) * width] = dot(
                    x_ref[t * lanes : (t + 1) * lanes, :], w_ref[...]
                ).astype(bf16)
        relkq_ref[:, :width] = dot(rel_ref[...], wk_ref[...]).astype(bf16)
        relkq_ref[:, width:] = dot(rel_ref[...], wq_ref[...]).astype(bf16)
        for h in range(heads):
            key_rel[h] = (
                dot(
                    qkv_ref[:, width + h * size : width + (h + 1) * size],
                    relkq_ref[:, width + h * size : width + (h + 1) * size],
                    ((1,), (1,)),
                )
                .astype(bf16)
                .astype(f32)
            )

    here = pl.ds(pl.multiple_of(step * lanes, lanes), lanes)
    pos_i = col_ref[here, 0:1]
    cx_i = col_ref[here, 1:2]
    cy_i = col_ref[here, 2:3]
    own_row = row_ref[0:1, here]
    ahead, mirror, across, vertical = [], [], [], []
    for t in range(tiles):
        span = slice(t * lanes, (t + 1) * lanes)
        ahead.append(ahead_of(pos_i, row_ref[0:1, span]))
        mirror.append(ahead_of(col_ref[span, 0:1], own_row))
        across.append(jnp.clip(jnp.right_shift(cx_i - row_ref[1:2, span], 5), -32, 31) + 32)
        vertical.append(jnp.clip(jnp.right_shift(cy_i - row_ref[2:3, span], 5), -32, 31) + 96)
    valid = row_ref[3:4, :] > 0
    for h in range(heads):
        cols = slice(h * size, (h + 1) * size)
        query = qkv_ref[here, cols]
        rel_scores = (
            dot(query, relkq_ref[:, cols], ((1,), (1,))).astype(bf16).astype(f32)
        )
        table = jnp.broadcast_to(tab_ref[0, h : h + 1, :], (lanes, lanes))
        pieces = []
        for t in range(tiles):
            span = slice(t * lanes, (t + 1) * lanes)
            content = dot(
                query, qkv_ref[span, width + h * size : width + (h + 1) * size], ((1,), (1,))
            )
            mirrored = pick(key_rel[h, span, :], mirror[t]).T
            bias = pick(table, across[t]) + pick(table, vertical[t])
            pieces.append(
                scale * (content + pick(rel_scores, ahead[t]) + mirrored) + bias
            )
        scores = jnp.where(valid, jnp.concatenate(pieces, axis=1), mask_value)
        top = jnp.max(scores, axis=1, keepdims=True)
        raised = jnp.exp(scores - top)
        probs = (raised * (1.0 / jnp.sum(raised, axis=1, keepdims=True))).astype(bf16)
        probs_ref[h] = probs
        att_ref[:, cols] = dot(
            probs, qkv_ref[:, 2 * width + h * size : 2 * width + (h + 1) * size]
        ).astype(bf16)


def attn_fwd(place, x_all, w_query, w_key, w_value, rel_table, tables, ints_row, ints_col):
    rows, model = x_all.shape
    parts, heads, _ = tables.shape
    width = w_query.shape[1] // parts
    tiles = rows // lanes
    buckets = rel_table.shape[0]
    whole = lambda *shape: pl.BlockSpec(shape, lambda i, at: (0,) * len(shape))
    column = pl.BlockSpec((model, width), lambda i, at: (0, at[0]))
    return pl.pallas_call(
        attn_fwd_kernel,
        out_shape=(
            jax.ShapeDtypeStruct((rows, width), bf16),
            jax.ShapeDtypeStruct((heads, rows, rows), bf16),
            jax.ShapeDtypeStruct((rows, 3 * width), bf16),
            jax.ShapeDtypeStruct((buckets, 2 * width), bf16),
        ),
        grid_spec=pltpu.PrefetchScalarGridSpec(
            num_scalar_prefetch=1,
            grid=(tiles,),
            in_specs=[
                whole(rows, model),
                column,
                column,
                column,
                whole(buckets, model),
                pl.BlockSpec((1, heads, lanes), lambda i, at: (at[0], 0, 0)),
                whole(8, rows),
                whole(rows, 8),
            ],
            out_specs=[
                pl.BlockSpec((lanes, width), lambda i, at: (i, 0)),
                pl.BlockSpec((heads, lanes, rows), lambda i, at: (0, i, 0)),
                whole(rows, 3 * width),
                whole(buckets, 2 * width),
            ],
            scratch_shapes=[pltpu.VMEM((heads, rows, lanes), f32)],
        ),
        compiler_params=pltpu.CompilerParams(vmem_limit_bytes=40 << 20),
        cost_estimate=pl.CostEstimate(
            flops=6 * 10**9, transcendentals=10**6, bytes_accessed=8 << 20
        ),
        name="attn_fwd",
    )(place, x_all, w_query, w_key, w_value, rel_table, tables, ints_row, ints_col)


def attn_bwd_kernel(
    ga_ref, qkv_ref, probs_ref, relkq_ref, row_ref, col_ref,
    dqkv_ref, drel_ref, boxes_ref, ds_ref,
):
    scale = 1.0 / math.sqrt(192.0)
    rows = ga_ref.shape[0]
    heads = probs_ref.shape[0]
    width = ga_ref.shape[1]
    size = width // heads
    tiles = rows // lanes
    span_width = 3 * lanes
    drel_ref[...] = jnp.zeros_like(drel_ref)
    boxes_ref[...] = jnp.zeros_like(boxes_ref)
    window = lax.broadcasted_iota(jnp.int32, (rows, span_width), 1)
    bucket = lax.broadcasted_iota(jnp.int32, (lanes, lanes), 1)
    label = lax.broadcasted_iota(jnp.int32, (rows, lanes), 1)
    all_pos = col_ref[:, 0:1]
    all_x, all_y = col_ref[:, 1:2], col_ref[:, 2:3]
    sector_x, sector_y = jnp.right_shift(all_x, 5), jnp.right_shift(all_y, 5)
    hot_x = (label == sector_x).astype(bf16)
    hot_y = (label == sector_y + 64).astype(bf16)
    hot_both = ((label == sector_x) | (label == sector_y + 64)).astype(bf16)

    def histogram(sums, total, at, base_row):
        first = at - base_row + (2 * lanes // 2 - 1) - bucket
        low = jnp.bitwise_and(first, lanes - 1)
        group = jnp.right_shift(first, 7)
        found = jnp.where(
            group == 0,
            pick(sums[:, :lanes], low),
            jnp.where(
                group == 1,
                pick(sums[:, lanes : 2 * lanes], low),
                pick(sums[:, 2 * lanes :], low),
            ),
        )
        found = jnp.where(bucket == 0, total, found)
        later = jnp.where(bucket == lanes - 1, 0.0, pltpu.roll(found, lanes - 1, 1))
        return found - later

    def by_rows(ib, carry):
        here = pl.ds(pl.multiple_of(ib * lanes, lanes), lanes)
        pos_i = col_ref[here, 0:1]
        cx_i, cy_i = col_ref[here, 1:2], col_ref[here, 2:3]
        base = jnp.min(pos_i, axis=0, keepdims=True)
        below = (all_pos <= base - 63 + window).astype(bf16)
        short_x = jnp.bitwise_and(cx_i, 31) < jnp.bitwise_and(row_ref[1:2, :], 31)
        short_y = jnp.bitwise_and(cy_i, 31) < jnp.bitwise_and(row_ref[2:3, :], 31)
        step_x = jnp.right_shift(cx_i, 5) + 32 - bucket
        step_y = jnp.right_shift(cy_i, 5) + 32 - (bucket - 64)
        in_x = (bucket < 64) & (step_x >= 0) & (step_x < 32)
        in_y = (bucket >= 64) & (step_y >= 0) & (step_y < 32)
        seek = jnp.where(in_x, step_x, jnp.where(in_y, step_y + 64, 0))
        inside = in_x | in_y
        for h in range(heads):
            cols = slice(h * size, (h + 1) * size)
            kcols = slice(width + h * size, width + (h + 1) * size)
            vcols = slice(2 * width + h * size, 2 * width + (h + 1) * size)
            probs = probs_ref[h, here, :].astype(f32)
            gained = dot(ga_ref[here, cols], qkv_ref[:, vcols], ((1,), (1,)))
            row_dots = jnp.sum(probs * gained, axis=1, keepdims=True)
            grad32 = probs * (gained - row_dots)
            grad = grad32.astype(bf16)
            ds_ref[h, here, :] = grad
            exact = grad.astype(f32)
            total = jnp.sum(exact, axis=1, keepdims=True)
            rel = histogram(dot(grad, below), total, pos_i, base)
            rel = (scale * rel).astype(bf16)
            query = qkv_ref[here, cols]
            dqkv_ref[here, cols] = (
                scale * dot(grad, qkv_ref[:, kcols]) + dot(rel, relkq_ref[:, cols])
            ).astype(bf16)
            drel_ref[:, cols] += dot(rel, query, ((0,), (0,)))
            grad_x = jnp.where(short_x, exact, 0.0).astype(bf16)
            grad_y = jnp.where(short_y, exact, 0.0).astype(bf16)
            plain = dot(grad, hot_both)
            less = dot(grad_x, hot_x) + dot(grad_y, hot_y)
            plain = jnp.where(inside, pick(plain, seek), 0.0)
            less = jnp.where(inside, pick(less, seek), 0.0)
            boxes_ref[2 * h : 2 * h + 1, :] += jnp.sum(plain, axis=0, keepdims=True)
            boxes_ref[2 * h + 1 : 2 * h + 2, :] += jnp.sum(less, axis=0, keepdims=True)
        return carry

    lax.fori_loop(0, tiles, by_rows, 0)

    def by_columns(jb, carry):
        here = pl.ds(pl.multiple_of(jb * lanes, lanes), lanes)
        pos_j = col_ref[here, 0:1]
        base = jnp.min(pos_j, axis=0, keepdims=True)
        below = (all_pos <= base - 63 + window).astype(bf16)
        for h in range(heads):
            cols = slice(h * size, (h + 1) * size)
            kcols = slice(width + h * size, width + (h + 1) * size)
            vcols = slice(2 * width + h * size, 2 * width + (h + 1) * size)
            grad = ds_ref[h, :, here]
            total = dot(grad, jnp.ones((rows, lanes), bf16), ((0,), (0,)))
            sums = dot(grad, below, ((0,), (0,)))
            mirror = (scale * histogram(sums, total, pos_j, base)).astype(bf16)
            dqkv_ref[here, kcols] = (
                scale * dot(grad, qkv_ref[:, cols], ((0,), (0,)))
                + dot(mirror, relkq_ref[:, kcols])
            ).astype(bf16)
            drel_ref[:, kcols] += dot(mirror, qkv_ref[here, kcols], ((0,), (0,)))
            dqkv_ref[here, vcols] = dot(
                probs_ref[h, :, here], ga_ref[:, cols], ((0,), (0,))
            ).astype(bf16)
        return carry

    lax.fori_loop(0, tiles, by_columns, 0)


def attn_bwd(grad_att, qkv, probs, relkq, ints_row, ints_col):
    rows, width = grad_att.shape
    heads = probs.shape[0]
    buckets = relkq.shape[0]
    inside = pl.BlockSpec(memory_space=pltpu.VMEM)
    return pl.pallas_call(
        attn_bwd_kernel,
        out_shape=(
            jax.ShapeDtypeStruct((rows, 3 * width), bf16),
            jax.ShapeDtypeStruct((buckets, 2 * width), f32),
            jax.ShapeDtypeStruct((2 * heads, lanes), f32),
        ),
        in_specs=[inside] * 6,
        out_specs=[inside] * 3,
        scratch_shapes=[pltpu.VMEM((heads, rows, rows), bf16)],
        compiler_params=pltpu.CompilerParams(vmem_limit_bytes=40 << 20),
        cost_estimate=pl.CostEstimate(
            flops=12 * 10**9, transcendentals=0, bytes_accessed=6 << 20
        ),
        name="attn_bwd",
    )(grad_att, qkv, probs, relkq, ints_row, ints_col)


def layer_norm(inputs, gain_vec, bias_vec):
    row_mean = jnp.mean(inputs, axis=-1, keepdims=True)
    centered = inputs - row_mean
    inverse = lax.rsqrt(jnp.mean(centered * centered, axis=-1, keepdims=True) + norm_eps)
    normed = centered * inverse
    return (normed * gain_vec + bias_vec, normed, inverse)


def norm_backward(grad_in, normed, inverse, gain_vec):
    grad_gain = jnp.sum(grad_in * normed, axis=0)
    grad_shift = jnp.sum(grad_in, axis=0)
    scaled = grad_in * gain_vec
    grad_input = inverse * (
        scaled
        - jnp.mean(scaled, axis=-1, keepdims=True)
        - normed * jnp.mean(scaled * normed, axis=-1, keepdims=True)
    )
    return (grad_input, grad_gain, grad_shift)


def bits_of(count):
    assert count & (count - 1) == 0
    return [1 << at for at in range(count.bit_length() - 1)]


def swap(array, axis, by):
    count = lax.axis_size(axis)
    return lax.ppermute(array, axis, [(i, i ^ by) for i in range(count)])


def offsets(count):
    order = [0]
    for bit in reversed(bits_of(count)):
        order = order + [at ^ bit for at in order]
    return order


def spread(shared, pieces):
    count = lax.axis_size("blk")
    got = {0: shared} if shared is not None else {}
    held = {(0, at): piece for at, piece in pieces.items()} if pieces else {}
    for bit in reversed(bits_of(count)):
        out_keys = [key for key in sorted(held) if key[1] & bit]
        out_shared = sorted(got)
        parts = [got[at] for at in out_shared] + [held[key] for key in out_keys]
        if bit == 1:
            came = [swap(part, "blk", bit) for part in parts]
        else:
            came = swap(jnp.concatenate(parts, axis=1), "blk", bit)
            edges = [0]
            for part in parts:
                edges.append(edges[-1] + part.shape[1])
            came = [came[:, a:b] for a, b in zip(edges[:-1], edges[1:])]
        for at, part in zip(out_shared, came):
            got[at ^ bit] = part
        for key, part in zip(out_keys, came[len(out_shared) :]):
            del held[key]
            held[(key[0] ^ bit, key[1] ^ bit)] = part
    return got, {key[0]: part for key, part in held.items()}


def by_place(stacked, place):
    count = len(stacked)
    for bit in bits_of(count):
        turned = (place & bit) != 0
        stacked = [jnp.where(turned, stacked[at ^ bit], stacked[at]) for at in range(count)]
    return stacked


def chunk_order(count):
    order = [0]
    for bit in reversed(bits_of(count)):
        order = order + [at | bit for at in order]
    return order


def for_docs(chunks, doc_place):
    moved = by_place(chunks, doc_place)
    return [moved[at] for at in chunk_order(len(chunks))]


def halve(keep, send, bits):
    count = lax.axis_size("docs")
    first = True
    current = keep
    for bit in bits:
        if not first:
            half = current.shape[0] // 2
            current, send = current[:half], current[half:]
        first = False
        came = swap(send, "docs", bit)
        current = (current.astype(f32) + came.astype(f32)).astype(bf16)
    return current


def shards(
    tokens, lengths, positions, token_boxes, ln1_gain, ln1_bias, w_query, w_key, w_value, w_out,
    rel_table, xbias_table, ybias_table, ln2_gain, ln2_bias, w_in, b_in, w_down, cotangent,
):
    doc_count, row_count, model = tokens.shape
    assert doc_count == 1 and row_count == lanes
    parts = lax.axis_size("blk")
    docs = lax.axis_size("docs")
    place = lax.axis_index("blk")
    doc_place = lax.axis_index("docs")
    heads = xbias_table.shape[1]
    own_heads = heads // parts
    width = model // parts
    buckets = rel_table.shape[0]
    boxes = xbias_table.shape[0]
    hidden_units = w_in.shape[1]
    order = offsets(parts)
    x_own = tokens[0]

    centers_x = jnp.right_shift(token_boxes[0] + token_boxes[2], 1)
    centers_y = jnp.right_shift(token_boxes[1] + token_boxes[3], 1)
    own_ints = jnp.concatenate([positions, centers_x, centers_y], axis=0)
    coded = jnp.concatenate(
        [jnp.right_shift(own_ints, 5), jnp.bitwise_and(own_ints, 31)], axis=0
    ).astype(bf16)
    coded = jnp.pad(coded.reshape(1, -1), ((0, 7), (0, model - coded.size)))
    got, _ = spread(jnp.concatenate([x_own, coded], axis=0), None)
    x_all = jnp.concatenate([got[at][:row_count] for at in order], axis=0)
    decoded = jnp.concatenate(
        [got[at][row_count : row_count + 1, : 6 * row_count].reshape(6, row_count) for at in order], axis=1
    ).astype(jnp.int32)
    ints = decoded[:3] * 32 + decoded[3:]
    slot_ids = jnp.concatenate(
        [
            (place ^ at) * row_count + lax.broadcasted_iota(jnp.int32, (1, row_count), 1)
            for at in order
        ],
        axis=1,
    )
    ints = jnp.concatenate(
        [ints, (slot_ids < lengths[0]).astype(jnp.int32), jnp.zeros((4, ints.shape[1]), jnp.int32)],
        axis=0,
    )
    ints_col = ints.T
    tables = jnp.concatenate([xbias_table.T, ybias_table.T], axis=1).astype(f32)
    tables = tables.reshape(parts, own_heads, 2 * boxes)

    attended_own, probs, qkv, relkq = attn_fwd(
        place.reshape(1), x_all, w_query, w_key, w_value, rel_table, tables, ints, ints_col
    )

    def row_block(array, at):
        t = order.index(at)
        return array[t * row_count : (t + 1) * row_count]

    _, came = spread(None, {at: row_block(attended_own, at) for at in order})
    attended = jnp.concatenate(by_place([came[at] for at in range(parts)], place), axis=1)
    attn_out = jnp.dot(attended, w_out, preferred_element_type=f32)
    hidden, normed1, inverse1 = layer_norm(x_own.astype(f32) + attn_out, ln1_gain, ln1_bias)
    hidden_low = hidden.astype(bf16)
    up_proj = jnp.dot(hidden_low, w_in, preferred_element_type=f32) + b_in
    activated, gelu_back = jax.vjp(lambda inputs: jax.nn.gelu(inputs, approximate=True), up_proj)
    activated_low = activated.astype(bf16)
    ffn_out = jnp.dot(activated_low, w_down, preferred_element_type=f32)
    normed_out, normed2, inverse2 = layer_norm(hidden + ffn_out, ln2_gain, ln2_bias)
    block_out = normed_out.astype(bf16)[None]
    grad_output = cotangent[0].astype(f32)
    grad_mix, grad_ln2_gain, grad_ln2_bias = norm_backward(grad_output, normed2, inverse2, ln2_gain)
    grad_ffn = grad_mix.astype(bf16)
    grad_act = jnp.dot(grad_ffn, w_down.T, preferred_element_type=f32)
    grad_up = gelu_back(grad_act)[0].astype(bf16)
    grad_b_in = jnp.sum(grad_up, axis=0, dtype=f32)
    grad_hidden = grad_mix + jnp.dot(grad_up, w_in.T, preferred_element_type=f32)
    grad_resid, grad_ln1_gain, grad_ln1_bias = norm_backward(
        grad_hidden, normed1, inverse1, ln1_gain
    )
    grad_attn = grad_resid.astype(bf16)
    grad_att = jnp.dot(grad_attn, w_out.T, preferred_element_type=f32).astype(bf16)

    def column_block(array, at, count):
        size = array.shape[1] // count
        return lax.dynamic_slice_in_dim(array, at * size, size, axis=1)

    _, came = spread(None, {at: column_block(grad_att, place ^ at, parts) for at in order})
    grad_att_own = jnp.concatenate([came[at] for at in order], axis=0)
    dqkv, drel, box_sums = attn_bwd(grad_att_own, qkv, probs, relkq, ints, ints_col)

    def docs_columns(array):
        size = array.shape[1] // docs
        chunks = [array[:, at * size : (at + 1) * size] for at in range(docs)]
        return jnp.concatenate(for_docs(chunks, doc_place), axis=1)

    strips = activated_low.reshape(row_count, docs, parts, -1)
    strips = [
        docs_columns(
            lax.dynamic_index_in_dim(strips, place ^ at, axis=2, keepdims=False).reshape(row_count, -1)
        )
        for at in range(parts)
    ]
    got, came = spread(docs_columns(hidden_low), dict(enumerate(strips)))
    hidden_all = jnp.concatenate([got[at] for at in order], axis=0)
    activated_all = jnp.concatenate([came[at] for at in order], axis=0)
    got, came = spread(grad_ffn, {at: column_block(grad_up, place ^ at, parts) for at in order})
    grad_ffn_all = jnp.concatenate([got[at] for at in order], axis=0)
    grad_up_all = jnp.concatenate([came[at] for at in order], axis=0)
    got, came = spread(
        docs_columns(attended), {at: column_block(grad_attn, place ^ at, parts) for at in order}
    )
    attended_all = jnp.concatenate([got[at] for at in order], axis=0)
    grad_attn_all = jnp.concatenate([came[at] for at in order], axis=0)

    def halves(left, right):
        middle = left.shape[1] // 2
        send = dot(left[:, middle:], right, ((0,), (0,))).astype(bf16)
        keep = dot(left[:, :middle], right, ((0,), (0,))).astype(bf16)
        return keep, send

    bits = bits_of(docs)
    down_part = halve(*halves(activated_all, grad_ffn_all), bits)
    in_part = halve(*halves(hidden_all, grad_up_all), bits)
    out_part = halve(*halves(attended_all, grad_attn_all), bits)

    drel_low = drel.astype(bf16)
    left = docs_columns(jnp.concatenate([x_all, rel_table], axis=0))
    right = jnp.concatenate(
        [
            dqkv,
            jnp.concatenate(
                [drel_low[:, width:], drel_low[:, :width], jnp.zeros((buckets, width), bf16)], axis=1
            ),
        ],
        axis=0,
    )
    grad_rel_table = dot(
        drel_low[:, :width], column_block(w_key, place, parts), ((1,), (1,))
    ) + dot(drel_low[:, width:], column_block(w_query, place, parts), ((1,), (1,)))
    plain, less = box_sums[0::2], box_sums[1::2]

    def box_grad(at):
        plain_here, less_here = plain[:, at : at + boxes], less[:, at : at + boxes]
        later = jnp.pad(less_here[:, 1:], ((0, 0), (0, 1)))
        grad = (plain_here - less_here + later).T
        return lax.dynamic_update_slice(jnp.zeros((boxes, heads), f32), grad, (0, place * own_heads))

    small = jnp.concatenate(
        [
            grad_rel_table.reshape(docs, -1),
            grad_ln1_gain.reshape(docs, -1),
            grad_ln1_bias.reshape(docs, -1),
            grad_ln2_gain.reshape(docs, -1),
            grad_ln2_bias.reshape(docs, -1),
            grad_b_in.reshape(docs, -1),
            box_grad(0).reshape(docs, -1),
            box_grad(boxes).reshape(docs, -1),
        ],
        axis=1,
    ).astype(bf16)
    small_width = small.shape[1]
    across = 3 * width
    small = jnp.pad(small, ((0, 0), (0, -small_width % (8 * across))))
    small = for_docs([small[at] for at in range(docs)], doc_place)
    small = jnp.stack(small).reshape(docs, -1, across)
    keep, send = halves(left, right)
    middle = docs // 2
    chunk_rows = model // docs

    def with_small(main, extra):
        main = main.reshape(middle, chunk_rows, across)
        return jnp.concatenate([main, extra], axis=1).reshape(-1, across)

    qkv_part = halve(with_small(keep, small[:middle]), with_small(send, small[middle:]), bits)

    _, came = spread(None, {at: row_block(dqkv, at) for at in order})
    came = by_place([came[at] for at in range(parts)], place)
    grad_tokens = grad_resid
    for at, weight in enumerate((w_query, w_key, w_value)):
        grad = jnp.concatenate([rows[:, at * width : (at + 1) * width] for rows in came], axis=1)
        grad_tokens = grad_tokens + dot(grad, weight, ((1,), (1,)))

    def whole(part):
        got, _ = spread(part, None)
        return by_place([got[at] for at in range(parts)], place)

    grad_w_down = jnp.concatenate(whole(down_part), axis=0).astype(f32)
    grad_w_in = jnp.concatenate(whole(in_part), axis=1).astype(f32)
    grad_w_out = jnp.concatenate(whole(out_part), axis=1).astype(f32)
    pieces = whole(qkv_part)
    grads = [
        jnp.concatenate(
            [piece[:chunk_rows, at * width : (at + 1) * width] for piece in pieces], axis=1
        ).astype(f32)
        for at in range(3)
    ]
    total = sum(piece[chunk_rows:].astype(f32) for piece in pieces).reshape(-1)
    sizes = [
        (buckets // docs, model),
        (model // docs,),
        (model // docs,),
        (model // docs,),
        (model // docs,),
        (hidden_units // docs,),
        (boxes // docs, heads),
        (boxes // docs, heads),
    ]
    small_out = []
    start = 0
    for size in sizes:
        small_out.append(total[start : start + math.prod(size)].reshape(size))
        start += math.prod(size)
    rel_out, ln1g, ln1b, ln2g, ln2b, b_in_out, xb, yb = small_out
    return (
        block_out, grad_tokens[None], ln1g, ln1b, grads[0], grads[1], grads[2], grad_w_out,
        rel_out, xb, yb, ln2g, ln2b, grad_w_in, b_in_out, grad_w_down,
    )


blocks = 4
slots = (0, 2, 1, 3)


def rows_of(handle, tile=None, column=None):
    array, lead = handle if isinstance(handle, tuple) else (handle, None)
    shape = array.shape[-2:] if tile is None else tile
    column = column or (lambda *grid: 0)
    if lead is None:
        return pl.BlockSpec(shape, lambda *grid: (0, column(*grid)))
    return pl.BlockSpec((None,) + shape, lambda *grid: (lead, 0, column(*grid)))


def array_of(handle):
    return handle[0] if isinstance(handle, tuple) else handle


def full(shape):
    return pl.BlockSpec(shape, lambda *grid: (0,) * len(shape))


def cost(us):
    return pl.CostEstimate(flops=int(us * 3 * 10**8), transcendentals=0, bytes_accessed=0)


def ordered(array, *before):
    return lax.optimization_barrier((array,) + before)[0]


def in_hbm(array):
    return pltpu.with_memory_space_constraint(array, pltpu.HBM)


def params(limit):
    return pltpu.CompilerParams(vmem_limit_bytes=limit << 20)


def gelu_parts(u):
    root = math.sqrt(2.0 / math.pi)
    inner = jnp.tanh(root * (u + 0.044715 * u * u * u))
    value = 0.5 * u * (1.0 + inner)
    slope = 0.5 * (1.0 + inner) + 0.5 * u * (1.0 - inner * inner) * root * (
        1.0 + 3.0 * 0.044715 * u * u
    )
    return value, slope


def scores_kernel(
    at_ref, x0, x1, x2, x3, i0, i1, i2, i3, wq_ref, wk_ref, wv_ref, rel_ref, tab_ref,
    own_ref, core_ref, far_ref, probs_ref, qkv_ref, relkq_ref, row_ref, col_ref,
    key_rel, queries, keys_t, values, rel_keys_t, sector_hot,
):
    scale = 1.0 / math.sqrt(192.0)
    step = pl.program_id(0)
    rows = blocks * lanes
    width = wq_ref.shape[1]
    heads = tab_ref.shape[1]
    size = width // heads

    @pl.when(step == 0)
    def _():
        for t, (x_ref, i_ref) in enumerate(zip((x0, x1, x2, x3), (i0, i1, i2, i3))):
            span = slice(t * lanes, (t + 1) * lanes)
            for at, w_ref in enumerate((wq_ref, wk_ref, wv_ref)):
                part = dot(x_ref[...], w_ref[...]).astype(bf16)
                qkv_ref[span, at * width : (at + 1) * width] = part
                if at == 1:
                    keys_t[:, span] = part.astype(f32).T.astype(bf16)
                else:
                    for h in range(heads):
                        (queries, None, values)[at][h, span, :] = part[:, h * size : (h + 1) * size]
            first = jnp.bitwise_xor(at_ref[0], slots[t]) * lanes
            slot = first + lax.broadcasted_iota(jnp.int32, (8, lanes), 1)
            kind = lax.broadcasted_iota(jnp.int32, (8, lanes), 0)
            ints = jnp.where(kind == 3, (slot < at_ref[1]).astype(jnp.int32), i_ref[...])
            row_ref[:, span] = ints
            col_ref[span, :] = ints.astype(f32).T.astype(jnp.int32)
        sector = lax.broadcasted_iota(jnp.int32, (32, rows), 0)
        for k in range(2):
            hot = (jnp.right_shift(row_ref[1 + k : 2 + k, :], 5) == sector).astype(f32).astype(bf16)
            sector_hot[k * 32 : (k + 1) * 32, :] = hot
        rel_keys = dot(rel_ref[...], wk_ref[...])
        relkq_ref[:, :width] = rel_keys.astype(bf16)
        rel_keys_t[...] = rel_keys.T.astype(bf16)
        relkq_ref[:, width:] = dot(rel_ref[...], wq_ref[...]).astype(bf16)
        for h in range(heads):
            cols = slice(width + h * size, width + (h + 1) * size)
            key_rel[h] = (
                dot(qkv_ref[:, cols], relkq_ref[:, cols], ((1,), (1,))).astype(bf16).astype(f32)
            )

    here = pl.ds(pl.multiple_of(step * lanes, lanes), lanes)
    pos_i = col_ref[here, 0:1]
    cx_i = col_ref[here, 1:2]
    cy_i = col_ref[here, 2:3]
    own_row = row_ref[0:1, here]
    lane = lax.broadcasted_iota(jnp.int32, (lanes, lanes), 1)
    on_x = jnp.bitwise_and(jnp.right_shift(lane, 5), 1) == 0
    seek = (
        jnp.where(on_x, jnp.right_shift(cx_i, 5), jnp.right_shift(cy_i, 5) + 64)
        + 32
        - jnp.bitwise_and(lane, 31)
        - (lane >= 64).astype(jnp.int32)
    )
    short_x = jnp.bitwise_and(cx_i, 31) < jnp.bitwise_and(row_ref[1:2, :], 31)
    short_y = jnp.bitwise_and(cy_i, 31) < jnp.bitwise_and(row_ref[2:3, :], 31)
    ahead, mirror = [], []
    for t in range(blocks):
        span = slice(t * lanes, (t + 1) * lanes)
        ahead.append(ahead_of(pos_i, row_ref[0:1, span]))
        mirror.append(ahead_of(col_ref[span, 0:1], own_row))
    valid = row_ref[3:4, :] > 0
    attended = []
    for h in range(heads):
        cols = slice(h * size, (h + 1) * size)
        query = queries[h, here, :]
        rel_scores = dot(query, rel_keys_t[cols, :]).astype(bf16).astype(f32)
        table = jnp.broadcast_to(tab_ref[0, h : h + 1, :], (lanes, lanes))
        by_sector = pick(table, seek).astype(bf16)
        content = dot(query, keys_t[cols, :])
        plain_x = dot(by_sector[:, 0:32], sector_hot[0:32, :])
        plain_y = dot(by_sector[:, 32:64], sector_hot[32:64, :])
        less_x = dot(by_sector[:, 64:96], sector_hot[0:32, :])
        less_y = dot(by_sector[:, 96:128], sector_hot[32:64, :])
        bias = jnp.where(short_x, less_x, plain_x) + jnp.where(short_y, less_y, plain_y)
        moved = []
        for t in range(blocks):
            span = slice(t * lanes, (t + 1) * lanes)
            moved.append(pick(rel_scores, ahead[t]) + pick(key_rel[h, span, :], mirror[t]).T)
        scores = scale * (content + jnp.concatenate(moved, axis=1)) + bias
        scores = jnp.where(valid, scores, mask_value)
        top = jnp.max(scores, axis=1, keepdims=True)
        raised = jnp.exp(scores - top)
        probs = (raised * (1.0 / jnp.sum(raised, axis=1, keepdims=True))).astype(bf16)
        probs_ref[h] = probs
        attended.append(dot(probs, values[h]).astype(bf16))
    attended = jnp.concatenate(attended, axis=1)
    for t, target in enumerate((own_ref, far_ref.at[0], core_ref, far_ref.at[1])):

        @pl.when(step == t)
        def _(target=target):
            target[...] = attended


def scores_call(at, xs, ints, w_query, w_key, w_value, rel_table, tables):
    rows, model = blocks * lanes, w_query.shape[0]
    parts, heads, _ = tables.shape
    width = w_query.shape[1] // parts
    buckets = rel_table.shape[0]
    column = pl.BlockSpec((model, width), lambda i, at: (0, at[0]))
    return pl.pallas_call(
        scores_kernel,
        out_shape=(
            jax.ShapeDtypeStruct((lanes, width), bf16),
            jax.ShapeDtypeStruct((lanes, width), bf16),
            jax.ShapeDtypeStruct((2, lanes, width), bf16),
            pltpu.HBM((heads, rows, rows), bf16),
            pltpu.HBM((rows, 3 * width), bf16),
            pltpu.HBM((buckets, 2 * width), bf16),
            pltpu.HBM((8, rows), jnp.int32),
            pltpu.HBM((rows, 8), jnp.int32),
        ),
        grid_spec=pltpu.PrefetchScalarGridSpec(
            num_scalar_prefetch=1,
            grid=(blocks,),
            in_specs=[rows_of(x) for x in xs]
            + [rows_of(i) for i in ints]
            + [
                column,
                column,
                column,
                full((buckets, model)),
                pl.BlockSpec((1, heads, lanes), lambda i, at: (at[0], 0, 0)),
            ],
            out_specs=[
                full((lanes, width)),
                full((lanes, width)),
                full((2, lanes, width)),
                pl.BlockSpec((heads, lanes, rows), lambda i, at: (0, i, 0)),
                full((rows, 3 * width)),
                full((buckets, 2 * width)),
                full((8, rows)),
                full((rows, 8)),
            ],
            scratch_shapes=[
                pltpu.VMEM((heads, rows, lanes), f32),
                pltpu.VMEM((heads, rows, width // heads), bf16),
                pltpu.VMEM((width, rows), bf16),
                pltpu.VMEM((heads, rows, width // heads), bf16),
                pltpu.VMEM((width, buckets), bf16),
                pltpu.VMEM((64, rows), bf16),
            ],
        ),
        compiler_params=params(18),
        cost_estimate=cost(25),
        name="scores",
    )(
        at, *map(array_of, xs), *map(array_of, ints), w_query, w_key, w_value, rel_table, tables
    )


def up_kernel(
    at_ref, a0, a1, a2, a3, x_ref, wout_ref, gain_ref, bias_ref, win_ref, bin_ref,
    far_ref, core_ref, own_ref, act_ref, slope_ref, normed_ref, inverse_ref, attended_ref,
    hidden_low,
):
    step = pl.program_id(0)
    width = a0.shape[1]
    tile = win_ref.shape[1]

    @pl.when(step == 0)
    def _():
        total = x_ref[...].astype(f32)
        for t, piece in enumerate((a0, a1, a2, a3)):
            first = pl.multiple_of(jnp.bitwise_xor(at_ref[0], slots[t]) * width, width)
            total = total + dot(piece[...], wout_ref[pl.ds(first, width), :])
            attended_ref[:, pl.ds(first, width)] = piece[...]
        centered = total - jnp.mean(total, axis=1, keepdims=True)
        inverse = lax.rsqrt(jnp.mean(centered * centered, axis=1, keepdims=True) + norm_eps)
        normed = centered * inverse
        normed_ref[...] = normed
        inverse_ref[...] = jnp.broadcast_to(inverse, inverse_ref.shape)
        hidden = (normed * gain_ref[...] + bias_ref[...]).astype(bf16)
        hidden_low[...] = hidden

    value, slope = gelu_parts(dot(hidden_low[...], win_ref[...]) + bin_ref[...])
    value = value.astype(bf16)
    act_ref[...] = value
    slope_ref[...] = slope.astype(bf16)
    strip = tile // blocks
    here = pl.ds(pl.multiple_of(step * strip, strip), strip)
    for t, target in enumerate((own_ref, far_ref.at[0], core_ref, far_ref.at[1])):
        first = pl.multiple_of(jnp.bitwise_xor(at_ref[0], slots[t]) * strip, strip)
        target[:, here] = act_ref[:, pl.ds(first, strip)]


def up_call(at, pieces, x_own, w_out, gain, bias, w_in, b_in, docs):
    rows, model = x_own.shape
    units = w_in.shape[1]
    tile = units // docs
    quarter = units // blocks
    column = lambda i, at: (0, i)
    return pl.pallas_call(
        up_kernel,
        out_shape=(
            jax.ShapeDtypeStruct((2, rows, quarter), bf16),
            jax.ShapeDtypeStruct((rows, quarter), bf16),
            jax.ShapeDtypeStruct((rows, quarter), bf16),
            jax.ShapeDtypeStruct((rows, units), bf16),
            jax.ShapeDtypeStruct((rows, units), bf16),
            jax.ShapeDtypeStruct((rows, model), f32),
            jax.ShapeDtypeStruct((rows, lanes), f32),
            jax.ShapeDtypeStruct((rows, model), bf16),
            jax.ShapeDtypeStruct((rows, model), bf16),
        ),
        grid_spec=pltpu.PrefetchScalarGridSpec(
            num_scalar_prefetch=1,
            grid=(docs,),
            in_specs=[rows_of(piece) for piece in pieces]
            + [
                full((rows, model)),
                full((model, model)),
                full((1, model)),
                full((1, model)),
                pl.BlockSpec((model, tile), column),
                pl.BlockSpec((1, tile), column),
            ],
            out_specs=[
                full((2, rows, quarter)),
                full((rows, quarter)),
                full((rows, quarter)),
                pl.BlockSpec((rows, tile), column),
                pl.BlockSpec((rows, tile), column),
                full((rows, model)),
                full((rows, lanes)),
                full((rows, model)),
                full((rows, model)),
            ],
        ),
        compiler_params=params(18),
        cost_estimate=cost(9),
        name="up",
    )(at, *map(array_of, pieces), x_own, w_out, gain, bias, w_in, b_in)


def norm_back(grad, normed, inverse, gain):
    scaled = grad * gain
    return inverse * (
        scaled
        - jnp.mean(scaled, axis=1, keepdims=True)
        - normed * jnp.mean(scaled * normed, axis=1, keepdims=True)
    )


def down_kernel(
    act_ref, wdown_ref, normed_ref, cot_ref, gain1_ref, bias1_ref, gain2_ref, bias2_ref,
    block_ref, mix_ref, low_ref, sums_ref,
):
    step = pl.program_id(0)

    @pl.when(step == 0)
    def _():
        mix_ref[...] = normed_ref[...] * gain1_ref[...] + bias1_ref[...]

    mix_ref[...] += dot(act_ref[...], wdown_ref[...])

    @pl.when(step == pl.num_programs(0) - 1)
    def _():
        mixed = mix_ref[...]
        centered = mixed - jnp.mean(mixed, axis=1, keepdims=True)
        inverse = lax.rsqrt(jnp.mean(centered * centered, axis=1, keepdims=True) + norm_eps)
        normed = centered * inverse
        block_ref[...] = (normed * gain2_ref[...] + bias2_ref[...]).astype(bf16)
        grad = cot_ref[...].astype(f32)
        sums_ref[0:1, :] = jnp.sum(grad * normed, axis=0, keepdims=True)
        sums_ref[1:2, :] = jnp.sum(grad, axis=0, keepdims=True)
        mix = norm_back(grad, normed, inverse, gain2_ref[...])
        mix_ref[...] = mix
        low_ref[...] = mix.astype(bf16)


def down_call(act, w_down, normed, cotangent, gain1, bias1, gain2, bias2, tile):
    rows, units = act.shape
    model = w_down.shape[1]
    return pl.pallas_call(
        down_kernel,
        out_shape=(
            jax.ShapeDtypeStruct((rows, model), bf16),
            jax.ShapeDtypeStruct((rows, model), f32),
            jax.ShapeDtypeStruct((rows, model), bf16),
            jax.ShapeDtypeStruct((8, model), f32),
        ),
        grid=(units // tile,),
        in_specs=[
            pl.BlockSpec((rows, tile), lambda i: (0, i)),
            pl.BlockSpec((tile, model), lambda i: (i, 0)),
            full((rows, model)),
            full((rows, model)),
        ]
        + [full((1, model))] * 4,
        out_specs=[full((rows, model))] * 3 + [full((8, model))],
        compiler_params=params(18),
        cost_estimate=cost(8),
        name="down",
    )(act, w_down, normed, cotangent, gain1, bias1, gain2, bias2)


def back_kernel(
    at_ref, wdown_ref, slope_ref, win_ref, wout_ref, normed_ref, inverse_ref, mix_ref, ffn_ref,
    attended_ref, gain1_ref, above_ref, hidden_ref,
    own_ref, core_ref, far_ref, resid_ref, upfar_ref, upcore_ref, upown_ref,
    outfar_ref, outcore_ref, outown_ref, sums_ref,
    total, grad_up,
):
    step = pl.program_id(0)
    steps = pl.num_programs(0)
    rows, tile = slope_ref.shape
    model = mix_ref.shape[1]
    width = model // blocks

    @pl.when(step == 0)
    def _():
        total[...] = mix_ref[...]

    grad = dot(ffn_ref[...], wdown_ref[...], ((1,), (1,))) * slope_ref[...].astype(f32)
    low = grad.astype(bf16)
    total[...] += dot(low, win_ref[...], ((1,), (1,)))
    per = model // tile
    part = step // per
    here = pl.ds(pl.multiple_of((step - part * per) * tile, tile), tile)
    grad_up[jnp.bitwise_xor(part, at_ref[0]), :, here] = low
    sums_ref[pl.ds(4 + part, 1), here] = jnp.sum(low.astype(f32), axis=0, keepdims=True)

    @pl.when(step == steps - 1)
    def _():
        upown_ref[...] = grad_up[0]
        upcore_ref[0] = hidden_ref[...]
        upcore_ref[1] = grad_up[1]
        upfar_ref[0] = hidden_ref[...]
        upfar_ref[1] = grad_up[2]
        upfar_ref[2] = grad_up[3]
        grad = total[...]
        normed = normed_ref[...]
        sums_ref[0:1, :] = jnp.sum(grad * normed, axis=0, keepdims=True)
        sums_ref[1:2, :] = jnp.sum(grad, axis=0, keepdims=True)
        sums_ref[2:4, :] = above_ref[0:2, :]
        resid = norm_back(grad, normed, inverse_ref[:, 0:1], gain1_ref[...])
        resid_ref[...] = resid
        low = resid.astype(bf16)
        total[...] = low.astype(f32)
        outfar_ref[:, :model] = attended_ref[...]
        outcore_ref[:, :model] = attended_ref[...]
        targets = (own_ref, core_ref, far_ref.at[0], far_ref.at[1])
        wides = (
            outown_ref, outcore_ref.at[:, pl.ds(model, width)],
            outfar_ref.at[:, pl.ds(model, width)], outfar_ref.at[:, pl.ds(model + width, width)],
        )
        for at, (target, wide) in enumerate(zip(targets, wides)):
            first = pl.multiple_of(jnp.bitwise_xor(at_ref[0], at) * width, width)
            target[...] = dot(low, wout_ref[pl.ds(first, width), :], ((1,), (1,))).astype(bf16)
            wide[...] = total[:, pl.ds(first, width)].astype(bf16)


def back_call(
    at, w_down, slope, w_in, w_out, normed, inverse, mix, grad_ffn, attended, gain1, above, hidden, tile,
):
    rows, units = slope.shape
    model = w_out.shape[0]
    width = model // blocks
    return pl.pallas_call(
        back_kernel,
        out_shape=(
            jax.ShapeDtypeStruct((rows, width), bf16),
            jax.ShapeDtypeStruct((rows, width), bf16),
            jax.ShapeDtypeStruct((2, rows, width), bf16),
            jax.ShapeDtypeStruct((rows, model), f32),
            jax.ShapeDtypeStruct((3, rows, model), bf16),
            jax.ShapeDtypeStruct((2, rows, model), bf16),
            jax.ShapeDtypeStruct((rows, model), bf16),
            jax.ShapeDtypeStruct((rows, model + 2 * width), bf16),
            jax.ShapeDtypeStruct((rows, model + width), bf16),
            jax.ShapeDtypeStruct((rows, width), bf16),
            jax.ShapeDtypeStruct((8, model), f32),
        ),
        grid_spec=pltpu.PrefetchScalarGridSpec(
            num_scalar_prefetch=1,
            grid=(units // tile,),
            in_specs=[
                pl.BlockSpec((tile, model), lambda i, at: (i, 0)),
                pl.BlockSpec((rows, tile), lambda i, at: (0, i)),
                pl.BlockSpec((model, tile), lambda i, at: (0, i)),
                full((model, model)),
                full((rows, model)),
                full((rows, lanes)),
                full((rows, model)),
                full((rows, model)),
                full((rows, model)),
                full((1, model)),
                full((8, model)),
                full((rows, model)),
            ],
            out_specs=[
                full((rows, width)),
                full((rows, width)),
                full((2, rows, width)),
                full((rows, model)),
                full((3, rows, model)),
                full((2, rows, model)),
                full((rows, model)),
                full((rows, model + 2 * width)),
                full((rows, model + width)),
                full((rows, width)),
                full((8, model)),
            ],
            scratch_shapes=[
                pltpu.VMEM((rows, model), f32),
                pltpu.VMEM((blocks, rows, model), bf16),
            ],
        ),
        compiler_params=params(18),
        cost_estimate=cost(12),
        name="back",
    )(at, w_down, slope, w_in, w_out, normed, inverse, mix, grad_ffn, attended, gain1, above, hidden)


def scores_grad_kernel(half, held, *refs):
    at_ref, g0, g1, g2, g3, qkv_ref, probs_ref, relkq_ref, row_ref, col_ref = refs[:10]
    refs = refs[10:]
    last = half == 1
    if last:
        wq_ref, wk_ref, sums_ref, before_ref, boxes_before = refs[:5]
        refs = refs[5:]
    refs = refs[held:]
    if last:
        dqkv_ref, own_ref, core_ref, far_ref, small_ref, ga_ref, ds_ref, drel, own_qkv, box_sums = refs
    else:
        dqkv_ref, box_sums, ga_ref, ds_ref, drel, own_qkv = refs
    scale = 1.0 / math.sqrt(192.0)
    rows = blocks * lanes
    width = qkv_ref.shape[1] // 3
    part = width // 2
    heads = probs_ref.shape[0]
    size = part // heads
    short = lanes // 2
    for t, piece in enumerate((g0, g1, g2, g3)):
        ga_ref[t * lanes : (t + 1) * lanes, :] = piece[...]
    for k in range(3):
        for h in range(heads):
            first = k * width + half * part + h * size
            own_qkv[k * heads + h] = qkv_ref[:, first : first + size]
    drel[...] = jnp.zeros_like(drel)
    box_sums[...] = jnp.zeros_like(box_sums)
    window = lax.broadcasted_iota(jnp.int32, (rows, 2 * lanes), 1)
    bucket = lax.broadcasted_iota(jnp.int32, (lanes, lanes), 1)
    label = lax.broadcasted_iota(jnp.int32, (rows, lanes), 1)
    all_pos = col_ref[:, 0:1]
    all_x, all_y = col_ref[:, 1:2], col_ref[:, 2:3]
    sector_x, sector_y = jnp.right_shift(all_x, 5), jnp.right_shift(all_y, 5)
    hot_x = (label == sector_x).astype(f32).astype(bf16)
    hot_y = (label == sector_y + 64).astype(f32).astype(bf16)
    hot_both = hot_x + hot_y

    def shares(grads, start):
        found = []
        for u in range(2):
            at = col_ref[pl.ds(pl.multiple_of(start + u * short, short), short), 0:1]
            base = jnp.min(at, axis=0, keepdims=True)
            below = (all_pos <= base - 63 + window) | (window == 2 * lanes - 1)
            stacked = jnp.concatenate([g[u * short : (u + 1) * short, :] for g in grads], axis=0)
            sums = dot(stacked, below.astype(f32).astype(bf16))
            first = at - base + (lanes - 1) - bucket[:short]
            first = jnp.concatenate([first] * heads, axis=0)
            low = jnp.bitwise_and(first, lanes - 1)
            value = jnp.where(
                first < lanes, pick(sums[:, :lanes], low), pick(sums[:, lanes:], low)
            )
            value = jnp.where(bucket == 0, sums[:, 2 * lanes - 1 :], value)
            later = jnp.where(bucket == lanes - 1, 0.0, pltpu.roll(value, lanes - 1, 1))
            found.append(scale * (value - later))
        return [
            jnp.concatenate([f[h * short : (h + 1) * short, :] for f in found], axis=0).astype(bf16)
            for h in range(heads)
        ]

    def by_rows(ib, carry):
        start = ib * lanes
        here = pl.ds(pl.multiple_of(start, lanes), lanes)
        cx_i, cy_i = col_ref[here, 1:2], col_ref[here, 2:3]
        short_x = jnp.bitwise_and(cx_i, 31) < jnp.bitwise_and(row_ref[1:2, :], 31)
        short_y = jnp.bitwise_and(cy_i, 31) < jnp.bitwise_and(row_ref[2:3, :], 31)
        short_x = short_x.astype(f32).astype(bf16)
        short_y = short_y.astype(f32).astype(bf16)
        step_x = jnp.right_shift(cx_i, 5) + 32 - bucket
        step_y = jnp.right_shift(cy_i, 5) + 32 - (bucket - 64)
        in_x = (bucket < 64) & (step_x >= 0) & (step_x < 32)
        in_y = (bucket >= 64) & (step_y >= 0) & (step_y < 32)
        seek = jnp.where(in_x, step_x, jnp.where(in_y, step_y + 64, 0))
        inside = in_x | in_y
        grads = []
        for h in range(heads):
            probs = probs_ref[h, here, :].astype(f32)
            gained = dot(ga_ref[here, h * size : (h + 1) * size], own_qkv[2 * heads + h], ((1,), (1,)))
            row_dots = jnp.sum(probs * gained, axis=1, keepdims=True)
            grad = (probs * (gained - row_dots)).astype(bf16)
            ds_ref[h, here, :] = grad
            grads.append(grad)
        rels = shares(grads, start)
        for h, (grad, rel) in enumerate(zip(grads, rels)):
            gcols = slice(h * size, (h + 1) * size)
            kgcols = slice(half * part + h * size, half * part + (h + 1) * size)
            dqkv_ref[here, gcols] = (
                scale * dot(grad, own_qkv[heads + h]) + dot(rel, relkq_ref[:, kgcols])
            ).astype(bf16)
            drel[:, gcols] += dot(rel, own_qkv[h, here, :], ((0,), (0,)))
        stacked = jnp.concatenate(grads, axis=0)
        plain = dot(stacked, hot_both)
        less = dot(jnp.concatenate([g * short_x for g in grads], axis=0), hot_x) + dot(
            jnp.concatenate([g * short_y for g in grads], axis=0), hot_y
        )
        for h in range(heads):
            span = slice(h * lanes, (h + 1) * lanes)
            own_plain = jnp.where(inside, pick(plain[span, :], seek), 0.0)
            own_less = jnp.where(inside, pick(less[span, :], seek), 0.0)
            box_sums[h : h + 1, :] += jnp.sum(own_plain, axis=0, keepdims=True)
            box_sums[8 + h : 9 + h, :] += jnp.sum(own_less, axis=0, keepdims=True)
        return carry

    lax.fori_loop(0, blocks, by_rows, 0)

    def by_columns(jb, carry):
        start = jb * lanes
        here = pl.ds(pl.multiple_of(start, lanes), lanes)
        grads = [ds_ref[h, :, here].T for h in range(heads)]
        mirrors = shares(grads, start)
        for h, (grad, mirror) in enumerate(zip(grads, mirrors)):
            gcols = slice(h * size, (h + 1) * size)
            kgcols = slice(part + h * size, part + (h + 1) * size)
            vgcols = slice(2 * part + h * size, 2 * part + (h + 1) * size)
            kcols = slice(width + half * part + h * size, width + half * part + (h + 1) * size)
            dqkv_ref[here, kgcols] = (
                scale * dot(grad, own_qkv[h]) + dot(mirror, relkq_ref[:, kcols])
            ).astype(bf16)
            drel[:, kgcols] += dot(mirror, own_qkv[heads + h, here, :], ((0,), (0,)))
            dqkv_ref[here, vgcols] = dot(
                probs_ref[h, :, here], ga_ref[:, gcols], ((0,), (0,))
            ).astype(bf16)
        return carry

    lax.fori_loop(0, blocks, by_columns, 0)
    keys, queries = drel[:, :part].astype(bf16), drel[:, part:].astype(bf16)
    dqkv_ref[rows:, :part] = queries
    dqkv_ref[rows:, part : 2 * part] = keys
    dqkv_ref[rows:, 2 * part :] = jnp.zeros((lanes, part), bf16)
    if not last:
        return
    for t, target in enumerate((own_ref, far_ref.at[0], core_ref, far_ref.at[1])):
        span = slice(t * lanes, (t + 1) * lanes)
        for k in range(3):
            first = k * width
            target[:, first : first + part] = before_ref[span, k * part : (k + 1) * part]
            target[:, first + part : first + width] = dqkv_ref[span, k * part : (k + 1) * part]
    queries = jnp.concatenate([before_ref[rows:, :part], queries], axis=1)
    keys = jnp.concatenate([before_ref[rows:, part : 2 * part], keys], axis=1)

    docs, small_rows, small_width = small_ref.shape
    per = lanes // docs
    table = (
        dot(keys, wk_ref[...], ((1,), (1,))) + dot(queries, wq_ref[...], ((1,), (1,)))
    ).astype(bf16)
    plain = jnp.concatenate([boxes_before[0:heads], box_sums[0:heads], box_sums[heads + heads : 8]], axis=0)
    less = jnp.concatenate(
        [boxes_before[8 : 8 + heads], box_sums[8 : 8 + heads], box_sums[8 + 2 * heads : 16]], axis=0
    )
    heads = 2 * heads
    place_lane = lax.broadcasted_iota(jnp.int32, (8, lanes), 1)
    later = jnp.where(
        jnp.bitwise_and(place_lane, 63) == 63, 0.0, pltpu.roll(less, lanes - 1, 1)
    )
    boxes = (plain - less + later).astype(bf16)
    row_at = lax.broadcasted_iota(jnp.int32, (8, lanes), 0)
    head_at = at_ref[0] * heads + row_at
    by_head = [
        dot(boxes, ((place_lane == head_at + k * 64) & (row_at < heads)).astype(bf16), ((0,), (0,)))
        for k in range(2)
    ]
    model = table.shape[1]
    edges = list(range(0, model, small_width)) + [model]
    rest = edges[-1] - edges[-2]
    lane = slice(rest, rest + lanes)
    line = (len(edges) - 2) * per
    count = lanes // 2 // docs
    for chunk in range(docs):
        own = slice(chunk * per, (chunk + 1) * per)
        for k, (first, end) in enumerate(zip(edges[:-1], edges[1:])):
            small_ref[chunk, k * per : (k + 1) * per, : end - first] = table[own, first:end].astype(f32)
        for k in range(4):
            small_ref[chunk, line + k : line + k + 1, lane] = (
                sums_ref[k : k + 1, chunk * lanes : (chunk + 1) * lanes]
            )
            first = (chunk * blocks + k) * lanes
            where = first // model
            small_ref[chunk, line + 4 + k : line + 5 + k, lane] = (
                sums_ref[4 + where : 5 + where, first - where * model : first - where * model + lanes]
            )
        begin = chunk * count
        small_ref[chunk, line + 8 : line + 8 + count, lane] = (
            by_head[0][begin : begin + count, :] + by_head[1][64 + begin : 64 + begin + count, :]
        )


def scores_grad_call(half, at, pieces, qkv, probs, relkq, row, col, after, docs=0, extra=()):
    rows = blocks * lanes
    heads = probs.shape[0] // 2
    width = qkv.shape[1] // 3
    part = width // 2
    model = width * blocks
    buckets = relkq.shape[0]
    column = pl.BlockSpec((model, width), lambda i, at: (0, at[0]))
    grads = jax.ShapeDtypeStruct((rows + buckets, 3 * part), bf16)
    box_shape = (16, lanes)
    scratch = [
        pltpu.VMEM((rows, part), bf16),
        pltpu.VMEM((heads, rows, rows), bf16),
        pltpu.VMEM((buckets, 2 * part), f32),
        pltpu.VMEM((3 * heads, rows, part // heads), bf16),
    ]
    extra_specs = []
    if half == 1:
        shapes = (
            grads,
            jax.ShapeDtypeStruct((lanes, 3 * width), bf16),
            jax.ShapeDtypeStruct((lanes, 3 * width), bf16),
            jax.ShapeDtypeStruct((2, lanes, 3 * width), bf16),
            jax.ShapeDtypeStruct((docs, 3 * buckets // docs, 3 * part), f32),
        )
        extra_specs = [column, column, full((8, model)), full(grads.shape), full(box_shape)]
        scratch = scratch + [pltpu.VMEM(box_shape, f32)]
    else:
        shapes = (grads, jax.ShapeDtypeStruct(box_shape, f32))
    at = ordered(at, *after) if after else at
    return pl.pallas_call(
        functools.partial(scores_grad_kernel, half, 0),
        out_shape=shapes,
        grid_spec=pltpu.PrefetchScalarGridSpec(
            num_scalar_prefetch=1,
            grid=(1,),
            in_specs=[rows_of(piece, (lanes, part), lambda i, at: half) for piece in pieces]
            + [
                full((rows, 3 * width)),
                pl.BlockSpec((heads, rows, rows), lambda i, at: (half, 0, 0)),
                full((buckets, 2 * width)),
                full((8, rows)),
                full((rows, 8)),
            ]
            + extra_specs,
            out_specs=[full(shape.shape) for shape in shapes],
            scratch_shapes=scratch,
        ),
        compiler_params=params(18),
        cost_estimate=cost(15),
        name="scores_grad",
    )(at, *map(array_of, pieces), qkv, probs, relkq, row, col, *extra)


def weight_grads_call(at, wholes, after=(), name="weight_grads"):
    count = 1 << len(wholes[0][1])
    chunk = lanes
    per = 2
    steps = count // per
    half = steps // 2

    def chunk_of(bits, which):
        def index(i, at):
            p = lax.rem(i + half, steps) * per + which
            total = 0
            for place, bit in enumerate(bits):
                total = total + jnp.bitwise_and(jnp.right_shift(p, len(bits) - 1 - place), 1) * bit
            return jnp.bitwise_xor(at[1], total)

        return index

    def kernel(at_ref, *refs):
        refs = list(refs)
        take = lambda number: [refs.pop(0) for _ in range(number)]
        ins = []
        for groups, bits, extra in wholes:
            sides = [(take(len(lefts) * per), take(len(rights))) for lefts, rights, _ in groups]
            ins.append((sides, take(per) if extra is not None else []))
        outs = [take(2) for _ in wholes]
        step = pl.program_id(0)
        for (sides, extras), (keep_ref, send_ref) in zip(ins, outs):
            results = []
            for own, right_refs in sides:
                right_all = refs.pop(0)

                @pl.when(step == 0)
                def _(right_refs=right_refs, right_all=right_all):
                    for k, ref in enumerate(right_refs):
                        right_all[k * lanes : (k + 1) * lanes, :] = ref[...]

                left = jnp.concatenate(
                    [
                        jnp.concatenate([own[k + which][...] for which in range(per)], axis=1)
                        for k in range(0, len(own), per)
                    ],
                    axis=0,
                )
                results.append(dot(left, right_all[...], ((0,), (0,))).astype(bf16))
            for target, mine in ((send_ref, step < half), (keep_ref, step >= half)):

                @pl.when(mine)
                def _(target=target, results=results, extras=extras):
                    for which in range(per):
                        first = 0
                        for result in results:
                            end = first + result.shape[1]
                            target[which, :chunk, first:end] = (
                                result[which * chunk : (which + 1) * chunk, :]
                            )
                            first = end
                        if extras:
                            target[which, chunk:, :] = extras[which][...].astype(bf16)

    in_specs, operands, scratch, shapes, out_specs = [], [], [], [], []
    for groups, bits, extra in wholes:
        total_width = sum(width for _, _, width in groups)
        tail = 0 if extra is None else extra.shape[1]
        for lefts, rights, width in groups:
            for handle in lefts:
                for which in range(per):
                    in_specs.append(rows_of(handle, (lanes, chunk), chunk_of(bits, which)))
                    operands.append(array_of(handle))
            for handle in rights:
                column = handle[2] if isinstance(handle, tuple) and len(handle) == 3 else 0
                handle = (
                    handle[:2] if isinstance(handle, tuple) and handle[1] is not None else array_of(handle)
                )
                in_specs.append(rows_of(handle, (lanes, width), lambda i, at, column=column: column))
                operands.append(array_of(handle))
            scratch.append(pltpu.VMEM((len(rights) * lanes, width), bf16))
        for which in range(per if extra is not None else 0):
            index = chunk_of(bits, which)
            in_specs.append(
                pl.BlockSpec(
                    (None, tail, total_width), lambda i, at, index=index: (index(i, at), 0, 0)
                )
            )
            operands.append(extra)
        shapes += [jax.ShapeDtypeStruct((count // 2, chunk + tail, total_width), bf16)] * 2
        block = (per, chunk + tail, total_width)
        out_specs += [
            pl.BlockSpec(block, lambda i, at: (jnp.maximum(i - half, 0), 0, 0)),
            pl.BlockSpec(block, lambda i, at: (jnp.minimum(i, half - 1), 0, 0)),
        ]
    at = ordered(at, *after) if after else at
    out = pl.pallas_call(
        kernel,
        out_shape=tuple(shapes),
        grid_spec=pltpu.PrefetchScalarGridSpec(
            num_scalar_prefetch=1,
            grid=(steps,),
            in_specs=in_specs,
            out_specs=out_specs,
            scratch_shapes=scratch,
        ),
        compiler_params=params(18),
        cost_estimate=cost(0.01),
        name=name,
    )(at, *operands)
    return [tuple(out[k : k + 2]) for k in range(0, len(out), 2)]


def tokens_grad_kernel(at_ref, d0, d1, d2, d3, resid_ref, wq_ref, wk_ref, wv_ref, *refs):
    out_ref = refs[-1]
    step = pl.program_id(0)
    width = wq_ref.shape[1]

    @pl.when(step == 0)
    def _():
        out_ref[...] = resid_ref[...]

    for t, piece in enumerate((d0, d1, d2, d3)):

        @pl.when(step == t)
        def _(piece=piece):
            total = out_ref[...]
            for at, w_ref in enumerate((wq_ref, wk_ref, wv_ref)):
                total = total + dot(
                    piece[:, at * width : (at + 1) * width], w_ref[...], ((1,), (1,))
                )
            out_ref[...] = total


def tokens_grad_call(at, pieces, resid, w_query, w_key, w_value, after):
    rows, model = resid.shape
    width = model // blocks
    tile = (rows, 3 * width)

    def column(i, at):
        offset = jnp.where(i == 1, 2, jnp.where(i == 2, 1, i))
        return (0, jnp.bitwise_xor(at[0], offset))

    weight = pl.BlockSpec((model, width), column)
    at = ordered(at, *after) if after else at
    return pl.pallas_call(
        tokens_grad_kernel,
        out_shape=jax.ShapeDtypeStruct((rows, model), f32),
        grid_spec=pltpu.PrefetchScalarGridSpec(
            num_scalar_prefetch=1,
            grid=(blocks,),
            in_specs=[rows_of(piece, tile) for piece in pieces]
            + [full((rows, model)), weight, weight, weight],
            out_specs=full((rows, model)),
        ),
        compiler_params=params(18),
        cost_estimate=cost(4),
        name="tokens_grad",
    )(at, *map(array_of, pieces), resid, w_query, w_key, w_value)


def parts_kernel(fields, at_ref, *refs):
    step = pl.program_id(0)
    parts, outs = refs[: blocks * fields], refs[blocks * fields :]
    for field in range(fields):
        for at in range(blocks):

            @pl.when(step == at)
            def _(part=parts[field * blocks + at], out=outs[field]):
                out[...] = part[...].astype(f32)


def parts_call(at, fields, name):
    in_specs, operands, shapes, out_specs = [], [], [], []
    for parts, axis in fields:
        rows, width = parts[0].shape
        in_specs += [full((rows, width))] * blocks
        operands += list(parts)
        shape = (rows * blocks, width) if axis == 0 else (rows, width * blocks)
        shapes.append(jax.ShapeDtypeStruct(shape, f32))

        def index(i, at, axis=axis):
            spot = jnp.bitwise_xor(at[0], i)
            return (spot, 0) if axis == 0 else (0, spot)

        out_specs.append(pl.BlockSpec((rows, width), index))
    return pl.pallas_call(
        functools.partial(parts_kernel, len(fields)),
        out_shape=tuple(shapes),
        grid_spec=pltpu.PrefetchScalarGridSpec(
            num_scalar_prefetch=1, grid=(blocks,), in_specs=in_specs, out_specs=out_specs
        ),
        compiler_params=params(18),
        cost_estimate=cost(2),
        name=name,
    )(at, *operands)


def last_kernel(at_ref, *refs):
    step = pl.program_id(0)
    firsts, seconds, outs = refs[:blocks], refs[blocks : 2 * blocks], refs[2 * blocks : 2 * blocks + 3]
    wout_ref, rel_ref, *small_refs = refs[2 * blocks + 3 :]
    norm_refs, (bin_ref, xbox_ref, ybox_ref) = small_refs[:4], small_refs[4:]
    for at in range(blocks):

        @pl.when(step == at)
        def _(first=firsts[at], second=seconds[at]):
            for k, out in enumerate(outs):
                span = slice(k * lanes, (k + 1) * lanes)
                out[:, :lanes] = first[:, span].astype(f32)
                out[:, lanes:] = second[:lanes, span].astype(f32)
            wout_ref[...] = first[:, 3 * lanes :].astype(f32)

    @pl.when(step == 0)
    def _():
        total = seconds[0][lanes:, :].astype(f32)
        for second in seconds[1:]:
            total = total + second[lanes:, :].astype(f32)
        rows = rel_ref.shape[0]
        width = total.shape[1]
        for k in range(3):
            end = min((k + 1) * width, rel_ref.shape[1])
            rel_ref[:, k * width : end] = total[k * rows : (k + 1) * rows, : end - k * width]
        rest = total[2 * rows :, width - lanes :]
        for k in range(4):
            norm_refs[k][...] = rest[k]
            bin_ref[k * lanes : (k + 1) * lanes] = rest[4 + k]
        heads = xbox_ref.shape[1]
        xbox_ref[...] = rest[8:16, :heads]
        ybox_ref[...] = rest[8:16, 64 : 64 + heads]


def last_call(at, firsts, seconds, buckets, model, heads):
    wide = jax.ShapeDtypeStruct((lanes, model), f32)
    small_shapes = ((buckets, model),) + ((lanes,),) * 4 + ((blocks * lanes,), (8, heads), (8, heads))
    column = pl.BlockSpec((lanes, model // blocks), lambda i, at: (0, jnp.bitwise_xor(at[0], i)))
    return pl.pallas_call(
        last_kernel,
        out_shape=(wide, wide, wide, wide)
        + tuple(jax.ShapeDtypeStruct(shape, f32) for shape in small_shapes),
        grid_spec=pltpu.PrefetchScalarGridSpec(
            num_scalar_prefetch=1,
            grid=(blocks,),
            in_specs=[full(part.shape) for part in firsts + seconds],
            out_specs=[column] * 4 + [full(shape) for shape in small_shapes],
        ),
        compiler_params=params(18),
        cost_estimate=cost(2),
        name="last",
    )(at, *firsts, *seconds)


class Halving:
    def __init__(self, halves, bits):
        self.keep, self.send = halves
        self.bits = list(bits)
        self.step()

    def step(self):
        self.came = swap(self.send, "docs", self.bits.pop(0))

    def add(self, *before):
        keep, came = self.keep, self.came
        if before:
            came = ordered(came, *before)
        total = lambda part: (keep[part].astype(f32) + came[part].astype(f32)).astype(bf16)
        if not self.bits:
            self.keep = self.send = total(slice(None))[0]
            return self.keep
        middle = keep.shape[0] // 2
        self.send = total(slice(middle, None))
        self.keep = total(slice(0, middle))
        sent = self.send
        self.step()
        return sent


def shards_tiles(
    tokens, lengths, positions, token_boxes, ln1_gain, ln1_bias, w_query, w_key, w_value, w_out,
    rel_table, xbias_table, ybias_table, ln2_gain, ln2_bias, w_in, b_in, w_down, cotangent,
):
    row_count, model = tokens.shape[1:]
    docs = lax.axis_size("docs")
    place = lax.axis_index("blk")
    doc_place = lax.axis_index("docs")
    heads = xbias_table.shape[1]
    boxes = xbias_table.shape[0]
    units = w_in.shape[1]
    width = model // blocks
    bits = bits_of(docs)
    other = [bits[1], bits[0]] + bits[2:]
    x_own = tokens[0]
    w_query, w_key, w_value = in_hbm(w_query), in_hbm(w_key), in_hbm(w_value)

    x_far = swap(x_own, "blk", 2)
    own_ints = jnp.concatenate(
        [
            positions,
            jnp.right_shift(token_boxes[0] + token_boxes[2], 1),
            jnp.right_shift(token_boxes[1] + token_boxes[3], 1),
            jnp.zeros((5, row_count), jnp.int32),
        ],
        axis=0,
    )
    ints_far = swap(own_ints, "blk", 2)
    x_core, ints_core = swap(x_own, "blk", 1), swap(own_ints, "blk", 1)
    x_both, ints_both = swap(ordered(x_far, ints_far), "blk", 1), swap(ints_far, "blk", 1)
    xs = tuple(map(in_hbm, (x_own, x_far, x_core, x_both)))
    tables = jnp.concatenate([xbias_table.T, ybias_table.T], axis=1).astype(f32)
    tables = tables.reshape(blocks, heads // blocks, 2 * boxes)
    at = jnp.stack([place.astype(jnp.int32), lengths[0]])
    spot = jnp.stack([place, doc_place]).astype(jnp.int32)
    att_own, att_core, att_far, probs, qkv, relkq, row, col = scores_call(
        at, xs, (own_ints, ints_far, ints_core, ints_both), w_query, w_key, w_value, rel_table, tables
    )

    came_far = swap(att_far, "blk", 2)
    came_core = swap(att_core, "blk", 1)
    came_both = swap(came_far, "blk", 1)
    line = lambda vector: vector.reshape(1, -1)
    far1, core1, act_own, act, slope, normed1, inverse1, attended, hidden = up_call(
        spot, (att_own, (came_far, 0), came_core, (came_both, 1)), x_own, w_out,
        line(ln1_gain), line(ln1_bias), in_hbm(w_in), line(b_in), docs,
    )
    got_far1 = swap(far1, "blk", 2)
    block_out, mix, grad_ffn, above = down_call(
        act, w_down, normed1, cotangent[0],
        line(ln1_gain), line(ln1_bias), line(ln2_gain), line(ln2_bias), units // docs,
    )
    (
        ga_own, ga_core, ga_far, grad_resid, up_far, up_core, up_own, far3, core3, gattn_own, sums,
    ) = back_call(
        spot, w_down, slope, w_in, w_out, normed1, inverse1, mix, grad_ffn, attended,
        line(ln1_gain), above, hidden, units // docs,
    )
    came_far = swap(ga_far, "blk", 2)
    came_core = swap(ga_core, "blk", 1)
    came_both = swap(came_far, "blk", 1)
    ga_all = (ga_own, (came_far, 0), came_core, (came_both, 1))
    ffn_far = swap(grad_ffn, "blk", 2)
    got_core1, got_both1 = swap(core1, "blk", 1), swap(ordered(got_far1, ga_own), "blk", 1)
    ffn_core, ffn_both = swap(grad_ffn, "blk", 1), swap(ordered(ffn_far, ga_own), "blk", 1)
    act_all = [act_own, (got_far1, 0), got_core1, (got_both1, 1)]
    gffn_all = [grad_ffn, ffn_far, ffn_core, ffn_both]
    (down_halves,) = weight_grads_call(
        spot, [([(act_all, gffn_all, model)], bits, None)], after=[ga_own], name="grad_down"
    )
    down_sum = Halving(down_halves, bits)
    got_far2 = swap(ordered(up_far, came_far), "blk", 2)
    first_grads, first_boxes = scores_grad_call(
        0, spot, ga_all, qkv, probs, relkq, row, col, [down_halves[0]]
    )
    got_core2, got_both2 = swap(up_core, "blk", 1), swap(ordered(got_far2, first_grads), "blk", 1)
    got_far3 = swap(ordered(far3, got_far2), "blk", 2)
    hidden_all = [hidden, (got_far2, 0), (got_core2, 0), (got_both2, 0)]
    up_all = [up_own, (got_far2, 1), (got_core2, 1), (got_both2, 2)]
    (in_halves,) = weight_grads_call(
        spot, [([(hidden_all, up_all, model)], bits, None)], after=[first_grads], name="grad_in"
    )
    in_sum = Halving(in_halves, bits)
    lefts = list(xs) + [rel_table]

    def rows_by_piece(grads):
        return [(grads.reshape(blocks + 1, lanes, -1), t) for t in range(blocks + 1)]

    got_core3, got_both3 = swap(core3, "blk", 1), swap(ordered(got_far3, in_halves[0]), "blk", 1)
    att_all = [far3, got_far3, got_core3, got_both3]
    per = model // width
    gattn_all = [
        gattn_own, (got_far3, None, per), (got_core3, None, per), (got_both3, None, per + 1),
    ]
    done = down_sum.add(in_halves[0])
    early = [done]
    early = [done]
    first_groups = [(lefts, rows_by_piece(first_grads), 3 * width // 2), (att_all, gattn_all, width)]
    (first_halves,) = weight_grads_call(
        spot, [(first_groups, other, None)], after=[in_halves[0]] + early, name="grad_qkv_out"
    )
    first_sum = Halving(first_halves, other)
    second_grads, dq_own, dq_core, dq_far, small = scores_grad_call(
        1, spot, ga_all, qkv, probs, relkq, row, col, [first_halves[0]], docs,
        (w_query, w_key, sums, first_grads, first_boxes),
    )
    done = down_sum.add(second_grads)
    done = in_sum.add(done)
    second_groups = [(lefts, rows_by_piece(second_grads), 3 * width // 2)]
    (second_halves,) = weight_grads_call(
        spot, [(second_groups, bits, small)], after=[done], name="grad_qkv"
    )
    second_sum = Halving(second_halves, bits)
    done = first_sum.add(second_halves[0])
    dq_far_got = ordered(swap(dq_far, "blk", 2), second_halves[0])
    dq_core_got, dq_both_got = swap(dq_core, "blk", 1), swap(dq_far_got, "blk", 1)
    grad_tokens = tokens_grad_call(
        spot, (dq_own, (dq_far_got, 0), dq_core_got, (dq_both_got, 1)), grad_resid,
        w_query, w_key, w_value, [done],
    )

    def whole(part, *before):
        far = swap(part, "blk", 2)
        held = ordered(far, *before) if before else far
        return (part, swap(part, "blk", 1), far, swap(held, "blk", 1))

    done = in_sum.add(grad_tokens)
    done = second_sum.add(done)
    done = down_sum.add(done)
    down_part = done
    done = first_sum.add(done)
    done = in_sum.add(done)
    in_part = done
    done = second_sum.add(done)
    done = first_sum.add(done)
    first_part = done
    done = second_sum.add(done)
    second_part = done
    grad_w_down, grad_w_in = parts_call(
        spot, ((whole(down_part, done), 0), (whole(in_part, done), 1)), "gather_parts"
    )
    *grads, grad_w_out, rel_out, n0, n1, n2, n3, b_in_out, xb, yb = last_call(
        spot, whole(first_part, grad_w_down), whole(second_part, grad_w_down), rel_table.shape[0] // docs, model, heads
    )
    norms = (n0, n1, n2, n3)
    return (
        block_out[None], grad_tokens[None], norms[0], norms[1], grads[0], grads[1], grads[2], grad_w_out,
        rel_out, xb, yb, norms[2], norms[3], grad_w_in, b_in_out, grad_w_down,
    )


def choose(*args):
    docs, parts = lax.axis_size("docs"), lax.axis_size("blk")
    tokens, w_in = args[0], args[15]
    model, units = w_in.shape
    fits = (
        parts == blocks
        and tokens.shape[1] == lanes
        and model // docs == lanes
        and units // docs == parts * lanes
        and docs & (docs - 1) == 0
        and docs > 2
        and units == blocks * model
    )
    return (shards_tiles if fits else shards)(*args)


def solution(mesh):
    rows = P("docs", "blk", None)
    placed = (
        rows, P("docs"), P("docs", "blk"), P(None, "docs", "blk"),
        *([P()] * 14), rows,
    )
    over_docs, over_docs2 = P("docs"), P("docs", None)
    return jax.shard_map(
        choose,
        mesh=mesh,
        in_specs=placed,
        out_specs=(
            rows, rows, over_docs, over_docs, over_docs2, over_docs2, over_docs2, over_docs2,
            over_docs2, over_docs2, over_docs2, over_docs, over_docs, over_docs2, over_docs, over_docs2,
        ),
        check_vma=False,
    )
```

```python
import functools
import math

import jax
import jax.numpy as jnp
from jax import lax
from jax.experimental import pallas as pl
from jax.experimental.pallas import tpu as pltpu
from jax.sharding import PartitionSpec as P

norm_eps = 1e-05
mask_value = -1e30
f32 = jnp.float32
bf16 = jnp.bfloat16
lanes = 128


def dot(a, b, contract=((1,), (0,))):
    return lax.dot_general(a, b, (contract, ((), ())), preferred_element_type=f32)


def pick(table, index):
    return jnp.take_along_axis(table, index, axis=1, mode="promise_in_bounds")


def ahead_of(first, second):
    return jnp.clip(first - second, -64, 63) + 64


def attn_fwd_kernel(
    place, x_ref, wq_ref, wk_ref, wv_ref, rel_ref, tab_ref, row_ref, col_ref,
    att_ref, probs_ref, qkv_ref, relkq_ref, key_rel,
):
    scale = 1.0 / math.sqrt(192.0)
    step = pl.program_id(0)
    rows = x_ref.shape[0]
    width = wq_ref.shape[1]
    heads = tab_ref.shape[1]
    size = width // heads
    tiles = rows // lanes

    @pl.when(step == 0)
    def _():
        for at, w_ref in enumerate((wq_ref, wk_ref, wv_ref)):
            for t in range(tiles):
                qkv_ref[t * lanes : (t + 1) * lanes, at * width : (at + 1) * width] = dot(
                    x_ref[t * lanes : (t + 1) * lanes, :], w_ref[...]
                ).astype(bf16)
        relkq_ref[:, :width] = dot(rel_ref[...], wk_ref[...]).astype(bf16)
        relkq_ref[:, width:] = dot(rel_ref[...], wq_ref[...]).astype(bf16)
        for h in range(heads):
            key_rel[h] = (
                dot(
                    qkv_ref[:, width + h * size : width + (h + 1) * size],
                    relkq_ref[:, width + h * size : width + (h + 1) * size],
                    ((1,), (1,)),
                )
                .astype(bf16)
                .astype(f32)
            )

    here = pl.ds(pl.multiple_of(step * lanes, lanes), lanes)
    pos_i = col_ref[here, 0:1]
    cx_i = col_ref[here, 1:2]
    cy_i = col_ref[here, 2:3]
    own_row = row_ref[0:1, here]
    ahead, mirror, across, vertical = [], [], [], []
    for t in range(tiles):
        span = slice(t * lanes, (t + 1) * lanes)
        ahead.append(ahead_of(pos_i, row_ref[0:1, span]))
        mirror.append(ahead_of(col_ref[span, 0:1], own_row))
        across.append(jnp.clip(jnp.right_shift(cx_i - row_ref[1:2, span], 5), -32, 31) + 32)
        vertical.append(jnp.clip(jnp.right_shift(cy_i - row_ref[2:3, span], 5), -32, 31) + 96)
    valid = row_ref[3:4, :] > 0
    for h in range(heads):
        cols = slice(h * size, (h + 1) * size)
        query = qkv_ref[here, cols]
        rel_scores = (
            dot(query, relkq_ref[:, cols], ((1,), (1,))).astype(bf16).astype(f32)
        )
        table = jnp.broadcast_to(tab_ref[0, h : h + 1, :], (lanes, lanes))
        pieces = []
        for t in range(tiles):
            span = slice(t * lanes, (t + 1) * lanes)
            content = dot(
                query, qkv_ref[span, width + h * size : width + (h + 1) * size], ((1,), (1,))
            )
            mirrored = pick(key_rel[h, span, :], mirror[t]).T
            bias = pick(table, across[t]) + pick(table, vertical[t])
            pieces.append(
                scale * (content + pick(rel_scores, ahead[t]) + mirrored) + bias
            )
        scores = jnp.where(valid, jnp.concatenate(pieces, axis=1), mask_value)
        top = jnp.max(scores, axis=1, keepdims=True)
        raised = jnp.exp(scores - top)
        probs = (raised * (1.0 / jnp.sum(raised, axis=1, keepdims=True))).astype(bf16)
        probs_ref[h] = probs
        att_ref[:, cols] = dot(
            probs, qkv_ref[:, 2 * width + h * size : 2 * width + (h + 1) * size]
        ).astype(bf16)


def attn_fwd(place, x_all, w_query, w_key, w_value, rel_table, tables, ints_row, ints_col):
    rows, model = x_all.shape
    parts, heads, _ = tables.shape
    width = w_query.shape[1] // parts
    tiles = rows // lanes
    buckets = rel_table.shape[0]
    whole = lambda *shape: pl.BlockSpec(shape, lambda i, at: (0,) * len(shape))
    column = pl.BlockSpec((model, width), lambda i, at: (0, at[0]))
    return pl.pallas_call(
        attn_fwd_kernel,
        out_shape=(
            jax.ShapeDtypeStruct((rows, width), bf16),
            jax.ShapeDtypeStruct((heads, rows, rows), bf16),
            jax.ShapeDtypeStruct((rows, 3 * width), bf16),
            jax.ShapeDtypeStruct((buckets, 2 * width), bf16),
        ),
        grid_spec=pltpu.PrefetchScalarGridSpec(
            num_scalar_prefetch=1,
            grid=(tiles,),
            in_specs=[
                whole(rows, model),
                column,
                column,
                column,
                whole(buckets, model),
                pl.BlockSpec((1, heads, lanes), lambda i, at: (at[0], 0, 0)),
                whole(8, rows),
                whole(rows, 8),
            ],
            out_specs=[
                pl.BlockSpec((lanes, width), lambda i, at: (i, 0)),
                pl.BlockSpec((heads, lanes, rows), lambda i, at: (0, i, 0)),
                whole(rows, 3 * width),
                whole(buckets, 2 * width),
            ],
            scratch_shapes=[pltpu.VMEM((heads, rows, lanes), f32)],
        ),
        compiler_params=pltpu.CompilerParams(vmem_limit_bytes=40 << 20),
        cost_estimate=pl.CostEstimate(
            flops=6 * 10**9, transcendentals=10**6, bytes_accessed=8 << 20
        ),
        name="attn_fwd",
    )(place, x_all, w_query, w_key, w_value, rel_table, tables, ints_row, ints_col)


def attn_bwd_kernel(
    ga_ref, qkv_ref, probs_ref, relkq_ref, row_ref, col_ref,
    dqkv_ref, drel_ref, boxes_ref, ds_ref,
):
    scale = 1.0 / math.sqrt(192.0)
    rows = ga_ref.shape[0]
    heads = probs_ref.shape[0]
    width = ga_ref.shape[1]
    size = width // heads
    tiles = rows // lanes
    span_width = 3 * lanes
    drel_ref[...] = jnp.zeros_like(drel_ref)
    boxes_ref[...] = jnp.zeros_like(boxes_ref)
    window = lax.broadcasted_iota(jnp.int32, (rows, span_width), 1)
    bucket = lax.broadcasted_iota(jnp.int32, (lanes, lanes), 1)
    label = lax.broadcasted_iota(jnp.int32, (rows, lanes), 1)
    all_pos = col_ref[:, 0:1]
    all_x, all_y = col_ref[:, 1:2], col_ref[:, 2:3]
    sector_x, sector_y = jnp.right_shift(all_x, 5), jnp.right_shift(all_y, 5)
    hot_x = (label == sector_x).astype(bf16)
    hot_y = (label == sector_y + 64).astype(bf16)
    hot_both = ((label == sector_x) | (label == sector_y + 64)).astype(bf16)

    def histogram(sums, total, at, base_row):
        first = at - base_row + (2 * lanes // 2 - 1) - bucket
        low = jnp.bitwise_and(first, lanes - 1)
        group = jnp.right_shift(first, 7)
        found = jnp.where(
            group == 0,
            pick(sums[:, :lanes], low),
            jnp.where(
                group == 1,
                pick(sums[:, lanes : 2 * lanes], low),
                pick(sums[:, 2 * lanes :], low),
            ),
        )
        found = jnp.where(bucket == 0, total, found)
        later = jnp.where(bucket == lanes - 1, 0.0, pltpu.roll(found, lanes - 1, 1))
        return found - later

    def by_rows(ib, carry):
        here = pl.ds(pl.multiple_of(ib * lanes, lanes), lanes)
        pos_i = col_ref[here, 0:1]
        cx_i, cy_i = col_ref[here, 1:2], col_ref[here, 2:3]
        base = jnp.min(pos_i, axis=0, keepdims=True)
        below = (all_pos <= base - 63 + window).astype(bf16)
        short_x = jnp.bitwise_and(cx_i, 31) < jnp.bitwise_and(row_ref[1:2, :], 31)
        short_y = jnp.bitwise_and(cy_i, 31) < jnp.bitwise_and(row_ref[2:3, :], 31)
        step_x = jnp.right_shift(cx_i, 5) + 32 - bucket
        step_y = jnp.right_shift(cy_i, 5) + 32 - (bucket - 64)
        in_x = (bucket < 64) & (step_x >= 0) & (step_x < 32)
        in_y = (bucket >= 64) & (step_y >= 0) & (step_y < 32)
        seek = jnp.where(in_x, step_x, jnp.where(in_y, step_y + 64, 0))
        inside = in_x | in_y
        for h in range(heads):
            cols = slice(h * size, (h + 1) * size)
            kcols = slice(width + h * size, width + (h + 1) * size)
            vcols = slice(2 * width + h * size, 2 * width + (h + 1) * size)
            probs = probs_ref[h, here, :].astype(f32)
            gained = dot(ga_ref[here, cols], qkv_ref[:, vcols], ((1,), (1,)))
            row_dots = jnp.sum(probs * gained, axis=1, keepdims=True)
            grad32 = probs * (gained - row_dots)
            grad = grad32.astype(bf16)
            ds_ref[h, here, :] = grad
            exact = grad.astype(f32)
            total = jnp.sum(exact, axis=1, keepdims=True)
            rel = histogram(dot(grad, below), total, pos_i, base)
            rel = (scale * rel).astype(bf16)
            query = qkv_ref[here, cols]
            dqkv_ref[here, cols] = (
                scale * dot(grad, qkv_ref[:, kcols]) + dot(rel, relkq_ref[:, cols])
            ).astype(bf16)
            drel_ref[:, cols] += dot(rel, query, ((0,), (0,)))
            grad_x = jnp.where(short_x, exact, 0.0).astype(bf16)
            grad_y = jnp.where(short_y, exact, 0.0).astype(bf16)
            plain = dot(grad, hot_both)
            less = dot(grad_x, hot_x) + dot(grad_y, hot_y)
            plain = jnp.where(inside, pick(plain, seek), 0.0)
            less = jnp.where(inside, pick(less, seek), 0.0)
            boxes_ref[2 * h : 2 * h + 1, :] += jnp.sum(plain, axis=0, keepdims=True)
            boxes_ref[2 * h + 1 : 2 * h + 2, :] += jnp.sum(less, axis=0, keepdims=True)
        return carry

    lax.fori_loop(0, tiles, by_rows, 0)

    def by_columns(jb, carry):
        here = pl.ds(pl.multiple_of(jb * lanes, lanes), lanes)
        pos_j = col_ref[here, 0:1]
        base = jnp.min(pos_j, axis=0, keepdims=True)
        below = (all_pos <= base - 63 + window).astype(bf16)
        for h in range(heads):
            cols = slice(h * size, (h + 1) * size)
            kcols = slice(width + h * size, width + (h + 1) * size)
            vcols = slice(2 * width + h * size, 2 * width + (h + 1) * size)
            grad = ds_ref[h, :, here]
            total = dot(grad, jnp.ones((rows, lanes), bf16), ((0,), (0,)))
            sums = dot(grad, below, ((0,), (0,)))
            mirror = (scale * histogram(sums, total, pos_j, base)).astype(bf16)
            dqkv_ref[here, kcols] = (
                scale * dot(grad, qkv_ref[:, cols], ((0,), (0,)))
                + dot(mirror, relkq_ref[:, kcols])
            ).astype(bf16)
            drel_ref[:, kcols] += dot(mirror, qkv_ref[here, kcols], ((0,), (0,)))
            dqkv_ref[here, vcols] = dot(
                probs_ref[h, :, here], ga_ref[:, cols], ((0,), (0,))
            ).astype(bf16)
        return carry

    lax.fori_loop(0, tiles, by_columns, 0)


def attn_bwd(grad_att, qkv, probs, relkq, ints_row, ints_col):
    rows, width = grad_att.shape
    heads = probs.shape[0]
    buckets = relkq.shape[0]
    inside = pl.BlockSpec(memory_space=pltpu.VMEM)
    return pl.pallas_call(
        attn_bwd_kernel,
        out_shape=(
            jax.ShapeDtypeStruct((rows, 3 * width), bf16),
            jax.ShapeDtypeStruct((buckets, 2 * width), f32),
            jax.ShapeDtypeStruct((2 * heads, lanes), f32),
        ),
        in_specs=[inside] * 6,
        out_specs=[inside] * 3,
        scratch_shapes=[pltpu.VMEM((heads, rows, rows), bf16)],
        compiler_params=pltpu.CompilerParams(vmem_limit_bytes=40 << 20),
        cost_estimate=pl.CostEstimate(
            flops=12 * 10**9, transcendentals=0, bytes_accessed=6 << 20
        ),
        name="attn_bwd",
    )(grad_att, qkv, probs, relkq, ints_row, ints_col)


def layer_norm(inputs, gain_vec, bias_vec):
    row_mean = jnp.mean(inputs, axis=-1, keepdims=True)
    centered = inputs - row_mean
    inverse = lax.rsqrt(jnp.mean(centered * centered, axis=-1, keepdims=True) + norm_eps)
    normed = centered * inverse
    return (normed * gain_vec + bias_vec, normed, inverse)


def norm_backward(grad_in, normed, inverse, gain_vec):
    grad_gain = jnp.sum(grad_in * normed, axis=0)
    grad_shift = jnp.sum(grad_in, axis=0)
    scaled = grad_in * gain_vec
    grad_input = inverse * (
        scaled
        - jnp.mean(scaled, axis=-1, keepdims=True)
        - normed * jnp.mean(scaled * normed, axis=-1, keepdims=True)
    )
    return (grad_input, grad_gain, grad_shift)


def bits_of(count):
    assert count & (count - 1) == 0
    return [1 << at for at in range(count.bit_length() - 1)]


def swap(array, axis, by):
    count = lax.axis_size(axis)
    return lax.ppermute(array, axis, [(i, i ^ by) for i in range(count)])


def offsets(count):
    order = [0]
    for bit in reversed(bits_of(count)):
        order = order + [at ^ bit for at in order]
    return order


def spread(shared, pieces):
    count = lax.axis_size("blk")
    got = {0: shared} if shared is not None else {}
    held = {(0, at): piece for at, piece in pieces.items()} if pieces else {}
    for bit in reversed(bits_of(count)):
        out_keys = [key for key in sorted(held) if key[1] & bit]
        out_shared = sorted(got)
        parts = [got[at] for at in out_shared] + [held[key] for key in out_keys]
        if bit == 1:
            came = [swap(part, "blk", bit) for part in parts]
        else:
            came = swap(jnp.concatenate(parts, axis=1), "blk", bit)
            edges = [0]
            for part in parts:
                edges.append(edges[-1] + part.shape[1])
            came = [came[:, a:b] for a, b in zip(edges[:-1], edges[1:])]
        for at, part in zip(out_shared, came):
            got[at ^ bit] = part
        for key, part in zip(out_keys, came[len(out_shared) :]):
            del held[key]
            held[(key[0] ^ bit, key[1] ^ bit)] = part
    return got, {key[0]: part for key, part in held.items()}


def by_place(stacked, place):
    count = len(stacked)
    for bit in bits_of(count):
        turned = (place & bit) != 0
        stacked = [jnp.where(turned, stacked[at ^ bit], stacked[at]) for at in range(count)]
    return stacked


def chunk_order(count):
    order = [0]
    for bit in reversed(bits_of(count)):
        order = order + [at | bit for at in order]
    return order


def for_docs(chunks, doc_place):
    moved = by_place(chunks, doc_place)
    return [moved[at] for at in chunk_order(len(chunks))]


def halve(keep, send, bits):
    count = lax.axis_size("docs")
    first = True
    current = keep
    for bit in bits:
        if not first:
            half = current.shape[0] // 2
            current, send = current[:half], current[half:]
        first = False
        came = swap(send, "docs", bit)
        current = (current.astype(f32) + came.astype(f32)).astype(bf16)
    return current


def shards(
    tokens, lengths, positions, token_boxes, ln1_gain, ln1_bias, w_query, w_key, w_value, w_out,
    rel_table, xbias_table, ybias_table, ln2_gain, ln2_bias, w_in, b_in, w_down, cotangent,
):
    doc_count, row_count, model = tokens.shape
    assert doc_count == 1 and row_count == lanes
    parts = lax.axis_size("blk")
    docs = lax.axis_size("docs")
    place = lax.axis_index("blk")
    doc_place = lax.axis_index("docs")
    heads = xbias_table.shape[1]
    own_heads = heads // parts
    width = model // parts
    buckets = rel_table.shape[0]
    boxes = xbias_table.shape[0]
    hidden_units = w_in.shape[1]
    order = offsets(parts)
    x_own = tokens[0]

    centers_x = jnp.right_shift(token_boxes[0] + token_boxes[2], 1)
    centers_y = jnp.right_shift(token_boxes[1] + token_boxes[3], 1)
    own_ints = jnp.concatenate([positions, centers_x, centers_y], axis=0)
    coded = jnp.concatenate(
        [jnp.right_shift(own_ints, 5), jnp.bitwise_and(own_ints, 31)], axis=0
    ).astype(bf16)
    coded = jnp.pad(coded.reshape(1, -1), ((0, 7), (0, model - coded.size)))
    got, _ = spread(jnp.concatenate([x_own, coded], axis=0), None)
    x_all = jnp.concatenate([got[at][:row_count] for at in order], axis=0)
    decoded = jnp.concatenate(
        [got[at][row_count : row_count + 1, : 6 * row_count].reshape(6, row_count) for at in order], axis=1
    ).astype(jnp.int32)
    ints = decoded[:3] * 32 + decoded[3:]
    slot_ids = jnp.concatenate(
        [
            (place ^ at) * row_count + lax.broadcasted_iota(jnp.int32, (1, row_count), 1)
            for at in order
        ],
        axis=1,
    )
    ints = jnp.concatenate(
        [ints, (slot_ids < lengths[0]).astype(jnp.int32), jnp.zeros((4, ints.shape[1]), jnp.int32)],
        axis=0,
    )
    ints_col = ints.T
    tables = jnp.concatenate([xbias_table.T, ybias_table.T], axis=1).astype(f32)
    tables = tables.reshape(parts, own_heads, 2 * boxes)

    attended_own, probs, qkv, relkq = attn_fwd(
        place.reshape(1), x_all, w_query, w_key, w_value, rel_table, tables, ints, ints_col
    )

    def row_block(array, at):
        t = order.index(at)
        return array[t * row_count : (t + 1) * row_count]

    _, came = spread(None, {at: row_block(attended_own, at) for at in order})
    attended = jnp.concatenate(by_place([came[at] for at in range(parts)], place), axis=1)
    attn_out = jnp.dot(attended, w_out, preferred_element_type=f32)
    hidden, normed1, inverse1 = layer_norm(x_own.astype(f32) + attn_out, ln1_gain, ln1_bias)
    hidden_low = hidden.astype(bf16)
    up_proj = jnp.dot(hidden_low, w_in, preferred_element_type=f32) + b_in
    activated, gelu_back = jax.vjp(lambda inputs: jax.nn.gelu(inputs, approximate=True), up_proj)
    activated_low = activated.astype(bf16)
    ffn_out = jnp.dot(activated_low, w_down, preferred_element_type=f32)
    normed_out, normed2, inverse2 = layer_norm(hidden + ffn_out, ln2_gain, ln2_bias)
    block_out = normed_out.astype(bf16)[None]
    grad_output = cotangent[0].astype(f32)
    grad_mix, grad_ln2_gain, grad_ln2_bias = norm_backward(grad_output, normed2, inverse2, ln2_gain)
    grad_ffn = grad_mix.astype(bf16)
    grad_act = jnp.dot(grad_ffn, w_down.T, preferred_element_type=f32)
    grad_up = gelu_back(grad_act)[0].astype(bf16)
    grad_b_in = jnp.sum(grad_up, axis=0, dtype=f32)
    grad_hidden = grad_mix + jnp.dot(grad_up, w_in.T, preferred_element_type=f32)
    grad_resid, grad_ln1_gain, grad_ln1_bias = norm_backward(
        grad_hidden, normed1, inverse1, ln1_gain
    )
    grad_attn = grad_resid.astype(bf16)
    grad_att = jnp.dot(grad_attn, w_out.T, preferred_element_type=f32).astype(bf16)

    def column_block(array, at, count):
        size = array.shape[1] // count
        return lax.dynamic_slice_in_dim(array, at * size, size, axis=1)

    _, came = spread(None, {at: column_block(grad_att, place ^ at, parts) for at in order})
    grad_att_own = jnp.concatenate([came[at] for at in order], axis=0)
    dqkv, drel, box_sums = attn_bwd(grad_att_own, qkv, probs, relkq, ints, ints_col)

    def docs_columns(array):
        size = array.shape[1] // docs
        chunks = [array[:, at * size : (at + 1) * size] for at in range(docs)]
        return jnp.concatenate(for_docs(chunks, doc_place), axis=1)

    strips = activated_low.reshape(row_count, docs, parts, -1)
    strips = [
        docs_columns(
            lax.dynamic_index_in_dim(strips, place ^ at, axis=2, keepdims=False).reshape(row_count, -1)
        )
        for at in range(parts)
    ]
    got, came = spread(docs_columns(hidden_low), dict(enumerate(strips)))
    hidden_all = jnp.concatenate([got[at] for at in order], axis=0)
    activated_all = jnp.concatenate([came[at] for at in order], axis=0)
    got, came = spread(grad_ffn, {at: column_block(grad_up, place ^ at, parts) for at in order})
    grad_ffn_all = jnp.concatenate([got[at] for at in order], axis=0)
    grad_up_all = jnp.concatenate([came[at] for at in order], axis=0)
    got, came = spread(
        docs_columns(attended), {at: column_block(grad_attn, place ^ at, parts) for at in order}
    )
    attended_all = jnp.concatenate([got[at] for at in order], axis=0)
    grad_attn_all = jnp.concatenate([came[at] for at in order], axis=0)

    def halves(left, right):
        middle = left.shape[1] // 2
        send = dot(left[:, middle:], right, ((0,), (0,))).astype(bf16)
        keep = dot(left[:, :middle], right, ((0,), (0,))).astype(bf16)
        return keep, send

    bits = bits_of(docs)
    down_part = halve(*halves(activated_all, grad_ffn_all), bits)
    in_part = halve(*halves(hidden_all, grad_up_all), bits)
    out_part = halve(*halves(attended_all, grad_attn_all), bits)

    drel_low = drel.astype(bf16)
    left = docs_columns(jnp.concatenate([x_all, rel_table], axis=0))
    right = jnp.concatenate(
        [
            dqkv,
            jnp.concatenate(
                [drel_low[:, width:], drel_low[:, :width], jnp.zeros((buckets, width), bf16)], axis=1
            ),
        ],
        axis=0,
    )
    grad_rel_table = dot(
        drel_low[:, :width], column_block(w_key, place, parts), ((1,), (1,))
    ) + dot(drel_low[:, width:], column_block(w_query, place, parts), ((1,), (1,)))
    plain, less = box_sums[0::2], box_sums[1::2]

    def box_grad(at):
        plain_here, less_here = plain[:, at : at + boxes], less[:, at : at + boxes]
        later = jnp.pad(less_here[:, 1:], ((0, 0), (0, 1)))
        grad = (plain_here - less_here + later).T
        return lax.dynamic_update_slice(jnp.zeros((boxes, heads), f32), grad, (0, place * own_heads))

    small = jnp.concatenate(
        [
            grad_rel_table.reshape(docs, -1),
            grad_ln1_gain.reshape(docs, -1),
            grad_ln1_bias.reshape(docs, -1),
            grad_ln2_gain.reshape(docs, -1),
            grad_ln2_bias.reshape(docs, -1),
            grad_b_in.reshape(docs, -1),
            box_grad(0).reshape(docs, -1),
            box_grad(boxes).reshape(docs, -1),
        ],
        axis=1,
    ).astype(bf16)
    small_width = small.shape[1]
    across = 3 * width
    small = jnp.pad(small, ((0, 0), (0, -small_width % (8 * across))))
    small = for_docs([small[at] for at in range(docs)], doc_place)
    small = jnp.stack(small).reshape(docs, -1, across)
    keep, send = halves(left, right)
    middle = docs // 2
    chunk_rows = model // docs

    def with_small(main, extra):
        main = main.reshape(middle, chunk_rows, across)
        return jnp.concatenate([main, extra], axis=1).reshape(-1, across)

    qkv_part = halve(with_small(keep, small[:middle]), with_small(send, small[middle:]), bits)

    _, came = spread(None, {at: row_block(dqkv, at) for at in order})
    came = by_place([came[at] for at in range(parts)], place)
    grad_tokens = grad_resid
    for at, weight in enumerate((w_query, w_key, w_value)):
        grad = jnp.concatenate([rows[:, at * width : (at + 1) * width] for rows in came], axis=1)
        grad_tokens = grad_tokens + dot(grad, weight, ((1,), (1,)))

    def whole(part):
        got, _ = spread(part, None)
        return by_place([got[at] for at in range(parts)], place)

    grad_w_down = jnp.concatenate(whole(down_part), axis=0).astype(f32)
    grad_w_in = jnp.concatenate(whole(in_part), axis=1).astype(f32)
    grad_w_out = jnp.concatenate(whole(out_part), axis=1).astype(f32)
    pieces = whole(qkv_part)
    grads = [
        jnp.concatenate(
            [piece[:chunk_rows, at * width : (at + 1) * width] for piece in pieces], axis=1
        ).astype(f32)
        for at in range(3)
    ]
    total = sum(piece[chunk_rows:].astype(f32) for piece in pieces).reshape(-1)
    sizes = [
        (buckets // docs, model),
        (model // docs,),
        (model // docs,),
        (model // docs,),
        (model // docs,),
        (hidden_units // docs,),
        (boxes // docs, heads),
        (boxes // docs, heads),
    ]
    small_out = []
    start = 0
    for size in sizes:
        small_out.append(total[start : start + math.prod(size)].reshape(size))
        start += math.prod(size)
    rel_out, ln1g, ln1b, ln2g, ln2b, b_in_out, xb, yb = small_out
    return (
        block_out, grad_tokens[None], ln1g, ln1b, grads[0], grads[1], grads[2], grad_w_out,
        rel_out, xb, yb, ln2g, ln2b, grad_w_in, b_in_out, grad_w_down,
    )


blocks = 4
slots = (0, 2, 1, 3)


def rows_of(handle, tile=None, column=None):
    array, lead = handle if isinstance(handle, tuple) else (handle, None)
    shape = array.shape[-2:] if tile is None else tile
    column = column or (lambda *grid: 0)
    if lead is None:
        return pl.BlockSpec(shape, lambda *grid: (0, column(*grid)))
    return pl.BlockSpec((None,) + shape, lambda *grid: (lead, 0, column(*grid)))


def array_of(handle):
    return handle[0] if isinstance(handle, tuple) else handle


def full(shape):
    return pl.BlockSpec(shape, lambda *grid: (0,) * len(shape))


def cost(us):
    return pl.CostEstimate(flops=int(us * 3 * 10**8), transcendentals=0, bytes_accessed=0)


def ordered(array, *before):
    return lax.optimization_barrier((array,) + before)[0]


def in_hbm(array):
    return pltpu.with_memory_space_constraint(array, pltpu.HBM)


def params(limit):
    return pltpu.CompilerParams(vmem_limit_bytes=limit << 20)


def gelu_parts(u):
    root = math.sqrt(2.0 / math.pi)
    inner = jnp.tanh(root * (u + 0.044715 * u * u * u))
    value = 0.5 * u * (1.0 + inner)
    slope = 0.5 * (1.0 + inner) + 0.5 * u * (1.0 - inner * inner) * root * (
        1.0 + 3.0 * 0.044715 * u * u
    )
    return value, slope


def scores_kernel(
    at_ref, x0, x1, x2, x3, i0, i1, i2, i3, wq_ref, wk_ref, wv_ref, rel_ref, tab_ref,
    own_ref, core_ref, far_ref, probs_ref, qkv_ref, relkq_ref, row_ref, col_ref,
    key_rel, queries, keys_t, values, rel_keys_t, sector_hot,
):
    scale = 1.0 / math.sqrt(192.0)
    step = pl.program_id(0)
    rows = blocks * lanes
    width = wq_ref.shape[1]
    heads = tab_ref.shape[1]
    size = width // heads

    @pl.when(step == 0)
    def _():
        for t, (x_ref, i_ref) in enumerate(zip((x0, x1, x2, x3), (i0, i1, i2, i3))):
            span = slice(t * lanes, (t + 1) * lanes)
            for at, w_ref in enumerate((wq_ref, wk_ref, wv_ref)):
                part = dot(x_ref[...], w_ref[...]).astype(bf16)
                qkv_ref[span, at * width : (at + 1) * width] = part
                if at == 1:
                    keys_t[:, span] = part.astype(f32).T.astype(bf16)
                else:
                    for h in range(heads):
                        (queries, None, values)[at][h, span, :] = part[:, h * size : (h + 1) * size]
            first = jnp.bitwise_xor(at_ref[0], slots[t]) * lanes
            slot = first + lax.broadcasted_iota(jnp.int32, (8, lanes), 1)
            kind = lax.broadcasted_iota(jnp.int32, (8, lanes), 0)
            ints = jnp.where(kind == 3, (slot < at_ref[1]).astype(jnp.int32), i_ref[...])
            row_ref[:, span] = ints
            col_ref[span, :] = ints.astype(f32).T.astype(jnp.int32)
        sector = lax.broadcasted_iota(jnp.int32, (32, rows), 0)
        for k in range(2):
            hot = (jnp.right_shift(row_ref[1 + k : 2 + k, :], 5) == sector).astype(f32).astype(bf16)
            sector_hot[k * 32 : (k + 1) * 32, :] = hot
        rel_keys = dot(rel_ref[...], wk_ref[...])
        relkq_ref[:, :width] = rel_keys.astype(bf16)
        rel_keys_t[...] = rel_keys.T.astype(bf16)
        relkq_ref[:, width:] = dot(rel_ref[...], wq_ref[...]).astype(bf16)
        for h in range(heads):
            cols = slice(width + h * size, width + (h + 1) * size)
            key_rel[h] = (
                dot(qkv_ref[:, cols], relkq_ref[:, cols], ((1,), (1,))).astype(bf16).astype(f32)
            )

    here = pl.ds(pl.multiple_of(step * lanes, lanes), lanes)
    pos_i = col_ref[here, 0:1]
    cx_i = col_ref[here, 1:2]
    cy_i = col_ref[here, 2:3]
    own_row = row_ref[0:1, here]
    lane = lax.broadcasted_iota(jnp.int32, (lanes, lanes), 1)
    on_x = jnp.bitwise_and(jnp.right_shift(lane, 5), 1) == 0
    seek = (
        jnp.where(on_x, jnp.right_shift(cx_i, 5), jnp.right_shift(cy_i, 5) + 64)
        + 32
        - jnp.bitwise_and(lane, 31)
        - (lane >= 64).astype(jnp.int32)
    )
    short_x = jnp.bitwise_and(cx_i, 31) < jnp.bitwise_and(row_ref[1:2, :], 31)
    short_y = jnp.bitwise_and(cy_i, 31) < jnp.bitwise_and(row_ref[2:3, :], 31)
    ahead, mirror = [], []
    for t in range(blocks):
        span = slice(t * lanes, (t + 1) * lanes)
        ahead.append(ahead_of(pos_i, row_ref[0:1, span]))
        mirror.append(ahead_of(col_ref[span, 0:1], own_row))
    valid = row_ref[3:4, :] > 0
    attended = []
    for h in range(heads):
        cols = slice(h * size, (h + 1) * size)
        query = queries[h, here, :]
        rel_scores = dot(query, rel_keys_t[cols, :]).astype(bf16).astype(f32)
        table = jnp.broadcast_to(tab_ref[0, h : h + 1, :], (lanes, lanes))
        by_sector = pick(table, seek).astype(bf16)
        content = dot(query, keys_t[cols, :])
        plain_x = dot(by_sector[:, 0:32], sector_hot[0:32, :])
        plain_y = dot(by_sector[:, 32:64], sector_hot[32:64, :])
        less_x = dot(by_sector[:, 64:96], sector_hot[0:32, :])
        less_y = dot(by_sector[:, 96:128], sector_hot[32:64, :])
        bias = jnp.where(short_x, less_x, plain_x) + jnp.where(short_y, less_y, plain_y)
        moved = []
        for t in range(blocks):
            span = slice(t * lanes, (t + 1) * lanes)
            moved.append(pick(rel_scores, ahead[t]) + pick(key_rel[h, span, :], mirror[t]).T)
        scores = scale * (content + jnp.concatenate(moved, axis=1)) + bias
        scores = jnp.where(valid, scores, mask_value)
        top = jnp.max(scores, axis=1, keepdims=True)
        raised = jnp.exp(scores - top)
        probs = (raised * (1.0 / jnp.sum(raised, axis=1, keepdims=True))).astype(bf16)
        probs_ref[h] = probs
        attended.append(dot(probs, values[h]).astype(bf16))
    attended = jnp.concatenate(attended, axis=1)
    for t, target in enumerate((own_ref, far_ref.at[0], core_ref, far_ref.at[1])):

        @pl.when(step == t)
        def _(target=target):
            target[...] = attended


def scores_call(at, xs, ints, w_query, w_key, w_value, rel_table, tables):
    rows, model = blocks * lanes, w_query.shape[0]
    parts, heads, _ = tables.shape
    width = w_query.shape[1] // parts
    buckets = rel_table.shape[0]
    column = pl.BlockSpec((model, width), lambda i, at: (0, at[0]))
    return pl.pallas_call(
        scores_kernel,
        out_shape=(
            jax.ShapeDtypeStruct((lanes, width), bf16),
            jax.ShapeDtypeStruct((lanes, width), bf16),
            jax.ShapeDtypeStruct((2, lanes, width), bf16),
            pltpu.HBM((heads, rows, rows), bf16),
            pltpu.HBM((rows, 3 * width), bf16),
            pltpu.HBM((buckets, 2 * width), bf16),
            pltpu.HBM((8, rows), jnp.int32),
            pltpu.HBM((rows, 8), jnp.int32),
        ),
        grid_spec=pltpu.PrefetchScalarGridSpec(
            num_scalar_prefetch=1,
            grid=(blocks,),
            in_specs=[rows_of(x) for x in xs]
            + [rows_of(i) for i in ints]
            + [
                column,
                column,
                column,
                full((buckets, model)),
                pl.BlockSpec((1, heads, lanes), lambda i, at: (at[0], 0, 0)),
            ],
            out_specs=[
                full((lanes, width)),
                full((lanes, width)),
                full((2, lanes, width)),
                pl.BlockSpec((heads, lanes, rows), lambda i, at: (0, i, 0)),
                full((rows, 3 * width)),
                full((buckets, 2 * width)),
                full((8, rows)),
                full((rows, 8)),
            ],
            scratch_shapes=[
                pltpu.VMEM((heads, rows, lanes), f32),
                pltpu.VMEM((heads, rows, width // heads), bf16),
                pltpu.VMEM((width, rows), bf16),
                pltpu.VMEM((heads, rows, width // heads), bf16),
                pltpu.VMEM((width, buckets), bf16),
                pltpu.VMEM((64, rows), bf16),
            ],
        ),
        compiler_params=params(18),
        cost_estimate=cost(25),
        name="scores",
    )(
        at, *map(array_of, xs), *map(array_of, ints), w_query, w_key, w_value, rel_table, tables
    )


def up_kernel(
    at_ref, a0, a1, a2, a3, x_ref, wout_ref, gain_ref, bias_ref, win_ref, bin_ref,
    far_ref, core_ref, own_ref, act_ref, slope_ref, normed_ref, inverse_ref, attended_ref,
    hidden_low,
):
    step = pl.program_id(0)
    width = a0.shape[1]
    tile = win_ref.shape[1]

    @pl.when(step == 0)
    def _():
        total = x_ref[...].astype(f32)
        for t, piece in enumerate((a0, a1, a2, a3)):
            first = pl.multiple_of(jnp.bitwise_xor(at_ref[0], slots[t]) * width, width)
            total = total + dot(piece[...], wout_ref[pl.ds(first, width), :])
            attended_ref[:, pl.ds(first, width)] = piece[...]
        centered = total - jnp.mean(total, axis=1, keepdims=True)
        inverse = lax.rsqrt(jnp.mean(centered * centered, axis=1, keepdims=True) + norm_eps)
        normed = centered * inverse
        normed_ref[...] = normed
        inverse_ref[...] = jnp.broadcast_to(inverse, inverse_ref.shape)
        hidden = (normed * gain_ref[...] + bias_ref[...]).astype(bf16)
        hidden_low[...] = hidden

    value, slope = gelu_parts(dot(hidden_low[...], win_ref[...]) + bin_ref[...])
    value = value.astype(bf16)
    act_ref[...] = value
    slope_ref[...] = slope.astype(bf16)
    strip = tile // blocks
    here = pl.ds(pl.multiple_of(step * strip, strip), strip)
    for t, target in enumerate((own_ref, far_ref.at[0], core_ref, far_ref.at[1])):
        first = pl.multiple_of(jnp.bitwise_xor(at_ref[0], slots[t]) * strip, strip)
        target[:, here] = act_ref[:, pl.ds(first, strip)]


def up_call(at, pieces, x_own, w_out, gain, bias, w_in, b_in, docs):
    rows, model = x_own.shape
    units = w_in.shape[1]
    tile = units // docs
    quarter = units // blocks
    column = lambda i, at: (0, i)
    return pl.pallas_call(
        up_kernel,
        out_shape=(
            jax.ShapeDtypeStruct((2, rows, quarter), bf16),
            jax.ShapeDtypeStruct((rows, quarter), bf16),
            jax.ShapeDtypeStruct((rows, quarter), bf16),
            jax.ShapeDtypeStruct((rows, units), bf16),
            jax.ShapeDtypeStruct((rows, units), bf16),
            jax.ShapeDtypeStruct((rows, model), f32),
            jax.ShapeDtypeStruct((rows, lanes), f32),
            jax.ShapeDtypeStruct((rows, model), bf16),
            jax.ShapeDtypeStruct((rows, model), bf16),
        ),
        grid_spec=pltpu.PrefetchScalarGridSpec(
            num_scalar_prefetch=1,
            grid=(docs,),
            in_specs=[rows_of(piece) for piece in pieces]
            + [
                full((rows, model)),
                full((model, model)),
                full((1, model)),
                full((1, model)),
                pl.BlockSpec((model, tile), column),
                pl.BlockSpec((1, tile), column),
            ],
            out_specs=[
                full((2, rows, quarter)),
                full((rows, quarter)),
                full((rows, quarter)),
                pl.BlockSpec((rows, tile), column),
                pl.BlockSpec((rows, tile), column),
                full((rows, model)),
                full((rows, lanes)),
                full((rows, model)),
                full((rows, model)),
            ],
        ),
        compiler_params=params(18),
        cost_estimate=cost(9),
        name="up",
    )(at, *map(array_of, pieces), x_own, w_out, gain, bias, w_in, b_in)


def norm_back(grad, normed, inverse, gain):
    scaled = grad * gain
    return inverse * (
        scaled
        - jnp.mean(scaled, axis=1, keepdims=True)
        - normed * jnp.mean(scaled * normed, axis=1, keepdims=True)
    )


def down_kernel(
    act_ref, wdown_ref, normed_ref, cot_ref, gain1_ref, bias1_ref, gain2_ref, bias2_ref,
    block_ref, mix_ref, low_ref, sums_ref,
):
    step = pl.program_id(0)

    @pl.when(step == 0)
    def _():
        mix_ref[...] = normed_ref[...] * gain1_ref[...] + bias1_ref[...]

    mix_ref[...] += dot(act_ref[...], wdown_ref[...])

    @pl.when(step == pl.num_programs(0) - 1)
    def _():
        mixed = mix_ref[...]
        centered = mixed - jnp.mean(mixed, axis=1, keepdims=True)
        inverse = lax.rsqrt(jnp.mean(centered * centered, axis=1, keepdims=True) + norm_eps)
        normed = centered * inverse
        block_ref[...] = (normed * gain2_ref[...] + bias2_ref[...]).astype(bf16)
        grad = cot_ref[...].astype(f32)
        sums_ref[0:1, :] = jnp.sum(grad * normed, axis=0, keepdims=True)
        sums_ref[1:2, :] = jnp.sum(grad, axis=0, keepdims=True)
        mix = norm_back(grad, normed, inverse, gain2_ref[...])
        mix_ref[...] = mix
        low_ref[...] = mix.astype(bf16)


def down_call(act, w_down, normed, cotangent, gain1, bias1, gain2, bias2, tile):
    rows, units = act.shape
    model = w_down.shape[1]
    return pl.pallas_call(
        down_kernel,
        out_shape=(
            jax.ShapeDtypeStruct((rows, model), bf16),
            jax.ShapeDtypeStruct((rows, model), f32),
            jax.ShapeDtypeStruct((rows, model), bf16),
            jax.ShapeDtypeStruct((8, model), f32),
        ),
        grid=(units // tile,),
        in_specs=[
            pl.BlockSpec((rows, tile), lambda i: (0, i)),
            pl.BlockSpec((tile, model), lambda i: (i, 0)),
            full((rows, model)),
            full((rows, model)),
        ]
        + [full((1, model))] * 4,
        out_specs=[full((rows, model))] * 3 + [full((8, model))],
        compiler_params=params(18),
        cost_estimate=cost(8),
        name="down",
    )(act, w_down, normed, cotangent, gain1, bias1, gain2, bias2)


def back_kernel(
    at_ref, wdown_ref, slope_ref, win_ref, wout_ref, normed_ref, inverse_ref, mix_ref, ffn_ref,
    attended_ref, gain1_ref, above_ref, hidden_ref,
    own_ref, core_ref, far_ref, resid_ref, upfar_ref, upcore_ref, upown_ref,
    outfar_ref, outcore_ref, outown_ref, sums_ref,
    total, grad_up,
):
    step = pl.program_id(0)
    steps = pl.num_programs(0)
    rows, tile = slope_ref.shape
    model = mix_ref.shape[1]
    width = model // blocks

    @pl.when(step == 0)
    def _():
        total[...] = mix_ref[...]

    grad = dot(ffn_ref[...], wdown_ref[...], ((1,), (1,))) * slope_ref[...].astype(f32)
    low = grad.astype(bf16)
    total[...] += dot(low, win_ref[...], ((1,), (1,)))
    per = model // tile
    part = step // per
    here = pl.ds(pl.multiple_of((step - part * per) * tile, tile), tile)
    grad_up[jnp.bitwise_xor(part, at_ref[0]), :, here] = low
    sums_ref[pl.ds(4 + part, 1), here] = jnp.sum(low.astype(f32), axis=0, keepdims=True)

    @pl.when(step == steps - 1)
    def _():
        upown_ref[...] = grad_up[0]
        upcore_ref[0] = hidden_ref[...]
        upcore_ref[1] = grad_up[1]
        upfar_ref[0] = hidden_ref[...]
        upfar_ref[1] = grad_up[2]
        upfar_ref[2] = grad_up[3]
        grad = total[...]
        normed = normed_ref[...]
        sums_ref[0:1, :] = jnp.sum(grad * normed, axis=0, keepdims=True)
        sums_ref[1:2, :] = jnp.sum(grad, axis=0, keepdims=True)
        sums_ref[2:4, :] = above_ref[0:2, :]
        resid = norm_back(grad, normed, inverse_ref[:, 0:1], gain1_ref[...])
        resid_ref[...] = resid
        low = resid.astype(bf16)
        total[...] = low.astype(f32)
        outfar_ref[:, :model] = attended_ref[...]
        outcore_ref[:, :model] = attended_ref[...]
        targets = (own_ref, core_ref, far_ref.at[0], far_ref.at[1])
        wides = (
            outown_ref, outcore_ref.at[:, pl.ds(model, width)],
            outfar_ref.at[:, pl.ds(model, width)], outfar_ref.at[:, pl.ds(model + width, width)],
        )
        for at, (target, wide) in enumerate(zip(targets, wides)):
            first = pl.multiple_of(jnp.bitwise_xor(at_ref[0], at) * width, width)
            target[...] = dot(low, wout_ref[pl.ds(first, width), :], ((1,), (1,))).astype(bf16)
            wide[...] = total[:, pl.ds(first, width)].astype(bf16)


def back_call(
    at, w_down, slope, w_in, w_out, normed, inverse, mix, grad_ffn, attended, gain1, above, hidden, tile,
):
    rows, units = slope.shape
    model = w_out.shape[0]
    width = model // blocks
    return pl.pallas_call(
        back_kernel,
        out_shape=(
            jax.ShapeDtypeStruct((rows, width), bf16),
            jax.ShapeDtypeStruct((rows, width), bf16),
            jax.ShapeDtypeStruct((2, rows, width), bf16),
            jax.ShapeDtypeStruct((rows, model), f32),
            jax.ShapeDtypeStruct((3, rows, model), bf16),
            jax.ShapeDtypeStruct((2, rows, model), bf16),
            jax.ShapeDtypeStruct((rows, model), bf16),
            jax.ShapeDtypeStruct((rows, model + 2 * width), bf16),
            jax.ShapeDtypeStruct((rows, model + width), bf16),
            jax.ShapeDtypeStruct((rows, width), bf16),
            jax.ShapeDtypeStruct((8, model), f32),
        ),
        grid_spec=pltpu.PrefetchScalarGridSpec(
            num_scalar_prefetch=1,
            grid=(units // tile,),
            in_specs=[
                pl.BlockSpec((tile, model), lambda i, at: (i, 0)),
                pl.BlockSpec((rows, tile), lambda i, at: (0, i)),
                pl.BlockSpec((model, tile), lambda i, at: (0, i)),
                full((model, model)),
                full((rows, model)),
                full((rows, lanes)),
                full((rows, model)),
                full((rows, model)),
                full((rows, model)),
                full((1, model)),
                full((8, model)),
                full((rows, model)),
            ],
            out_specs=[
                full((rows, width)),
                full((rows, width)),
                full((2, rows, width)),
                full((rows, model)),
                full((3, rows, model)),
                full((2, rows, model)),
                full((rows, model)),
                full((rows, model + 2 * width)),
                full((rows, model + width)),
                full((rows, width)),
                full((8, model)),
            ],
            scratch_shapes=[
                pltpu.VMEM((rows, model), f32),
                pltpu.VMEM((blocks, rows, model), bf16),
            ],
        ),
        compiler_params=params(18),
        cost_estimate=cost(12),
        name="back",
    )(at, w_down, slope, w_in, w_out, normed, inverse, mix, grad_ffn, attended, gain1, above, hidden)


def scores_grad_kernel(half, held, *refs):
    at_ref, g0, g1, g2, g3, qkv_ref, probs_ref, relkq_ref, row_ref, col_ref = refs[:10]
    refs = refs[10:]
    last = half == 1
    if last:
        wq_ref, wk_ref, sums_ref, before_ref, boxes_before = refs[:5]
        refs = refs[5:]
    refs = refs[held:]
    if last:
        dqkv_ref, own_ref, core_ref, far_ref, small_ref, ga_ref, ds_ref, drel, own_qkv, box_sums = refs
    else:
        dqkv_ref, box_sums, ga_ref, ds_ref, drel, own_qkv = refs
    scale = 1.0 / math.sqrt(192.0)
    rows = blocks * lanes
    width = qkv_ref.shape[1] // 3
    part = width // 2
    heads = probs_ref.shape[0]
    size = part // heads
    short = lanes // 2
    for t, piece in enumerate((g0, g1, g2, g3)):
        ga_ref[t * lanes : (t + 1) * lanes, :] = piece[...]
    for k in range(3):
        for h in range(heads):
            first = k * width + half * part + h * size
            own_qkv[k * heads + h] = qkv_ref[:, first : first + size]
    drel[...] = jnp.zeros_like(drel)
    box_sums[...] = jnp.zeros_like(box_sums)
    window = lax.broadcasted_iota(jnp.int32, (rows, 2 * lanes), 1)
    bucket = lax.broadcasted_iota(jnp.int32, (lanes, lanes), 1)
    label = lax.broadcasted_iota(jnp.int32, (rows, lanes), 1)
    all_pos = col_ref[:, 0:1]
    all_x, all_y = col_ref[:, 1:2], col_ref[:, 2:3]
    sector_x, sector_y = jnp.right_shift(all_x, 5), jnp.right_shift(all_y, 5)
    hot_x = (label == sector_x).astype(f32).astype(bf16)
    hot_y = (label == sector_y + 64).astype(f32).astype(bf16)
    hot_both = hot_x + hot_y

    def shares(grads, start):
        found = []
        for u in range(2):
            at = col_ref[pl.ds(pl.multiple_of(start + u * short, short), short), 0:1]
            base = jnp.min(at, axis=0, keepdims=True)
            below = (all_pos <= base - 63 + window) | (window == 2 * lanes - 1)
            stacked = jnp.concatenate([g[u * short : (u + 1) * short, :] for g in grads], axis=0)
            sums = dot(stacked, below.astype(f32).astype(bf16))
            first = at - base + (lanes - 1) - bucket[:short]
            first = jnp.concatenate([first] * heads, axis=0)
            low = jnp.bitwise_and(first, lanes - 1)
            value = jnp.where(
                first < lanes, pick(sums[:, :lanes], low), pick(sums[:, lanes:], low)
            )
            value = jnp.where(bucket == 0, sums[:, 2 * lanes - 1 :], value)
            later = jnp.where(bucket == lanes - 1, 0.0, pltpu.roll(value, lanes - 1, 1))
            found.append(scale * (value - later))
        return [
            jnp.concatenate([f[h * short : (h + 1) * short, :] for f in found], axis=0).astype(bf16)
            for h in range(heads)
        ]

    def by_rows(ib, carry):
        start = ib * lanes
        here = pl.ds(pl.multiple_of(start, lanes), lanes)
        cx_i, cy_i = col_ref[here, 1:2], col_ref[here, 2:3]
        short_x = jnp.bitwise_and(cx_i, 31) < jnp.bitwise_and(row_ref[1:2, :], 31)
        short_y = jnp.bitwise_and(cy_i, 31) < jnp.bitwise_and(row_ref[2:3, :], 31)
        short_x = short_x.astype(f32).astype(bf16)
        short_y = short_y.astype(f32).astype(bf16)
        step_x = jnp.right_shift(cx_i, 5) + 32 - bucket
        step_y = jnp.right_shift(cy_i, 5) + 32 - (bucket - 64)
        in_x = (bucket < 64) & (step_x >= 0) & (step_x < 32)
        in_y = (bucket >= 64) & (step_y >= 0) & (step_y < 32)
        seek = jnp.where(in_x, step_x, jnp.where(in_y, step_y + 64, 0))
        inside = in_x | in_y
        grads = []
        for h in range(heads):
            probs = probs_ref[h, here, :].astype(f32)
            gained = dot(ga_ref[here, h * size : (h + 1) * size], own_qkv[2 * heads + h], ((1,), (1,)))
            row_dots = jnp.sum(probs * gained, axis=1, keepdims=True)
            grad = (probs * (gained - row_dots)).astype(bf16)
            ds_ref[h, here, :] = grad
            grads.append(grad)
        rels = shares(grads, start)
        for h, (grad, rel) in enumerate(zip(grads, rels)):
            gcols = slice(h * size, (h + 1) * size)
            kgcols = slice(half * part + h * size, half * part + (h + 1) * size)
            dqkv_ref[here, gcols] = (
                scale * dot(grad, own_qkv[heads + h]) + dot(rel, relkq_ref[:, kgcols])
            ).astype(bf16)
            drel[:, gcols] += dot(rel, own_qkv[h, here, :], ((0,), (0,)))
        stacked = jnp.concatenate(grads, axis=0)
        plain = dot(stacked, hot_both)
        less = dot(jnp.concatenate([g * short_x for g in grads], axis=0), hot_x) + dot(
            jnp.concatenate([g * short_y for g in grads], axis=0), hot_y
        )
        for h in range(heads):
            span = slice(h * lanes, (h + 1) * lanes)
            own_plain = jnp.where(inside, pick(plain[span, :], seek), 0.0)
            own_less = jnp.where(inside, pick(less[span, :], seek), 0.0)
            box_sums[h : h + 1, :] += jnp.sum(own_plain, axis=0, keepdims=True)
            box_sums[8 + h : 9 + h, :] += jnp.sum(own_less, axis=0, keepdims=True)
        return carry

    lax.fori_loop(0, blocks, by_rows, 0)

    def by_columns(jb, carry):
        start = jb * lanes
        here = pl.ds(pl.multiple_of(start, lanes), lanes)
        grads = [ds_ref[h, :, here].T for h in range(heads)]
        mirrors = shares(grads, start)
        for h, (grad, mirror) in enumerate(zip(grads, mirrors)):
            gcols = slice(h * size, (h + 1) * size)
            kgcols = slice(part + h * size, part + (h + 1) * size)
            vgcols = slice(2 * part + h * size, 2 * part + (h + 1) * size)
            kcols = slice(width + half * part + h * size, width + half * part + (h + 1) * size)
            dqkv_ref[here, kgcols] = (
                scale * dot(grad, own_qkv[h]) + dot(mirror, relkq_ref[:, kcols])
            ).astype(bf16)
            drel[:, kgcols] += dot(mirror, own_qkv[heads + h, here, :], ((0,), (0,)))
            dqkv_ref[here, vgcols] = dot(
                probs_ref[h, :, here], ga_ref[:, gcols], ((0,), (0,))
            ).astype(bf16)
        return carry

    lax.fori_loop(0, blocks, by_columns, 0)
    keys, queries = drel[:, :part].astype(bf16), drel[:, part:].astype(bf16)
    dqkv_ref[rows:, :part] = queries
    dqkv_ref[rows:, part : 2 * part] = keys
    dqkv_ref[rows:, 2 * part :] = jnp.zeros((lanes, part), bf16)
    if not last:
        return
    for t, target in enumerate((own_ref, far_ref.at[0], core_ref, far_ref.at[1])):
        span = slice(t * lanes, (t + 1) * lanes)
        for k in range(3):
            first = k * width
            target[:, first : first + part] = before_ref[span, k * part : (k + 1) * part]
            target[:, first + part : first + width] = dqkv_ref[span, k * part : (k + 1) * part]
    queries = jnp.concatenate([before_ref[rows:, :part], queries], axis=1)
    keys = jnp.concatenate([before_ref[rows:, part : 2 * part], keys], axis=1)

    docs, small_rows, small_width = small_ref.shape
    per = lanes // docs
    table = (
        dot(keys, wk_ref[...], ((1,), (1,))) + dot(queries, wq_ref[...], ((1,), (1,)))
    ).astype(bf16)
    plain = jnp.concatenate([boxes_before[0:heads], box_sums[0:heads], box_sums[heads + heads : 8]], axis=0)
    less = jnp.concatenate(
        [boxes_before[8 : 8 + heads], box_sums[8 : 8 + heads], box_sums[8 + 2 * heads : 16]], axis=0
    )
    heads = 2 * heads
    place_lane = lax.broadcasted_iota(jnp.int32, (8, lanes), 1)
    later = jnp.where(
        jnp.bitwise_and(place_lane, 63) == 63, 0.0, pltpu.roll(less, lanes - 1, 1)
    )
    boxes = (plain - less + later).astype(bf16)
    row_at = lax.broadcasted_iota(jnp.int32, (8, lanes), 0)
    head_at = at_ref[0] * heads + row_at
    by_head = [
        dot(boxes, ((place_lane == head_at + k * 64) & (row_at < heads)).astype(bf16), ((0,), (0,)))
        for k in range(2)
    ]
    model = table.shape[1]
    edges = list(range(0, model, small_width)) + [model]
    rest = edges[-1] - edges[-2]
    lane = slice(rest, rest + lanes)
    line = (len(edges) - 2) * per
    count = lanes // 2 // docs
    for chunk in range(docs):
        own = slice(chunk * per, (chunk + 1) * per)
        for k, (first, end) in enumerate(zip(edges[:-1], edges[1:])):
            small_ref[chunk, k * per : (k + 1) * per, : end - first] = table[own, first:end].astype(f32)
        for k in range(4):
            small_ref[chunk, line + k : line + k + 1, lane] = (
                sums_ref[k : k + 1, chunk * lanes : (chunk + 1) * lanes]
            )
            first = (chunk * blocks + k) * lanes
            where = first // model
            small_ref[chunk, line + 4 + k : line + 5 + k, lane] = (
                sums_ref[4 + where : 5 + where, first - where * model : first - where * model + lanes]
            )
        begin = chunk * count
        small_ref[chunk, line + 8 : line + 8 + count, lane] = (
            by_head[0][begin : begin + count, :] + by_head[1][64 + begin : 64 + begin + count, :]
        )


def scores_grad_call(half, at, pieces, qkv, probs, relkq, row, col, after, docs=0, extra=()):
    rows = blocks * lanes
    heads = probs.shape[0] // 2
    width = qkv.shape[1] // 3
    part = width // 2
    model = width * blocks
    buckets = relkq.shape[0]
    column = pl.BlockSpec((model, width), lambda i, at: (0, at[0]))
    grads = jax.ShapeDtypeStruct((rows + buckets, 3 * part), bf16)
    box_shape = (16, lanes)
    scratch = [
        pltpu.VMEM((rows, part), bf16),
        pltpu.VMEM((heads, rows, rows), bf16),
        pltpu.VMEM((buckets, 2 * part), f32),
        pltpu.VMEM((3 * heads, rows, part // heads), bf16),
    ]
    extra_specs = []
    if half == 1:
        shapes = (
            grads,
            jax.ShapeDtypeStruct((lanes, 3 * width), bf16),
            jax.ShapeDtypeStruct((lanes, 3 * width), bf16),
            jax.ShapeDtypeStruct((2, lanes, 3 * width), bf16),
            jax.ShapeDtypeStruct((docs, 3 * buckets // docs, 3 * part), f32),
        )
        extra_specs = [column, column, full((8, model)), full(grads.shape), full(box_shape)]
        scratch = scratch + [pltpu.VMEM(box_shape, f32)]
    else:
        shapes = (grads, jax.ShapeDtypeStruct(box_shape, f32))
    at = ordered(at, *after) if after else at
    return pl.pallas_call(
        functools.partial(scores_grad_kernel, half, 0),
        out_shape=shapes,
        grid_spec=pltpu.PrefetchScalarGridSpec(
            num_scalar_prefetch=1,
            grid=(1,),
            in_specs=[rows_of(piece, (lanes, part), lambda i, at: half) for piece in pieces]
            + [
                full((rows, 3 * width)),
                pl.BlockSpec((heads, rows, rows), lambda i, at: (half, 0, 0)),
                full((buckets, 2 * width)),
                full((8, rows)),
                full((rows, 8)),
            ]
            + extra_specs,
            out_specs=[full(shape.shape) for shape in shapes],
            scratch_shapes=scratch,
        ),
        compiler_params=params(18),
        cost_estimate=cost(15),
        name="scores_grad",
    )(at, *map(array_of, pieces), qkv, probs, relkq, row, col, *extra)


def weight_grads_call(at, wholes, after=(), name="weight_grads"):
    count = 1 << len(wholes[0][1])
    chunk = lanes
    per = 2
    steps = count // per
    half = steps // 2

    def chunk_of(bits, which):
        def index(i, at):
            p = lax.rem(i + half, steps) * per + which
            total = 0
            for place, bit in enumerate(bits):
                total = total + jnp.bitwise_and(jnp.right_shift(p, len(bits) - 1 - place), 1) * bit
            return jnp.bitwise_xor(at[1], total)

        return index

    def kernel(at_ref, *refs):
        refs = list(refs)
        take = lambda number: [refs.pop(0) for _ in range(number)]
        ins = []
        for groups, bits, extra in wholes:
            sides = [(take(len(lefts) * per), take(len(rights))) for lefts, rights, _ in groups]
            ins.append((sides, take(per) if extra is not None else []))
        outs = [take(2) for _ in wholes]
        step = pl.program_id(0)
        for (sides, extras), (keep_ref, send_ref) in zip(ins, outs):
            results = []
            for own, right_refs in sides:
                right_all = refs.pop(0)

                @pl.when(step == 0)
                def _(right_refs=right_refs, right_all=right_all):
                    for k, ref in enumerate(right_refs):
                        right_all[k * lanes : (k + 1) * lanes, :] = ref[...]

                left = jnp.concatenate(
                    [
                        jnp.concatenate([own[k + which][...] for which in range(per)], axis=1)
                        for k in range(0, len(own), per)
                    ],
                    axis=0,
                )
                results.append(dot(left, right_all[...], ((0,), (0,))).astype(bf16))
            for target, mine in ((send_ref, step < half), (keep_ref, step >= half)):

                @pl.when(mine)
                def _(target=target, results=results, extras=extras):
                    for which in range(per):
                        first = 0
                        for result in results:
                            end = first + result.shape[1]
                            target[which, :chunk, first:end] = (
                                result[which * chunk : (which + 1) * chunk, :]
                            )
                            first = end
                        if extras:
                            target[which, chunk:, :] = extras[which][...].astype(bf16)

    in_specs, operands, scratch, shapes, out_specs = [], [], [], [], []
    for groups, bits, extra in wholes:
        total_width = sum(width for _, _, width in groups)
        tail = 0 if extra is None else extra.shape[1]
        for lefts, rights, width in groups:
            for handle in lefts:
                for which in range(per):
                    in_specs.append(rows_of(handle, (lanes, chunk), chunk_of(bits, which)))
                    operands.append(array_of(handle))
            for handle in rights:
                column = handle[2] if isinstance(handle, tuple) and len(handle) == 3 else 0
                handle = (
                    handle[:2] if isinstance(handle, tuple) and handle[1] is not None else array_of(handle)
                )
                in_specs.append(rows_of(handle, (lanes, width), lambda i, at, column=column: column))
                operands.append(array_of(handle))
            scratch.append(pltpu.VMEM((len(rights) * lanes, width), bf16))
        for which in range(per if extra is not None else 0):
            index = chunk_of(bits, which)
            in_specs.append(
                pl.BlockSpec(
                    (None, tail, total_width), lambda i, at, index=index: (index(i, at), 0, 0)
                )
            )
            operands.append(extra)
        shapes += [jax.ShapeDtypeStruct((count // 2, chunk + tail, total_width), bf16)] * 2
        block = (per, chunk + tail, total_width)
        out_specs += [
            pl.BlockSpec(block, lambda i, at: (jnp.maximum(i - half, 0), 0, 0)),
            pl.BlockSpec(block, lambda i, at: (jnp.minimum(i, half - 1), 0, 0)),
        ]
    at = ordered(at, *after) if after else at
    out = pl.pallas_call(
        kernel,
        out_shape=tuple(shapes),
        grid_spec=pltpu.PrefetchScalarGridSpec(
            num_scalar_prefetch=1,
            grid=(steps,),
            in_specs=in_specs,
            out_specs=out_specs,
            scratch_shapes=scratch,
        ),
        compiler_params=params(18),
        cost_estimate=cost(0.01),
        name=name,
    )(at, *operands)
    return [tuple(out[k : k + 2]) for k in range(0, len(out), 2)]


def tokens_grad_kernel(at_ref, d0, d1, d2, d3, resid_ref, wq_ref, wk_ref, wv_ref, *refs):
    out_ref = refs[-1]
    step = pl.program_id(0)
    width = wq_ref.shape[1]

    @pl.when(step == 0)
    def _():
        out_ref[...] = resid_ref[...]

    for t, piece in enumerate((d0, d1, d2, d3)):

        @pl.when(step == t)
        def _(piece=piece):
            total = out_ref[...]
            for at, w_ref in enumerate((wq_ref, wk_ref, wv_ref)):
                total = total + dot(
                    piece[:, at * width : (at + 1) * width], w_ref[...], ((1,), (1,))
                )
            out_ref[...] = total


def tokens_grad_call(at, pieces, resid, w_query, w_key, w_value, after):
    rows, model = resid.shape
    width = model // blocks
    tile = (rows, 3 * width)

    def column(i, at):
        offset = jnp.where(i == 1, 2, jnp.where(i == 2, 1, i))
        return (0, jnp.bitwise_xor(at[0], offset))

    weight = pl.BlockSpec((model, width), column)
    at = ordered(at, *after) if after else at
    return pl.pallas_call(
        tokens_grad_kernel,
        out_shape=jax.ShapeDtypeStruct((rows, model), f32),
        grid_spec=pltpu.PrefetchScalarGridSpec(
            num_scalar_prefetch=1,
            grid=(blocks,),
            in_specs=[rows_of(piece, tile) for piece in pieces]
            + [full((rows, model)), weight, weight, weight],
            out_specs=full((rows, model)),
        ),
        compiler_params=params(18),
        cost_estimate=cost(4),
        name="tokens_grad",
    )(at, *map(array_of, pieces), resid, w_query, w_key, w_value)


def parts_kernel(fields, at_ref, *refs):
    step = pl.program_id(0)
    parts, outs = refs[: blocks * fields], refs[blocks * fields :]
    for field in range(fields):
        for at in range(blocks):

            @pl.when(step == at)
            def _(part=parts[field * blocks + at], out=outs[field]):
                out[...] = part[...].astype(f32)


def parts_call(at, fields, name):
    in_specs, operands, shapes, out_specs = [], [], [], []
    for parts, axis in fields:
        rows, width = parts[0].shape
        in_specs += [full((rows, width))] * blocks
        operands += list(parts)
        shape = (rows * blocks, width) if axis == 0 else (rows, width * blocks)
        shapes.append(jax.ShapeDtypeStruct(shape, f32))

        def index(i, at, axis=axis):
            spot = jnp.bitwise_xor(at[0], i)
            return (spot, 0) if axis == 0 else (0, spot)

        out_specs.append(pl.BlockSpec((rows, width), index))
    return pl.pallas_call(
        functools.partial(parts_kernel, len(fields)),
        out_shape=tuple(shapes),
        grid_spec=pltpu.PrefetchScalarGridSpec(
            num_scalar_prefetch=1, grid=(blocks,), in_specs=in_specs, out_specs=out_specs
        ),
        compiler_params=params(18),
        cost_estimate=cost(2),
        name=name,
    )(at, *operands)


def last_kernel(at_ref, *refs):
    step = pl.program_id(0)
    firsts, seconds, outs = refs[:blocks], refs[blocks : 2 * blocks], refs[2 * blocks : 2 * blocks + 3]
    wout_ref, rel_ref, *small_refs = refs[2 * blocks + 3 :]
    norm_refs, (bin_ref, xbox_ref, ybox_ref) = small_refs[:4], small_refs[4:]
    for at in range(blocks):

        @pl.when(step == at)
        def _(first=firsts[at], second=seconds[at]):
            for k, out in enumerate(outs):
                span = slice(k * lanes, (k + 1) * lanes)
                out[:, :lanes] = first[:, span].astype(f32)
                out[:, lanes:] = second[:lanes, span].astype(f32)
            wout_ref[...] = first[:, 3 * lanes :].astype(f32)

    @pl.when(step == 0)
    def _():
        total = seconds[0][lanes:, :].astype(f32)
        for second in seconds[1:]:
            total = total + second[lanes:, :].astype(f32)
        rows = rel_ref.shape[0]
        width = total.shape[1]
        for k in range(3):
            end = min((k + 1) * width, rel_ref.shape[1])
            rel_ref[:, k * width : end] = total[k * rows : (k + 1) * rows, : end - k * width]
        rest = total[2 * rows :, width - lanes :]
        for k in range(4):
            norm_refs[k][...] = rest[k]
            bin_ref[k * lanes : (k + 1) * lanes] = rest[4 + k]
        heads = xbox_ref.shape[1]
        xbox_ref[...] = rest[8:16, :heads]
        ybox_ref[...] = rest[8:16, 64 : 64 + heads]


def last_call(at, firsts, seconds, buckets, model, heads):
    wide = jax.ShapeDtypeStruct((lanes, model), f32)
    small_shapes = ((buckets, model),) + ((lanes,),) * 4 + ((blocks * lanes,), (8, heads), (8, heads))
    column = pl.BlockSpec((lanes, model // blocks), lambda i, at: (0, jnp.bitwise_xor(at[0], i)))
    return pl.pallas_call(
        last_kernel,
        out_shape=(wide, wide, wide, wide)
        + tuple(jax.ShapeDtypeStruct(shape, f32) for shape in small_shapes),
        grid_spec=pltpu.PrefetchScalarGridSpec(
            num_scalar_prefetch=1,
            grid=(blocks,),
            in_specs=[full(part.shape) for part in firsts + seconds],
            out_specs=[column] * 4 + [full(shape) for shape in small_shapes],
        ),
        compiler_params=params(18),
        cost_estimate=cost(2),
        name="last",
    )(at, *firsts, *seconds)


class Halving:
    def __init__(self, halves, bits):
        self.keep, self.send = halves
        self.bits = list(bits)
        self.step()

    def step(self):
        self.came = swap(self.send, "docs", self.bits.pop(0))

    def add(self, *before):
        keep, came = self.keep, self.came
        if before:
            came = ordered(came, *before)
        total = lambda part: (keep[part].astype(f32) + came[part].astype(f32)).astype(bf16)
        if not self.bits:
            self.keep = self.send = total(slice(None))[0]
            return self.keep
        middle = keep.shape[0] // 2
        self.send = total(slice(middle, None))
        self.keep = total(slice(0, middle))
        sent = self.send
        self.step()
        return sent


def shards_tiles(
    tokens, lengths, positions, token_boxes, ln1_gain, ln1_bias, w_query, w_key, w_value, w_out,
    rel_table, xbias_table, ybias_table, ln2_gain, ln2_bias, w_in, b_in, w_down, cotangent,
):
    row_count, model = tokens.shape[1:]
    docs = lax.axis_size("docs")
    place = lax.axis_index("blk")
    doc_place = lax.axis_index("docs")
    heads = xbias_table.shape[1]
    boxes = xbias_table.shape[0]
    units = w_in.shape[1]
    width = model // blocks
    bits = bits_of(docs)
    other = [bits[1], bits[0]] + bits[2:]
    x_own = tokens[0]
    w_query, w_key, w_value = in_hbm(w_query), in_hbm(w_key), in_hbm(w_value)

    x_far = swap(x_own, "blk", 2)
    own_ints = jnp.concatenate(
        [
            positions,
            jnp.right_shift(token_boxes[0] + token_boxes[2], 1),
            jnp.right_shift(token_boxes[1] + token_boxes[3], 1),
            jnp.zeros((5, row_count), jnp.int32),
        ],
        axis=0,
    )
    ints_far = swap(own_ints, "blk", 2)
    x_core, ints_core = swap(x_own, "blk", 1), swap(own_ints, "blk", 1)
    x_both, ints_both = swap(ordered(x_far, ints_far), "blk", 1), swap(ints_far, "blk", 1)
    xs = (in_hbm(x_own), x_far, x_core, x_both)
    tables = jnp.concatenate([xbias_table.T, ybias_table.T], axis=1).astype(f32)
    tables = tables.reshape(blocks, heads // blocks, 2 * boxes)
    at = jnp.stack([place.astype(jnp.int32), lengths[0]])
    spot = jnp.stack([place, doc_place]).astype(jnp.int32)
    att_own, att_core, att_far, probs, qkv, relkq, row, col = scores_call(
        at, xs, (own_ints, ints_far, ints_core, ints_both), w_query, w_key, w_value, rel_table, tables
    )

    came_far = swap(att_far, "blk", 2)
    came_core = swap(att_core, "blk", 1)
    came_both = swap(came_far, "blk", 1)
    line = lambda vector: vector.reshape(1, -1)
    far1, core1, act_own, act, slope, normed1, inverse1, attended, hidden = up_call(
        spot, (att_own, (came_far, 0), came_core, (came_both, 1)), x_own, w_out,
        line(ln1_gain), line(ln1_bias), in_hbm(w_in), line(b_in), docs,
    )
    got_far1 = swap(far1, "blk", 2)
    block_out, mix, grad_ffn, above = down_call(
        act, w_down, normed1, cotangent[0],
        line(ln1_gain), line(ln1_bias), line(ln2_gain), line(ln2_bias), units // docs,
    )
    (
        ga_own, ga_core, ga_far, grad_resid, up_far, up_core, up_own, far3, core3, gattn_own, sums,
    ) = back_call(
        spot, w_down, slope, w_in, w_out, normed1, inverse1, mix, grad_ffn, attended,
        line(ln1_gain), above, hidden, units // docs,
    )
    came_far = swap(ga_far, "blk", 2)
    came_core = swap(ga_core, "blk", 1)
    came_both = swap(came_far, "blk", 1)
    ga_all = (ga_own, (came_far, 0), came_core, (came_both, 1))
    ffn_far = swap(grad_ffn, "blk", 2)
    got_core1, got_both1 = swap(core1, "blk", 1), swap(ordered(got_far1, ga_own), "blk", 1)
    ffn_core, ffn_both = swap(grad_ffn, "blk", 1), swap(ordered(ffn_far, ga_own), "blk", 1)
    act_all = [act_own, (got_far1, 0), got_core1, (got_both1, 1)]
    gffn_all = [grad_ffn, ffn_far, ffn_core, ffn_both]
    (down_halves,) = weight_grads_call(
        spot, [([(act_all, gffn_all, model)], bits, None)], after=[ga_own], name="grad_down"
    )
    down_sum = Halving(down_halves, bits)
    got_far2 = swap(ordered(up_far, came_far), "blk", 2)
    first_grads, first_boxes = scores_grad_call(
        0, spot, ga_all, qkv, probs, relkq, row, col, [down_halves[0]]
    )
    got_core2, got_both2 = swap(up_core, "blk", 1), swap(ordered(got_far2, first_grads), "blk", 1)
    got_far3 = swap(ordered(far3, got_far2), "blk", 2)
    hidden_all = [hidden, (got_far2, 0), (got_core2, 0), (got_both2, 0)]
    up_all = [up_own, (got_far2, 1), (got_core2, 1), (got_both2, 2)]
    (in_halves,) = weight_grads_call(
        spot, [([(hidden_all, up_all, model)], bits, None)], after=[first_grads], name="grad_in"
    )
    in_sum = Halving(in_halves, bits)
    lefts = list(xs) + [rel_table]

    def rows_by_piece(grads):
        return [(grads.reshape(blocks + 1, lanes, -1), t) for t in range(blocks + 1)]

    got_core3, got_both3 = swap(core3, "blk", 1), swap(ordered(got_far3, in_halves[0]), "blk", 1)
    att_all = [far3, got_far3, got_core3, got_both3]
    per = model // width
    gattn_all = [
        gattn_own, (got_far3, None, per), (got_core3, None, per), (got_both3, None, per + 1),
    ]
    done = down_sum.add(in_halves[0])
    early = [done]
    early = [done]
    first_groups = [(lefts, rows_by_piece(first_grads), 3 * width // 2), (att_all, gattn_all, width)]
    (first_halves,) = weight_grads_call(
        spot, [(first_groups, other, None)], after=[in_halves[0]] + early, name="grad_qkv_out"
    )
    first_sum = Halving(first_halves, other)
    second_grads, dq_own, dq_core, dq_far, small = scores_grad_call(
        1, spot, ga_all, qkv, probs, relkq, row, col, [first_halves[0]], docs,
        (w_query, w_key, sums, first_grads, first_boxes),
    )
    done = down_sum.add(second_grads)
    done = in_sum.add(done)
    second_groups = [(lefts, rows_by_piece(second_grads), 3 * width // 2)]
    (second_halves,) = weight_grads_call(
        spot, [(second_groups, bits, small)], after=[done], name="grad_qkv"
    )
    second_sum = Halving(second_halves, bits)
    done = first_sum.add(second_halves[0])
    dq_far_got = ordered(swap(dq_far, "blk", 2), second_halves[0])
    dq_core_got, dq_both_got = swap(dq_core, "blk", 1), swap(dq_far_got, "blk", 1)
    grad_tokens = tokens_grad_call(
        spot, (dq_own, (dq_far_got, 0), dq_core_got, (dq_both_got, 1)), grad_resid,
        w_query, w_key, w_value, [done],
    )

    def whole(part, *before):
        far = swap(part, "blk", 2)
        held = ordered(far, *before) if before else far
        return (part, swap(part, "blk", 1), far, swap(held, "blk", 1))

    done = in_sum.add(grad_tokens)
    done = second_sum.add(done)
    done = down_sum.add(done)
    down_part = done
    done = first_sum.add(done)
    done = in_sum.add(done)
    in_part = done
    done = second_sum.add(done)
    done = first_sum.add(done)
    first_part = done
    done = second_sum.add(done)
    second_part = done
    grad_w_down, grad_w_in = parts_call(
        spot, ((whole(down_part, done), 0), (whole(in_part, done), 1)), "gather_parts"
    )
    *grads, grad_w_out, rel_out, n0, n1, n2, n3, b_in_out, xb, yb = last_call(
        spot, whole(first_part, grad_w_down), whole(second_part, grad_w_down), rel_table.shape[0] // docs, model, heads
    )
    norms = (n0, n1, n2, n3)
    return (
        block_out[None], grad_tokens[None], norms[0], norms[1], grads[0], grads[1], grads[2], grad_w_out,
        rel_out, xb, yb, norms[2], norms[3], grad_w_in, b_in_out, grad_w_down,
    )


def choose(*args):
    docs, parts = lax.axis_size("docs"), lax.axis_size("blk")
    tokens, w_in = args[0], args[15]
    model, units = w_in.shape
    fits = (
        parts == blocks
        and tokens.shape[1] == lanes
        and model // docs == lanes
        and units // docs == parts * lanes
        and docs & (docs - 1) == 0
        and docs > 2
        and units == blocks * model
    )
    return (shards_tiles if fits else shards)(*args)


def solution(mesh):
    rows = P("docs", "blk", None)
    placed = (
        rows, P("docs"), P("docs", "blk"), P(None, "docs", "blk"),
        *([P()] * 14), rows,
    )
    over_docs, over_docs2 = P("docs"), P("docs", None)
    return jax.shard_map(
        choose,
        mesh=mesh,
        in_specs=placed,
        out_specs=(
            rows, rows, over_docs, over_docs, over_docs2, over_docs2, over_docs2, over_docs2,
            over_docs2, over_docs2, over_docs2, over_docs, over_docs, over_docs2, over_docs, over_docs2,
        ),
        check_vma=False,
    )
```
